32 devices in a mesh: seq: 16 (over z, y, core), dp: 2 (over x).
Axes of the slice: x: 2, y: 2, z: 4, core: 2. Of those that a mesh axis runs over, the one named last changes fastest.
Arguments:
- tokens: bfloat16 [2, 2048, 1024], P('dp', 'seq'), may hold values from -6 to 6
- cotangent: bfloat16 [2, 2048, 1024], P('dp', 'seq'), may hold values from -6 to 6
- lengths: int32 [2], replicated, may hold values from 512 to 2048, as said below
- assign: int32 [2], replicated, may hold values from 0 to 1, each once
- w_qkv: bfloat16 [1024, 3072], P(('seq', 'dp')), may hold values from -0.1875 to 0.1875
- qv_bias: bfloat16 [2, 1024], P(None, ('seq', 'dp')), may hold values from -4 to 4
- w_out: bfloat16 [1024, 1024], P(('seq', 'dp')), may hold values from -1.5 to 1.5
- out_bias: bfloat16 [1024], P(('seq', 'dp')), may hold values from -1.5 to 1.5
- w_up: bfloat16 [1024, 4096], P(('seq', 'dp')), may hold values from -0.1875 to 0.1875
- up_bias: bfloat16 [4096], P(('seq', 'dp')), may hold values from -4 to 4
- w_down: bfloat16 [4096, 1024], P(('seq', 'dp')), may hold values from -0.09375 to 0.09375
- down_bias: bfloat16 [1024], P(('seq', 'dp')), may hold values from -3 to 3
- norm_gain: bfloat16 [4, 1024], P(None, ('seq', 'dp')), may hold values from 0.5 to 1.5
- norm_shift: bfloat16 [4, 1024], P(None, ('seq', 'dp')), may hold values from -4 to 4
Outputs:
- output: bfloat16 [2, 2048, 1024], P('dp', 'seq')
- input_grad: bfloat16 [2, 2048, 1024], P('dp', 'seq')
- grad_w_qkv: float32 [1024, 3072], P(('seq', 'dp'))
- grad_qv_bias: float32 [2, 1024], P(None, ('seq', 'dp'))
- grad_w_out: float32 [1024, 1024], P(('seq', 'dp'))
- grad_out_bias: float32 [1024], P(('seq', 'dp'))
- grad_w_up: float32 [1024, 4096], P(('seq', 'dp'))
- grad_up_bias: float32 [4096], P(('seq', 'dp'))
- grad_w_down: float32 [4096, 1024], P(('seq', 'dp'))
- grad_down_bias: float32 [1024], P(('seq', 'dp'))
- grad_norm_gain: float32 [4, 1024], P(None, ('seq', 'dp'))
- grad_norm_shift: float32 [4, 1024], P(None, ('seq', 'dp'))
The draws below stay inside these ranges and needn't reach their ends.
Inputs may be any that keep to these rules, and one draw needn't show every extreme that they name: `lengths`: each sequence's valid positions; some sequence fills its whole slot of 2048. `assign`: every sequence stands in exactly one slot.
All inputs are finite; a program needn't handle non-finite values.
Results may differ from the reference program's by a relative error of at most 0.01.
Values may be sent and summed in bfloat16 or wider, within the bound.
A program may use at most 192 MiB of HBM per device.

```python
import math
import jax
import jax.numpy as jnp
from jax import lax

D = 1024
H = 16
HD = 64
FF = 4096
SLOT = 2048
SEQS = 2


def draw_lengths(key, part):
    first_key, second_key = jax.random.split(jax.random.fold_in(key, 11))
    drawn = jax.random.randint(first_key, (SEQS,), SLOT // 4, SLOT + 1)
    chosen = jax.random.randint(second_key, (), 0, SEQS)
    return drawn.at[chosen].set(SLOT).astype(jnp.int32)


def steps_of(own_key, dims, pieces, least, largest):
    factor_of, own = 1.0, jax.random.fold_in(own_key, 6)
    for position, shards_of in pieces:
        steps = jnp.exp(jax.random.uniform(jax.random.fold_in(own, position), (shards_of,), jnp.float32, least / len(pieces), largest / len(pieces)))
        factor_of = factor_of * jnp.repeat(steps, dims[position] // shards_of).reshape([-1 if axis == position else 1 for axis in range(len(dims))])
    return factor_of


def noise(key, dims, scale, most, cuts=(), held_as=jnp.bfloat16):
    values = jax.random.normal(key, dims, jnp.float32) * scale
    if len(cuts) > 0:
        values = steps_of(key, dims, cuts, -0.22, 0.18) * values
    return jnp.clip(values, min=-most, max=most).astype(held_as)


def setup_inputs(seed: int = 0) -> dict:
    key_of = jax.random.split(jax.random.key(seed), 15)
    tokens = noise(key_of[0], (SEQS, SLOT, D), 1.0, 6.0, ((0, 2), (1, 16)))
    cotangent = noise(key_of[1], (SEQS, SLOT, D), 1.0, 6.0, ((0, 2), (1, 16)))
    lengths = draw_lengths(jax.random.fold_in(key_of[14], 71), 0)
    assign = jax.random.permutation(key_of[3], SEQS).astype(jnp.int32)
    w_qkv = noise(key_of[4], (D, 3 * D), D ** -0.5, 0.1875, ((0, 32),))
    qv_bias = noise(key_of[5], (2, D), 0.3, 4.0, ((1, 32),))
    w_out = noise(key_of[6], (D, D), (D // 64) ** -0.5, 1.5, ((0, 32),))
    out_bias = noise(key_of[7], (D,), 0.1, 1.5, ((0, 32),))
    w_up = noise(key_of[8], (D, FF), D ** -0.5, 0.1875, ((0, 32),))
    up_bias = noise(key_of[9], (FF,), 0.3, 4.0, ((0, 32),))
    w_down = noise(key_of[10], (FF, D), FF ** -0.5, 0.09375, ((0, 32),))
    down_bias = noise(key_of[11], (D,), 0.2, 3.0, ((0, 32),))
    norm_gain = jnp.clip(1.0 + 0.1 * jax.random.normal(key_of[12], (4, D), jnp.float32), 0.5, 1.5).astype(jnp.bfloat16)
    norm_shift = noise(key_of[13], (4, D), 0.3, 4.0, ((1, 32),))
    return {"tokens": tokens, "cotangent": cotangent, "lengths": lengths, "assign": assign, "w_qkv": w_qkv, "qv_bias": qv_bias, "w_out": w_out, "out_bias": out_bias, "w_up": w_up, "up_bias": up_bias, "w_down": w_down, "down_bias": down_bias, "norm_gain": norm_gain, "norm_shift": norm_shift}


RELAX_SCALE = 32.0
NORM_EPSILON = 1e-05
HIGHEST = lax.Precision.HIGHEST

@jax.custom_vjp
def low(v):
    return lax.optimization_barrier(v.astype(jnp.bfloat16)).astype(jnp.float32)

@jax.custom_vjp
def low_back(v):
    return v

def low_keep(v):
    return (low(v), None)

def low_pass(kept, grad):
    return (grad,)

def back_keep(v):
    return (v, None)

def back_low(kept, grad):
    return (low(grad),)
low.defvjp(low_keep, low_pass)
low_back.defvjp(back_keep, back_low)

def both_round(value):
    return low_back(low(value))

def norm_rows(values, gain, shift):
    center = values - lax.optimization_barrier(jnp.mean(values, -1, keepdims=True))
    spread = lax.optimization_barrier(jnp.mean(center * center, -1, keepdims=True))
    return center * lax.rsqrt(spread + NORM_EPSILON) * gain + shift

def product(left, right):
    return jnp.dot(left, right, precision=HIGHEST)

def attention(queries, keys, values, valid):
    block_rows = min(512, SLOT)
    block_count = SLOT // block_rows
    key_heads = keys.reshape(SLOT, H, HD)
    value_heads = values.reshape(SLOT, H, HD)
    key_place = jnp.arange(SLOT, dtype=jnp.int32)
    factor = 1.0 / (RELAX_SCALE * math.sqrt(HD))

    def one_block(inputs):
        query_block, block_first = inputs
        scores = jnp.einsum('qhd,khd->hqk', query_block.reshape(block_rows, H, HD), key_heads, precision=HIGHEST) * factor
        scores = low_back(scores)
        query_place = block_first + jnp.arange(block_rows, dtype=jnp.int32)
        allowed = (key_place[None, :] <= query_place[:, None]) & (key_place[None, :] < valid)
        row_max = lax.optimization_barrier(jnp.max(jnp.where(allowed, scores, -jnp.inf), -1, keepdims=True))
        exp_terms = jnp.exp(jnp.where(allowed, RELAX_SCALE * (scores - row_max), -jnp.inf))
        probs = low(exp_terms / lax.optimization_barrier(jnp.sum(exp_terms, -1, keepdims=True)))
        mixed = jnp.einsum('hqk,khd->qhd', probs, value_heads, precision=HIGHEST)
        return mixed.reshape(block_rows, H * HD)
    block_firsts = jnp.arange(block_count, dtype=jnp.int32) * block_rows
    result = lax.map(jax.checkpoint(one_block), (queries.reshape(block_count, block_rows, H * HD), block_firsts))
    return result.reshape(SLOT, H * HD)

def layer_forward(hidden, weights, valid):
    w_qkv, qv_bias, w_out, out_bias, w_up, up_bias, w_down, down_bias, norm_gain, norm_shift = weights
    first_normed = low(norm_rows(hidden, norm_gain[0], norm_shift[0]))
    projected = product(first_normed, w_qkv)
    queries = both_round(projected[:, :D] + qv_bias[0])
    keys = both_round(projected[:, D:2 * D])
    values = both_round(projected[:, 2 * D:] + qv_bias[1])
    attended = both_round(attention(queries, keys, values, valid))
    branch = low_back(product(attended, w_out) + out_bias)
    middle = hidden + norm_rows(branch, norm_gain[1], norm_shift[1])
    third_normed = low(norm_rows(middle, norm_gain[2], norm_shift[2]))
    up_pre = low_back(product(third_normed, w_up) + up_bias)
    activated = low(jax.nn.gelu(up_pre, approximate=False))
    down_pre = low_back(product(activated, w_down) + down_bias)
    return middle + norm_rows(down_pre, norm_gain[3], norm_shift[3])

def reference(tokens, cotangent, lengths, assign, w_qkv, qv_bias, w_out, out_bias, w_up, up_bias, w_down, down_bias, norm_gain, norm_shift):
    params = tuple((item.astype(jnp.float32) for item in (w_qkv, qv_bias, w_out, out_bias, w_up, up_bias, w_down, down_bias, norm_gain, norm_shift)))
    slot_lengths = lengths[assign].astype(jnp.int32)
    place = jnp.arange(SLOT, dtype=jnp.int32)

    def per_slot(totals, inputs):
        slot_tokens, slot_cotangent, valid = inputs

        def forward_fn(hidden, *weights):
            return layer_forward(hidden, weights, valid)
        result, pull = jax.vjp(forward_fn, slot_tokens.astype(jnp.float32), *params)
        keep_rows = (place < valid).astype(jnp.float32)[:, None]
        grads = pull(slot_cotangent.astype(jnp.float32) * keep_rows)
        totals = tuple((total + grad for total, grad in zip(totals, grads[1:])))
        return (totals, (result.astype(jnp.bfloat16), grads[0].astype(jnp.bfloat16)))
    initial = tuple((jnp.zeros_like(item) for item in params))
    totals, (outputs, input_grads) = lax.scan(per_slot, initial, (tokens, cotangent, slot_lengths))
    return (outputs, input_grads, totals[0], totals[1], totals[2], totals[3], totals[4], totals[5], totals[6], totals[7], totals[8], totals[9])
```

```python
import functools
import math

import jax
import jax.numpy as jnp
from jax import lax
from jax.experimental import pallas as pl
from jax.experimental.pallas import tpu as pltpu
from jax.sharding import PartitionSpec as P


HD = 64


RELAX_SCALE = 32.0
NORM_EPSILON = 1e-05


def norm_rows(values, gain, shift):
    center = values - jnp.mean(values, -1, keepdims=True)
    spread = jnp.mean(center * center, -1, keepdims=True)
    return center * lax.rsqrt(spread + NORM_EPSILON) * gain + shift


def exact_gelu(values):
    return jax.nn.gelu(values, approximate=False)


def contract_rows(left, right):
    return lax.dot_general(
        left, right, (((0,), (0,)), ((), ())), preferred_element_type=jnp.float32
    )


def contract_cols(left, right):
    return lax.dot_general(
        left, right, (((1,), (1,)), ((), ())), preferred_element_type=jnp.float32
    )


def split_heads(block):
    return block.reshape(block.shape[0], 2, HD)


def pair_scores(query_part, key_part):
    factor = 1.0 / (RELAX_SCALE * math.sqrt(HD))
    return (
        jnp.einsum(
            "qhd,khd->hqk",
            split_heads(query_part),
            split_heads(key_part),
            preferred_element_type=jnp.float32,
        )
        * factor
    )


def kept_probs(scores, allowed, row_max, row_total):
    exp_terms = jnp.exp(jnp.where(allowed, RELAX_SCALE * (scores - row_max), -jnp.inf))
    return exp_terms / row_total


def body(
    tokens,
    cotangent,
    lengths,
    assign,
    w_qkv,
    qv_bias,
    w_out,
    out_bias,
    w_up,
    up_bias,
    w_down,
    down_bias,
    norm_gain,
    norm_shift,
):
    gathered = (
        lax.all_gather(w_qkv, ("seq", "dp"), axis=0, tiled=True),
        lax.all_gather(w_out, ("seq", "dp"), axis=0, tiled=True),
        lax.all_gather(w_up, ("seq", "dp"), axis=0, tiled=True),
        lax.all_gather(w_down, ("seq", "dp"), axis=0, tiled=True),
        lax.all_gather(qv_bias, ("seq", "dp"), axis=1, tiled=True),
        lax.all_gather(out_bias, ("seq", "dp"), axis=0, tiled=True),
        lax.all_gather(up_bias, ("seq", "dp"), axis=0, tiled=True),
        lax.all_gather(down_bias, ("seq", "dp"), axis=0, tiled=True),
        lax.all_gather(norm_gain, ("seq", "dp"), axis=1, tiled=True),
        lax.all_gather(norm_shift, ("seq", "dp"), axis=1, tiled=True),
    )
    qkv_full, out_full, up_full, down_full = (gathered[0], gathered[1], gathered[2], gathered[3])
    qv_shift = gathered[4].astype(jnp.float32)
    out_shift = gathered[5].astype(jnp.float32)
    up_shift = gathered[6].astype(jnp.float32)
    down_shift = gathered[7].astype(jnp.float32)
    gains = gathered[8].astype(jnp.float32)
    shifts = gathered[9].astype(jnp.float32)
    row_count = tokens.shape[1]
    model_width = tokens.shape[2]
    pair_cols = 2 * HD
    pair_count = model_width // pair_cols
    slot_rows = row_count * lax.axis_size("seq")
    factor = 1.0 / (RELAX_SCALE * math.sqrt(HD))
    valid = lengths[assign[lax.axis_index("dp")]]
    own_place = lax.axis_index("seq") * row_count + jnp.arange(row_count, dtype=jnp.int32)
    all_place = jnp.arange(slot_rows, dtype=jnp.int32)
    allowed = (all_place[None, :] <= own_place[:, None]) & (all_place[None, :] < valid)
    pair_ids = jnp.arange(pair_count, dtype=jnp.int32)
    hidden = tokens[0].astype(jnp.float32)
    normed_first, pull_first = jax.vjp(norm_rows, hidden, gains[0], shifts[0])
    normed_low = normed_first.astype(jnp.bfloat16)
    projected = jnp.dot(normed_low, qkv_full, preferred_element_type=jnp.float32)
    queries = (projected[:, :model_width] + qv_shift[0]).astype(jnp.bfloat16)
    key_own = projected[:, model_width : 2 * model_width].astype(jnp.bfloat16)
    value_own = (projected[:, 2 * model_width :] + qv_shift[1]).astype(jnp.bfloat16)
    keys, values = (
        lax.all_gather(key_own, "seq", axis=0, tiled=True),
        lax.all_gather(value_own, "seq", axis=0, tiled=True),
    )

    def columns(block, pair_index):
        return lax.dynamic_slice_in_dim(block, pair_index * pair_cols, pair_cols, 1)

    def merge_pairs(stack):
        return stack.transpose(1, 0, 2).reshape(stack.shape[1], model_width)

    def attend(pair_index):
        scores = pair_scores(columns(queries, pair_index), columns(keys, pair_index))
        row_max = jnp.max(jnp.where(allowed, scores, -jnp.inf), -1, keepdims=True)
        exp_terms = jnp.exp(jnp.where(allowed, RELAX_SCALE * (scores - row_max), -jnp.inf))
        row_total = jnp.sum(exp_terms, -1, keepdims=True)
        probs = (exp_terms / row_total).astype(jnp.bfloat16)
        mixed = jnp.einsum(
            "hqk,khd->qhd",
            probs,
            split_heads(columns(values, pair_index)),
            preferred_element_type=jnp.float32,
        )
        return (mixed.reshape(row_count, pair_cols), row_max[..., 0], row_total[..., 0])

    mixed_pairs, max_pairs, total_pairs = lax.map(attend, pair_ids)
    attended = merge_pairs(mixed_pairs).astype(jnp.bfloat16)
    branch = jnp.dot(attended, out_full, preferred_element_type=jnp.float32) + out_shift
    normed_second, pull_second = jax.vjp(norm_rows, branch, gains[1], shifts[1])
    middle = hidden + normed_second
    normed_third, pull_third = jax.vjp(norm_rows, middle, gains[2], shifts[2])
    third_low = normed_third.astype(jnp.bfloat16)
    up_pre = jnp.dot(third_low, up_full, preferred_element_type=jnp.float32) + up_shift
    activated, pull_gelu = jax.vjp(exact_gelu, up_pre)
    active_low = activated.astype(jnp.bfloat16)
    down_pre = jnp.dot(active_low, down_full, preferred_element_type=jnp.float32) + down_shift
    normed_fourth, pull_fourth = jax.vjp(norm_rows, down_pre, gains[3], shifts[3])
    output = (middle + normed_fourth).astype(jnp.bfloat16)[None]
    again = (
        lax.all_gather(w_qkv, ("seq", "dp"), axis=0, tiled=True),
        lax.all_gather(w_out, ("seq", "dp"), axis=0, tiled=True),
        lax.all_gather(w_up, ("seq", "dp"), axis=0, tiled=True),
        lax.all_gather(w_down, ("seq", "dp"), axis=0, tiled=True),
    )
    qkv_back, out_back, up_back, down_back = (again[0], again[1], again[2], again[3])
    keep_rows = (own_place < valid).astype(jnp.float32)[:, None]
    grad_out = cotangent[0].astype(jnp.float32) * keep_rows
    grad_down, grad_gain_four, grad_shift_four = pull_fourth(grad_out)
    grad_down_low = grad_down.astype(jnp.bfloat16)
    grad_w_down = contract_rows(active_low, grad_down_low)
    grad_b_down = jnp.sum(grad_down_low.astype(jnp.float32), 0)
    (grad_up,) = pull_gelu(contract_cols(grad_down_low, down_back))
    grad_up_low = grad_up.astype(jnp.bfloat16)
    grad_w_up = contract_rows(third_low, grad_up_low)
    grad_b_up = jnp.sum(grad_up_low.astype(jnp.float32), 0)
    grad_middle_part, grad_gain_three, grad_shift_three = pull_third(
        contract_cols(grad_up_low, up_back)
    )
    grad_middle = grad_out + grad_middle_part
    grad_branch, grad_gain_two, grad_shift_two = pull_second(grad_middle)
    grad_branch_low = grad_branch.astype(jnp.bfloat16)
    grad_w_out = contract_rows(attended, grad_branch_low)
    grad_b_out = jnp.sum(grad_branch_low.astype(jnp.float32), 0)
    grad_attended = contract_cols(grad_branch_low, out_back).astype(jnp.bfloat16)

    def query_side(pair_index):
        scores = pair_scores(columns(queries, pair_index), columns(keys, pair_index))
        probs = kept_probs(
            scores, allowed, max_pairs[pair_index][..., None], total_pairs[pair_index][..., None]
        )
        grad_part = columns(grad_attended, pair_index)
        grad_probs = jnp.einsum(
            "qhd,khd->hqk",
            split_heads(grad_part),
            split_heads(columns(values, pair_index)),
            preferred_element_type=jnp.float32,
        )
        delta = jnp.sum(probs * grad_probs, -1, keepdims=True)
        grad_scores = (RELAX_SCALE * probs * (grad_probs - delta)).astype(jnp.bfloat16)
        grad_query = (
            jnp.einsum(
                "hqk,khd->qhd",
                grad_scores,
                split_heads(columns(keys, pair_index)),
                preferred_element_type=jnp.float32,
            )
            * factor
        )
        return (grad_query.reshape(row_count, pair_cols), grad_scores, probs, delta)

    def both_sides(pair_index):
        grad_query, grad_scores, probs, delta = query_side(pair_index)
        grad_part = columns(grad_attended, pair_index)
        grad_key = (
            jnp.einsum(
                "hqk,qhd->khd",
                grad_scores,
                split_heads(columns(queries, pair_index)),
                preferred_element_type=jnp.float32,
            )
            * factor
        )
        grad_value = jnp.einsum(
            "hqk,qhd->khd",
            probs.astype(jnp.bfloat16),
            split_heads(grad_part),
            preferred_element_type=jnp.float32,
        )
        return (
            grad_query,
            grad_key.reshape(slot_rows, pair_cols),
            grad_value.reshape(slot_rows, pair_cols),
        )

    query_pairs, key_terms, value_terms = lax.map(both_sides, pair_ids)
    key_pairs, value_pairs = (
        lax.psum_scatter(
            key_terms.astype(jnp.bfloat16), "seq", scatter_dimension=1, tiled=True
        ).astype(jnp.float32),
        lax.psum_scatter(
            value_terms.astype(jnp.bfloat16), "seq", scatter_dimension=1, tiled=True
        ).astype(jnp.float32),
    )
    grad_q_low = merge_pairs(query_pairs).astype(jnp.bfloat16)
    grad_k_low = merge_pairs(key_pairs).astype(jnp.bfloat16)
    grad_v_low = merge_pairs(value_pairs).astype(jnp.bfloat16)
    grad_projected = jnp.concatenate([grad_q_low, grad_k_low, grad_v_low], 1)
    grad_w_qkv = contract_rows(normed_low, grad_projected)
    grad_qv = jnp.stack(
        [jnp.sum(grad_q_low.astype(jnp.float32), 0), jnp.sum(grad_v_low.astype(jnp.float32), 0)]
    )
    grad_hidden_part, grad_gain_one, grad_shift_one = pull_first(
        contract_cols(grad_projected, qkv_back)
    )
    input_grad = (grad_middle + grad_hidden_part).astype(jnp.bfloat16)[None]
    grad_gains = jnp.stack([grad_gain_one, grad_gain_two, grad_gain_three, grad_gain_four])
    grad_shifts = jnp.stack([grad_shift_one, grad_shift_two, grad_shift_three, grad_shift_four])
    owned = (
        lax.psum_scatter(grad_w_qkv, ("seq", "dp"), scatter_dimension=0, tiled=True),
        lax.psum_scatter(grad_w_out, ("seq", "dp"), scatter_dimension=0, tiled=True),
        lax.psum_scatter(grad_w_up, ("seq", "dp"), scatter_dimension=0, tiled=True),
        lax.psum_scatter(grad_w_down, ("seq", "dp"), scatter_dimension=0, tiled=True),
        lax.psum_scatter(grad_qv, ("seq", "dp"), scatter_dimension=1, tiled=True),
        lax.psum_scatter(grad_b_out, ("seq", "dp"), scatter_dimension=0, tiled=True),
        lax.psum_scatter(grad_b_up, ("seq", "dp"), scatter_dimension=0, tiled=True),
        lax.psum_scatter(grad_b_down, ("seq", "dp"), scatter_dimension=0, tiled=True),
        lax.psum_scatter(grad_gains, ("seq", "dp"), scatter_dimension=1, tiled=True),
        lax.psum_scatter(grad_shifts, ("seq", "dp"), scatter_dimension=1, tiled=True),
    )
    return (
        output,
        input_grad,
        owned[0],
        owned[4],
        owned[1],
        owned[5],
        owned[2],
        owned[6],
        owned[3],
        owned[7],
        owned[8],
        owned[9],
    )


MESH = pl.DeviceIdType.MESH

def place():
    seq = lax.axis_index("seq")
    x = lax.axis_index("dp")
    return seq // 4, (seq // 2) % 2, seq % 2, x

def device(z, y, c, x):
    return (z * 4 + y * 2 + c, x)

def entry_barrier():
    z, y, c, x = place()
    barrier = pltpu.get_barrier_semaphore()
    def signal(dev):
        pl.semaphore_signal(barrier, inc=1, device_id=dev, device_id_type=MESH)
    signal(device(z, y, 1 - c, x))
    signal(device(z, 1 - y, c, x))
    signal(device(z, y, c, 1 - x))
    @pl.when(z > 0)
    def _(): signal(device(z - 1, y, c, x))
    @pl.when(z < 3)
    def _(): signal(device(z + 1, y, c, x))
    pl.semaphore_wait(barrier, 3 + (z + 2) // 3 + (5 - z) // 3)

def gather_kernel(split, *refs):
    n = len(split)
    srcs, outs = refs[:n], refs[n:2 * n]
    send_sem, recv_sem, core_sem, own_sem = refs[2 * n:]
    z, y, c, x = place()
    entry_barrier()

    def chunk(w, s, zz, yy, xx):
        if split[w]:
            return outs[w].at[zz, yy, s, xx]
        return outs[w].at[zz, yy, xx, s]

    def copy(w, s, zz, yy, xx, dev, slot):
        return pltpu.make_async_remote_copy(
            src_ref=chunk(w, s, zz, yy, xx), dst_ref=chunk(w, s, zz, yy, xx),
            send_sem=send_sem.at[w, s, slot], recv_sem=recv_sem.at[w, s, zz * 4 + yy * 2 + xx],
            device_id=dev, device_id_type=MESH)

    def lateral(s):
        if s == 0:
            return (1 - y, x), device(z, 1 - y, c, x), device(z, y, c, 1 - x)
        return (y, 1 - x), device(z, y, c, 1 - x), device(z, 1 - y, c, x)

    up, down = device(z + 1, y, c, x), device(z - 1, y, c, x)

    for w in range(n):
        if split[w]:
            pltpu.make_async_remote_copy(
                src_ref=srcs[w].at[1 - c], dst_ref=outs[w].at[z, y, c, x],
                send_sem=core_sem.at[w, 0], recv_sem=core_sem.at[w, 1],
                device_id=device(z, y, 1 - c, x), device_id_type=MESH).start()
            pltpu.make_async_copy(srcs[w].at[c], outs[w].at[z, y, c, x], own_sem.at[w]).start()
        else:
            pltpu.make_async_copy(srcs[w], outs[w].at[z, y, x], own_sem.at[w]).start()

    def first_wait(w):
        if split[w]:
            pltpu.make_async_copy(srcs[w].at[c], outs[w].at[z, y, c, x], own_sem.at[w]).wait()
            pltpu.make_async_remote_copy(
                src_ref=srcs[w].at[1 - c], dst_ref=outs[w].at[z, y, 1 - c, x],
                send_sem=core_sem.at[w, 0], recv_sem=core_sem.at[w, 1],
                device_id=device(z, y, 1 - c, x), device_id_type=MESH).wait()
        else:
            pltpu.make_async_copy(srcs[w], outs[w].at[z, y, x], own_sem.at[w]).wait()

    for w in range(n):
        first_wait(w)
        for s in range(2):
            lat, one, two = lateral(s)
            @pl.when(z < 3)
            def _(): copy(w, s, z, y, x, up, z).start()
            @pl.when(z > 0)
            def _(): copy(w, s, z, y, x, down, 4 + z).start()
            copy(w, s, z, y, x, one, 8 + z).start()
            copy(w, s, z, y, x, two, 12 + z).start()

    def pass_on(w, s, zz):
        lat, one, two = lateral(s)
        copy(w, s, zz, lat[0], lat[1], one, 8 + zz).wait_recv()
        copy(w, s, zz, lat[0], lat[1], two, 16 + zz).start()

    def step(d, _):
        for w in range(n):
            for s in range(2):
                lat, one, two = lateral(s)
                @pl.when(z >= d)
                def _():
                    zz = z - d
                    copy(w, s, zz, y, x, up, zz).wait_recv()
                    @pl.when(z < 3)
                    def _(): copy(w, s, zz, y, x, up, zz).start()
                    copy(w, s, zz, y, x, one, 8 + zz).start()
                    copy(w, s, zz, y, x, two, 12 + zz).start()
                @pl.when(z + d <= 3)
                def _():
                    zz = z + d
                    copy(w, s, zz, y, x, down, 4 + zz).wait_recv()
                    @pl.when(z > 0)
                    def _(): copy(w, s, zz, y, x, down, 4 + zz).start()
                    copy(w, s, zz, y, x, one, 8 + zz).start()
                    copy(w, s, zz, y, x, two, 12 + zz).start()
                @pl.when(d == 1)
                def _():
                    pass_on(w, s, z)
                @pl.when((d > 1) & (z >= d - 1))
                def _(): pass_on(w, s, z - d + 1)
                @pl.when((d > 1) & (z + d - 1 <= 3))
                def _(): pass_on(w, s, z + d - 1)
        return 0
    lax.fori_loop(1, 4, step, 0)
    for w in range(n):
        for s in range(2):
            @pl.when(z == 3)
            def _(): pass_on(w, s, 0)
            @pl.when(z == 0)
            def _(): pass_on(w, s, 3)

    def finish(zz, _):
        for w in range(n):
            for s in range(2):
                lat, one, two = lateral(s)
                other = (1 - lat[0], 1 - lat[1])
                copy(w, s, zz, other[0], other[1], two, 12 + zz).wait_recv()
                copy(w, s, zz, 1 - y, 1 - x, two, 16 + zz).wait_recv()
                @pl.when((zz <= z) & (z < 3))
                def _(): copy(w, s, zz, y, x, up, zz).wait_send()
                @pl.when((zz >= z) & (z > 0))
                def _(): copy(w, s, zz, y, x, down, 4 + zz).wait_send()
                copy(w, s, zz, y, x, one, 8 + zz).wait_send()
                copy(w, s, zz, y, x, two, 12 + zz).wait_send()
                copy(w, s, zz, lat[0], lat[1], two, 16 + zz).wait_send()
        return 0
    lax.fori_loop(0, 4, finish, 0)

def gather(split, srcs, cid):
    n = len(srcs)
    outs = []
    for sp, a in zip(split, srcs):
        outs.append(jax.ShapeDtypeStruct((4, 2, 2, 2) + a.shape[1:], a.dtype))
    anyspec = pl.BlockSpec(memory_space=pl.ANY)
    return pl.pallas_call(
        functools.partial(gather_kernel, tuple(split)),
        out_shape=tuple(outs),
        in_specs=[pl.BlockSpec(memory_space=pltpu.VMEM)] * n,
        out_specs=(anyspec,) * n,
        scratch_shapes=[pltpu.SemaphoreType.DMA((n, 2, 20)), pltpu.SemaphoreType.DMA((n, 2, 16)),
                        pltpu.SemaphoreType.DMA((n, 2)), pltpu.SemaphoreType.DMA((n,))],
        compiler_params=pltpu.CompilerParams(collective_id=cid, has_side_effects=True, vmem_limit_bytes=48 << 20),
        name="gather",
    )(*srcs)

def reduce_kernel(split, *refs):
    n = len(split)
    terms, outs = refs[:n], refs[n:2 * n]
    r1, s2, r2, tz, ru, rd = (refs[(2 + k) * n:(3 + k) * n] for k in range(6))
    send_sem, recv_sem, core_sem = refs[8 * n:8 * n + 3]
    z, y, c, x = place()
    entry_barrier()
    up, down = device(z + 1, y, c, x), device(z - 1, y, c, x)

    def term(w, s, zz, l1, l2):
        yy, xx = (l1, l2) if s == 0 else (l2, l1)
        if split[w]:
            return terms[w].at[zz, yy, s, xx]
        return terms[w].at[zz, yy, xx, s]

    def own(s):
        return (y, x) if s == 0 else (x, y)

    def one_two(s):
        a, b = device(z, 1 - y, c, x), device(z, y, c, 1 - x)
        return (a, b) if s == 0 else (b, a)

    def remote(src, dst, w, s, send, recv, dev):
        return pltpu.make_async_remote_copy(
            src_ref=src, dst_ref=dst, send_sem=send_sem.at[w, s, send], recv_sem=recv_sem.at[w, s, recv],
            device_id=dev, device_id_type=MESH)

    def copy1(w, s, zz, l1):
        return remote(term(w, s, zz, l1, 1 - own(s)[1]), r1[w].at[s, zz, l1], w, s, zz * 2 + l1, zz * 2 + l1, one_two(s)[1])

    def copy2(w, s, zz):
        return remote(s2[w].at[s, zz], r2[w].at[s, zz], w, s, 8 + zz, 8 + zz, one_two(s)[0])

    def copy_up(w, s, zz):
        return remote(tz[w].at[s, zz], ru[w].at[s, zz], w, s, 12 + zz, 12 + zz, up)

    def copy_down(w, s, zz):
        return remote(tz[w].at[s, zz], rd[w].at[s, zz], w, s, 12 + zz, 16 + zz, down)

    f32 = jnp.float32
    order = (3, 0, 2, 1)

    def stage1(w):
        for zz in order:
            for s in range(2):
                copy1(w, s, zz, 1 - own(s)[0]).start()
        for zz in order:
            for s in range(2):
                copy1(w, s, zz, own(s)[0]).start()

    def stage2(w):
        for zz in order:
            for s in range(2):
                o1, o2 = own(s)
                copy1(w, s, zz, 1 - o1).wait_recv()
                total = term(w, s, zz, 1 - o1, o2)[...].astype(f32) + r1[w][s, zz, 1 - o1].astype(f32)
                s2[w][s, zz] = total.astype(s2[w].dtype)
                copy2(w, s, zz).start()

    def local(w, s, zz):
        o1, o2 = own(s)
        copy1(w, s, zz, o1).wait_recv()
        copy2(w, s, zz).wait_recv()
        return term(w, s, zz, o1, o2)[...].astype(f32) + r1[w][s, zz, o1].astype(f32) + r2[w][s, zz].astype(f32)

    def stage3(w):
        for zz in order:
            for s in range(2):
                @pl.when(zz > z)
                def _():
                    tz[w][s, zz] = local(w, s, zz).astype(tz[w].dtype)
                    @pl.when(z > 0)
                    def _():
                        copy_up(w, s, zz).wait_recv()
                        tz[w][s, zz] = (tz[w][s, zz].astype(f32) + ru[w][s, zz].astype(f32)).astype(tz[w].dtype)
                    copy_up(w, s, zz).start()
                @pl.when(zz < z)
                def _():
                    tz[w][s, zz] = local(w, s, zz).astype(tz[w].dtype)
                    @pl.when(z < 3)
                    def _():
                        copy_down(w, s, zz).wait_recv()
                        tz[w][s, zz] = (tz[w][s, zz].astype(f32) + rd[w][s, zz].astype(f32)).astype(tz[w].dtype)
                    copy_down(w, s, zz).start()

    def last(w):
        for s in range(2):
            total = local(w, s, z)
            slot = c if split[w] else s
            @pl.when(z > 0)
            def _(): copy_up(w, s, z).wait_recv()
            @pl.when(z < 3)
            def _(): copy_down(w, s, z).wait_recv()
            below = jnp.where(z > 0, ru[w][s, z].astype(f32), 0.0)
            above = jnp.where(z < 3, rd[w][s, z].astype(f32), 0.0)
            total = total + below + above
            if split[w]:
                @pl.when(c == s)
                def _(): outs[w][slot] = total
                @pl.when(c != s)
                def _():
                    core_stage(w)[...] = total
                    core_copy(w).start()
            else:
                outs[w][s] = total

    cores = refs[8 * n + 3:]
    def core_stage(w):
        return cores[w]
    def core_copy(w):
        return pltpu.make_async_remote_copy(
            src_ref=cores[w], dst_ref=outs[w].at[c], send_sem=core_sem.at[w, 0], recv_sem=core_sem.at[w, 1],
            device_id=device(z, y, 1 - c, x), device_id_type=MESH)

    stages = (stage1, stage2, stage3, last)
    for t in range(n + 3):
        for k, stage in enumerate(stages):
            if 0 <= t - k < n:
                stage(t - k)
    for w in range(n):
        if split[w]:
            pltpu.make_async_remote_copy(
                src_ref=cores[w], dst_ref=outs[w].at[1 - c], send_sem=core_sem.at[w, 0], recv_sem=core_sem.at[w, 1],
                device_id=device(z, y, 1 - c, x), device_id_type=MESH).wait()
    def finish(zz, _):
        for w in range(n):
            for s in range(2):
                copy1(w, s, zz, 0).wait_send()
                copy1(w, s, zz, 1).wait_send()
                copy2(w, s, zz).wait_send()
                @pl.when(zz > z)
                def _(): copy_up(w, s, zz).wait_send()
                @pl.when(zz < z)
                def _(): copy_down(w, s, zz).wait_send()
        return 0
    lax.fori_loop(0, 4, finish, 0)

def reduce_terms(split, terms, cid):
    n = len(terms)
    tiles = [t.shape[4:] for t in terms]
    V = lambda shape, dt: pltpu.VMEM(shape, dt)
    scratch = []
    for lead in ((2, 4, 2), (2, 4), (2, 4), (2, 4), (2, 4), (2, 4)):
        scratch += [V(lead + t, a.dtype) for t, a in zip(tiles, terms)]
    scratch += [pltpu.SemaphoreType.DMA((n, 2, 16)), pltpu.SemaphoreType.DMA((n, 2, 20)), pltpu.SemaphoreType.DMA((n, 2))]
    scratch += [V(t if sp else (8, 128), jnp.float32) for sp, t in zip(split, tiles)]
    vm = pl.BlockSpec(memory_space=pltpu.VMEM)
    return pl.pallas_call(
        functools.partial(reduce_kernel, tuple(split)),
        out_shape=tuple(jax.ShapeDtypeStruct((2,) + t, jnp.float32) for t in tiles),
        in_specs=[vm] * n, out_specs=(vm,) * n, scratch_shapes=scratch,
        compiler_params=pltpu.CompilerParams(collective_id=cid, has_side_effects=True, vmem_limit_bytes=60 << 20),
        name="reduce_terms",
    )(*terms)


def is_small(mesh):
    return mesh.shape["seq"] == 16 and mesh.shape["dp"] == 2


def exchange_kernel(src, out, send_sem, recv_sem, own_sem):
    z, y, c, x = place()
    me = z * 2 + y
    barrier = pltpu.get_barrier_semaphore()

    def peer(k):
        other = lax.rem(me + k, 8)
        return other, device(other // 2, other % 2, c, x)

    for k in range(1, 8):
        pl.semaphore_signal(barrier, inc=1, device_id=peer(k)[1], device_id_type=MESH)
    own = pltpu.make_async_copy(src.at[me], out.at[me], own_sem)
    own.start()
    pl.semaphore_wait(barrier, 7)

    def copy(k):
        other, dev = peer(k)
        return pltpu.make_async_remote_copy(
            src_ref=src.at[other], dst_ref=out.at[me], send_sem=send_sem.at[k], recv_sem=recv_sem.at[8 - k],
            device_id=dev, device_id_type=MESH)

    for k in (4, 3, 5, 2, 6, 1, 7):
        copy(k).start()
    own.wait()
    for k in range(1, 8):
        other, dev = peer(k)
        pltpu.make_async_remote_copy(
            src_ref=src.at[other], dst_ref=out.at[other], send_sem=send_sem.at[k], recv_sem=recv_sem.at[k],
            device_id=dev, device_id_type=MESH).wait_recv()
    for k in range(1, 8):
        copy(k).wait_send()


def exchange(blocks, cid):
    vm = pl.BlockSpec(memory_space=pltpu.VMEM)
    return pl.pallas_call(
        exchange_kernel, out_shape=jax.ShapeDtypeStruct(blocks.shape, blocks.dtype),
        in_specs=[vm], out_specs=vm,
        scratch_shapes=[pltpu.SemaphoreType.DMA((8,)), pltpu.SemaphoreType.DMA((8,)), pltpu.SemaphoreType.DMA],
        compiler_params=pltpu.CompilerParams(collective_id=cid, has_side_effects=True),
        name="exchange",
    )(blocks)


def dot_nt(a, b):
    return lax.dot_general(a, b, (((1,), (1,)), ((), ())), preferred_element_type=jnp.float32)


def dot_nn(a, b):
    return jnp.dot(a, b, preferred_element_type=jnp.float32)


BQ = 256
MASKED = -1e30


def load_heads(valid, packed, q_ref, k_ref):
    rows = q_ref.shape[0]
    qk = packed[:, :256].reshape(rows, 128)
    kq = jnp.concatenate([qk[:, 64:], qk[:, :64]], axis=1)
    lane = lax.broadcasted_iota(jnp.int32, (rows, 128), 1)
    spot = lax.broadcasted_iota(jnp.int32, (rows, 128), 0)
    past = jnp.where(spot < valid, 0.0, MASKED)
    q_ref[...] = jnp.where(lane < 64, qk.astype(jnp.float32), jnp.where(lane == 64, 1.0, 0.0)).astype(jnp.bfloat16)
    k_ref[...] = jnp.where(lane < 64, kq.astype(jnp.float32), jnp.where(lane == 64, past, 0.0)).astype(jnp.bfloat16)


def unpack_rows(halves):
    n = halves.shape[0]
    return jnp.concatenate([halves[:, :, :64], halves[:, :, 64:]], axis=1).reshape(n * 256, 64)


def block_probs(q_ref, k_ref, i):
    n = (i + 1) * BQ
    scores = dot_nt(k_ref[:n], q_ref[i * BQ:n])
    key = lax.broadcasted_iota(jnp.int32, (BQ, BQ), 0)
    query = lax.broadcasted_iota(jnp.int32, (BQ, BQ), 1)
    corner = jnp.where(key <= query, scores[n - BQ:], MASKED)
    scores = jnp.concatenate([scores[:n - BQ], corner], axis=0) if i else corner
    top = jnp.max(scores, axis=0, keepdims=True)
    terms = jnp.exp((scores - top) * 0.125)
    return terms, 1.0 / jnp.sum(terms, axis=0, keepdims=True)


def attend_kernel(valid_ref, packed, out_ref, q_ref, k_ref, vt_ref):
    load_heads(valid_ref[0], packed, q_ref, k_ref)
    unit = jnp.where(
        lax.broadcasted_iota(jnp.int32, (64, 64), 0) == lax.broadcasted_iota(jnp.int32, (64, 64), 1), 1.0, 0.0
    ).astype(jnp.bfloat16)
    vt_ref[...] = dot_nt(unit, unpack_rows(packed[:, 256:])).astype(jnp.bfloat16)
    for i in range(q_ref.shape[0] // BQ):
        n = (i + 1) * BQ
        terms, scale = block_probs(q_ref, k_ref, i)
        probs = (terms * scale).astype(jnp.bfloat16)
        mixed = dot_nn(vt_ref[:, :n], probs).T
        out_ref[i] = jnp.concatenate([mixed[:128], mixed[128:]], axis=1).astype(jnp.bfloat16)


def attend_back_kernel(valid_ref, packed, grad, out_ref, q_ref, k_ref, v_ref, g_ref, kt_ref, dk_ref, dv_ref):
    load_heads(valid_ref[0], packed, q_ref, k_ref)
    v_ref[...] = unpack_rows(packed[:, 256:])
    g_ref[...] = unpack_rows(grad[...])
    unit = jnp.where(
        lax.broadcasted_iota(jnp.int32, (64, 128), 0) == lax.broadcasted_iota(jnp.int32, (64, 128), 1), 1.0, 0.0
    ).astype(jnp.bfloat16)
    kt_ref[...] = dot_nt(unit, k_ref[...]).astype(jnp.bfloat16)
    dk_ref[...] = jnp.zeros_like(dk_ref)
    dv_ref[...] = jnp.zeros_like(dv_ref)
    blocks = q_ref.shape[0] // BQ
    for i in range(blocks):
        n = (i + 1) * BQ
        terms, scale = block_probs(q_ref, k_ref, i)
        probs = terms * scale
        grad_probs = dot_nt(v_ref[:n], g_ref[i * BQ:n])
        delta = jnp.sum(probs * grad_probs, axis=0, keepdims=True)
        grad_scores = (probs * (grad_probs - delta)).astype(jnp.bfloat16)
        grad_query = dot_nn(kt_ref[:, :n], grad_scores).T * 0.125
        out_ref[i, :256, :64] = grad_query.astype(jnp.bfloat16)
        dk_ref[:n] += dot_nn(grad_scores, q_ref[i * BQ:n])
        dv_ref[:n] += dot_nn(probs.astype(jnp.bfloat16), g_ref[i * BQ:n])
    for i in range(blocks):
        rows = slice(i * BQ, (i + 1) * BQ)
        out_ref[i, :256, 64:] = (dk_ref[rows, :64] * 0.125).astype(jnp.bfloat16)
        value = dv_ref[rows].astype(jnp.bfloat16)
        out_ref[i, 256:] = jnp.concatenate([value[:128], value[128:]], axis=1)


def attend(valid, packed):
    rows = packed.shape[0] * 256
    vm = pl.BlockSpec(memory_space=pltpu.VMEM)
    return pl.pallas_call(
        attend_kernel,
        out_shape=jax.ShapeDtypeStruct((packed.shape[0], 128, 128), jnp.bfloat16),
        in_specs=[pl.BlockSpec(memory_space=pltpu.SMEM), vm], out_specs=vm,
        scratch_shapes=[pltpu.VMEM((rows, 128), jnp.bfloat16)] * 2 + [pltpu.VMEM((64, rows), jnp.bfloat16)],
        compiler_params=pltpu.CompilerParams(vmem_limit_bytes=48 << 20),
        name="attend",
    )(valid, packed)


def attend_back(valid, packed, grad):
    rows = packed.shape[0] * 256
    vm = pl.BlockSpec(memory_space=pltpu.VMEM)
    return pl.pallas_call(
        attend_back_kernel,
        out_shape=jax.ShapeDtypeStruct(packed.shape, jnp.bfloat16),
        in_specs=[pl.BlockSpec(memory_space=pltpu.SMEM), vm, vm], out_specs=vm,
        scratch_shapes=[pltpu.VMEM((rows, 128), jnp.bfloat16)] * 2 + [pltpu.VMEM((rows, 64), jnp.bfloat16)] * 2
        + [pltpu.VMEM((64, rows), jnp.bfloat16), pltpu.VMEM((rows, 128), jnp.float32), pltpu.VMEM((rows, 64), jnp.float32)],
        compiler_params=pltpu.CompilerParams(vmem_limit_bytes=48 << 20),
        name="attend_back",
    )(valid, packed, grad)


def by_parity(weight, width):
    rows, cols = weight.shape
    return weight.reshape(rows, cols // (2 * width), 2, width).transpose(2, 0, 1, 3).reshape(2, rows, cols // 2)


def from_parity(halves, width):
    _, rows, cols = halves.shape
    return halves.reshape(2, rows, cols // width, width).transpose(1, 2, 0, 3).reshape(rows, 2 * cols)


def pack_half_rows(block):
    return block.reshape(2, 128, 8, HD).transpose(2, 1, 0, 3).reshape(8, 128, 128)


def unpack_half_rows(packed):
    return packed.reshape(8, 128, 2, HD).transpose(2, 1, 0, 3).reshape(256, 8 * HD)


def fast_body(tokens, cotangent, lengths, assign, w_qkv, qv_bias, w_out, out_bias, w_up, up_bias, w_down, down_bias,
              norm_gain, norm_shift):
    bf16, f32 = jnp.bfloat16, jnp.float32
    z, y, c, x = place()
    rows, width = tokens.shape[1:]
    valid = lengths[assign[x]].astype(jnp.int32)

    small = jnp.concatenate([qv_bias, out_bias[None], down_bias[None], norm_gain, norm_shift], 0).astype(f32)
    small = jnp.concatenate([jnp.pad(small, ((0, 0), (0, 96))), up_bias.astype(f32)[None], jnp.zeros((3, 128), f32)], 0)
    split = (True, True, False, True, False)
    gathered = gather(split, [
        jnp.stack([small, small]), by_parity(w_qkv, HD), w_out.reshape(2, -1, width),
        by_parity(w_up, 256), w_down.reshape(2, -1, width)], 0)
    small_all = gathered[0].reshape(32, 16, 128)
    vectors = small_all[:, :12, :32].transpose(1, 0, 2).reshape(12, width)
    qv_half = vectors[:2].reshape(2, 8, 2, HD)
    qv_half = jnp.where(c == 0, qv_half[:, :, 0], qv_half[:, :, 1]).reshape(2, 512)
    out_full, down_full, gains, shifts = vectors[2], vectors[3], vectors[4:8], vectors[8:12]
    up_half = small_all[:, 12].reshape(8, 2, 256)
    up_half = jnp.where(c == 0, up_half[:, 0], up_half[:, 1]).reshape(2048)
    wq = gathered[1].reshape(width, 1536)
    wo = gathered[2].reshape(512, width)
    wu = gathered[3].reshape(width, 2048)
    wd = gathered[4].reshape(2048, width)

    swap = [(i, i ^ 1) for i in range(16)]

    def both_cores(block):
        other = lax.ppermute(block, "seq", swap)
        return jnp.concatenate([jnp.where(c == 0, block, other), jnp.where(c == 0, other, block)], 0)

    def core_sum(part):
        return part + lax.ppermute(part, "seq", swap)

    hidden = both_cores(tokens[0]).astype(f32)
    cot = both_cores(cotangent[0]).astype(f32)
    spot = (z * 2 + y) * 256 + jnp.arange(256, dtype=jnp.int32)

    first, pull_first = jax.vjp(norm_rows, hidden, gains[0], shifts[0])
    first = first.astype(bf16)
    projected = dot_nn(first, wq)
    q = (projected[:, :512] + qv_half[0]).astype(bf16)
    k = projected[:, 512:1024].astype(bf16)
    v = (projected[:, 1024:] + qv_half[1]).astype(bf16)
    qk = jnp.concatenate([q.reshape(256, 8, HD), k.reshape(256, 8, HD)], 2).transpose(1, 0, 2)
    packed = exchange(jnp.concatenate([qk, pack_half_rows(v)], 1), 1)
    attended = unpack_half_rows(exchange(attend(valid[None], packed), 2))

    branch = core_sum(dot_nn(attended, wo)) + out_full
    second, pull_second = jax.vjp(norm_rows, branch, gains[1], shifts[1])
    middle = hidden + second
    third, pull_third = jax.vjp(norm_rows, middle, gains[2], shifts[2])
    third = third.astype(bf16)
    up_pre = dot_nn(third, wu) + up_half
    active, pull_gelu = jax.vjp(exact_gelu, up_pre)
    active = active.astype(bf16)
    down_pre = core_sum(dot_nn(active, wd)) + down_full
    fourth, pull_fourth = jax.vjp(norm_rows, down_pre, gains[3], shifts[3])
    output = (middle + fourth).astype(bf16)

    grad_out = cot * (spot < valid).astype(f32)[:, None]
    grad_down, gain4, shift4 = pull_fourth(grad_out)
    grad_down = grad_down.astype(bf16)
    gw_down = contract_rows(active, grad_down).astype(bf16)
    (grad_up,) = pull_gelu(dot_nt(grad_down, wd))
    grad_up = grad_up.astype(bf16)
    gw_up = contract_rows(third, grad_up).astype(bf16)
    part, gain3, shift3 = pull_third(core_sum(dot_nt(grad_up, wu)))
    grad_middle = grad_out + part
    grad_branch, gain2, shift2 = pull_second(grad_middle)
    grad_branch = grad_branch.astype(bf16)
    gw_out = contract_rows(attended, grad_branch).astype(bf16)
    grad_att = dot_nt(grad_branch, wo).astype(bf16)
    grad_packed = exchange(pack_half_rows(grad_att), 3)
    back = exchange(attend_back(valid[None], packed, grad_packed), 4)
    grad_qk = back[:, :256].reshape(8, 256, 2, HD).transpose(1, 2, 0, 3).reshape(256, 1024)
    grad_proj = jnp.concatenate([grad_qk, unpack_half_rows(back[:, 256:])], 1)
    gw_qkv = contract_rows(first, grad_proj).astype(bf16)
    part, gain1, shift1 = pull_first(core_sum(dot_nt(grad_proj, wq)))
    input_grad = (grad_middle + part).astype(bf16)

    halved = 0.5 * jnp.stack([
        jnp.sum(grad_branch.astype(f32), 0), jnp.sum(grad_down.astype(f32), 0),
        gain1, gain2, gain3, gain4, shift1, shift2, shift3, shift4])
    sums = jnp.sum(grad_proj.astype(f32), 0)
    sums_qv = jnp.stack([sums[:512], sums[1024:]]).reshape(2, 8, 1, HD)
    mine = (jnp.arange(2) == c)
    sums_qv = jnp.where(mine[None, None, :, None], sums_qv, 0.0).reshape(2, width)
    vecs = jnp.concatenate([sums_qv, halved], 0).reshape(12, 32, 32).transpose(1, 0, 2)
    sums_up = jnp.sum(grad_up.astype(f32), 0).reshape(8, 1, 256)
    sums_up = jnp.where(mine[None, :, None], sums_up, 0.0).reshape(32, 1, 128)
    small_terms = jnp.concatenate([jnp.pad(vecs, ((0, 0), (0, 0), (0, 96))), sums_up, jnp.zeros((32, 3, 128), f32)], 1)

    r_down, r_up, r_out, r_qkv, r_small = reduce_terms((False, True, False, True, True), [
        gw_down.reshape(4, 2, 2, 2, 64, width), gw_up.reshape(4, 2, 2, 2, 32, 2048),
        gw_out.reshape(4, 2, 2, 2, 16, width), gw_qkv.reshape(4, 2, 2, 2, 32, 1536),
        small_terms.reshape(4, 2, 2, 2, 16, 128)], 5)
    small = r_small[0] + r_small[1]

    def own_rows(block):
        return lax.dynamic_slice_in_dim(block, c * rows, rows, 0)[None]

    return (
        own_rows(output), own_rows(input_grad), from_parity(r_qkv, HD), small[:2, :32], r_out.reshape(32, width),
        small[2, :32], from_parity(r_up, 256), small[12], r_down.reshape(128, width), small[3, :32],
        small[4:8, :32], small[8:12, :32])


def solution(mesh):
    return jax.shard_map(
        fast_body if is_small(mesh) else body,
        mesh=mesh,
        in_specs=(
            P("dp", "seq", None),
            P("dp", "seq", None),
            P(),
            P(),
            P(("seq", "dp"), None),
            P(None, ("seq", "dp")),
            P(("seq", "dp"), None),
            P(("seq", "dp")),
            P(("seq", "dp"), None),
            P(("seq", "dp")),
            P(("seq", "dp"), None),
            P(("seq", "dp")),
            P(None, ("seq", "dp")),
            P(None, ("seq", "dp")),
        ),
        out_specs=(
            P("dp", "seq", None),
            P("dp", "seq", None),
            P(("seq", "dp"), None),
            P(None, ("seq", "dp")),
            P(("seq", "dp"), None),
            P(("seq", "dp")),
            P(("seq", "dp"), None),
            P(("seq", "dp")),
            P(("seq", "dp"), None),
            P(("seq", "dp")),
            P(None, ("seq", "dp")),
            P(None, ("seq", "dp")),
        ),
        check_vma=False,
    )
```

```python
import functools
import math

import jax
import jax.numpy as jnp
from jax import lax
from jax.experimental import pallas as pl
from jax.experimental.pallas import tpu as pltpu
from jax.sharding import PartitionSpec as P


HD = 64


RELAX_SCALE = 32.0
NORM_EPSILON = 1e-05


def norm_rows(values, gain, shift):
    center = values - jnp.mean(values, -1, keepdims=True)
    spread = jnp.mean(center * center, -1, keepdims=True)
    return center * lax.rsqrt(spread + NORM_EPSILON) * gain + shift


def exact_gelu(values):
    return jax.nn.gelu(values, approximate=False)


def contract_rows(left, right):
    return lax.dot_general(
        left, right, (((0,), (0,)), ((), ())), preferred_element_type=jnp.float32
    )


def contract_cols(left, right):
    return lax.dot_general(
        left, right, (((1,), (1,)), ((), ())), preferred_element_type=jnp.float32
    )


def split_heads(block):
    return block.reshape(block.shape[0], 2, HD)


def pair_scores(query_part, key_part):
    factor = 1.0 / (RELAX_SCALE * math.sqrt(HD))
    return (
        jnp.einsum(
            "qhd,khd->hqk",
            split_heads(query_part),
            split_heads(key_part),
            preferred_element_type=jnp.float32,
        )
        * factor
    )


def kept_probs(scores, allowed, row_max, row_total):
    exp_terms = jnp.exp(jnp.where(allowed, RELAX_SCALE * (scores - row_max), -jnp.inf))
    return exp_terms / row_total


def body(
    tokens,
    cotangent,
    lengths,
    assign,
    w_qkv,
    qv_bias,
    w_out,
    out_bias,
    w_up,
    up_bias,
    w_down,
    down_bias,
    norm_gain,
    norm_shift,
):
    gathered = (
        lax.all_gather(w_qkv, ("seq", "dp"), axis=0, tiled=True),
        lax.all_gather(w_out, ("seq", "dp"), axis=0, tiled=True),
        lax.all_gather(w_up, ("seq", "dp"), axis=0, tiled=True),
        lax.all_gather(w_down, ("seq", "dp"), axis=0, tiled=True),
        lax.all_gather(qv_bias, ("seq", "dp"), axis=1, tiled=True),
        lax.all_gather(out_bias, ("seq", "dp"), axis=0, tiled=True),
        lax.all_gather(up_bias, ("seq", "dp"), axis=0, tiled=True),
        lax.all_gather(down_bias, ("seq", "dp"), axis=0, tiled=True),
        lax.all_gather(norm_gain, ("seq", "dp"), axis=1, tiled=True),
        lax.all_gather(norm_shift, ("seq", "dp"), axis=1, tiled=True),
    )
    qkv_full, out_full, up_full, down_full = (gathered[0], gathered[1], gathered[2], gathered[3])
    qv_shift = gathered[4].astype(jnp.float32)
    out_shift = gathered[5].astype(jnp.float32)
    up_shift = gathered[6].astype(jnp.float32)
    down_shift = gathered[7].astype(jnp.float32)
    gains = gathered[8].astype(jnp.float32)
    shifts = gathered[9].astype(jnp.float32)
    row_count = tokens.shape[1]
    model_width = tokens.shape[2]
    pair_cols = 2 * HD
    pair_count = model_width // pair_cols
    slot_rows = row_count * lax.axis_size("seq")
    factor = 1.0 / (RELAX_SCALE * math.sqrt(HD))
    valid = lengths[assign[lax.axis_index("dp")]]
    own_place = lax.axis_index("seq") * row_count + jnp.arange(row_count, dtype=jnp.int32)
    all_place = jnp.arange(slot_rows, dtype=jnp.int32)
    allowed = (all_place[None, :] <= own_place[:, None]) & (all_place[None, :] < valid)
    pair_ids = jnp.arange(pair_count, dtype=jnp.int32)
    hidden = tokens[0].astype(jnp.float32)
    normed_first, pull_first = jax.vjp(norm_rows, hidden, gains[0], shifts[0])
    normed_low = normed_first.astype(jnp.bfloat16)
    projected = jnp.dot(normed_low, qkv_full, preferred_element_type=jnp.float32)
    queries = (projected[:, :model_width] + qv_shift[0]).astype(jnp.bfloat16)
    key_own = projected[:, model_width : 2 * model_width].astype(jnp.bfloat16)
    value_own = (projected[:, 2 * model_width :] + qv_shift[1]).astype(jnp.bfloat16)
    keys, values = (
        lax.all_gather(key_own, "seq", axis=0, tiled=True),
        lax.all_gather(value_own, "seq", axis=0, tiled=True),
    )

    def columns(block, pair_index):
        return lax.dynamic_slice_in_dim(block, pair_index * pair_cols, pair_cols, 1)

    def merge_pairs(stack):
        return stack.transpose(1, 0, 2).reshape(stack.shape[1], model_width)

    def attend(pair_index):
        scores = pair_scores(columns(queries, pair_index), columns(keys, pair_index))
        row_max = jnp.max(jnp.where(allowed, scores, -jnp.inf), -1, keepdims=True)
        exp_terms = jnp.exp(jnp.where(allowed, RELAX_SCALE * (scores - row_max), -jnp.inf))
        row_total = jnp.sum(exp_terms, -1, keepdims=True)
        probs = (exp_terms / row_total).astype(jnp.bfloat16)
        mixed = jnp.einsum(
            "hqk,khd->qhd",
            probs,
            split_heads(columns(values, pair_index)),
            preferred_element_type=jnp.float32,
        )
        return (mixed.reshape(row_count, pair_cols), row_max[..., 0], row_total[..., 0])

    mixed_pairs, max_pairs, total_pairs = lax.map(attend, pair_ids)
    attended = merge_pairs(mixed_pairs).astype(jnp.bfloat16)
    branch = jnp.dot(attended, out_full, preferred_element_type=jnp.float32) + out_shift
    normed_second, pull_second = jax.vjp(norm_rows, branch, gains[1], shifts[1])
    middle = hidden + normed_second
    normed_third, pull_third = jax.vjp(norm_rows, middle, gains[2], shifts[2])
    third_low = normed_third.astype(jnp.bfloat16)
    up_pre = jnp.dot(third_low, up_full, preferred_element_type=jnp.float32) + up_shift
    activated, pull_gelu = jax.vjp(exact_gelu, up_pre)
    active_low = activated.astype(jnp.bfloat16)
    down_pre = jnp.dot(active_low, down_full, preferred_element_type=jnp.float32) + down_shift
    normed_fourth, pull_fourth = jax.vjp(norm_rows, down_pre, gains[3], shifts[3])
    output = (middle + normed_fourth).astype(jnp.bfloat16)[None]
    again = (
        lax.all_gather(w_qkv, ("seq", "dp"), axis=0, tiled=True),
        lax.all_gather(w_out, ("seq", "dp"), axis=0, tiled=True),
        lax.all_gather(w_up, ("seq", "dp"), axis=0, tiled=True),
        lax.all_gather(w_down, ("seq", "dp"), axis=0, tiled=True),
    )
    qkv_back, out_back, up_back, down_back = (again[0], again[1], again[2], again[3])
    keep_rows = (own_place < valid).astype(jnp.float32)[:, None]
    grad_out = cotangent[0].astype(jnp.float32) * keep_rows
    grad_down, grad_gain_four, grad_shift_four = pull_fourth(grad_out)
    grad_down_low = grad_down.astype(jnp.bfloat16)
    grad_w_down = contract_rows(active_low, grad_down_low)
    grad_b_down = jnp.sum(grad_down_low.astype(jnp.float32), 0)
    (grad_up,) = pull_gelu(contract_cols(grad_down_low, down_back))
    grad_up_low = grad_up.astype(jnp.bfloat16)
    grad_w_up = contract_rows(third_low, grad_up_low)
    grad_b_up = jnp.sum(grad_up_low.astype(jnp.float32), 0)
    grad_middle_part, grad_gain_three, grad_shift_three = pull_third(
        contract_cols(grad_up_low, up_back)
    )
    grad_middle = grad_out + grad_middle_part
    grad_branch, grad_gain_two, grad_shift_two = pull_second(grad_middle)
    grad_branch_low = grad_branch.astype(jnp.bfloat16)
    grad_w_out = contract_rows(attended, grad_branch_low)
    grad_b_out = jnp.sum(grad_branch_low.astype(jnp.float32), 0)
    grad_attended = contract_cols(grad_branch_low, out_back).astype(jnp.bfloat16)

    def query_side(pair_index):
        scores = pair_scores(columns(queries, pair_index), columns(keys, pair_index))
        probs = kept_probs(
            scores, allowed, max_pairs[pair_index][..., None], total_pairs[pair_index][..., None]
        )
        grad_part = columns(grad_attended, pair_index)
        grad_probs = jnp.einsum(
            "qhd,khd->hqk",
            split_heads(grad_part),
            split_heads(columns(values, pair_index)),
            preferred_element_type=jnp.float32,
        )
        delta = jnp.sum(probs * grad_probs, -1, keepdims=True)
        grad_scores = (RELAX_SCALE * probs * (grad_probs - delta)).astype(jnp.bfloat16)
        grad_query = (
            jnp.einsum(
                "hqk,khd->qhd",
                grad_scores,
                split_heads(columns(keys, pair_index)),
                preferred_element_type=jnp.float32,
            )
            * factor
        )
        return (grad_query.reshape(row_count, pair_cols), grad_scores, probs, delta)

    def both_sides(pair_index):
        grad_query, grad_scores, probs, delta = query_side(pair_index)
        grad_part = columns(grad_attended, pair_index)
        grad_key = (
            jnp.einsum(
                "hqk,qhd->khd",
                grad_scores,
                split_heads(columns(queries, pair_index)),
                preferred_element_type=jnp.float32,
            )
            * factor
        )
        grad_value = jnp.einsum(
            "hqk,qhd->khd",
            probs.astype(jnp.bfloat16),
            split_heads(grad_part),
            preferred_element_type=jnp.float32,
        )
        return (
            grad_query,
            grad_key.reshape(slot_rows, pair_cols),
            grad_value.reshape(slot_rows, pair_cols),
        )

    query_pairs, key_terms, value_terms = lax.map(both_sides, pair_ids)
    key_pairs, value_pairs = (
        lax.psum_scatter(
            key_terms.astype(jnp.bfloat16), "seq", scatter_dimension=1, tiled=True
        ).astype(jnp.float32),
        lax.psum_scatter(
            value_terms.astype(jnp.bfloat16), "seq", scatter_dimension=1, tiled=True
        ).astype(jnp.float32),
    )
    grad_q_low = merge_pairs(query_pairs).astype(jnp.bfloat16)
    grad_k_low = merge_pairs(key_pairs).astype(jnp.bfloat16)
    grad_v_low = merge_pairs(value_pairs).astype(jnp.bfloat16)
    grad_projected = jnp.concatenate([grad_q_low, grad_k_low, grad_v_low], 1)
    grad_w_qkv = contract_rows(normed_low, grad_projected)
    grad_qv = jnp.stack(
        [jnp.sum(grad_q_low.astype(jnp.float32), 0), jnp.sum(grad_v_low.astype(jnp.float32), 0)]
    )
    grad_hidden_part, grad_gain_one, grad_shift_one = pull_first(
        contract_cols(grad_projected, qkv_back)
    )
    input_grad = (grad_middle + grad_hidden_part).astype(jnp.bfloat16)[None]
    grad_gains = jnp.stack([grad_gain_one, grad_gain_two, grad_gain_three, grad_gain_four])
    grad_shifts = jnp.stack([grad_shift_one, grad_shift_two, grad_shift_three, grad_shift_four])
    owned = (
        lax.psum_scatter(grad_w_qkv, ("seq", "dp"), scatter_dimension=0, tiled=True),
        lax.psum_scatter(grad_w_out, ("seq", "dp"), scatter_dimension=0, tiled=True),
        lax.psum_scatter(grad_w_up, ("seq", "dp"), scatter_dimension=0, tiled=True),
        lax.psum_scatter(grad_w_down, ("seq", "dp"), scatter_dimension=0, tiled=True),
        lax.psum_scatter(grad_qv, ("seq", "dp"), scatter_dimension=1, tiled=True),
        lax.psum_scatter(grad_b_out, ("seq", "dp"), scatter_dimension=0, tiled=True),
        lax.psum_scatter(grad_b_up, ("seq", "dp"), scatter_dimension=0, tiled=True),
        lax.psum_scatter(grad_b_down, ("seq", "dp"), scatter_dimension=0, tiled=True),
        lax.psum_scatter(grad_gains, ("seq", "dp"), scatter_dimension=1, tiled=True),
        lax.psum_scatter(grad_shifts, ("seq", "dp"), scatter_dimension=1, tiled=True),
    )
    return (
        output,
        input_grad,
        owned[0],
        owned[4],
        owned[1],
        owned[5],
        owned[2],
        owned[6],
        owned[3],
        owned[7],
        owned[8],
        owned[9],
    )


MESH = pl.DeviceIdType.MESH

def place():
    seq = lax.axis_index("seq")
    x = lax.axis_index("dp")
    return seq // 4, (seq // 2) % 2, seq % 2, x

def device(z, y, c, x):
    return (z * 4 + y * 2 + c, x)

def entry_barrier():
    z, y, c, x = place()
    barrier = pltpu.get_barrier_semaphore()
    def signal(dev):
        pl.semaphore_signal(barrier, inc=1, device_id=dev, device_id_type=MESH)
    signal(device(z, y, 1 - c, x))
    signal(device(z, 1 - y, c, x))
    signal(device(z, y, c, 1 - x))
    @pl.when(z > 0)
    def _(): signal(device(z - 1, y, c, x))
    @pl.when(z < 3)
    def _(): signal(device(z + 1, y, c, x))
    pl.semaphore_wait(barrier, 3 + (z + 2) // 3 + (5 - z) // 3)

def gather_kernel(split, *refs):
    n = len(split)
    srcs, outs = refs[:n], refs[n:2 * n]
    send_sem, recv_sem, core_sem, own_sem = refs[2 * n:]
    z, y, c, x = place()
    entry_barrier()

    def chunk(w, s, zz, yy, xx):
        if split[w]:
            return outs[w].at[zz, yy, s, xx]
        return outs[w].at[zz, yy, xx, s]

    def copy(w, s, zz, yy, xx, dev, slot):
        return pltpu.make_async_remote_copy(
            src_ref=chunk(w, s, zz, yy, xx), dst_ref=chunk(w, s, zz, yy, xx),
            send_sem=send_sem.at[w, s, slot], recv_sem=recv_sem.at[w, s, zz * 4 + yy * 2 + xx],
            device_id=dev, device_id_type=MESH)

    def lateral(s):
        if s == 0:
            return (1 - y, x), device(z, 1 - y, c, x), device(z, y, c, 1 - x)
        return (y, 1 - x), device(z, y, c, 1 - x), device(z, 1 - y, c, x)

    up, down = device(z + 1, y, c, x), device(z - 1, y, c, x)

    for w in range(n):
        if split[w]:
            pltpu.make_async_remote_copy(
                src_ref=srcs[w].at[1 - c], dst_ref=outs[w].at[z, y, c, x],
                send_sem=core_sem.at[w, 0], recv_sem=core_sem.at[w, 1],
                device_id=device(z, y, 1 - c, x), device_id_type=MESH).start()
            pltpu.make_async_copy(srcs[w].at[c], outs[w].at[z, y, c, x], own_sem.at[w]).start()
        else:
            pltpu.make_async_copy(srcs[w], outs[w].at[z, y, x], own_sem.at[w]).start()

    def first_wait(w):
        if split[w]:
            pltpu.make_async_copy(srcs[w].at[c], outs[w].at[z, y, c, x], own_sem.at[w]).wait()
            pltpu.make_async_remote_copy(
                src_ref=srcs[w].at[1 - c], dst_ref=outs[w].at[z, y, 1 - c, x],
                send_sem=core_sem.at[w, 0], recv_sem=core_sem.at[w, 1],
                device_id=device(z, y, 1 - c, x), device_id_type=MESH).wait()
        else:
            pltpu.make_async_copy(srcs[w], outs[w].at[z, y, x], own_sem.at[w]).wait()

    for w in range(n):
        first_wait(w)
        for s in range(2):
            lat, one, two = lateral(s)
            @pl.when(z < 3)
            def _(): copy(w, s, z, y, x, up, z).start()
            @pl.when(z > 0)
            def _(): copy(w, s, z, y, x, down, 4 + z).start()
            copy(w, s, z, y, x, one, 8 + z).start()
            copy(w, s, z, y, x, two, 12 + z).start()

    def pass_on(w, s, zz):
        lat, one, two = lateral(s)
        copy(w, s, zz, lat[0], lat[1], one, 8 + zz).wait_recv()
        copy(w, s, zz, lat[0], lat[1], two, 16 + zz).start()

    def step(d, _):
        for w in range(n):
            for s in range(2):
                lat, one, two = lateral(s)
                @pl.when(z >= d)
                def _():
                    zz = z - d
                    copy(w, s, zz, y, x, up, zz).wait_recv()
                    @pl.when(z < 3)
                    def _(): copy(w, s, zz, y, x, up, zz).start()
                    copy(w, s, zz, y, x, one, 8 + zz).start()
                    copy(w, s, zz, y, x, two, 12 + zz).start()
                @pl.when(z + d <= 3)
                def _():
                    zz = z + d
                    copy(w, s, zz, y, x, down, 4 + zz).wait_recv()
                    @pl.when(z > 0)
                    def _(): copy(w, s, zz, y, x, down, 4 + zz).start()
                    copy(w, s, zz, y, x, one, 8 + zz).start()
                    copy(w, s, zz, y, x, two, 12 + zz).start()
                @pl.when(d == 1)
                def _():
                    pass_on(w, s, z)
                @pl.when((d > 1) & (z >= d - 1))
                def _(): pass_on(w, s, z - d + 1)
                @pl.when((d > 1) & (z + d - 1 <= 3))
                def _(): pass_on(w, s, z + d - 1)
        return 0
    lax.fori_loop(1, 4, step, 0)
    for w in range(n):
        for s in range(2):
            @pl.when(z == 3)
            def _(): pass_on(w, s, 0)
            @pl.when(z == 0)
            def _(): pass_on(w, s, 3)

    def finish(zz, _):
        for w in range(n):
            for s in range(2):
                lat, one, two = lateral(s)
                other = (1 - lat[0], 1 - lat[1])
                copy(w, s, zz, other[0], other[1], two, 12 + zz).wait_recv()
                copy(w, s, zz, 1 - y, 1 - x, two, 16 + zz).wait_recv()
                @pl.when((zz <= z) & (z < 3))
                def _(): copy(w, s, zz, y, x, up, zz).wait_send()
                @pl.when((zz >= z) & (z > 0))
                def _(): copy(w, s, zz, y, x, down, 4 + zz).wait_send()
                copy(w, s, zz, y, x, one, 8 + zz).wait_send()
                copy(w, s, zz, y, x, two, 12 + zz).wait_send()
                copy(w, s, zz, lat[0], lat[1], two, 16 + zz).wait_send()
        return 0
    lax.fori_loop(0, 4, finish, 0)

def gather(split, srcs, cid):
    n = len(srcs)
    outs = []
    for sp, a in zip(split, srcs):
        outs.append(jax.ShapeDtypeStruct((4, 2, 2, 2) + a.shape[1:], a.dtype))
    anyspec = pl.BlockSpec(memory_space=pl.ANY)
    return pl.pallas_call(
        functools.partial(gather_kernel, tuple(split)),
        out_shape=tuple(outs),
        in_specs=[pl.BlockSpec(memory_space=pltpu.VMEM)] * n,
        out_specs=(anyspec,) * n,
        scratch_shapes=[pltpu.SemaphoreType.DMA((n, 2, 20)), pltpu.SemaphoreType.DMA((n, 2, 16)),
                        pltpu.SemaphoreType.DMA((n, 2)), pltpu.SemaphoreType.DMA((n,))],
        compiler_params=pltpu.CompilerParams(collective_id=cid, has_side_effects=True, vmem_limit_bytes=48 << 20),
        name="gather",
    )(*srcs)

def reduce_kernel(split, *refs):
    n = len(split)
    terms, outs = refs[:n], refs[n:2 * n]
    r1, s2, r2, tz, ru, rd = (refs[(2 + k) * n:(3 + k) * n] for k in range(6))
    send_sem, recv_sem, core_sem = refs[8 * n:8 * n + 3]
    z, y, c, x = place()
    entry_barrier()
    up, down = device(z + 1, y, c, x), device(z - 1, y, c, x)

    def term(w, s, zz, l1, l2):
        yy, xx = (l1, l2) if s == 0 else (l2, l1)
        if split[w]:
            return terms[w].at[zz, yy, s, xx]
        return terms[w].at[zz, yy, xx, s]

    def own(s):
        return (y, x) if s == 0 else (x, y)

    def one_two(s):
        a, b = device(z, 1 - y, c, x), device(z, y, c, 1 - x)
        return (a, b) if s == 0 else (b, a)

    def remote(src, dst, w, s, send, recv, dev):
        return pltpu.make_async_remote_copy(
            src_ref=src, dst_ref=dst, send_sem=send_sem.at[w, s, send], recv_sem=recv_sem.at[w, s, recv],
            device_id=dev, device_id_type=MESH)

    def copy1(w, s, zz, l1):
        return remote(term(w, s, zz, l1, 1 - own(s)[1]), r1[w].at[s, zz, l1], w, s, zz * 2 + l1, zz * 2 + l1, one_two(s)[1])

    def copy2(w, s, zz):
        return remote(s2[w].at[s, zz], r2[w].at[s, zz], w, s, 8 + zz, 8 + zz, one_two(s)[0])

    def copy_up(w, s, zz):
        return remote(tz[w].at[s, zz], ru[w].at[s, zz], w, s, 12 + zz, 12 + zz, up)

    def copy_down(w, s, zz):
        return remote(tz[w].at[s, zz], rd[w].at[s, zz], w, s, 12 + zz, 16 + zz, down)

    f32 = jnp.float32
    order = (3, 0, 2, 1)

    def stage1(w):
        for zz in order:
            for s in range(2):
                copy1(w, s, zz, 1 - own(s)[0]).start()
        for zz in order:
            for s in range(2):
                copy1(w, s, zz, own(s)[0]).start()

    def stage2(w):
        for zz in order:
            for s in range(2):
                o1, o2 = own(s)
                copy1(w, s, zz, 1 - o1).wait_recv()
                total = term(w, s, zz, 1 - o1, o2)[...].astype(f32) + r1[w][s, zz, 1 - o1].astype(f32)
                s2[w][s, zz] = total.astype(s2[w].dtype)
                copy2(w, s, zz).start()

    def local(w, s, zz):
        o1, o2 = own(s)
        copy1(w, s, zz, o1).wait_recv()
        copy2(w, s, zz).wait_recv()
        return term(w, s, zz, o1, o2)[...].astype(f32) + r1[w][s, zz, o1].astype(f32) + r2[w][s, zz].astype(f32)

    def stage3(w):
        for zz in order:
            for s in range(2):
                @pl.when(zz > z)
                def _():
                    tz[w][s, zz] = local(w, s, zz).astype(tz[w].dtype)
                    @pl.when(z > 0)
                    def _():
                        copy_up(w, s, zz).wait_recv()
                        tz[w][s, zz] = (tz[w][s, zz].astype(f32) + ru[w][s, zz].astype(f32)).astype(tz[w].dtype)
                    copy_up(w, s, zz).start()
                @pl.when(zz < z)
                def _():
                    tz[w][s, zz] = local(w, s, zz).astype(tz[w].dtype)
                    @pl.when(z < 3)
                    def _():
                        copy_down(w, s, zz).wait_recv()
                        tz[w][s, zz] = (tz[w][s, zz].astype(f32) + rd[w][s, zz].astype(f32)).astype(tz[w].dtype)
                    copy_down(w, s, zz).start()

    def last(w):
        for s in range(2):
            total = local(w, s, z)
            slot = c if split[w] else s
            @pl.when(z > 0)
            def _(): copy_up(w, s, z).wait_recv()
            @pl.when(z < 3)
            def _(): copy_down(w, s, z).wait_recv()
            below = jnp.where(z > 0, ru[w][s, z].astype(f32), 0.0)
            above = jnp.where(z < 3, rd[w][s, z].astype(f32), 0.0)
            total = total + below + above
            if split[w]:
                @pl.when(c == s)
                def _(): outs[w][slot] = total
                @pl.when(c != s)
                def _():
                    core_stage(w)[...] = total
                    core_copy(w).start()
            else:
                outs[w][s] = total

    cores = refs[8 * n + 3:]
    def core_stage(w):
        return cores[w]
    def core_copy(w):
        return pltpu.make_async_remote_copy(
            src_ref=cores[w], dst_ref=outs[w].at[c], send_sem=core_sem.at[w, 0], recv_sem=core_sem.at[w, 1],
            device_id=device(z, y, 1 - c, x), device_id_type=MESH)

    stages = (stage1, stage2, stage3, last)
    for t in range(n + 3):
        for k, stage in enumerate(stages):
            if 0 <= t - k < n:
                stage(t - k)
    for w in range(n):
        if split[w]:
            pltpu.make_async_remote_copy(
                src_ref=cores[w], dst_ref=outs[w].at[1 - c], send_sem=core_sem.at[w, 0], recv_sem=core_sem.at[w, 1],
                device_id=device(z, y, 1 - c, x), device_id_type=MESH).wait()
    def finish(zz, _):
        for w in range(n):
            for s in range(2):
                copy1(w, s, zz, 0).wait_send()
                copy1(w, s, zz, 1).wait_send()
                copy2(w, s, zz).wait_send()
                @pl.when(zz > z)
                def _(): copy_up(w, s, zz).wait_send()
                @pl.when(zz < z)
                def _(): copy_down(w, s, zz).wait_send()
        return 0
    lax.fori_loop(0, 4, finish, 0)

def reduce_terms(split, terms, cid):
    n = len(terms)
    tiles = [t.shape[4:] for t in terms]
    V = lambda shape, dt: pltpu.VMEM(shape, dt)
    scratch = []
    for lead in ((2, 4, 2), (2, 4), (2, 4), (2, 4), (2, 4), (2, 4)):
        scratch += [V(lead + t, a.dtype) for t, a in zip(tiles, terms)]
    scratch += [pltpu.SemaphoreType.DMA((n, 2, 16)), pltpu.SemaphoreType.DMA((n, 2, 20)), pltpu.SemaphoreType.DMA((n, 2))]
    scratch += [V(t if sp else (8, 128), jnp.float32) for sp, t in zip(split, tiles)]
    vm = pl.BlockSpec(memory_space=pltpu.VMEM)
    return pl.pallas_call(
        functools.partial(reduce_kernel, tuple(split)),
        out_shape=tuple(jax.ShapeDtypeStruct((2,) + t, jnp.float32) for t in tiles),
        in_specs=[vm] * n, out_specs=(vm,) * n, scratch_shapes=scratch,
        compiler_params=pltpu.CompilerParams(collective_id=cid, has_side_effects=True, vmem_limit_bytes=60 << 20),
        name="reduce_terms",
    )(*terms)


def is_small(mesh):
    return mesh.shape["seq"] == 16 and mesh.shape["dp"] == 2


def exchange_kernel(src, out, send_sem, recv_sem, own_sem):
    z, y, c, x = place()
    me = z * 2 + y
    barrier = pltpu.get_barrier_semaphore()

    def peer(k):
        other = lax.rem(me + k, 8)
        return other, device(other // 2, other % 2, c, x)

    for k in range(1, 8):
        pl.semaphore_signal(barrier, inc=1, device_id=peer(k)[1], device_id_type=MESH)
    own = pltpu.make_async_copy(src.at[me], out.at[me], own_sem)
    own.start()
    pl.semaphore_wait(barrier, 7)

    def copy(k):
        other, dev = peer(k)
        return pltpu.make_async_remote_copy(
            src_ref=src.at[other], dst_ref=out.at[me], send_sem=send_sem.at[k], recv_sem=recv_sem.at[8 - k],
            device_id=dev, device_id_type=MESH)

    for k in (4, 3, 5, 2, 6, 1, 7):
        copy(k).start()
    own.wait()
    for k in range(1, 8):
        other, dev = peer(k)
        pltpu.make_async_remote_copy(
            src_ref=src.at[other], dst_ref=out.at[other], send_sem=send_sem.at[k], recv_sem=recv_sem.at[k],
            device_id=dev, device_id_type=MESH).wait_recv()
    for k in range(1, 8):
        copy(k).wait_send()


def exchange(blocks, cid):
    vm = pl.BlockSpec(memory_space=pltpu.VMEM)
    return pl.pallas_call(
        exchange_kernel, out_shape=jax.ShapeDtypeStruct(blocks.shape, blocks.dtype),
        in_specs=[vm], out_specs=vm,
        scratch_shapes=[pltpu.SemaphoreType.DMA((8,)), pltpu.SemaphoreType.DMA((8,)), pltpu.SemaphoreType.DMA],
        compiler_params=pltpu.CompilerParams(collective_id=cid, has_side_effects=True),
        name="exchange",
    )(blocks)


def dot_nt(a, b):
    return lax.dot_general(a, b, (((1,), (1,)), ((), ())), preferred_element_type=jnp.float32)


def dot_nn(a, b):
    return jnp.dot(a, b, preferred_element_type=jnp.float32)


BQ = 256
MASKED = -1e30


def load_heads(valid, packed, q_ref, k_ref):
    rows = q_ref.shape[0]
    qk = packed[:, :256].reshape(rows, 128)
    kq = jnp.concatenate([qk[:, 64:], qk[:, :64]], axis=1)
    lane = lax.broadcasted_iota(jnp.int32, (rows, 128), 1)
    spot = lax.broadcasted_iota(jnp.int32, (rows, 128), 0)
    past = jnp.where(spot < valid, 0.0, MASKED)
    q_ref[...] = jnp.where(lane < 64, qk.astype(jnp.float32), jnp.where(lane == 64, 1.0, 0.0)).astype(jnp.bfloat16)
    k_ref[...] = jnp.where(lane < 64, kq.astype(jnp.float32), jnp.where(lane == 64, past, 0.0)).astype(jnp.bfloat16)


def unpack_rows(halves):
    n = halves.shape[0]
    return jnp.concatenate([halves[:, :, :64], halves[:, :, 64:]], axis=1).reshape(n * 256, 64)


def block_probs(q_ref, k_ref, i):
    n = (i + 1) * BQ
    scores = dot_nt(k_ref[:n], q_ref[i * BQ:n])
    key = lax.broadcasted_iota(jnp.int32, (BQ, BQ), 0)
    query = lax.broadcasted_iota(jnp.int32, (BQ, BQ), 1)
    corner = jnp.where(key <= query, scores[n - BQ:], MASKED)
    scores = jnp.concatenate([scores[:n - BQ], corner], axis=0) if i else corner
    top = jnp.max(scores, axis=0, keepdims=True)
    terms = jnp.exp((scores - top) * 0.125)
    return terms, 1.0 / jnp.sum(terms, axis=0, keepdims=True)


def attend_kernel(valid_ref, packed, out_ref, q_ref, k_ref, vt_ref):
    load_heads(valid_ref[0], packed, q_ref, k_ref)
    unit = jnp.where(
        lax.broadcasted_iota(jnp.int32, (64, 64), 0) == lax.broadcasted_iota(jnp.int32, (64, 64), 1), 1.0, 0.0
    ).astype(jnp.bfloat16)
    vt_ref[...] = dot_nt(unit, unpack_rows(packed[:, 256:])).astype(jnp.bfloat16)
    for i in range(q_ref.shape[0] // BQ):
        n = (i + 1) * BQ
        terms, scale = block_probs(q_ref, k_ref, i)
        probs = (terms * scale).astype(jnp.bfloat16)
        mixed = dot_nn(vt_ref[:, :n], probs).T
        out_ref[i] = jnp.concatenate([mixed[:128], mixed[128:]], axis=1).astype(jnp.bfloat16)


def attend_back_kernel(valid_ref, packed, grad, out_ref, q_ref, k_ref, v_ref, g_ref, kt_ref, dk_ref, dv_ref):
    load_heads(valid_ref[0], packed, q_ref, k_ref)
    v_ref[...] = unpack_rows(packed[:, 256:])
    g_ref[...] = unpack_rows(grad[...])
    unit = jnp.where(
        lax.broadcasted_iota(jnp.int32, (64, 128), 0) == lax.broadcasted_iota(jnp.int32, (64, 128), 1), 1.0, 0.0
    ).astype(jnp.bfloat16)
    kt_ref[...] = dot_nt(unit, k_ref[...]).astype(jnp.bfloat16)
    dk_ref[...] = jnp.zeros_like(dk_ref)
    dv_ref[...] = jnp.zeros_like(dv_ref)
    blocks = q_ref.shape[0] // BQ
    for i in range(blocks):
        n = (i + 1) * BQ
        terms, scale = block_probs(q_ref, k_ref, i)
        probs = terms * scale
        grad_probs = dot_nt(v_ref[:n], g_ref[i * BQ:n])
        delta = jnp.sum(probs * grad_probs, axis=0, keepdims=True)
        grad_scores = (probs * (grad_probs - delta)).astype(jnp.bfloat16)
        grad_query = dot_nn(kt_ref[:, :n], grad_scores).T * 0.125
        out_ref[i, :256, :64] = grad_query.astype(jnp.bfloat16)
        dk_ref[:n] += dot_nn(grad_scores, q_ref[i * BQ:n])
        dv_ref[:n] += dot_nn(probs.astype(jnp.bfloat16), g_ref[i * BQ:n])
    for i in range(blocks):
        rows = slice(i * BQ, (i + 1) * BQ)
        out_ref[i, :256, 64:] = (dk_ref[rows, :64] * 0.125).astype(jnp.bfloat16)
        value = dv_ref[rows].astype(jnp.bfloat16)
        out_ref[i, 256:] = jnp.concatenate([value[:128], value[128:]], axis=1)


def attend(valid, packed):
    rows = packed.shape[0] * 256
    vm = pl.BlockSpec(memory_space=pltpu.VMEM)
    return pl.pallas_call(
        attend_kernel,
        out_shape=jax.ShapeDtypeStruct((packed.shape[0], 128, 128), jnp.bfloat16),
        in_specs=[pl.BlockSpec(memory_space=pltpu.SMEM), vm], out_specs=vm,
        scratch_shapes=[pltpu.VMEM((rows, 128), jnp.bfloat16)] * 2 + [pltpu.VMEM((64, rows), jnp.bfloat16)],
        compiler_params=pltpu.CompilerParams(vmem_limit_bytes=48 << 20),
        name="attend",
    )(valid, packed)


def attend_back(valid, packed, grad):
    rows = packed.shape[0] * 256
    vm = pl.BlockSpec(memory_space=pltpu.VMEM)
    return pl.pallas_call(
        attend_back_kernel,
        out_shape=jax.ShapeDtypeStruct(packed.shape, jnp.bfloat16),
        in_specs=[pl.BlockSpec(memory_space=pltpu.SMEM), vm, vm], out_specs=vm,
        scratch_shapes=[pltpu.VMEM((rows, 128), jnp.bfloat16)] * 2 + [pltpu.VMEM((rows, 64), jnp.bfloat16)] * 2
        + [pltpu.VMEM((64, rows), jnp.bfloat16), pltpu.VMEM((rows, 128), jnp.float32), pltpu.VMEM((rows, 64), jnp.float32)],
        compiler_params=pltpu.CompilerParams(vmem_limit_bytes=48 << 20),
        name="attend_back",
    )(valid, packed, grad)


def by_parity(weight, width):
    rows, cols = weight.shape
    return weight.reshape(rows, cols // (2 * width), 2, width).transpose(2, 0, 1, 3).reshape(2, rows, cols // 2)


def from_parity(halves, width):
    _, rows, cols = halves.shape
    return halves.reshape(2, rows, cols // width, width).transpose(1, 2, 0, 3).reshape(rows, 2 * cols)


def pack_half_rows(block):
    return block.reshape(2, 128, 8, HD).transpose(2, 1, 0, 3).reshape(8, 128, 128)


def unpack_half_rows(packed):
    return packed.reshape(8, 128, 2, HD).transpose(2, 1, 0, 3).reshape(256, 8 * HD)


def ring_up(block):
    return lax.ppermute(block, "seq", [(s, (s + 4) % 16) for s in range(16)])


def flip_y(block):
    return lax.ppermute(block, "seq", [(s, s ^ 2) for s in range(16)])


def flip_core(block):
    return lax.ppermute(block, "seq", [(s, s ^ 1) for s in range(16)])


def flip_x(block):
    return lax.ppermute(block, "dp", [(0, 1), (1, 0)])


def after(value, *others):
    return lax.optimization_barrier((value,) + others)[0]


def pick(block, index, axis):
    return lax.dynamic_index_in_dim(block, index, axis, keepdims=False)


def arrange_kernel(spot_ref, *refs):
    ups, downs, out_up, out_down = refs[:6], refs[6:12], refs[12], refs[13]
    step = pl.program_id(0)
    for k in range(6):
        first = (0, 2, 4, 8, 10, 12)[k]
        @pl.when((step >= first) & (step < first + (2, 2, 4)[k % 3]))
        def _():
            for h in range(2):
                for core in range(2):
                    row = (h * 2 + core) * 32
                    out_up[0, 0, core, 0, :, h * 1024:(h + 1) * 1024] = ups[k][0, row:row + 32]
            out_down[0, 0, 0] = downs[k][0]


def arrange(spot, ups, downs):
    def coords(step, spot_ref, swapped):
        one, two = (step // 2) % 2, (step // 4) % 2
        z = lax.rem(spot_ref[0] + 4 - (step // 8) * 2 - step % 2, 4)
        y, x = (two, one) if swapped else (one, two)
        return z, lax.rem(spot_ref[1] + y, 2), lax.rem(spot_ref[2] + x, 2)

    def source(k, half):
        first, count = (0, 2, 4, 8, 10, 12)[k], (2, 2, 4)[k % 3]
        return pl.BlockSpec((1, 128, 1024), lambda i, r: (jnp.clip(i - first, 0, count - 1), half, 0))

    def up_place(i, r):
        z, y, x = coords(i, r, False)
        return z, y, 0, x, 0, 0

    def down_place(i, r):
        z, y, x = coords(i, r, True)
        return z, y, x, 0, 0

    return pl.pallas_call(
        arrange_kernel,
        out_shape=(jax.ShapeDtypeStruct((4, 2, 2, 2, 32, 2048), jnp.bfloat16),
                   jax.ShapeDtypeStruct((4, 2, 2, 128, 1024), jnp.bfloat16)),
        grid_spec=pltpu.PrefetchScalarGridSpec(
            num_scalar_prefetch=1, grid=(16,),
            in_specs=[source(k, 0) for k in range(6)] + [source(k, 1 if k % 3 == 0 else 0) for k in range(6)],
            out_specs=(pl.BlockSpec((1, 1, 2, 1, 32, 2048), up_place), pl.BlockSpec((1, 1, 1, 128, 1024), down_place))),
        compiler_params=pltpu.CompilerParams(vmem_limit_bytes=32 << 20),
        cost_estimate=pl.CostEstimate(flops=0, bytes_accessed=16 << 20, transcendentals=0),
        name="arrange",
    )(spot, *ups, *downs)


def ring_block(w_up, w_down, c):
    up = w_up.reshape(32, 2, 4, 2, 256).transpose(3, 1, 0, 2, 4).reshape(2, 2, 32, 1024)
    mine, other = pick(up, c, 0), flip_core(pick(up, 1 - c, 0))
    up = jnp.where(c == 0, jnp.stack([mine, other], 1), jnp.stack([other, mine], 1))
    return jnp.concatenate([up.reshape(128, 1024), w_down], 0)


def spread(first, second):
    piece = jnp.stack([first, second])
    up, down = piece[:, :128], piece[:, 128:]
    up_one, down_one = flip_y(up), flip_x(down)
    up_two = flip_x(jnp.concatenate([up, up_one], 0))
    down_two = flip_y(jnp.concatenate([down, down_one], 0))
    return piece, (up_one, up_two), (down_one, down_two)


def add_low(mine, other):
    return (mine.astype(jnp.float32) + other.astype(jnp.float32)).astype(jnp.bfloat16)


def reduce_piece(gw_up, gw_down, z, y, x, offsets):
    up = jnp.stack([pick(gw_up, lax.rem(z + d, 4), 0) for d in offsets])
    down = jnp.stack([pick(gw_down, lax.rem(z + d, 4), 0) for d in offsets])
    up_one = flip_x(pick(up, 1 - x, 3))
    down_one = flip_y(pick(down, 1 - y, 1))
    up = add_low(pick(up, x, 3), up_one)
    down = add_low(pick(down, y, 1), down_one)
    up_two = flip_y(pick(up, 1 - y, 1))
    down_two = flip_x(pick(down, 1 - x, 1))
    return add_low(pick(up, y, 1), up_two), add_low(pick(down, x, 1), down_two)


def ring_reduce(first, second):
    total = []
    for a, b in zip(first, second):
        run = add_low(a[1], ring_up(a[0]))
        run = add_low(b[0], ring_up(run))
        total.append(b[1].astype(jnp.float32) + ring_up(run).astype(jnp.float32))
    return total


def fast_body(tokens, cotangent, lengths, assign, w_qkv, qv_bias, w_out, out_bias, w_up, up_bias, w_down, down_bias,
              norm_gain, norm_shift):
    bf16, f32 = jnp.bfloat16, jnp.float32
    z, y, c, x = place()
    rows, width = tokens.shape[1:]
    valid = lengths[assign[x]].astype(jnp.int32)

    small = jnp.concatenate([qv_bias, out_bias[None], down_bias[None], norm_gain, norm_shift], 0).astype(f32)
    small = jnp.concatenate([jnp.pad(small, ((0, 0), (0, 96))), up_bias.astype(f32)[None], jnp.zeros((3, 128), f32)], 0)
    block = ring_block(w_up, w_down, c)
    gathered = gather((True, True, False), [
        jnp.stack([small, small]), by_parity(w_qkv, HD), w_out.reshape(2, -1, width)], 0)
    block0 = after(block, gathered[1])
    block1 = ring_up(block0)
    near = spread(block0, block1)
    block2 = ring_up(block1)
    far = spread(block2, ring_up(block2))
    wu, wd = arrange(
        jnp.stack([z, y, x]).astype(jnp.int32),
        (near[0],) + near[1] + (far[0],) + far[1], (near[0],) + near[2] + (far[0],) + far[2])
    small_all = gathered[0].reshape(32, 16, 128)
    vectors = small_all[:, :12, :32].transpose(1, 0, 2).reshape(12, width)
    qv_half = vectors[:2].reshape(2, 8, 2, HD)
    qv_half = jnp.where(c == 0, qv_half[:, :, 0], qv_half[:, :, 1]).reshape(2, 512)
    out_full, down_full, gains, shifts = vectors[2], vectors[3], vectors[4:8], vectors[8:12]
    up_half = small_all[:, 12].reshape(8, 2, 256)
    up_half = jnp.where(c == 0, up_half[:, 0], up_half[:, 1]).reshape(2048)
    wq = gathered[1].reshape(width, 1536)
    wo = gathered[2].reshape(512, width)
    wu = wu.reshape(width, 2048)
    wd = wd.reshape(2048, width)

    swap = [(i, i ^ 1) for i in range(16)]

    def both_cores(block):
        other = lax.ppermute(block, "seq", swap)
        return jnp.concatenate([jnp.where(c == 0, block, other), jnp.where(c == 0, other, block)], 0)

    def core_sum(part):
        return part + lax.ppermute(part, "seq", swap)

    hidden = both_cores(tokens[0]).astype(f32)
    cot = both_cores(cotangent[0]).astype(f32)
    spot = (z * 2 + y) * 256 + jnp.arange(256, dtype=jnp.int32)

    first, pull_first = jax.vjp(norm_rows, hidden, gains[0], shifts[0])
    first = first.astype(bf16)
    projected = dot_nn(first, wq)
    q = (projected[:, :512] + qv_half[0]).astype(bf16)
    k = projected[:, 512:1024].astype(bf16)
    v = (projected[:, 1024:] + qv_half[1]).astype(bf16)
    qk = jnp.concatenate([q.reshape(256, 8, HD), k.reshape(256, 8, HD)], 2).transpose(1, 0, 2)
    packed = exchange(jnp.concatenate([qk, pack_half_rows(v)], 1), 1)
    attended = unpack_half_rows(exchange(attend(valid[None], packed), 2))

    branch = core_sum(dot_nn(attended, wo)) + out_full
    second, pull_second = jax.vjp(norm_rows, branch, gains[1], shifts[1])
    middle = hidden + second
    third, pull_third = jax.vjp(norm_rows, middle, gains[2], shifts[2])
    third = third.astype(bf16)
    up_pre = dot_nn(third, wu) + up_half
    active, pull_gelu = jax.vjp(exact_gelu, up_pre)
    active = active.astype(bf16)
    down_pre = core_sum(dot_nn(active, wd)) + down_full
    fourth, pull_fourth = jax.vjp(norm_rows, down_pre, gains[3], shifts[3])
    output = (middle + fourth).astype(bf16)

    grad_out = cot * (spot < valid).astype(f32)[:, None]
    grad_down, gain4, shift4 = pull_fourth(grad_out)
    grad_down = grad_down.astype(bf16)
    gw_down = contract_rows(active, grad_down).astype(bf16)
    gw_down = gw_down.reshape(4, 2, 2, 128, width)
    (grad_up,) = pull_gelu(dot_nt(grad_down, wd))
    grad_up = grad_up.astype(bf16)
    gw_up = contract_rows(third, grad_up).astype(bf16).reshape(4, 2, 2, 2, 32, 2048)
    ffn_sums = ring_reduce(
        reduce_piece(gw_up, gw_down, z, y, x, (3, 2)), reduce_piece(gw_up, gw_down, z, y, x, (1, 0)))
    up_mine, up_other = pick(ffn_sums[0], c, 0), flip_core(pick(ffn_sums[0], 1 - c, 0))
    r_up = jnp.where(c == 0, jnp.stack([up_mine, up_other]), jnp.stack([up_other, up_mine]))
    r_down = ffn_sums[1]
    part, gain3, shift3 = pull_third(core_sum(dot_nt(grad_up, wu)))
    grad_middle = grad_out + part
    grad_branch, gain2, shift2 = pull_second(grad_middle)
    grad_branch = grad_branch.astype(bf16)
    gw_out = contract_rows(attended, grad_branch).astype(bf16)
    grad_att = dot_nt(grad_branch, wo).astype(bf16)
    grad_packed = exchange(pack_half_rows(grad_att), 3)
    back = exchange(attend_back(valid[None], packed, grad_packed), 4)
    grad_qk = back[:, :256].reshape(8, 256, 2, HD).transpose(1, 2, 0, 3).reshape(256, 1024)
    grad_proj = jnp.concatenate([grad_qk, unpack_half_rows(back[:, 256:])], 1)
    gw_qkv = contract_rows(first, grad_proj).astype(bf16)
    part, gain1, shift1 = pull_first(core_sum(dot_nt(grad_proj, wq)))
    input_grad = (grad_middle + part).astype(bf16)

    halved = 0.5 * jnp.stack([
        jnp.sum(grad_branch.astype(f32), 0), jnp.sum(grad_down.astype(f32), 0),
        gain1, gain2, gain3, gain4, shift1, shift2, shift3, shift4])
    sums = jnp.sum(grad_proj.astype(f32), 0)
    sums_qv = jnp.stack([sums[:512], sums[1024:]]).reshape(2, 8, 1, HD)
    mine = (jnp.arange(2) == c)
    sums_qv = jnp.where(mine[None, None, :, None], sums_qv, 0.0).reshape(2, width)
    vecs = jnp.concatenate([sums_qv, halved], 0).reshape(12, 32, 32).transpose(1, 0, 2)
    sums_up = jnp.sum(grad_up.astype(f32), 0).reshape(8, 1, 256)
    sums_up = jnp.where(mine[None, :, None], sums_up, 0.0).reshape(32, 1, 128)
    small_terms = jnp.concatenate([jnp.pad(vecs, ((0, 0), (0, 0), (0, 96))), sums_up, jnp.zeros((32, 3, 128), f32)], 1)

    r_out, r_qkv, r_small = reduce_terms((False, True, True), [
        gw_out.reshape(4, 2, 2, 2, 16, width), gw_qkv.reshape(4, 2, 2, 2, 32, 1536),
        small_terms.reshape(4, 2, 2, 2, 16, 128)], 5)
    small = r_small[0] + r_small[1]

    def own_rows(block):
        return lax.dynamic_slice_in_dim(block, c * rows, rows, 0)[None]

    return (
        own_rows(output), own_rows(input_grad), from_parity(r_qkv, HD), small[:2, :32], r_out.reshape(32, width),
        small[2, :32], from_parity(r_up, 256), small[12], r_down.reshape(128, width), small[3, :32],
        small[4:8, :32], small[8:12, :32])


def solution(mesh):
    return jax.shard_map(
        fast_body if is_small(mesh) else body,
        mesh=mesh,
        in_specs=(
            P("dp", "seq", None),
            P("dp", "seq", None),
            P(),
            P(),
            P(("seq", "dp"), None),
            P(None, ("seq", "dp")),
            P(("seq", "dp"), None),
            P(("seq", "dp")),
            P(("seq", "dp"), None),
            P(("seq", "dp")),
            P(("seq", "dp"), None),
            P(("seq", "dp")),
            P(None, ("seq", "dp")),
            P(None, ("seq", "dp")),
        ),
        out_specs=(
            P("dp", "seq", None),
            P("dp", "seq", None),
            P(("seq", "dp"), None),
            P(None, ("seq", "dp")),
            P(("seq", "dp"), None),
            P(("seq", "dp")),
            P(("seq", "dp"), None),
            P(("seq", "dp")),
            P(("seq", "dp"), None),
            P(("seq", "dp")),
            P(None, ("seq", "dp")),
            P(None, ("seq", "dp")),
        ),
        check_vma=False,
    )
```

```python
import functools
import math

import jax
import jax.numpy as jnp
from jax import lax
from jax.experimental import pallas as pl
from jax.experimental.pallas import tpu as pltpu
from jax.sharding import PartitionSpec as P


HD = 64


RELAX_SCALE = 32.0
NORM_EPSILON = 1e-05


def norm_rows(values, gain, shift):
    center = values - jnp.mean(values, -1, keepdims=True)
    spread = jnp.mean(center * center, -1, keepdims=True)
    return center * lax.rsqrt(spread + NORM_EPSILON) * gain + shift


def exact_gelu(values):
    return jax.nn.gelu(values, approximate=False)


def contract_rows(left, right):
    return lax.dot_general(
        left, right, (((0,), (0,)), ((), ())), preferred_element_type=jnp.float32
    )


def contract_cols(left, right):
    return lax.dot_general(
        left, right, (((1,), (1,)), ((), ())), preferred_element_type=jnp.float32
    )


def split_heads(block):
    return block.reshape(block.shape[0], 2, HD)


def pair_scores(query_part, key_part):
    factor = 1.0 / (RELAX_SCALE * math.sqrt(HD))
    return (
        jnp.einsum(
            "qhd,khd->hqk",
            split_heads(query_part),
            split_heads(key_part),
            preferred_element_type=jnp.float32,
        )
        * factor
    )


def kept_probs(scores, allowed, row_max, row_total):
    exp_terms = jnp.exp(jnp.where(allowed, RELAX_SCALE * (scores - row_max), -jnp.inf))
    return exp_terms / row_total


def body(
    tokens,
    cotangent,
    lengths,
    assign,
    w_qkv,
    qv_bias,
    w_out,
    out_bias,
    w_up,
    up_bias,
    w_down,
    down_bias,
    norm_gain,
    norm_shift,
):
    gathered = (
        lax.all_gather(w_qkv, ("seq", "dp"), axis=0, tiled=True),
        lax.all_gather(w_out, ("seq", "dp"), axis=0, tiled=True),
        lax.all_gather(w_up, ("seq", "dp"), axis=0, tiled=True),
        lax.all_gather(w_down, ("seq", "dp"), axis=0, tiled=True),
        lax.all_gather(qv_bias, ("seq", "dp"), axis=1, tiled=True),
        lax.all_gather(out_bias, ("seq", "dp"), axis=0, tiled=True),
        lax.all_gather(up_bias, ("seq", "dp"), axis=0, tiled=True),
        lax.all_gather(down_bias, ("seq", "dp"), axis=0, tiled=True),
        lax.all_gather(norm_gain, ("seq", "dp"), axis=1, tiled=True),
        lax.all_gather(norm_shift, ("seq", "dp"), axis=1, tiled=True),
    )
    qkv_full, out_full, up_full, down_full = (gathered[0], gathered[1], gathered[2], gathered[3])
    qv_shift = gathered[4].astype(jnp.float32)
    out_shift = gathered[5].astype(jnp.float32)
    up_shift = gathered[6].astype(jnp.float32)
    down_shift = gathered[7].astype(jnp.float32)
    gains = gathered[8].astype(jnp.float32)
    shifts = gathered[9].astype(jnp.float32)
    row_count = tokens.shape[1]
    model_width = tokens.shape[2]
    pair_cols = 2 * HD
    pair_count = model_width // pair_cols
    slot_rows = row_count * lax.axis_size("seq")
    factor = 1.0 / (RELAX_SCALE * math.sqrt(HD))
    valid = lengths[assign[lax.axis_index("dp")]]
    own_place = lax.axis_index("seq") * row_count + jnp.arange(row_count, dtype=jnp.int32)
    all_place = jnp.arange(slot_rows, dtype=jnp.int32)
    allowed = (all_place[None, :] <= own_place[:, None]) & (all_place[None, :] < valid)
    pair_ids = jnp.arange(pair_count, dtype=jnp.int32)
    hidden = tokens[0].astype(jnp.float32)
    normed_first, pull_first = jax.vjp(norm_rows, hidden, gains[0], shifts[0])
    normed_low = normed_first.astype(jnp.bfloat16)
    projected = jnp.dot(normed_low, qkv_full, preferred_element_type=jnp.float32)
    queries = (projected[:, :model_width] + qv_shift[0]).astype(jnp.bfloat16)
    key_own = projected[:, model_width : 2 * model_width].astype(jnp.bfloat16)
    value_own = (projected[:, 2 * model_width :] + qv_shift[1]).astype(jnp.bfloat16)
    keys, values = (
        lax.all_gather(key_own, "seq", axis=0, tiled=True),
        lax.all_gather(value_own, "seq", axis=0, tiled=True),
    )

    def columns(block, pair_index):
        return lax.dynamic_slice_in_dim(block, pair_index * pair_cols, pair_cols, 1)

    def merge_pairs(stack):
        return stack.transpose(1, 0, 2).reshape(stack.shape[1], model_width)

    def attend(pair_index):
        scores = pair_scores(columns(queries, pair_index), columns(keys, pair_index))
        row_max = jnp.max(jnp.where(allowed, scores, -jnp.inf), -1, keepdims=True)
        exp_terms = jnp.exp(jnp.where(allowed, RELAX_SCALE * (scores - row_max), -jnp.inf))
        row_total = jnp.sum(exp_terms, -1, keepdims=True)
        probs = (exp_terms / row_total).astype(jnp.bfloat16)
        mixed = jnp.einsum(
            "hqk,khd->qhd",
            probs,
            split_heads(columns(values, pair_index)),
            preferred_element_type=jnp.float32,
        )
        return (mixed.reshape(row_count, pair_cols), row_max[..., 0], row_total[..., 0])

    mixed_pairs, max_pairs, total_pairs = lax.map(attend, pair_ids)
    attended = merge_pairs(mixed_pairs).astype(jnp.bfloat16)
    branch = jnp.dot(attended, out_full, preferred_element_type=jnp.float32) + out_shift
    normed_second, pull_second = jax.vjp(norm_rows, branch, gains[1], shifts[1])
    middle = hidden + normed_second
    normed_third, pull_third = jax.vjp(norm_rows, middle, gains[2], shifts[2])
    third_low = normed_third.astype(jnp.bfloat16)
    up_pre = jnp.dot(third_low, up_full, preferred_element_type=jnp.float32) + up_shift
    activated, pull_gelu = jax.vjp(exact_gelu, up_pre)
    active_low = activated.astype(jnp.bfloat16)
    down_pre = jnp.dot(active_low, down_full, preferred_element_type=jnp.float32) + down_shift
    normed_fourth, pull_fourth = jax.vjp(norm_rows, down_pre, gains[3], shifts[3])
    output = (middle + normed_fourth).astype(jnp.bfloat16)[None]
    again = (
        lax.all_gather(w_qkv, ("seq", "dp"), axis=0, tiled=True),
        lax.all_gather(w_out, ("seq", "dp"), axis=0, tiled=True),
        lax.all_gather(w_up, ("seq", "dp"), axis=0, tiled=True),
        lax.all_gather(w_down, ("seq", "dp"), axis=0, tiled=True),
    )
    qkv_back, out_back, up_back, down_back = (again[0], again[1], again[2], again[3])
    keep_rows = (own_place < valid).astype(jnp.float32)[:, None]
    grad_out = cotangent[0].astype(jnp.float32) * keep_rows
    grad_down, grad_gain_four, grad_shift_four = pull_fourth(grad_out)
    grad_down_low = grad_down.astype(jnp.bfloat16)
    grad_w_down = contract_rows(active_low, grad_down_low)
    grad_b_down = jnp.sum(grad_down_low.astype(jnp.float32), 0)
    (grad_up,) = pull_gelu(contract_cols(grad_down_low, down_back))
    grad_up_low = grad_up.astype(jnp.bfloat16)
    grad_w_up = contract_rows(third_low, grad_up_low)
    grad_b_up = jnp.sum(grad_up_low.astype(jnp.float32), 0)
    grad_middle_part, grad_gain_three, grad_shift_three = pull_third(
        contract_cols(grad_up_low, up_back)
    )
    grad_middle = grad_out + grad_middle_part
    grad_branch, grad_gain_two, grad_shift_two = pull_second(grad_middle)
    grad_branch_low = grad_branch.astype(jnp.bfloat16)
    grad_w_out = contract_rows(attended, grad_branch_low)
    grad_b_out = jnp.sum(grad_branch_low.astype(jnp.float32), 0)
    grad_attended = contract_cols(grad_branch_low, out_back).astype(jnp.bfloat16)

    def query_side(pair_index):
        scores = pair_scores(columns(queries, pair_index), columns(keys, pair_index))
        probs = kept_probs(
            scores, allowed, max_pairs[pair_index][..., None], total_pairs[pair_index][..., None]
        )
        grad_part = columns(grad_attended, pair_index)
        grad_probs = jnp.einsum(
            "qhd,khd->hqk",
            split_heads(grad_part),
            split_heads(columns(values, pair_index)),
            preferred_element_type=jnp.float32,
        )
        delta = jnp.sum(probs * grad_probs, -1, keepdims=True)
        grad_scores = (RELAX_SCALE * probs * (grad_probs - delta)).astype(jnp.bfloat16)
        grad_query = (
            jnp.einsum(
                "hqk,khd->qhd",
                grad_scores,
                split_heads(columns(keys, pair_index)),
                preferred_element_type=jnp.float32,
            )
            * factor
        )
        return (grad_query.reshape(row_count, pair_cols), grad_scores, probs, delta)

    def both_sides(pair_index):
        grad_query, grad_scores, probs, delta = query_side(pair_index)
        grad_part = columns(grad_attended, pair_index)
        grad_key = (
            jnp.einsum(
                "hqk,qhd->khd",
                grad_scores,
                split_heads(columns(queries, pair_index)),
                preferred_element_type=jnp.float32,
            )
            * factor
        )
        grad_value = jnp.einsum(
            "hqk,qhd->khd",
            probs.astype(jnp.bfloat16),
            split_heads(grad_part),
            preferred_element_type=jnp.float32,
        )
        return (
            grad_query,
            grad_key.reshape(slot_rows, pair_cols),
            grad_value.reshape(slot_rows, pair_cols),
        )

    query_pairs, key_terms, value_terms = lax.map(both_sides, pair_ids)
    key_pairs, value_pairs = (
        lax.psum_scatter(
            key_terms.astype(jnp.bfloat16), "seq", scatter_dimension=1, tiled=True
        ).astype(jnp.float32),
        lax.psum_scatter(
            value_terms.astype(jnp.bfloat16), "seq", scatter_dimension=1, tiled=True
        ).astype(jnp.float32),
    )
    grad_q_low = merge_pairs(query_pairs).astype(jnp.bfloat16)
    grad_k_low = merge_pairs(key_pairs).astype(jnp.bfloat16)
    grad_v_low = merge_pairs(value_pairs).astype(jnp.bfloat16)
    grad_projected = jnp.concatenate([grad_q_low, grad_k_low, grad_v_low], 1)
    grad_w_qkv = contract_rows(normed_low, grad_projected)
    grad_qv = jnp.stack(
        [jnp.sum(grad_q_low.astype(jnp.float32), 0), jnp.sum(grad_v_low.astype(jnp.float32), 0)]
    )
    grad_hidden_part, grad_gain_one, grad_shift_one = pull_first(
        contract_cols(grad_projected, qkv_back)
    )
    input_grad = (grad_middle + grad_hidden_part).astype(jnp.bfloat16)[None]
    grad_gains = jnp.stack([grad_gain_one, grad_gain_two, grad_gain_three, grad_gain_four])
    grad_shifts = jnp.stack([grad_shift_one, grad_shift_two, grad_shift_three, grad_shift_four])
    owned = (
        lax.psum_scatter(grad_w_qkv, ("seq", "dp"), scatter_dimension=0, tiled=True),
        lax.psum_scatter(grad_w_out, ("seq", "dp"), scatter_dimension=0, tiled=True),
        lax.psum_scatter(grad_w_up, ("seq", "dp"), scatter_dimension=0, tiled=True),
        lax.psum_scatter(grad_w_down, ("seq", "dp"), scatter_dimension=0, tiled=True),
        lax.psum_scatter(grad_qv, ("seq", "dp"), scatter_dimension=1, tiled=True),
        lax.psum_scatter(grad_b_out, ("seq", "dp"), scatter_dimension=0, tiled=True),
        lax.psum_scatter(grad_b_up, ("seq", "dp"), scatter_dimension=0, tiled=True),
        lax.psum_scatter(grad_b_down, ("seq", "dp"), scatter_dimension=0, tiled=True),
        lax.psum_scatter(grad_gains, ("seq", "dp"), scatter_dimension=1, tiled=True),
        lax.psum_scatter(grad_shifts, ("seq", "dp"), scatter_dimension=1, tiled=True),
    )
    return (
        output,
        input_grad,
        owned[0],
        owned[4],
        owned[1],
        owned[5],
        owned[2],
        owned[6],
        owned[3],
        owned[7],
        owned[8],
        owned[9],
    )


MESH = pl.DeviceIdType.MESH


def is_small(mesh):
    return mesh.shape["seq"] == 16 and mesh.shape["dp"] == 2


def place():
    seq = lax.axis_index("seq")
    return seq // 8, (seq // 4) % 2, (seq // 2) % 2, seq % 2, lax.axis_index("dp")


def exchange_kernel(scatter, src, out, send_sem, recv_sem, own_sem):
    a, b, y, c, x = place()
    barrier = pltpu.get_barrier_semaphore()

    def peer(k):
        return lax.rem(a + k // 2, 2), lax.rem(y + k % 2, 2)

    def device(k):
        pa, py = peer(k)
        return (pa * 8 + b * 4 + py * 2 + c, x)

    def source(k):
        pa, py = peer(k)
        return src.at[pa * 2 + py] if scatter else src.at[pa, :, py]

    def target(k):
        pa, py = peer(k)
        return out.at[pa, :, py] if scatter else out.at[pa * 2 + py]

    for k in range(1, 4):
        pl.semaphore_signal(barrier, inc=1, device_id=device(k), device_id_type=MESH)
    own = pltpu.make_async_copy(source(0), target(0), own_sem)
    own.start()
    pl.semaphore_wait(barrier, 3)

    def copy(k, dst):
        return pltpu.make_async_remote_copy(
            src_ref=source(k), dst_ref=target(dst), send_sem=send_sem.at[k], recv_sem=recv_sem.at[k],
            device_id=device(k), device_id_type=MESH)

    for k in (3, 2, 1):
        copy(k, 0).start()
    own.wait()
    for k in (3, 2, 1):
        copy(k, k).wait_recv()
    for k in (3, 2, 1):
        copy(k, 0).wait_send()


def exchange(blocks, scatter, cid):
    vm = pl.BlockSpec(memory_space=pltpu.VMEM)
    rows = blocks.shape[-2]
    shape = (2, 2, 2, rows, 128) if scatter else (4, 2, rows, 128)
    return pl.pallas_call(
        functools.partial(exchange_kernel, scatter), out_shape=jax.ShapeDtypeStruct(shape, blocks.dtype),
        in_specs=[vm], out_specs=vm,
        scratch_shapes=[pltpu.SemaphoreType.DMA((4,)), pltpu.SemaphoreType.DMA((4,)), pltpu.SemaphoreType.DMA],
        compiler_params=pltpu.CompilerParams(collective_id=cid, has_side_effects=True),
        cost_estimate=pl.CostEstimate(flops=0, bytes_accessed=rows * 100000, transcendentals=0),
        name="exchange",
    )(blocks)


def dot_nt(a, b):
    return lax.dot_general(a, b, (((1,), (1,)), ((), ())), preferred_element_type=jnp.float32)


def dot_nn(a, b):
    return jnp.dot(a, b, preferred_element_type=jnp.float32)


BQ = 256
MASKED = -1e30


def load_heads(valid, packed, q_ref, k_ref):
    rows = q_ref.shape[0]
    qk = packed[:, :256].reshape(rows, 128)
    kq = jnp.concatenate([qk[:, 64:], qk[:, :64]], axis=1)
    lane = lax.broadcasted_iota(jnp.int32, (rows, 128), 1)
    spot = lax.broadcasted_iota(jnp.int32, (rows, 128), 0)
    past = jnp.where(spot < valid, 0.0, MASKED)
    q_ref[...] = jnp.where(lane < 64, qk.astype(jnp.float32), jnp.where(lane == 64, 1.0, 0.0)).astype(jnp.bfloat16)
    k_ref[...] = jnp.where(lane < 64, kq.astype(jnp.float32), jnp.where(lane == 64, past, 0.0)).astype(jnp.bfloat16)


def unpack_rows(halves):
    n = halves.shape[0]
    return jnp.concatenate([halves[:, :, :64], halves[:, :, 64:]], axis=1).reshape(n * 256, 64)


def block_probs(q_ref, k_ref, i):
    n = (i + 1) * BQ
    scores = dot_nt(k_ref[:n], q_ref[i * BQ:n])
    key = lax.broadcasted_iota(jnp.int32, (BQ, BQ), 0)
    query = lax.broadcasted_iota(jnp.int32, (BQ, BQ), 1)
    corner = jnp.where(key <= query, scores[n - BQ:], MASKED)
    scores = jnp.concatenate([scores[:n - BQ], corner], axis=0) if i else corner
    top = jnp.max(scores, axis=0, keepdims=True)
    terms = jnp.exp((scores - top) * 0.125)
    return terms, 1.0 / jnp.sum(terms, axis=0, keepdims=True)


def attend_kernel(valid_ref, packed, out_ref, q_ref, k_ref, vt_ref):
    load_heads(valid_ref[0], packed, q_ref, k_ref)
    unit = jnp.where(
        lax.broadcasted_iota(jnp.int32, (64, 64), 0) == lax.broadcasted_iota(jnp.int32, (64, 64), 1), 1.0, 0.0
    ).astype(jnp.bfloat16)
    vt_ref[...] = dot_nt(unit, unpack_rows(packed[:, 256:])).astype(jnp.bfloat16)
    for i in range(q_ref.shape[0] // BQ):
        n = (i + 1) * BQ
        terms, scale = block_probs(q_ref, k_ref, i)
        probs = (terms * scale).astype(jnp.bfloat16)
        mixed = dot_nn(vt_ref[:, :n], probs).T
        out_ref[i] = jnp.concatenate([mixed[:128], mixed[128:]], axis=1).astype(jnp.bfloat16)


def attend_back_kernel(valid_ref, packed, grad, out_ref, q_ref, k_ref, v_ref, g_ref, kt_ref, dk_ref, dv_ref):
    load_heads(valid_ref[0], packed, q_ref, k_ref)
    v_ref[...] = unpack_rows(packed[:, 256:])
    g_ref[...] = unpack_rows(grad[...])
    unit = jnp.where(
        lax.broadcasted_iota(jnp.int32, (64, 128), 0) == lax.broadcasted_iota(jnp.int32, (64, 128), 1), 1.0, 0.0
    ).astype(jnp.bfloat16)
    kt_ref[...] = dot_nt(unit, k_ref[...]).astype(jnp.bfloat16)
    dk_ref[...] = jnp.zeros_like(dk_ref)
    dv_ref[...] = jnp.zeros_like(dv_ref)
    blocks = q_ref.shape[0] // BQ
    for i in range(blocks):
        n = (i + 1) * BQ
        terms, scale = block_probs(q_ref, k_ref, i)
        probs = terms * scale
        grad_probs = dot_nt(v_ref[:n], g_ref[i * BQ:n])
        delta = jnp.sum(probs * grad_probs, axis=0, keepdims=True)
        grad_scores = (probs * (grad_probs - delta)).astype(jnp.bfloat16)
        grad_query = dot_nn(kt_ref[:, :n], grad_scores).T * 0.125
        out_ref[i, :256, :64] = grad_query.astype(jnp.bfloat16)
        dk_ref[:n] += dot_nn(grad_scores, q_ref[i * BQ:n])
        dv_ref[:n] += dot_nn(probs.astype(jnp.bfloat16), g_ref[i * BQ:n])
    for i in range(blocks):
        rows = slice(i * BQ, (i + 1) * BQ)
        out_ref[i, :256, 64:] = (dk_ref[rows, :64] * 0.125).astype(jnp.bfloat16)
        value = dv_ref[rows].astype(jnp.bfloat16)
        out_ref[i, 256:] = jnp.concatenate([value[:128], value[128:]], axis=1)


def attend(valid, packed):
    rows = packed.shape[0] * 256
    vm = pl.BlockSpec(memory_space=pltpu.VMEM)
    return pl.pallas_call(
        attend_kernel,
        out_shape=jax.ShapeDtypeStruct((packed.shape[0], 128, 128), jnp.bfloat16),
        in_specs=[pl.BlockSpec(memory_space=pltpu.SMEM), vm], out_specs=vm,
        scratch_shapes=[pltpu.VMEM((rows, 128), jnp.bfloat16)] * 2 + [pltpu.VMEM((64, rows), jnp.bfloat16)],
        compiler_params=pltpu.CompilerParams(vmem_limit_bytes=48 << 20),
        name="attend",
    )(valid, packed)


def attend_back(valid, packed, grad):
    rows = packed.shape[0] * 256
    vm = pl.BlockSpec(memory_space=pltpu.VMEM)
    return pl.pallas_call(
        attend_back_kernel,
        out_shape=jax.ShapeDtypeStruct(packed.shape, jnp.bfloat16),
        in_specs=[pl.BlockSpec(memory_space=pltpu.SMEM), vm, vm], out_specs=vm,
        scratch_shapes=[pltpu.VMEM((rows, 128), jnp.bfloat16)] * 2 + [pltpu.VMEM((rows, 64), jnp.bfloat16)] * 2
        + [pltpu.VMEM((64, rows), jnp.bfloat16), pltpu.VMEM((rows, 128), jnp.float32), pltpu.VMEM((rows, 64), jnp.float32)],
        compiler_params=pltpu.CompilerParams(vmem_limit_bytes=48 << 20),
        name="attend_back",
    )(valid, packed, grad)


def flip(bits, block):
    return lax.ppermute(block, "seq", [(s, s ^ bits) for s in range(16)])


flip_a, flip_b, flip_y, flip_core, flip_far = (functools.partial(flip, bits) for bits in (8, 4, 2, 1, 5))


def flip_x(block):
    return lax.ppermute(block, "dp", [(0, 1), (1, 0)])


def after(value, *others):
    return lax.optimization_barrier((value,) + others)[0]


def pick(block, index, axis, keepdims=False):
    return lax.dynamic_index_in_dim(block, index, axis, keepdims=keepdims)


def swap_if(flag, block, axis):
    return jnp.where(flag == 0, block, lax.rev(block, (axis,)))


def sort_ranks(block, b, c):
    return swap_if(c, swap_if(b, block, 0), 1)


def to_ranks(block, b, c):
    mine = pick(pick(block, b, 0), c, 0)
    core = flip_core(pick(pick(block, b, 0), 1 - c, 0))
    near = flip_b(pick(pick(block, 1 - b, 0), c, 0))
    far = flip_far(pick(pick(block, 1 - b, 0), 1 - c, 0))
    return jnp.stack([jnp.stack([mine, core]), jnp.stack([near, far])])


def gather_rows(block):
    core, near = flip_core(block), flip_b(block)
    return jnp.concatenate([block, core, near, flip_core(near)], 0)


def scatter_rows(part):
    part = part.reshape(2, 2, part.shape[0] // 4, part.shape[1])
    far = part[1, 0] + flip_core(part[1, 1])
    near = part[0, 0] + flip_core(part[0, 1])
    return near + flip_b(far.astype(jnp.bfloat16)).astype(jnp.float32)


def cube_start(block):
    return jnp.stack([block, flip_a(block)])


def cube_one(flip_one, block):
    return jnp.concatenate([block, flip_one(block)], 0)


def arrange_kernel(count, spot_ref, *refs):
    for k in range(count):
        block, out = refs[k], refs[count + k]
        if len(out.shape) == 7:
            for i in range(2):
                for j in range(2):
                    out[0, i, 0, j, 0] = block[0, i, j]
        else:
            out[0, 0, 0] = block[0]


def arrange(spot, blocks):
    def coords(i, r, y_first):
        second, first, a = i // 4, (i // 2) % 2, i % 2
        y, x = (first, second) if y_first else (second, first)
        return lax.rem(r[0] + a, 2), lax.rem(r[1] + y, 2), lax.rem(r[2] + x, 2)

    def specs(block, y_first):
        shape = block.shape
        if len(shape) == 5:
            def out_place(i, r):
                a, y, x = coords(i, r, y_first)
                return a, 0, y, 0, x, 0, 0
            return (pl.BlockSpec((1,) + shape[1:], lambda i, r: (i, 0, 0, 0, 0)),
                    pl.BlockSpec((1, 2, 1, 2, 1) + shape[3:], out_place),
                    jax.ShapeDtypeStruct((2,) * 5 + shape[3:], block.dtype))

        def out_place(i, r):
            return coords(i, r, y_first) + (0, 0)
        return (pl.BlockSpec((1,) + shape[1:], lambda i, r: (i, 0, 0)),
                pl.BlockSpec((1, 1, 1) + shape[1:], out_place),
                jax.ShapeDtypeStruct((2, 2, 2) + shape[1:], block.dtype))

    made = [specs(*entry) for entry in blocks]
    return pl.pallas_call(
        functools.partial(arrange_kernel, len(blocks)),
        out_shape=tuple(m[2] for m in made),
        grid_spec=pltpu.PrefetchScalarGridSpec(
            num_scalar_prefetch=1, grid=(8,), in_specs=[m[0] for m in made], out_specs=tuple(m[1] for m in made)),
        compiler_params=pltpu.CompilerParams(vmem_limit_bytes=32 << 20),
        cost_estimate=pl.CostEstimate(flops=0, bytes_accessed=8 << 20, transcendentals=0),
        name="arrange",
    )(spot, *[entry[0] for entry in blocks])


def add_low(mine, other):
    return (mine.astype(jnp.float32) + other.astype(jnp.float32)).astype(jnp.bfloat16)


def fold(terms, flip_one, index, axis):
    return add_low(pick(terms, index, axis, True), flip_one(pick(terms, 1 - index, axis, True)))


def fold_last(terms, flip_one, index, axis):
    return (pick(terms, index, axis, True).astype(jnp.float32)
            + flip_one(pick(terms, 1 - index, axis, True)).astype(jnp.float32))


def pack_heads(block, b, c):
    block = sort_ranks(block.reshape(2, 2, 128, 4, HD), b, c)
    return block.transpose(3, 0, 2, 1, 4).reshape(4, 2, 128, 128)


def unpack_heads(packed):
    return packed.reshape(4, 2, 128, 2, HD).transpose(1, 3, 2, 0, 4).reshape(2, 2, 128, 4 * HD)


def fast_body(tokens, cotangent, lengths, assign, w_qkv, qv_bias, w_out, out_bias, w_up, up_bias, w_down, down_bias,
              norm_gain, norm_shift):
    bf16, f32 = jnp.bfloat16, jnp.float32
    a, b, y, c, x = place()
    spot = jnp.stack([a, y, x]).astype(jnp.int32)
    width = tokens.shape[2]
    valid = lengths[assign[x]].astype(jnp.int32)

    qkv = w_qkv.reshape(32, 3, 2, 2, 2, 2, HD)
    qk_ranks = qkv[:, :2].transpose(3, 5, 0, 2, 4, 1, 6).reshape(2, 2, 32, 512)
    v_ranks = qkv[:, 2].transpose(2, 4, 0, 1, 3, 5).reshape(2, 2, 32, 256)
    qkv_block = to_ranks(jnp.concatenate([qk_ranks, v_ranks], 3), b, c)
    small = jnp.concatenate([qv_bias.reshape(-1), out_bias, down_bias, norm_gain.reshape(-1), norm_shift.reshape(-1), up_bias])
    small = jnp.pad(small.reshape(4, 128), ((0, 12), (0, 0)))
    small_core, small_near = flip_core(small), flip_b(small)
    small = jnp.stack([small, small_core, small_near, flip_core(small_near)]).reshape(2, 2, 16, 128)

    qkv_block = sort_ranks(qkv_block, b, c)
    qk_one, v_one = cube_start(qkv_block[..., :512]), cube_start(qkv_block[..., 512:])
    out_one, small = cube_start(w_out), cube_start(small)
    rows = gather_rows(tokens[0])
    qk_two, v_two, out_two, small = cube_one(flip_y, qk_one), cube_one(flip_x, v_one), cube_one(flip_x, out_one), cube_one(flip_y, small)
    qk_all, v_all, out_all, small = cube_one(flip_x, qk_two), cube_one(flip_y, v_two), cube_one(flip_y, out_two), cube_one(flip_x, small)
    wqk, wv, wo = arrange(spot, [(qk_all, True), (v_all, False), (out_all, False)])
    wqk, wv, wo = wqk.reshape(width, 512), wv.reshape(width, 256), wo.reshape(256, width)

    up = w_up.reshape(32, 2, 2, 2, 2, 2, 128).transpose(2, 4, 0, 1, 3, 5, 6).reshape(2, 2, 32, 1024)
    up_block = sort_ranks(to_ranks(after(up, qkv_block), b, c), b, c)
    up_one, down_one = cube_start(after(up_block, qk_one)), cube_start(after(w_down, qk_one))
    up_two, down_two = cube_one(flip_y, after(up_one, qk_all)), cube_one(flip_x, after(down_one, v_all))

    small = small.reshape(2, 2, 2, 2, 2, 16, 128).astype(f32)
    for axis, flag in enumerate((x, y, a, b, c)):
        small = swap_if(flag, small, axis)
    small = small.transpose(2, 3, 1, 4, 0, 5, 6)[..., :4, :]
    vectors = small[..., :3, :].reshape(32, 12, 32).transpose(1, 0, 2).reshape(12, width)
    qv_half = pick(pick(vectors[:2].reshape(2, 2, 2, 2, 2, HD), b, 2), c, 3).reshape(2, 4, HD)
    qk_shift = jnp.concatenate([qv_half[0], jnp.zeros((4, HD), f32)], 1).reshape(512)
    v_shift = qv_half[1].reshape(256)
    out_full, down_full, gains, shifts = vectors[2], vectors[3], vectors[4:8], vectors[8:12]
    up_shift = pick(pick(small[..., 3, :], b, 1), c, 2).reshape(1024)

    hidden = tokens[0].astype(f32)
    first = norm_rows(rows.astype(f32), gains[0], shifts[0]).astype(bf16)
    qk = (dot_nn(first, wqk) + qk_shift).astype(bf16)
    v = (dot_nn(first, wv) + v_shift).astype(bf16)
    qk = sort_ranks(qk.reshape(2, 2, 128, 4, 128), b, c).transpose(3, 0, 1, 2, 4).reshape(4, 2, 256, 128)
    packed = exchange(jnp.concatenate([qk, pack_heads(v, b, c)], 2), True, 1).reshape(8, 384, 128)
    attended = exchange(attend(valid[None], packed).reshape(2, 2, 2, 128, 128), False, 2)
    attended = sort_ranks(unpack_heads(attended), b, c).reshape(512, 256)

    up_all, down_all = cube_one(flip_x, up_two), cube_one(flip_y, after(down_two, attended))
    branch = scatter_rows(dot_nn(attended, wo)) + out_full
    second, pull_second = jax.vjp(norm_rows, branch, gains[1], shifts[1])
    middle = hidden + second
    third, pull_third = jax.vjp(norm_rows, middle, gains[2], shifts[2])
    third = gather_rows(third.astype(bf16))
    wu, wd = arrange(spot, [(up_all, True), (down_all, False)])
    wu, wd = wu.reshape(width, 1024), wd.reshape(1024, width)
    up_pre = dot_nn(third, wu) + up_shift
    active, pull_gelu = jax.vjp(exact_gelu, up_pre)
    active = active.astype(bf16)
    down_pre = scatter_rows(dot_nn(active, wd)) + down_full
    fourth, pull_fourth = jax.vjp(norm_rows, down_pre, gains[3], shifts[3])
    output = (middle + fourth).astype(bf16)

    own_spot = lax.axis_index("seq") * 128 + jnp.arange(128, dtype=jnp.int32)
    grad_out = cotangent[0].astype(f32) * (own_spot < valid).astype(f32)[:, None]
    grad_down, gain4, shift4 = pull_fourth(grad_out)
    grad_down = grad_down.astype(bf16)
    down_rows = gather_rows(grad_down)
    gw_down = contract_rows(active, down_rows).astype(bf16).reshape(2, 2, 2, 128, width)
    down_sum = fold(gw_down, flip_y, y, 1)
    (grad_up,) = pull_gelu(dot_nt(down_rows, wd))
    grad_up = grad_up.astype(bf16)
    gw_up = contract_rows(third, grad_up).astype(bf16).reshape(2, 2, 2, 2, 2, 32, 1024)
    up_sum = fold(gw_up, flip_x, x, 4)
    part, gain3, shift3 = pull_third(scatter_rows(dot_nt(grad_up, wu)))
    grad_middle = grad_out + part
    grad_branch, gain2, shift2 = pull_second(grad_middle)
    grad_branch = grad_branch.astype(bf16)
    branch_rows = gather_rows(grad_branch)
    grad_att = dot_nt(branch_rows, wo).astype(bf16)
    grad_packed = exchange(pack_heads(grad_att, b, c), True, 3).reshape(8, 128, 128)
    back = attend_back(valid[None], packed, grad_packed)

    up_sum = fold(after(up_sum, grad_packed), flip_y, y, 2)
    down_sum = fold(after(down_sum, grad_packed), flip_x, x, 2)
    gw_out = contract_rows(attended, branch_rows).astype(bf16).reshape(2, 2, 2, 32, width)
    back = exchange(back.reshape(2, 2, 2, 384, 128), False, 4)
    grad_qk = back[:, :, :256].reshape(4, 2, 2, 128, 128).transpose(1, 2, 3, 0, 4).reshape(2, 2, 128, 512)
    grad_qk = sort_ranks(grad_qk, b, c).reshape(512, 512)
    grad_v = sort_ranks(unpack_heads(back[:, :, 256:]), b, c).reshape(512, 256)
    gw_qk = contract_rows(first, grad_qk).astype(bf16).reshape(2, 2, 2, 2, 2, 32, 512)
    gw_v = contract_rows(first, grad_v).astype(bf16).reshape(2, 2, 2, 2, 2, 32, 256)
    _, pull_first = jax.vjp(norm_rows, hidden, gains[0], shifts[0])
    part, gain1, shift1 = pull_first(scatter_rows(dot_nt(grad_qk, wqk) + dot_nt(grad_v, wv)))
    input_grad = (grad_middle + part).astype(bf16)

    out_sum = fold(fold(gw_out, flip_y, y, 1), flip_x, x, 2)
    qk_sum = fold(fold(gw_qk, flip_x, x, 4), flip_y, y, 2)
    v_sum = fold(fold(gw_v, flip_y, y, 2), flip_x, x, 4)
    r_qk = fold_last(qk_sum, flip_a, a, 0).reshape(2, 2, 32, 512)
    r_v = fold_last(v_sum, flip_a, a, 0).reshape(2, 2, 32, 256)
    r_out = fold_last(out_sum, flip_a, a, 0).reshape(32, width)
    r_up = fold_last(after(up_sum, back), flip_a, a, 0).reshape(2, 2, 32, 1024)
    r_down = fold_last(after(down_sum, back), flip_a, a, 0).reshape(128, width)

    def own_columns(block):
        return sort_ranks(to_ranks(block, b, c), b, c)

    r_qkv = own_columns(jnp.concatenate([r_qk, r_v], 3))
    r_up = own_columns(r_up).reshape(2, 2, 32, 2, 2, 2, 128).transpose(2, 3, 0, 4, 1, 5, 6).reshape(32, 4096)
    out_qk = r_qkv[..., :512].reshape(2, 2, 32, 2, 2, 2, HD).transpose(2, 5, 3, 0, 4, 1, 6).reshape(32, 2048)
    out_v = r_qkv[..., 512:].reshape(2, 2, 32, 2, 2, HD).transpose(2, 3, 0, 4, 1, 5).reshape(32, 1024)

    def in_ranks(block, axes):
        for axis, flag in axes:
            spots = lax.broadcasted_iota(jnp.int32, [2 if i == axis else 1 for i in range(block.ndim)], axis)
            block = jnp.where(spots == flag, block, 0.0)
        return block

    def head_sums(block):
        sums = jnp.sum(block.astype(f32), 0).reshape(2, 1, 2, 1, -1)[..., :HD]
        sums = jnp.broadcast_to(sums, (2, 2, 2, 2, HD))
        return in_ranks(sums, ((1, b), (3, c))).reshape(1, width)

    whole = jnp.stack([
        jnp.sum(grad_branch.astype(f32), 0), jnp.sum(grad_down.astype(f32), 0),
        gain1, gain2, gain3, gain4, shift1, shift2, shift3, shift4])
    vecs = jnp.concatenate([head_sums(grad_qk), head_sums(grad_v), whole], 0)
    vecs = vecs.reshape(12, 32, 32).transpose(1, 0, 2).reshape(2, 2, 2, 2, 2, 3, 128)
    sums_up = jnp.broadcast_to(jnp.sum(grad_up.astype(f32), 0).reshape(2, 1, 2, 1, 2, 1, 128), (2, 2, 2, 2, 2, 1, 128))
    sums_up = in_ranks(sums_up, ((1, b), (3, c)))
    terms = jnp.concatenate([vecs, sums_up, jnp.zeros((2, 2, 2, 2, 2, 4, 128), f32)], 5)
    for flip_one, index, axis in ((flip_x, x, 4), (flip_y, y, 2), (flip_a, a, 0), (flip_b, b, 1), (flip_core, c, 3)):
        terms = pick(terms, index, axis, True) + flip_one(pick(terms, 1 - index, axis, True))
    small = terms.reshape(8, 128)
    vectors = small[:3].reshape(12, 32)

    return (
        output[None], input_grad[None], jnp.concatenate([out_qk, out_v], 1), vectors[:2], r_out,
        vectors[2], r_up, small[3], r_down, vectors[3], vectors[4:8], vectors[8:12])


def solution(mesh):
    return jax.shard_map(
        fast_body if is_small(mesh) else body,
        mesh=mesh,
        in_specs=(
            P("dp", "seq", None),
            P("dp", "seq", None),
            P(),
            P(),
            P(("seq", "dp"), None),
            P(None, ("seq", "dp")),
            P(("seq", "dp"), None),
            P(("seq", "dp")),
            P(("seq", "dp"), None),
            P(("seq", "dp")),
            P(("seq", "dp"), None),
            P(("seq", "dp")),
            P(None, ("seq", "dp")),
            P(None, ("seq", "dp")),
        ),
        out_specs=(
            P("dp", "seq", None),
            P("dp", "seq", None),
            P(("seq", "dp"), None),
            P(None, ("seq", "dp")),
            P(("seq", "dp"), None),
            P(("seq", "dp")),
            P(("seq", "dp"), None),
            P(("seq", "dp")),
            P(("seq", "dp"), None),
            P(("seq", "dp")),
            P(None, ("seq", "dp")),
            P(None, ("seq", "dp")),
        ),
        check_vma=False,
    )
```

```python
import functools
import math

import jax
import jax.numpy as jnp
from jax import lax
from jax.experimental import pallas as pl
from jax.experimental.pallas import tpu as pltpu
from jax.sharding import PartitionSpec as P


HD = 64


RELAX_SCALE = 32.0
NORM_EPSILON = 1e-05


def norm_rows(values, gain, shift):
    center = values - jnp.mean(values, -1, keepdims=True)
    spread = jnp.mean(center * center, -1, keepdims=True)
    return center * lax.rsqrt(spread + NORM_EPSILON) * gain + shift


def exact_gelu(values):
    return jax.nn.gelu(values, approximate=False)


def contract_rows(left, right):
    return lax.dot_general(
        left, right, (((0,), (0,)), ((), ())), preferred_element_type=jnp.float32
    )


def contract_cols(left, right):
    return lax.dot_general(
        left, right, (((1,), (1,)), ((), ())), preferred_element_type=jnp.float32
    )


def split_heads(block):
    return block.reshape(block.shape[0], 2, HD)


def pair_scores(query_part, key_part):
    factor = 1.0 / (RELAX_SCALE * math.sqrt(HD))
    return (
        jnp.einsum(
            "qhd,khd->hqk",
            split_heads(query_part),
            split_heads(key_part),
            preferred_element_type=jnp.float32,
        )
        * factor
    )


def kept_probs(scores, allowed, row_max, row_total):
    exp_terms = jnp.exp(jnp.where(allowed, RELAX_SCALE * (scores - row_max), -jnp.inf))
    return exp_terms / row_total


def body(
    tokens,
    cotangent,
    lengths,
    assign,
    w_qkv,
    qv_bias,
    w_out,
    out_bias,
    w_up,
    up_bias,
    w_down,
    down_bias,
    norm_gain,
    norm_shift,
):
    gathered = (
        lax.all_gather(w_qkv, ("seq", "dp"), axis=0, tiled=True),
        lax.all_gather(w_out, ("seq", "dp"), axis=0, tiled=True),
        lax.all_gather(w_up, ("seq", "dp"), axis=0, tiled=True),
        lax.all_gather(w_down, ("seq", "dp"), axis=0, tiled=True),
        lax.all_gather(qv_bias, ("seq", "dp"), axis=1, tiled=True),
        lax.all_gather(out_bias, ("seq", "dp"), axis=0, tiled=True),
        lax.all_gather(up_bias, ("seq", "dp"), axis=0, tiled=True),
        lax.all_gather(down_bias, ("seq", "dp"), axis=0, tiled=True),
        lax.all_gather(norm_gain, ("seq", "dp"), axis=1, tiled=True),
        lax.all_gather(norm_shift, ("seq", "dp"), axis=1, tiled=True),
    )
    qkv_full, out_full, up_full, down_full = (gathered[0], gathered[1], gathered[2], gathered[3])
    qv_shift = gathered[4].astype(jnp.float32)
    out_shift = gathered[5].astype(jnp.float32)
    up_shift = gathered[6].astype(jnp.float32)
    down_shift = gathered[7].astype(jnp.float32)
    gains = gathered[8].astype(jnp.float32)
    shifts = gathered[9].astype(jnp.float32)
    row_count = tokens.shape[1]
    model_width = tokens.shape[2]
    pair_cols = 2 * HD
    pair_count = model_width // pair_cols
    slot_rows = row_count * lax.axis_size("seq")
    factor = 1.0 / (RELAX_SCALE * math.sqrt(HD))
    valid = lengths[assign[lax.axis_index("dp")]]
    own_place = lax.axis_index("seq") * row_count + jnp.arange(row_count, dtype=jnp.int32)
    all_place = jnp.arange(slot_rows, dtype=jnp.int32)
    allowed = (all_place[None, :] <= own_place[:, None]) & (all_place[None, :] < valid)
    pair_ids = jnp.arange(pair_count, dtype=jnp.int32)
    hidden = tokens[0].astype(jnp.float32)
    normed_first, pull_first = jax.vjp(norm_rows, hidden, gains[0], shifts[0])
    normed_low = normed_first.astype(jnp.bfloat16)
    projected = jnp.dot(normed_low, qkv_full, preferred_element_type=jnp.float32)
    queries = (projected[:, :model_width] + qv_shift[0]).astype(jnp.bfloat16)
    key_own = projected[:, model_width : 2 * model_width].astype(jnp.bfloat16)
    value_own = (projected[:, 2 * model_width :] + qv_shift[1]).astype(jnp.bfloat16)
    keys, values = (
        lax.all_gather(key_own, "seq", axis=0, tiled=True),
        lax.all_gather(value_own, "seq", axis=0, tiled=True),
    )

    def columns(block, pair_index):
        return lax.dynamic_slice_in_dim(block, pair_index * pair_cols, pair_cols, 1)

    def merge_pairs(stack):
        return stack.transpose(1, 0, 2).reshape(stack.shape[1], model_width)

    def attend(pair_index):
        scores = pair_scores(columns(queries, pair_index), columns(keys, pair_index))
        row_max = jnp.max(jnp.where(allowed, scores, -jnp.inf), -1, keepdims=True)
        exp_terms = jnp.exp(jnp.where(allowed, RELAX_SCALE * (scores - row_max), -jnp.inf))
        row_total = jnp.sum(exp_terms, -1, keepdims=True)
        probs = (exp_terms / row_total).astype(jnp.bfloat16)
        mixed = jnp.einsum(
            "hqk,khd->qhd",
            probs,
            split_heads(columns(values, pair_index)),
            preferred_element_type=jnp.float32,
        )
        return (mixed.reshape(row_count, pair_cols), row_max[..., 0], row_total[..., 0])

    mixed_pairs, max_pairs, total_pairs = lax.map(attend, pair_ids)
    attended = merge_pairs(mixed_pairs).astype(jnp.bfloat16)
    branch = jnp.dot(attended, out_full, preferred_element_type=jnp.float32) + out_shift
    normed_second, pull_second = jax.vjp(norm_rows, branch, gains[1], shifts[1])
    middle = hidden + normed_second
    normed_third, pull_third = jax.vjp(norm_rows, middle, gains[2], shifts[2])
    third_low = normed_third.astype(jnp.bfloat16)
    up_pre = jnp.dot(third_low, up_full, preferred_element_type=jnp.float32) + up_shift
    activated, pull_gelu = jax.vjp(exact_gelu, up_pre)
    active_low = activated.astype(jnp.bfloat16)
    down_pre = jnp.dot(active_low, down_full, preferred_element_type=jnp.float32) + down_shift
    normed_fourth, pull_fourth = jax.vjp(norm_rows, down_pre, gains[3], shifts[3])
    output = (middle + normed_fourth).astype(jnp.bfloat16)[None]
    again = (
        lax.all_gather(w_qkv, ("seq", "dp"), axis=0, tiled=True),
        lax.all_gather(w_out, ("seq", "dp"), axis=0, tiled=True),
        lax.all_gather(w_up, ("seq", "dp"), axis=0, tiled=True),
        lax.all_gather(w_down, ("seq", "dp"), axis=0, tiled=True),
    )
    qkv_back, out_back, up_back, down_back = (again[0], again[1], again[2], again[3])
    keep_rows = (own_place < valid).astype(jnp.float32)[:, None]
    grad_out = cotangent[0].astype(jnp.float32) * keep_rows
    grad_down, grad_gain_four, grad_shift_four = pull_fourth(grad_out)
    grad_down_low = grad_down.astype(jnp.bfloat16)
    grad_w_down = contract_rows(active_low, grad_down_low)
    grad_b_down = jnp.sum(grad_down_low.astype(jnp.float32), 0)
    (grad_up,) = pull_gelu(contract_cols(grad_down_low, down_back))
    grad_up_low = grad_up.astype(jnp.bfloat16)
    grad_w_up = contract_rows(third_low, grad_up_low)
    grad_b_up = jnp.sum(grad_up_low.astype(jnp.float32), 0)
    grad_middle_part, grad_gain_three, grad_shift_three = pull_third(
        contract_cols(grad_up_low, up_back)
    )
    grad_middle = grad_out + grad_middle_part
    grad_branch, grad_gain_two, grad_shift_two = pull_second(grad_middle)
    grad_branch_low = grad_branch.astype(jnp.bfloat16)
    grad_w_out = contract_rows(attended, grad_branch_low)
    grad_b_out = jnp.sum(grad_branch_low.astype(jnp.float32), 0)
    grad_attended = contract_cols(grad_branch_low, out_back).astype(jnp.bfloat16)

    def query_side(pair_index):
        scores = pair_scores(columns(queries, pair_index), columns(keys, pair_index))
        probs = kept_probs(
            scores, allowed, max_pairs[pair_index][..., None], total_pairs[pair_index][..., None]
        )
        grad_part = columns(grad_attended, pair_index)
        grad_probs = jnp.einsum(
            "qhd,khd->hqk",
            split_heads(grad_part),
            split_heads(columns(values, pair_index)),
            preferred_element_type=jnp.float32,
        )
        delta = jnp.sum(probs * grad_probs, -1, keepdims=True)
        grad_scores = (RELAX_SCALE * probs * (grad_probs - delta)).astype(jnp.bfloat16)
        grad_query = (
            jnp.einsum(
                "hqk,khd->qhd",
                grad_scores,
                split_heads(columns(keys, pair_index)),
                preferred_element_type=jnp.float32,
            )
            * factor
        )
        return (grad_query.reshape(row_count, pair_cols), grad_scores, probs, delta)

    def both_sides(pair_index):
        grad_query, grad_scores, probs, delta = query_side(pair_index)
        grad_part = columns(grad_attended, pair_index)
        grad_key = (
            jnp.einsum(
                "hqk,qhd->khd",
                grad_scores,
                split_heads(columns(queries, pair_index)),
                preferred_element_type=jnp.float32,
            )
            * factor
        )
        grad_value = jnp.einsum(
            "hqk,qhd->khd",
            probs.astype(jnp.bfloat16),
            split_heads(grad_part),
            preferred_element_type=jnp.float32,
        )
        return (
            grad_query,
            grad_key.reshape(slot_rows, pair_cols),
            grad_value.reshape(slot_rows, pair_cols),
        )

    query_pairs, key_terms, value_terms = lax.map(both_sides, pair_ids)
    key_pairs, value_pairs = (
        lax.psum_scatter(
            key_terms.astype(jnp.bfloat16), "seq", scatter_dimension=1, tiled=True
        ).astype(jnp.float32),
        lax.psum_scatter(
            value_terms.astype(jnp.bfloat16), "seq", scatter_dimension=1, tiled=True
        ).astype(jnp.float32),
    )
    grad_q_low = merge_pairs(query_pairs).astype(jnp.bfloat16)
    grad_k_low = merge_pairs(key_pairs).astype(jnp.bfloat16)
    grad_v_low = merge_pairs(value_pairs).astype(jnp.bfloat16)
    grad_projected = jnp.concatenate([grad_q_low, grad_k_low, grad_v_low], 1)
    grad_w_qkv = contract_rows(normed_low, grad_projected)
    grad_qv = jnp.stack(
        [jnp.sum(grad_q_low.astype(jnp.float32), 0), jnp.sum(grad_v_low.astype(jnp.float32), 0)]
    )
    grad_hidden_part, grad_gain_one, grad_shift_one = pull_first(
        contract_cols(grad_projected, qkv_back)
    )
    input_grad = (grad_middle + grad_hidden_part).astype(jnp.bfloat16)[None]
    grad_gains = jnp.stack([grad_gain_one, grad_gain_two, grad_gain_three, grad_gain_four])
    grad_shifts = jnp.stack([grad_shift_one, grad_shift_two, grad_shift_three, grad_shift_four])
    owned = (
        lax.psum_scatter(grad_w_qkv, ("seq", "dp"), scatter_dimension=0, tiled=True),
        lax.psum_scatter(grad_w_out, ("seq", "dp"), scatter_dimension=0, tiled=True),
        lax.psum_scatter(grad_w_up, ("seq", "dp"), scatter_dimension=0, tiled=True),
        lax.psum_scatter(grad_w_down, ("seq", "dp"), scatter_dimension=0, tiled=True),
        lax.psum_scatter(grad_qv, ("seq", "dp"), scatter_dimension=1, tiled=True),
        lax.psum_scatter(grad_b_out, ("seq", "dp"), scatter_dimension=0, tiled=True),
        lax.psum_scatter(grad_b_up, ("seq", "dp"), scatter_dimension=0, tiled=True),
        lax.psum_scatter(grad_b_down, ("seq", "dp"), scatter_dimension=0, tiled=True),
        lax.psum_scatter(grad_gains, ("seq", "dp"), scatter_dimension=1, tiled=True),
        lax.psum_scatter(grad_shifts, ("seq", "dp"), scatter_dimension=1, tiled=True),
    )
    return (
        output,
        input_grad,
        owned[0],
        owned[4],
        owned[1],
        owned[5],
        owned[2],
        owned[6],
        owned[3],
        owned[7],
        owned[8],
        owned[9],
    )


MESH = pl.DeviceIdType.MESH


def is_small(mesh):
    return mesh.shape["seq"] == 16 and mesh.shape["dp"] == 2


def place():
    seq = lax.axis_index("seq")
    return seq // 8, (seq // 4) % 2, (seq // 2) % 2, seq % 2, lax.axis_index("dp")


def exchange_kernel(scatter, src, out, send_sem, recv_sem, own_sem):
    a, b, y, c, x = place()
    barrier = pltpu.get_barrier_semaphore()

    def peer(k):
        return lax.rem(a + k // 2, 2), lax.rem(y + k % 2, 2)

    def device(k):
        pa, py = peer(k)
        return (pa * 8 + b * 4 + py * 2 + c, x)

    def source(k):
        pa, py = peer(k)
        return src.at[pa * 2 + py] if scatter else src.at[pa, :, py]

    def target(k):
        pa, py = peer(k)
        return out.at[pa, :, py] if scatter else out.at[pa * 2 + py]

    for k in range(1, 4):
        pl.semaphore_signal(barrier, inc=1, device_id=device(k), device_id_type=MESH)
    own = pltpu.make_async_copy(source(0), target(0), own_sem)
    own.start()
    pl.semaphore_wait(barrier, 3)

    def copy(k, dst):
        return pltpu.make_async_remote_copy(
            src_ref=source(k), dst_ref=target(dst), send_sem=send_sem.at[k], recv_sem=recv_sem.at[k],
            device_id=device(k), device_id_type=MESH)

    for k in (3, 2, 1):
        copy(k, 0).start()
    own.wait()
    for k in (3, 2, 1):
        copy(k, k).wait_recv()
    for k in (3, 2, 1):
        copy(k, 0).wait_send()


def exchange(blocks, scatter, cid):
    vm = pl.BlockSpec(memory_space=pltpu.VMEM)
    rows = blocks.shape[-2]
    shape = (2, 2, 2, rows, 128) if scatter else (4, 2, rows, 128)
    return pl.pallas_call(
        functools.partial(exchange_kernel, scatter), out_shape=jax.ShapeDtypeStruct(shape, blocks.dtype),
        in_specs=[vm], out_specs=vm,
        scratch_shapes=[pltpu.SemaphoreType.DMA((4,)), pltpu.SemaphoreType.DMA((4,)), pltpu.SemaphoreType.DMA],
        compiler_params=pltpu.CompilerParams(collective_id=cid, has_side_effects=True),
        cost_estimate=pl.CostEstimate(flops=0, bytes_accessed=rows * 100000, transcendentals=0),
        name="exchange",
    )(blocks)


def dot_nt(a, b):
    return lax.dot_general(a, b, (((1,), (1,)), ((), ())), preferred_element_type=jnp.float32)


def dot_nn(a, b):
    return jnp.dot(a, b, preferred_element_type=jnp.float32)


BQ = 256
MASKED = -1e30


def load_heads(valid, packed, q_ref, k_ref):
    rows = q_ref.shape[0]
    qk = packed[:, :256].reshape(rows, 128)
    kq = jnp.concatenate([qk[:, 64:], qk[:, :64]], axis=1)
    lane = lax.broadcasted_iota(jnp.int32, (rows, 128), 1)
    spot = lax.broadcasted_iota(jnp.int32, (rows, 128), 0)
    past = jnp.where(spot < valid, 0.0, MASKED)
    q_ref[...] = jnp.where(lane < 64, qk.astype(jnp.float32), jnp.where(lane == 64, 1.0, 0.0)).astype(jnp.bfloat16)
    k_ref[...] = jnp.where(lane < 64, kq.astype(jnp.float32), jnp.where(lane == 64, past, 0.0)).astype(jnp.bfloat16)


def unpack_rows(halves):
    n = halves.shape[0]
    return jnp.concatenate([halves[:, :, :64], halves[:, :, 64:]], axis=1).reshape(n * 256, 64)


def block_probs(q_ref, k_ref, i):
    n = (i + 1) * BQ
    scores = dot_nt(k_ref[:n], q_ref[i * BQ:n])
    key = lax.broadcasted_iota(jnp.int32, (BQ, BQ), 0)
    query = lax.broadcasted_iota(jnp.int32, (BQ, BQ), 1)
    corner = jnp.where(key <= query, scores[n - BQ:], MASKED)
    scores = jnp.concatenate([scores[:n - BQ], corner], axis=0) if i else corner
    top = jnp.max(scores, axis=0, keepdims=True)
    terms = jnp.exp((scores - top) * 0.125)
    return terms, 1.0 / jnp.sum(terms, axis=0, keepdims=True)


def attend_kernel(valid_ref, packed, out_ref, q_ref, k_ref, vt_ref):
    load_heads(valid_ref[0], packed, q_ref, k_ref)
    unit = jnp.where(
        lax.broadcasted_iota(jnp.int32, (64, 64), 0) == lax.broadcasted_iota(jnp.int32, (64, 64), 1), 1.0, 0.0
    ).astype(jnp.bfloat16)
    vt_ref[...] = dot_nt(unit, unpack_rows(packed[:, 256:])).astype(jnp.bfloat16)
    for i in range(q_ref.shape[0] // BQ):
        n = (i + 1) * BQ
        terms, scale = block_probs(q_ref, k_ref, i)
        probs = (terms * scale).astype(jnp.bfloat16)
        mixed = dot_nn(vt_ref[:, :n], probs).T
        out_ref[i] = jnp.concatenate([mixed[:128], mixed[128:]], axis=1).astype(jnp.bfloat16)


def attend_back_kernel(valid_ref, packed, grad, out_ref, q_ref, k_ref, v_ref, g_ref, kt_ref, dk_ref, dv_ref):
    load_heads(valid_ref[0], packed, q_ref, k_ref)
    v_ref[...] = unpack_rows(packed[:, 256:])
    g_ref[...] = unpack_rows(grad[...])
    unit = jnp.where(
        lax.broadcasted_iota(jnp.int32, (64, 128), 0) == lax.broadcasted_iota(jnp.int32, (64, 128), 1), 1.0, 0.0
    ).astype(jnp.bfloat16)
    kt_ref[...] = dot_nt(unit, k_ref[...]).astype(jnp.bfloat16)
    dk_ref[...] = jnp.zeros_like(dk_ref)
    dv_ref[...] = jnp.zeros_like(dv_ref)
    blocks = q_ref.shape[0] // BQ
    for i in range(blocks):
        n = (i + 1) * BQ
        terms, scale = block_probs(q_ref, k_ref, i)
        probs = terms * scale
        grad_probs = dot_nt(v_ref[:n], g_ref[i * BQ:n])
        delta = jnp.sum(probs * grad_probs, axis=0, keepdims=True)
        grad_scores = (probs * (grad_probs - delta)).astype(jnp.bfloat16)
        grad_query = dot_nn(kt_ref[:, :n], grad_scores).T * 0.125
        out_ref[i, :256, :64] = grad_query.astype(jnp.bfloat16)
        dk_ref[:n] += dot_nn(grad_scores, q_ref[i * BQ:n])
        dv_ref[:n] += dot_nn(probs.astype(jnp.bfloat16), g_ref[i * BQ:n])
    for i in range(blocks):
        rows = slice(i * BQ, (i + 1) * BQ)
        out_ref[i, :256, 64:] = (dk_ref[rows, :64] * 0.125).astype(jnp.bfloat16)
        value = dv_ref[rows].astype(jnp.bfloat16)
        out_ref[i, 256:] = jnp.concatenate([value[:128], value[128:]], axis=1)


def attend(valid, packed):
    rows = packed.shape[0] * 256
    vm = pl.BlockSpec(memory_space=pltpu.VMEM)
    return pl.pallas_call(
        attend_kernel,
        out_shape=jax.ShapeDtypeStruct((packed.shape[0], 128, 128), jnp.bfloat16),
        in_specs=[pl.BlockSpec(memory_space=pltpu.SMEM), vm], out_specs=vm,
        scratch_shapes=[pltpu.VMEM((rows, 128), jnp.bfloat16)] * 2 + [pltpu.VMEM((64, rows), jnp.bfloat16)],
        compiler_params=pltpu.CompilerParams(vmem_limit_bytes=48 << 20),
        name="attend",
    )(valid, packed)


def attend_back(valid, packed, grad):
    rows = packed.shape[0] * 256
    vm = pl.BlockSpec(memory_space=pltpu.VMEM)
    return pl.pallas_call(
        attend_back_kernel,
        out_shape=jax.ShapeDtypeStruct(packed.shape, jnp.bfloat16),
        in_specs=[pl.BlockSpec(memory_space=pltpu.SMEM), vm, vm], out_specs=vm,
        scratch_shapes=[pltpu.VMEM((rows, 128), jnp.bfloat16)] * 2 + [pltpu.VMEM((rows, 64), jnp.bfloat16)] * 2
        + [pltpu.VMEM((64, rows), jnp.bfloat16), pltpu.VMEM((rows, 128), jnp.float32), pltpu.VMEM((rows, 64), jnp.float32)],
        compiler_params=pltpu.CompilerParams(vmem_limit_bytes=48 << 20),
        name="attend_back",
    )(valid, packed, grad)


def flip(bits, block):
    return lax.ppermute(block, "seq", [(s, s ^ bits) for s in range(16)])


flip_a, flip_b, flip_y, flip_core, flip_far = (functools.partial(flip, bits) for bits in (8, 4, 2, 1, 5))


def flip_x(block):
    return lax.ppermute(block, "dp", [(0, 1), (1, 0)])


def after(value, *others):
    return lax.optimization_barrier((value,) + others)[0]


def pick(block, index, axis, keepdims=False):
    return lax.dynamic_index_in_dim(block, index, axis, keepdims=keepdims)


def swap_if(flag, block, axis):
    return jnp.where(flag == 0, block, lax.rev(block, (axis,)))


def sort_ranks(block, b, c):
    return swap_if(c, swap_if(b, block, 0), 1)


def to_ranks(block, b, c):
    mine = pick(pick(block, b, 0), c, 0)
    core = flip_core(pick(pick(block, b, 0), 1 - c, 0))
    near = flip_b(pick(pick(block, 1 - b, 0), c, 0))
    far = flip_far(pick(pick(block, 1 - b, 0), 1 - c, 0))
    return jnp.stack([jnp.stack([mine, core]), jnp.stack([near, far])])


def gather_rows(block):
    core, near = flip_core(block), flip_b(block)
    return jnp.concatenate([block, core, near, flip_core(near)], 0)


def scatter_rows(part):
    part = part.reshape(2, 2, part.shape[0] // 4, part.shape[1])
    far = part[1, 0] + flip_core(part[1, 1])
    near = part[0, 0] + flip_core(part[0, 1])
    return near + flip_b(far.astype(jnp.bfloat16)).astype(jnp.float32)


def cube_start(block):
    return jnp.stack([block, flip_a(block)])


def cube_one(flip_one, block):
    return jnp.concatenate([block, flip_one(block)], 0)


def arrange_kernel(count, spot_ref, *refs):
    for k in range(count):
        block, out = refs[k], refs[count + k]
        if len(out.shape) == 7:
            for i in range(2):
                for j in range(2):
                    out[0, i, 0, j, 0] = block[0, i, j]
        else:
            out[0, 0, 0] = block[0]


def arrange(spot, blocks):
    def coords(i, r, y_first):
        second, first, a = i // 4, (i // 2) % 2, i % 2
        y, x = (first, second) if y_first else (second, first)
        return lax.rem(r[0] + a, 2), lax.rem(r[1] + y, 2), lax.rem(r[2] + x, 2)

    def specs(block, y_first):
        shape = block.shape
        if len(shape) == 5:
            def out_place(i, r):
                a, y, x = coords(i, r, y_first)
                return a, 0, y, 0, x, 0, 0
            return (pl.BlockSpec((1,) + shape[1:], lambda i, r: (i, 0, 0, 0, 0)),
                    pl.BlockSpec((1, 2, 1, 2, 1) + shape[3:], out_place),
                    jax.ShapeDtypeStruct((2,) * 5 + shape[3:], block.dtype))

        def out_place(i, r):
            return coords(i, r, y_first) + (0, 0)
        return (pl.BlockSpec((1,) + shape[1:], lambda i, r: (i, 0, 0)),
                pl.BlockSpec((1, 1, 1) + shape[1:], out_place),
                jax.ShapeDtypeStruct((2, 2, 2) + shape[1:], block.dtype))

    made = [specs(*entry) for entry in blocks]
    return pl.pallas_call(
        functools.partial(arrange_kernel, len(blocks)),
        out_shape=tuple(m[2] for m in made),
        grid_spec=pltpu.PrefetchScalarGridSpec(
            num_scalar_prefetch=1, grid=(8,), in_specs=[m[0] for m in made], out_specs=tuple(m[1] for m in made)),
        compiler_params=pltpu.CompilerParams(vmem_limit_bytes=32 << 20),
        cost_estimate=pl.CostEstimate(flops=0, bytes_accessed=8 << 20, transcendentals=0),
        name="arrange",
    )(spot, *[entry[0] for entry in blocks])


def add_low(mine, other):
    return (mine.astype(jnp.float32) + other.astype(jnp.float32)).astype(jnp.bfloat16)


def fold(terms, flip_one, index, axis):
    return add_low(pick(terms, index, axis, True), flip_one(pick(terms, 1 - index, axis, True)))


def reduce_kernel(q_ref, o_ref, u_ref, d_ref, s_ref, rq, ro, ru, rd, rs,
                  r1q, t2q, r2q, t3q, r3q, fq, gq, r1o, t2o, r2o, t3o, r3o, r3u, fu, gu, r3d,
                  sx, s1, sy, s2, sa, s3, sb, s4, sc, send_sem, recv_sem):
    a, b, y, c, x = place()
    f32, bf16 = jnp.float32, jnp.bfloat16
    barrier = pltpu.get_barrier_semaphore()

    def at(pa, pb, py, pc, px):
        return (pa * 8 + pb * 4 + py * 2 + pc, px)

    to_x, to_y, to_a = at(a, b, y, c, 1 - x), at(a, b, 1 - y, c, x), at(1 - a, b, y, c, x)
    ranks = [(lax.rem(b + k // 2, 2), lax.rem(c + k % 2, 2)) for k in range(4)]
    to_rank = [at(a, ranks[k][0], y, ranks[k][1], x) for k in range(4)]
    to_b, to_c = to_rank[2], to_rank[1]
    for dev in [to_x, to_y, to_a] + to_rank[1:]:
        pl.semaphore_signal(barrier, inc=1, device_id=dev, device_id_type=MESH)
    pl.semaphore_wait(barrier, 6)

    made = []

    def remote(src, dst, dev):
        k = len(made)
        made.append(pltpu.make_async_remote_copy(
            src_ref=src, dst_ref=dst, send_sem=send_sem.at[k], recv_sem=recv_sem.at[k],
            device_id=dev, device_id_type=MESH))
        return made[-1]

    def low(*values):
        return sum(v.astype(f32) for v in values)

    places = [1 - a, a]
    halves = [slice(0, 512), slice(512, 1024)]
    lateral = [(to_x, to_y), (to_y, to_x)]

    cu = remote(u_ref.at[1 - a], r3u, to_a)
    cd = remote(d_ref.at[1 - a], r3d, to_a)
    q1, q2, o1, o2 = {}, {}, {}, {}
    for i in range(2):
        for s in range(2):
            p = places[i]
            q1[s, i] = remote(q_ref.at[p, 0, :, :, 1 - x] if s == 0 else q_ref.at[p, 1, 1 - y], r1q.at[s, i], lateral[s][0])
            o1[s, i] = remote(o_ref.at[p, :, 1 - x, :, halves[0]] if s == 0 else o_ref.at[p, 1 - y, :, :, halves[1]],
                              r1o.at[s, i], lateral[s][0])
            q2[s, i] = remote(t2q.at[s, i], r2q.at[s, i], lateral[s][1])
            o2[s, i] = remote(t2o.at[s, i], r2o.at[s, i], lateral[s][1])
    q3 = [remote(t3q.at[s], r3q.at[s], to_a) for s in range(2)]
    o3 = [remote(t3o.at[s], r3o.at[s], to_a) for s in range(2)]
    qr = [remote(fq.at[ranks[k][0], ranks[k][1]], gq.at[k - 1], to_rank[k]) for k in range(1, 4)]
    ur = [remote(fu.at[ranks[k][0], ranks[k][1]], gu.at[k - 1], to_rank[k]) for k in range(1, 4)]
    vx = remote(s_ref.at[:, :, :, :, 1 - x], sx, to_x)
    vy = remote(s1.at[:, :, 1 - y], sy, to_y)
    va = remote(s2.at[1 - a], sa, to_a)
    vb = remote(s3.at[1 - b], sb, to_b)
    vc = remote(s4.at[1 - c], sc, to_c)

    cu.start()
    vx.start()
    for i in range(2):
        for s in range(2):
            q1[s, i].start()
            o1[s, i].start()
    cd.start()

    def q_terms(s, i, far):
        p = places[i]
        if s == 0:
            v = 1 - y if far else y
            return q_ref[p, 0, v, :, x], r1q[0, i, v]
        v = 1 - x if far else x
        return q_ref[p, 1, y, :, v], r1q[1, i, :, v]

    def o_terms(s, i, far):
        p = places[i]
        if s == 0:
            v = 1 - y if far else y
            return o_ref[p, v, x, :, halves[0]], r1o[0, i, v]
        v = 1 - x if far else x
        return o_ref[p, y, v, :, halves[1]], r1o[1, i, v]

    for i in range(2):
        for s in range(2):
            q1[s, i].wait_recv()
            t2q[s, i] = low(*q_terms(s, i, True)).astype(bf16)
            q2[s, i].start()
            o1[s, i].wait_recv()
            t2o[s, i] = low(*o_terms(s, i, True)).astype(bf16)
            o2[s, i].start()
        if i == 0:
            vx.wait_recv()
            s1[...] = s_ref[:, :, :, :, x] + sx[...]
            vy.start()
            for s in range(2):
                q2[s, 0].wait_recv()
                t3q[s] = low(*q_terms(s, 0, False), r2q[s, 0]).astype(bf16)
                q3[s].start()
                o2[s, 0].wait_recv()
                t3o[s] = low(*o_terms(s, 0, False), r2o[s, 0]).astype(bf16)
                o3[s].start()
    vy.wait_recv()
    s2[...] = s1[:, :, y] + sy[...]
    va.start()

    cu.wait_recv()
    for k in range(1, 4):
        pb, pc = ranks[k]
        fu[pb, pc] = low(u_ref[a, pb, pc], r3u[pb, pc]).astype(bf16)
        ur[k - 1].start()
    ru[b, c] = low(u_ref[a, b, c], r3u[b, c])

    for s in range(2):
        q2[s, 1].wait_recv()
        o2[s, 1].wait_recv()
        q3[s].wait_recv()
        total = low(*q_terms(s, 1, False), r2q[s, 1], r3q[s])
        fq[s] = total.astype(bf16)
        for j in range(2):
            @pl.when((b == s) & (c == j))
            def _():
                rq[s, j] = total[j]
        o3[s].wait_recv()
        ro[:, halves[s]] = low(*o_terms(s, 1, False), r2o[s, 1], r3o[s])
    for k in (3, 2, 1):
        qr[k - 1].start()
    va.wait_recv()
    s3[...] = s2[a] + sa[...]
    vb.start()
    cd.wait_recv()
    rd[...] = low(d_ref[a], r3d[...])
    vb.wait_recv()
    s4[...] = s3[b] + sb[...]
    vc.start()
    for k in (1, 2, 3):
        pb, pc = ranks[k]
        ur[k - 1].wait_recv()
        ru[pb, pc] = gu[k - 1].astype(f32)
    for k in (1, 2, 3):
        pb, pc = ranks[k]
        qr[k - 1].wait_recv()
        rq[pb, pc] = gq[k - 1].astype(f32)
    vc.wait_recv()
    rs[...] = s4[c] + sc[...]
    for copy in made:
        copy.wait_send()


def reduce_all(gw_qkv, gw_out, up_sum, down_sum, small, cid):
    f32, bf16 = jnp.float32, jnp.bfloat16
    V = pltpu.VMEM
    vm = pl.BlockSpec(memory_space=V)
    S = jax.ShapeDtypeStruct
    q, o = gw_qkv.shape[5:], (gw_out.shape[3], 512)
    u, d, s = up_sum.shape[1:], down_sum.shape[1:], small.shape[5:]
    scratch = [
        V((2, 2, 2, 2) + q, bf16), V((2, 2, 2) + q, bf16), V((2, 2, 2) + q, bf16), V((2, 2) + q, bf16), V((2, 2) + q, bf16),
        V((2, 2) + q, bf16), V((3,) + q, bf16),
        V((2, 2, 2) + o, bf16), V((2, 2) + o, bf16), V((2, 2) + o, bf16), V((2,) + o, bf16), V((2,) + o, bf16),
        V(u, bf16), V(u, bf16), V((3,) + u[2:], bf16), V(d, bf16),
        V((2, 2, 2, 2) + s, f32), V((2, 2, 2, 2) + s, f32), V((2, 2, 2) + s, f32), V((2, 2, 2) + s, f32), V((2, 2) + s, f32),
        V((2, 2) + s, f32), V((2,) + s, f32), V((2,) + s, f32), V(s, f32),
        pltpu.SemaphoreType.DMA((33,)), pltpu.SemaphoreType.DMA((33,))]
    return pl.pallas_call(
        reduce_kernel,
        out_shape=(S((2, 2) + q, f32), S((o[0], 1024), f32), S(u, f32), S(d, f32), S(s, f32)),
        in_specs=[vm] * 5, out_specs=(vm,) * 5, scratch_shapes=scratch,
        compiler_params=pltpu.CompilerParams(collective_id=cid, has_side_effects=True, vmem_limit_bytes=40 << 20),
        name="reduce_all",
    )(gw_qkv, gw_out, up_sum, down_sum, small)


def pack_heads(block, b, c):
    block = sort_ranks(block.reshape(2, 2, 128, 4, HD), b, c)
    return block.transpose(3, 0, 2, 1, 4).reshape(4, 2, 128, 128)


def unpack_heads(packed):
    return packed.reshape(4, 2, 128, 2, HD).transpose(1, 3, 2, 0, 4).reshape(2, 2, 128, 4 * HD)


def fast_body(tokens, cotangent, lengths, assign, w_qkv, qv_bias, w_out, out_bias, w_up, up_bias, w_down, down_bias,
              norm_gain, norm_shift):
    bf16, f32 = jnp.bfloat16, jnp.float32
    a, b, y, c, x = place()
    spot = jnp.stack([a, y, x]).astype(jnp.int32)
    width = tokens.shape[2]
    valid = lengths[assign[x]].astype(jnp.int32)

    qkv = w_qkv.reshape(32, 3, 2, 2, 2, 2, HD)
    qk_ranks = qkv[:, :2].transpose(3, 5, 0, 2, 4, 1, 6).reshape(2, 2, 32, 512)
    v_ranks = qkv[:, 2].transpose(2, 4, 0, 1, 3, 5).reshape(2, 2, 32, 256)
    qkv_block = to_ranks(jnp.concatenate([qk_ranks, v_ranks], 3), b, c)
    small = jnp.concatenate([qv_bias.reshape(-1), out_bias, down_bias, norm_gain.reshape(-1), norm_shift.reshape(-1), up_bias])
    small = jnp.pad(small.reshape(4, 128), ((0, 12), (0, 0)))
    small_core, small_near = flip_core(small), flip_b(small)
    small = jnp.stack([small, small_core, small_near, flip_core(small_near)]).reshape(2, 2, 16, 128)

    qkv_block = sort_ranks(qkv_block, b, c)
    qk_one, v_one = cube_start(qkv_block[..., :512]), cube_start(qkv_block[..., 512:])
    out_one, small = cube_start(w_out), cube_start(small)
    rows = gather_rows(tokens[0])
    qk_two, v_two, out_two, small = cube_one(flip_y, qk_one), cube_one(flip_x, v_one), cube_one(flip_x, out_one), cube_one(flip_y, small)
    qk_all, v_all, out_all, small = cube_one(flip_x, qk_two), cube_one(flip_y, v_two), cube_one(flip_y, out_two), cube_one(flip_x, small)
    wqk, wv, wo = arrange(spot, [(qk_all, True), (v_all, False), (out_all, False)])
    wqkv, wo = jnp.concatenate([wqk.reshape(width, 512), wv.reshape(width, 256)], 1), wo.reshape(256, width)

    up = w_up.reshape(32, 2, 2, 2, 2, 2, 128).transpose(2, 4, 0, 1, 3, 5, 6).reshape(2, 2, 32, 1024)
    up_block = sort_ranks(to_ranks(after(up, qkv_block), b, c), b, c)
    up_one, down_one = cube_start(after(up_block, qk_one)), cube_start(after(w_down, qk_one))
    small = small.reshape(2, 2, 2, 2, 2, 16, 128).astype(f32)
    for axis, flag in enumerate((x, y, a, b, c)):
        small = swap_if(flag, small, axis)
    small = small.transpose(2, 3, 1, 4, 0, 5, 6)[..., :4, :]
    vectors = small[..., :3, :].reshape(32, 12, 32).transpose(1, 0, 2).reshape(12, width)
    qv_half = pick(pick(vectors[:2].reshape(2, 2, 2, 2, 2, HD), b, 2), c, 3).reshape(2, 4, HD)
    qk_shift = jnp.concatenate([qv_half[0], jnp.zeros((4, HD), f32)], 1).reshape(512)
    v_shift = qv_half[1].reshape(256)
    out_full, down_full, gains, shifts = vectors[2], vectors[3], vectors[4:8], vectors[8:12]
    up_shift = pick(pick(small[..., 3, :], b, 1), c, 2).reshape(1024)

    hidden = tokens[0].astype(f32)
    first = norm_rows(rows.astype(f32), gains[0], shifts[0]).astype(bf16)
    up_two, down_two = cube_one(flip_x, up_one), cube_one(flip_y, down_one)
    first = after(first, up_one, down_one)
    projected = (dot_nn(first, wqkv) + jnp.concatenate([qk_shift, v_shift])).astype(bf16)
    qk, v = projected[:, :512], projected[:, 512:]
    qk = sort_ranks(qk.reshape(2, 2, 128, 4, 128), b, c).transpose(3, 0, 1, 2, 4).reshape(4, 2, 256, 128)
    packed = exchange(after(jnp.concatenate([qk, pack_heads(v, b, c)], 2), up_two, down_two), True, 1).reshape(8, 384, 128)
    down_all = cube_one(flip_x, down_two)
    attended = attend(valid[None], packed).reshape(2, 2, 2, 128, 128)
    attended = exchange(after(attended, down_all), False, 2)
    attended = sort_ranks(unpack_heads(attended), b, c).reshape(512, 256)

    up_all = cube_one(flip_y, after(up_two, attended))
    branch = scatter_rows(dot_nn(attended, wo)) + out_full
    second, pull_second = jax.vjp(norm_rows, branch, gains[1], shifts[1])
    middle = hidden + second
    third, pull_third = jax.vjp(norm_rows, middle, gains[2], shifts[2])
    third = gather_rows(third.astype(bf16))
    wu, wd = arrange(spot, [(up_all, False), (down_all, True)])
    wu, wd = wu.reshape(width, 1024), wd.reshape(1024, width)
    up_pre = dot_nn(third, wu) + up_shift
    active, pull_gelu = jax.vjp(exact_gelu, up_pre)
    active = active.astype(bf16)
    down_pre = scatter_rows(dot_nn(active, wd)) + down_full
    fourth, pull_fourth = jax.vjp(norm_rows, down_pre, gains[3], shifts[3])
    output = (middle + fourth).astype(bf16)

    own_spot = lax.axis_index("seq") * 128 + jnp.arange(128, dtype=jnp.int32)
    grad_out = cotangent[0].astype(f32) * (own_spot < valid).astype(f32)[:, None]
    grad_down, gain4, shift4 = pull_fourth(grad_out)
    grad_down = grad_down.astype(bf16)
    down_rows = gather_rows(grad_down)
    gw_down = contract_rows(active, down_rows).astype(bf16).reshape(2, 2, 2, 128, width)
    down_term = flip_y(pick(gw_down, 1 - y, 1, True))
    (grad_up,) = pull_gelu(dot_nt(after(down_rows, gw_down), wd))
    grad_up = grad_up.astype(bf16)
    gw_up = contract_rows(third, grad_up).astype(bf16).reshape(2, 2, 2, 2, 2, 32, 1024)
    up_term = flip_x(pick(gw_up, 1 - x, 4, True))
    part, gain3, shift3 = pull_third(scatter_rows(dot_nt(after(grad_up, gw_up), wu)))
    grad_middle = grad_out + part
    grad_branch, gain2, shift2 = pull_second(grad_middle)
    grad_branch = grad_branch.astype(bf16)
    branch_rows = gather_rows(grad_branch)
    grad_att = dot_nt(branch_rows, wo).astype(bf16)
    down_sum = add_low(pick(gw_down, y, 1, True), down_term)
    grad_packed = exchange(after(pack_heads(grad_att, b, c), down_sum), True, 3).reshape(8, 128, 128)
    up_sum = add_low(pick(gw_up, x, 4, True), after(up_term, grad_packed))
    back = attend_back(valid[None], packed, grad_packed)

    up_sum = fold(up_sum, flip_y, y, 2)
    down_sum = fold(down_sum, flip_x, x, 2)
    back = after(back, up_sum)
    gw_out = contract_rows(attended, branch_rows).astype(bf16).reshape(2, 2, 2, 32, width)
    back = exchange(back.reshape(2, 2, 2, 384, 128), False, 4)
    grad_qk = back[:, :, :256].reshape(4, 2, 2, 128, 128).transpose(1, 2, 3, 0, 4).reshape(2, 2, 128, 512)
    grad_qk = sort_ranks(grad_qk, b, c).reshape(512, 512)
    grad_v = sort_ranks(unpack_heads(back[:, :, 256:]), b, c).reshape(512, 256)
    grad_qkv = jnp.concatenate([grad_qk, grad_v], 1)
    gw_qkv = contract_rows(first, grad_qkv).astype(bf16).reshape(2, 2, 2, 2, 2, 32, 768)
    _, pull_first = jax.vjp(norm_rows, hidden, gains[0], shifts[0])
    part, gain1, shift1 = pull_first(scatter_rows(dot_nt(grad_qkv, wqkv)))
    input_grad = (grad_middle + part).astype(bf16)

    def in_ranks(block, axes):
        for axis, flag in axes:
            spots = lax.broadcasted_iota(jnp.int32, [2 if i == axis else 1 for i in range(block.ndim)], axis)
            block = jnp.where(spots == flag, block, 0.0)
        return block

    def head_sums(block):
        sums = jnp.sum(block.astype(f32), 0).reshape(2, 1, 2, 1, -1)[..., :HD]
        sums = jnp.broadcast_to(sums, (2, 2, 2, 2, HD))
        return in_ranks(sums, ((1, b), (3, c))).reshape(1, width)

    whole = jnp.stack([
        jnp.sum(grad_branch.astype(f32), 0), jnp.sum(grad_down.astype(f32), 0),
        gain1, gain2, gain3, gain4, shift1, shift2, shift3, shift4])
    vecs = jnp.concatenate([head_sums(grad_qk), head_sums(grad_v), whole], 0)
    vecs = vecs.reshape(12, 32, 32).transpose(1, 0, 2).reshape(2, 2, 2, 2, 2, 3, 128)
    sums_up = jnp.broadcast_to(jnp.sum(grad_up.astype(f32), 0).reshape(2, 1, 2, 1, 2, 1, 128), (2, 2, 2, 2, 2, 1, 128))
    sums_up = in_ranks(sums_up, ((1, b), (3, c)))
    terms = jnp.concatenate([vecs, sums_up, jnp.zeros((2, 2, 2, 2, 2, 4, 128), f32)], 5)
    r_qkv, r_out, r_up, r_down, small = reduce_all(gw_qkv, gw_out, up_sum[:, :, 0, :, 0], down_sum[:, 0, 0], terms, 5)
    r_up = r_up.reshape(2, 2, 32, 2, 2, 2, 128).transpose(2, 3, 0, 4, 1, 5, 6).reshape(32, 4096)
    out_qk = r_qkv[..., :512].reshape(2, 2, 32, 2, 2, 2, HD).transpose(2, 5, 3, 0, 4, 1, 6).reshape(32, 2048)
    out_v = r_qkv[..., 512:].reshape(2, 2, 32, 2, 2, HD).transpose(2, 3, 0, 4, 1, 5).reshape(32, 1024)
    vectors = small[:3].reshape(12, 32)

    return (
        output[None], input_grad[None], jnp.concatenate([out_qk, out_v], 1), vectors[:2], r_out,
        vectors[2], r_up, small[3], r_down, vectors[3], vectors[4:8], vectors[8:12])


def solution(mesh):
    return jax.shard_map(
        fast_body if is_small(mesh) else body,
        mesh=mesh,
        in_specs=(
            P("dp", "seq", None),
            P("dp", "seq", None),
            P(),
            P(),
            P(("seq", "dp"), None),
            P(None, ("seq", "dp")),
            P(("seq", "dp"), None),
            P(("seq", "dp")),
            P(("seq", "dp"), None),
            P(("seq", "dp")),
            P(("seq", "dp"), None),
            P(("seq", "dp")),
            P(None, ("seq", "dp")),
            P(None, ("seq", "dp")),
        ),
        out_specs=(
            P("dp", "seq", None),
            P("dp", "seq", None),
            P(("seq", "dp"), None),
            P(None, ("seq", "dp")),
            P(("seq", "dp"), None),
            P(("seq", "dp")),
            P(("seq", "dp"), None),
            P(("seq", "dp")),
            P(("seq", "dp"), None),
            P(("seq", "dp")),
            P(None, ("seq", "dp")),
            P(None, ("seq", "dp")),
        ),
        check_vma=False,
    )
```

```python
import functools
import math

import jax
import jax.numpy as jnp
from jax import lax
from jax.experimental import pallas as pl
from jax.experimental.pallas import tpu as pltpu
from jax.sharding import PartitionSpec as P


HD = 64


RELAX_SCALE = 32.0
NORM_EPSILON = 1e-05


def norm_rows(values, gain, shift):
    center = values - jnp.mean(values, -1, keepdims=True)
    spread = jnp.mean(center * center, -1, keepdims=True)
    return center * lax.rsqrt(spread + NORM_EPSILON) * gain + shift


def exact_gelu(values):
    return jax.nn.gelu(values, approximate=False)


def contract_rows(left, right):
    return lax.dot_general(
        left, right, (((0,), (0,)), ((), ())), preferred_element_type=jnp.float32
    )


def contract_cols(left, right):
    return lax.dot_general(
        left, right, (((1,), (1,)), ((), ())), preferred_element_type=jnp.float32
    )


def split_heads(block):
    return block.reshape(block.shape[0], 2, HD)


def pair_scores(query_part, key_part):
    factor = 1.0 / (RELAX_SCALE * math.sqrt(HD))
    return (
        jnp.einsum(
            "qhd,khd->hqk",
            split_heads(query_part),
            split_heads(key_part),
            preferred_element_type=jnp.float32,
        )
        * factor
    )


def kept_probs(scores, allowed, row_max, row_total):
    exp_terms = jnp.exp(jnp.where(allowed, RELAX_SCALE * (scores - row_max), -jnp.inf))
    return exp_terms / row_total


def body(
    tokens,
    cotangent,
    lengths,
    assign,
    w_qkv,
    qv_bias,
    w_out,
    out_bias,
    w_up,
    up_bias,
    w_down,
    down_bias,
    norm_gain,
    norm_shift,
):
    gathered = (
        lax.all_gather(w_qkv, ("seq", "dp"), axis=0, tiled=True),
        lax.all_gather(w_out, ("seq", "dp"), axis=0, tiled=True),
        lax.all_gather(w_up, ("seq", "dp"), axis=0, tiled=True),
        lax.all_gather(w_down, ("seq", "dp"), axis=0, tiled=True),
        lax.all_gather(qv_bias, ("seq", "dp"), axis=1, tiled=True),
        lax.all_gather(out_bias, ("seq", "dp"), axis=0, tiled=True),
        lax.all_gather(up_bias, ("seq", "dp"), axis=0, tiled=True),
        lax.all_gather(down_bias, ("seq", "dp"), axis=0, tiled=True),
        lax.all_gather(norm_gain, ("seq", "dp"), axis=1, tiled=True),
        lax.all_gather(norm_shift, ("seq", "dp"), axis=1, tiled=True),
    )
    qkv_full, out_full, up_full, down_full = (gathered[0], gathered[1], gathered[2], gathered[3])
    qv_shift = gathered[4].astype(jnp.float32)
    out_shift = gathered[5].astype(jnp.float32)
    up_shift = gathered[6].astype(jnp.float32)
    down_shift = gathered[7].astype(jnp.float32)
    gains = gathered[8].astype(jnp.float32)
    shifts = gathered[9].astype(jnp.float32)
    row_count = tokens.shape[1]
    model_width = tokens.shape[2]
    pair_cols = 2 * HD
    pair_count = model_width // pair_cols
    slot_rows = row_count * lax.axis_size("seq")
    factor = 1.0 / (RELAX_SCALE * math.sqrt(HD))
    valid = lengths[assign[lax.axis_index("dp")]]
    own_place = lax.axis_index("seq") * row_count + jnp.arange(row_count, dtype=jnp.int32)
    all_place = jnp.arange(slot_rows, dtype=jnp.int32)
    allowed = (all_place[None, :] <= own_place[:, None]) & (all_place[None, :] < valid)
    pair_ids = jnp.arange(pair_count, dtype=jnp.int32)
    hidden = tokens[0].astype(jnp.float32)
    normed_first, pull_first = jax.vjp(norm_rows, hidden, gains[0], shifts[0])
    normed_low = normed_first.astype(jnp.bfloat16)
    projected = jnp.dot(normed_low, qkv_full, preferred_element_type=jnp.float32)
    queries = (projected[:, :model_width] + qv_shift[0]).astype(jnp.bfloat16)
    key_own = projected[:, model_width : 2 * model_width].astype(jnp.bfloat16)
    value_own = (projected[:, 2 * model_width :] + qv_shift[1]).astype(jnp.bfloat16)
    keys, values = (
        lax.all_gather(key_own, "seq", axis=0, tiled=True),
        lax.all_gather(value_own, "seq", axis=0, tiled=True),
    )

    def columns(block, pair_index):
        return lax.dynamic_slice_in_dim(block, pair_index * pair_cols, pair_cols, 1)

    def merge_pairs(stack):
        return stack.transpose(1, 0, 2).reshape(stack.shape[1], model_width)

    def attend(pair_index):
        scores = pair_scores(columns(queries, pair_index), columns(keys, pair_index))
        row_max = jnp.max(jnp.where(allowed, scores, -jnp.inf), -1, keepdims=True)
        exp_terms = jnp.exp(jnp.where(allowed, RELAX_SCALE * (scores - row_max), -jnp.inf))
        row_total = jnp.sum(exp_terms, -1, keepdims=True)
        probs = (exp_terms / row_total).astype(jnp.bfloat16)
        mixed = jnp.einsum(
            "hqk,khd->qhd",
            probs,
            split_heads(columns(values, pair_index)),
            preferred_element_type=jnp.float32,
        )
        return (mixed.reshape(row_count, pair_cols), row_max[..., 0], row_total[..., 0])

    mixed_pairs, max_pairs, total_pairs = lax.map(attend, pair_ids)
    attended = merge_pairs(mixed_pairs).astype(jnp.bfloat16)
    branch = jnp.dot(attended, out_full, preferred_element_type=jnp.float32) + out_shift
    normed_second, pull_second = jax.vjp(norm_rows, branch, gains[1], shifts[1])
    middle = hidden + normed_second
    normed_third, pull_third = jax.vjp(norm_rows, middle, gains[2], shifts[2])
    third_low = normed_third.astype(jnp.bfloat16)
    up_pre = jnp.dot(third_low, up_full, preferred_element_type=jnp.float32) + up_shift
    activated, pull_gelu = jax.vjp(exact_gelu, up_pre)
    active_low = activated.astype(jnp.bfloat16)
    down_pre = jnp.dot(active_low, down_full, preferred_element_type=jnp.float32) + down_shift
    normed_fourth, pull_fourth = jax.vjp(norm_rows, down_pre, gains[3], shifts[3])
    output = (middle + normed_fourth).astype(jnp.bfloat16)[None]
    again = (
        lax.all_gather(w_qkv, ("seq", "dp"), axis=0, tiled=True),
        lax.all_gather(w_out, ("seq", "dp"), axis=0, tiled=True),
        lax.all_gather(w_up, ("seq", "dp"), axis=0, tiled=True),
        lax.all_gather(w_down, ("seq", "dp"), axis=0, tiled=True),
    )
    qkv_back, out_back, up_back, down_back = (again[0], again[1], again[2], again[3])
    keep_rows = (own_place < valid).astype(jnp.float32)[:, None]
    grad_out = cotangent[0].astype(jnp.float32) * keep_rows
    grad_down, grad_gain_four, grad_shift_four = pull_fourth(grad_out)
    grad_down_low = grad_down.astype(jnp.bfloat16)
    grad_w_down = contract_rows(active_low, grad_down_low)
    grad_b_down = jnp.sum(grad_down_low.astype(jnp.float32), 0)
    (grad_up,) = pull_gelu(contract_cols(grad_down_low, down_back))
    grad_up_low = grad_up.astype(jnp.bfloat16)
    grad_w_up = contract_rows(third_low, grad_up_low)
    grad_b_up = jnp.sum(grad_up_low.astype(jnp.float32), 0)
    grad_middle_part, grad_gain_three, grad_shift_three = pull_third(
        contract_cols(grad_up_low, up_back)
    )
    grad_middle = grad_out + grad_middle_part
    grad_branch, grad_gain_two, grad_shift_two = pull_second(grad_middle)
    grad_branch_low = grad_branch.astype(jnp.bfloat16)
    grad_w_out = contract_rows(attended, grad_branch_low)
    grad_b_out = jnp.sum(grad_branch_low.astype(jnp.float32), 0)
    grad_attended = contract_cols(grad_branch_low, out_back).astype(jnp.bfloat16)

    def query_side(pair_index):
        scores = pair_scores(columns(queries, pair_index), columns(keys, pair_index))
        probs = kept_probs(
            scores, allowed, max_pairs[pair_index][..., None], total_pairs[pair_index][..., None]
        )
        grad_part = columns(grad_attended, pair_index)
        grad_probs = jnp.einsum(
            "qhd,khd->hqk",
            split_heads(grad_part),
            split_heads(columns(values, pair_index)),
            preferred_element_type=jnp.float32,
        )
        delta = jnp.sum(probs * grad_probs, -1, keepdims=True)
        grad_scores = (RELAX_SCALE * probs * (grad_probs - delta)).astype(jnp.bfloat16)
        grad_query = (
            jnp.einsum(
                "hqk,khd->qhd",
                grad_scores,
                split_heads(columns(keys, pair_index)),
                preferred_element_type=jnp.float32,
            )
            * factor
        )
        return (grad_query.reshape(row_count, pair_cols), grad_scores, probs, delta)

    def both_sides(pair_index):
        grad_query, grad_scores, probs, delta = query_side(pair_index)
        grad_part = columns(grad_attended, pair_index)
        grad_key = (
            jnp.einsum(
                "hqk,qhd->khd",
                grad_scores,
                split_heads(columns(queries, pair_index)),
                preferred_element_type=jnp.float32,
            )
            * factor
        )
        grad_value = jnp.einsum(
            "hqk,qhd->khd",
            probs.astype(jnp.bfloat16),
            split_heads(grad_part),
            preferred_element_type=jnp.float32,
        )
        return (
            grad_query,
            grad_key.reshape(slot_rows, pair_cols),
            grad_value.reshape(slot_rows, pair_cols),
        )

    query_pairs, key_terms, value_terms = lax.map(both_sides, pair_ids)
    key_pairs, value_pairs = (
        lax.psum_scatter(
            key_terms.astype(jnp.bfloat16), "seq", scatter_dimension=1, tiled=True
        ).astype(jnp.float32),
        lax.psum_scatter(
            value_terms.astype(jnp.bfloat16), "seq", scatter_dimension=1, tiled=True
        ).astype(jnp.float32),
    )
    grad_q_low = merge_pairs(query_pairs).astype(jnp.bfloat16)
    grad_k_low = merge_pairs(key_pairs).astype(jnp.bfloat16)
    grad_v_low = merge_pairs(value_pairs).astype(jnp.bfloat16)
    grad_projected = jnp.concatenate([grad_q_low, grad_k_low, grad_v_low], 1)
    grad_w_qkv = contract_rows(normed_low, grad_projected)
    grad_qv = jnp.stack(
        [jnp.sum(grad_q_low.astype(jnp.float32), 0), jnp.sum(grad_v_low.astype(jnp.float32), 0)]
    )
    grad_hidden_part, grad_gain_one, grad_shift_one = pull_first(
        contract_cols(grad_projected, qkv_back)
    )
    input_grad = (grad_middle + grad_hidden_part).astype(jnp.bfloat16)[None]
    grad_gains = jnp.stack([grad_gain_one, grad_gain_two, grad_gain_three, grad_gain_four])
    grad_shifts = jnp.stack([grad_shift_one, grad_shift_two, grad_shift_three, grad_shift_four])
    owned = (
        lax.psum_scatter(grad_w_qkv, ("seq", "dp"), scatter_dimension=0, tiled=True),
        lax.psum_scatter(grad_w_out, ("seq", "dp"), scatter_dimension=0, tiled=True),
        lax.psum_scatter(grad_w_up, ("seq", "dp"), scatter_dimension=0, tiled=True),
        lax.psum_scatter(grad_w_down, ("seq", "dp"), scatter_dimension=0, tiled=True),
        lax.psum_scatter(grad_qv, ("seq", "dp"), scatter_dimension=1, tiled=True),
        lax.psum_scatter(grad_b_out, ("seq", "dp"), scatter_dimension=0, tiled=True),
        lax.psum_scatter(grad_b_up, ("seq", "dp"), scatter_dimension=0, tiled=True),
        lax.psum_scatter(grad_b_down, ("seq", "dp"), scatter_dimension=0, tiled=True),
        lax.psum_scatter(grad_gains, ("seq", "dp"), scatter_dimension=1, tiled=True),
        lax.psum_scatter(grad_shifts, ("seq", "dp"), scatter_dimension=1, tiled=True),
    )
    return (
        output,
        input_grad,
        owned[0],
        owned[4],
        owned[1],
        owned[5],
        owned[2],
        owned[6],
        owned[3],
        owned[7],
        owned[8],
        owned[9],
    )


MESH = pl.DeviceIdType.MESH


def is_small(mesh):
    return mesh.shape["seq"] == 16 and mesh.shape["dp"] == 2


def place():
    seq = lax.axis_index("seq")
    return seq // 8, (seq // 4) % 2, (seq // 2) % 2, seq % 2, lax.axis_index("dp")


def exchange_kernel(scatter, src, out, send_sem, recv_sem, own_sem):
    a, b, y, c, x = place()
    barrier = pltpu.get_barrier_semaphore()

    def peer(k):
        return lax.rem(a + k // 2, 2), lax.rem(y + k % 2, 2)

    def device(k):
        pa, py = peer(k)
        return (pa * 8 + b * 4 + py * 2 + c, x)

    def source(k):
        pa, py = peer(k)
        return src.at[pa * 2 + py] if scatter else src.at[pa, :, py]

    def target(k):
        pa, py = peer(k)
        return out.at[pa, :, py] if scatter else out.at[pa * 2 + py]

    for k in range(1, 4):
        pl.semaphore_signal(barrier, inc=1, device_id=device(k), device_id_type=MESH)
    own = pltpu.make_async_copy(source(0), target(0), own_sem)
    own.start()
    pl.semaphore_wait(barrier, 3)

    def copy(k, dst):
        return pltpu.make_async_remote_copy(
            src_ref=source(k), dst_ref=target(dst), send_sem=send_sem.at[k], recv_sem=recv_sem.at[k],
            device_id=device(k), device_id_type=MESH)

    for k in (3, 2, 1):
        copy(k, 0).start()
    own.wait()
    for k in (3, 2, 1):
        copy(k, k).wait_recv()
    for k in (3, 2, 1):
        copy(k, 0).wait_send()


def exchange(blocks, scatter, cid):
    vm = pl.BlockSpec(memory_space=pltpu.VMEM)
    rows = blocks.shape[-2]
    shape = (2, 2, 2, rows, 128) if scatter else (4, 2, rows, 128)
    return pl.pallas_call(
        functools.partial(exchange_kernel, scatter), out_shape=jax.ShapeDtypeStruct(shape, blocks.dtype),
        in_specs=[vm], out_specs=vm,
        scratch_shapes=[pltpu.SemaphoreType.DMA((4,)), pltpu.SemaphoreType.DMA((4,)), pltpu.SemaphoreType.DMA],
        compiler_params=pltpu.CompilerParams(collective_id=cid, has_side_effects=True),
        cost_estimate=pl.CostEstimate(flops=0, bytes_accessed=rows * 100000, transcendentals=0),
        name="exchange",
    )(blocks)


def dot_nt(a, b):
    return lax.dot_general(a, b, (((1,), (1,)), ((), ())), preferred_element_type=jnp.float32)


def dot_nn(a, b):
    return jnp.dot(a, b, preferred_element_type=jnp.float32)


BQ = 256
MASKED = -1e30


def load_heads(valid, packed, q_ref, k_ref):
    rows = q_ref.shape[0]
    qk = packed[:, :256].reshape(rows, 128)
    kq = jnp.concatenate([qk[:, 64:], qk[:, :64]], axis=1)
    lane = lax.broadcasted_iota(jnp.int32, (rows, 128), 1)
    spot = lax.broadcasted_iota(jnp.int32, (rows, 128), 0)
    past = jnp.where(spot < valid, 0.0, MASKED)
    q_ref[...] = jnp.where(lane < 64, qk.astype(jnp.float32), jnp.where(lane == 64, 1.0, 0.0)).astype(jnp.bfloat16)
    k_ref[...] = jnp.where(lane < 64, kq.astype(jnp.float32), jnp.where(lane == 64, past, 0.0)).astype(jnp.bfloat16)


def unpack_rows(halves):
    n = halves.shape[0]
    return jnp.concatenate([halves[:, :, :64], halves[:, :, 64:]], axis=1).reshape(n * 256, 64)


def block_probs(q_ref, k_ref, i):
    n = (i + 1) * BQ
    scores = dot_nt(k_ref[:n], q_ref[i * BQ:n])
    key = lax.broadcasted_iota(jnp.int32, (BQ, BQ), 0)
    query = lax.broadcasted_iota(jnp.int32, (BQ, BQ), 1)
    corner = jnp.where(key <= query, scores[n - BQ:], MASKED)
    scores = jnp.concatenate([scores[:n - BQ], corner], axis=0) if i else corner
    top = jnp.max(scores, axis=0, keepdims=True)
    terms = jnp.exp((scores - top) * 0.125)
    return terms, 1.0 / jnp.sum(terms, axis=0, keepdims=True)


def attend_kernel(valid_ref, packed, out_ref, q_ref, k_ref, vt_ref):
    load_heads(valid_ref[0], packed, q_ref, k_ref)
    unit = jnp.where(
        lax.broadcasted_iota(jnp.int32, (64, 64), 0) == lax.broadcasted_iota(jnp.int32, (64, 64), 1), 1.0, 0.0
    ).astype(jnp.bfloat16)
    vt_ref[...] = dot_nt(unit, unpack_rows(packed[:, 256:])).astype(jnp.bfloat16)
    for i in range(q_ref.shape[0] // BQ):
        n = (i + 1) * BQ
        terms, scale = block_probs(q_ref, k_ref, i)
        probs = (terms * scale).astype(jnp.bfloat16)
        mixed = dot_nn(vt_ref[:, :n], probs).T
        out_ref[i] = jnp.concatenate([mixed[:128], mixed[128:]], axis=1).astype(jnp.bfloat16)


def attend_back_kernel(valid_ref, packed, grad, out_ref, q_ref, k_ref, v_ref, g_ref, kt_ref, dk_ref, dv_ref):
    load_heads(valid_ref[0], packed, q_ref, k_ref)
    v_ref[...] = unpack_rows(packed[:, 256:])
    g_ref[...] = unpack_rows(grad[...])
    unit = jnp.where(
        lax.broadcasted_iota(jnp.int32, (64, 128), 0) == lax.broadcasted_iota(jnp.int32, (64, 128), 1), 1.0, 0.0
    ).astype(jnp.bfloat16)
    kt_ref[...] = dot_nt(unit, k_ref[...]).astype(jnp.bfloat16)
    dk_ref[...] = jnp.zeros_like(dk_ref)
    dv_ref[...] = jnp.zeros_like(dv_ref)
    blocks = q_ref.shape[0] // BQ
    for i in range(blocks):
        n = (i + 1) * BQ
        terms, scale = block_probs(q_ref, k_ref, i)
        probs = terms * scale
        grad_probs = dot_nt(v_ref[:n], g_ref[i * BQ:n])
        delta = jnp.sum(probs * grad_probs, axis=0, keepdims=True)
        grad_scores = (probs * (grad_probs - delta)).astype(jnp.bfloat16)
        grad_query = dot_nn(kt_ref[:, :n], grad_scores).T * 0.125
        out_ref[i, :256, :64] = grad_query.astype(jnp.bfloat16)
        dk_ref[:n] += dot_nn(grad_scores, q_ref[i * BQ:n])
        dv_ref[:n] += dot_nn(probs.astype(jnp.bfloat16), g_ref[i * BQ:n])
    for i in range(blocks):
        rows = slice(i * BQ, (i + 1) * BQ)
        out_ref[i, :256, 64:] = (dk_ref[rows, :64] * 0.125).astype(jnp.bfloat16)
        value = dv_ref[rows].astype(jnp.bfloat16)
        out_ref[i, 256:] = jnp.concatenate([value[:128], value[128:]], axis=1)


def attend(valid, packed):
    rows = packed.shape[0] * 256
    vm = pl.BlockSpec(memory_space=pltpu.VMEM)
    return pl.pallas_call(
        attend_kernel,
        out_shape=jax.ShapeDtypeStruct((packed.shape[0], 128, 128), jnp.bfloat16),
        in_specs=[pl.BlockSpec(memory_space=pltpu.SMEM), vm], out_specs=vm,
        scratch_shapes=[pltpu.VMEM((rows, 128), jnp.bfloat16)] * 2 + [pltpu.VMEM((64, rows), jnp.bfloat16)],
        compiler_params=pltpu.CompilerParams(vmem_limit_bytes=48 << 20),
        name="attend",
    )(valid, packed)


def attend_back(valid, packed, grad):
    rows = packed.shape[0] * 256
    vm = pl.BlockSpec(memory_space=pltpu.VMEM)
    return pl.pallas_call(
        attend_back_kernel,
        out_shape=jax.ShapeDtypeStruct(packed.shape, jnp.bfloat16),
        in_specs=[pl.BlockSpec(memory_space=pltpu.SMEM), vm, vm], out_specs=vm,
        scratch_shapes=[pltpu.VMEM((rows, 128), jnp.bfloat16)] * 2 + [pltpu.VMEM((rows, 64), jnp.bfloat16)] * 2
        + [pltpu.VMEM((64, rows), jnp.bfloat16), pltpu.VMEM((rows, 128), jnp.float32), pltpu.VMEM((rows, 64), jnp.float32)],
        compiler_params=pltpu.CompilerParams(vmem_limit_bytes=48 << 20),
        name="attend_back",
    )(valid, packed, grad)


def flip(bits, block):
    return lax.ppermute(block, "seq", [(s, s ^ bits) for s in range(16)])


flip_a, flip_b, flip_y, flip_core, flip_far = (functools.partial(flip, bits) for bits in (8, 4, 2, 1, 5))


def flip_x(block):
    return lax.ppermute(block, "dp", [(0, 1), (1, 0)])


def after(value, *others):
    return lax.optimization_barrier((value,) + others)[0]


def pick(block, index, axis, keepdims=False):
    return lax.dynamic_index_in_dim(block, index, axis, keepdims=keepdims)


def swap_if(flag, block, axis):
    return jnp.where(flag == 0, block, lax.rev(block, (axis,)))


def sort_ranks(block, b, c):
    return swap_if(c, swap_if(b, block, 0), 1)


def to_ranks(block, b, c):
    mine = pick(pick(block, b, 0), c, 0)
    core = flip_core(pick(pick(block, b, 0), 1 - c, 0))
    near = flip_b(pick(pick(block, 1 - b, 0), c, 0))
    far = flip_far(pick(pick(block, 1 - b, 0), 1 - c, 0))
    return jnp.stack([jnp.stack([mine, core]), jnp.stack([near, far])])


def gather_rows(block):
    core, near = flip_core(block), flip_b(block)
    return jnp.concatenate([block, core, near, flip_core(near)], 0)


def scatter_rows(part):
    part = part.reshape(2, 2, part.shape[0] // 4, part.shape[1])
    far = part[1, 0] + flip_core(part[1, 1])
    near = part[0, 0] + flip_core(part[0, 1])
    return near + flip_b(far.astype(jnp.bfloat16)).astype(jnp.float32)


def cube_start(block):
    return jnp.stack([block, flip_a(block)])


def cube_one(flip_one, block):
    return jnp.concatenate([block, flip_one(block)], 0)


def arrange_kernel(count, spot_ref, *refs):
    for k in range(count):
        block, out = refs[k], refs[count + k]
        if len(out.shape) == 7:
            for i in range(2):
                for j in range(2):
                    out[0, i, 0, j, 0] = block[0, i, j]
        else:
            out[0, 0, 0] = block[0]


def arrange(spot, blocks):
    def coords(i, r, y_first):
        second, first, a = i // 4, (i // 2) % 2, i % 2
        y, x = (first, second) if y_first else (second, first)
        return lax.rem(r[0] + a, 2), lax.rem(r[1] + y, 2), lax.rem(r[2] + x, 2)

    def specs(block, y_first):
        shape = block.shape
        if len(shape) == 5:
            def out_place(i, r):
                a, y, x = coords(i, r, y_first)
                return a, 0, y, 0, x, 0, 0
            return (pl.BlockSpec((1,) + shape[1:], lambda i, r: (i, 0, 0, 0, 0)),
                    pl.BlockSpec((1, 2, 1, 2, 1) + shape[3:], out_place),
                    jax.ShapeDtypeStruct((2,) * 5 + shape[3:], block.dtype))

        def out_place(i, r):
            return coords(i, r, y_first) + (0, 0)
        return (pl.BlockSpec((1,) + shape[1:], lambda i, r: (i, 0, 0)),
                pl.BlockSpec((1, 1, 1) + shape[1:], out_place),
                jax.ShapeDtypeStruct((2, 2, 2) + shape[1:], block.dtype))

    made = [specs(*entry) for entry in blocks]
    return pl.pallas_call(
        functools.partial(arrange_kernel, len(blocks)),
        out_shape=tuple(m[2] for m in made),
        grid_spec=pltpu.PrefetchScalarGridSpec(
            num_scalar_prefetch=1, grid=(8,), in_specs=[m[0] for m in made], out_specs=tuple(m[1] for m in made)),
        compiler_params=pltpu.CompilerParams(vmem_limit_bytes=32 << 20),
        cost_estimate=pl.CostEstimate(flops=0, bytes_accessed=8 << 20, transcendentals=0),
        name="arrange",
    )(spot, *[entry[0] for entry in blocks])


def add_low(mine, other):
    return (mine.astype(jnp.float32) + other.astype(jnp.float32)).astype(jnp.bfloat16)


def fold(terms, flip_one, index, axis):
    return add_low(pick(terms, index, axis, True), flip_one(pick(terms, 1 - index, axis, True)))


def reduce_kernel(q_ref, o_ref, u_ref, d_ref, s_ref, out_q, ro, out_u, rd, rs,
                  rq, ru, r1q, t2q, r2q, t3q, r3q, fq, gq, r1o, t2o, r2o, t3o, r3o, r3u, fu, gu, r3d,
                  sx, s1, sy, s2, sa, s3, sb, s4, sc, send_sem, recv_sem):
    a, b, y, c, x = place()
    f32, bf16 = jnp.float32, jnp.bfloat16
    barrier = pltpu.get_barrier_semaphore()

    def at(pa, pb, py, pc, px):
        return (pa * 8 + pb * 4 + py * 2 + pc, px)

    to_x, to_y, to_a = at(a, b, y, c, 1 - x), at(a, b, 1 - y, c, x), at(1 - a, b, y, c, x)
    ranks = [(lax.rem(b + k // 2, 2), lax.rem(c + k % 2, 2)) for k in range(4)]
    to_rank = [at(a, ranks[k][0], y, ranks[k][1], x) for k in range(4)]
    to_b, to_c = to_rank[2], to_rank[1]
    for dev in [to_x, to_y, to_a] + to_rank[1:]:
        pl.semaphore_signal(barrier, inc=1, device_id=dev, device_id_type=MESH)
    pl.semaphore_wait(barrier, 6)

    made = []

    def remote(src, dst, dev):
        k = len(made)
        made.append(pltpu.make_async_remote_copy(
            src_ref=src, dst_ref=dst, send_sem=send_sem.at[k], recv_sem=recv_sem.at[k],
            device_id=dev, device_id_type=MESH))
        return made[-1]

    def low(*values):
        return sum(v.astype(f32) for v in values)

    places = [1 - a, a]
    halves = [slice(0, 512), slice(512, 1024)]
    lateral = [(to_x, to_y), (to_y, to_x)]

    cu = remote(u_ref.at[1 - a], r3u, to_a)
    cd = remote(d_ref.at[1 - a], r3d, to_a)
    q1, q2, o1, o2 = {}, {}, {}, {}
    for i in range(2):
        for s in range(2):
            p = places[i]
            q1[s, i] = remote(q_ref.at[p, 0, :, :, 1 - x] if s == 0 else q_ref.at[p, 1, 1 - y], r1q.at[s, i], lateral[s][0])
            o1[s, i] = remote(o_ref.at[p, :, 1 - x, :, halves[0]] if s == 0 else o_ref.at[p, 1 - y, :, :, halves[1]],
                              r1o.at[s, i], lateral[s][0])
            q2[s, i] = remote(t2q.at[s, i], r2q.at[s, i], lateral[s][1])
            o2[s, i] = remote(t2o.at[s, i], r2o.at[s, i], lateral[s][1])
    q3 = [remote(t3q.at[s], r3q.at[s], to_a) for s in range(2)]
    o3 = [remote(t3o.at[s], r3o.at[s], to_a) for s in range(2)]
    qr = [remote(fq.at[ranks[k][0], ranks[k][1]], gq.at[k - 1], to_rank[k]) for k in range(1, 4)]
    ur = [remote(fu.at[ranks[k][0], ranks[k][1]], gu.at[k - 1], to_rank[k]) for k in range(1, 4)]
    vx = remote(s_ref.at[:, :, :, :, 1 - x], sx, to_x)
    vy = remote(s1.at[:, :, 1 - y], sy, to_y)
    va = remote(s2.at[1 - a], sa, to_a)
    vb = remote(s3.at[1 - b], sb, to_b)
    vc = remote(s4.at[1 - c], sc, to_c)

    cu.start()
    vx.start()
    for i in range(2):
        for s in range(2):
            q1[s, i].start()
            o1[s, i].start()
    cd.start()

    def q_terms(s, i, far):
        p = places[i]
        if s == 0:
            v = 1 - y if far else y
            return q_ref[p, 0, v, :, x], r1q[0, i, v]
        v = 1 - x if far else x
        return q_ref[p, 1, y, :, v], r1q[1, i, :, v]

    def o_terms(s, i, far):
        p = places[i]
        if s == 0:
            v = 1 - y if far else y
            return o_ref[p, v, x, :, halves[0]], r1o[0, i, v]
        v = 1 - x if far else x
        return o_ref[p, y, v, :, halves[1]], r1o[1, i, v]

    for i in range(2):
        for s in range(2):
            q1[s, i].wait_recv()
            t2q[s, i] = low(*q_terms(s, i, True)).astype(bf16)
            q2[s, i].start()
            o1[s, i].wait_recv()
            t2o[s, i] = low(*o_terms(s, i, True)).astype(bf16)
            o2[s, i].start()
        if i == 0:
            vx.wait_recv()
            s1[...] = s_ref[:, :, :, :, x] + sx[...]
            vy.start()
            for s in range(2):
                q2[s, 0].wait_recv()
                t3q[s] = low(*q_terms(s, 0, False), r2q[s, 0]).astype(bf16)
                q3[s].start()
                o2[s, 0].wait_recv()
                t3o[s] = low(*o_terms(s, 0, False), r2o[s, 0]).astype(bf16)
                o3[s].start()
    vy.wait_recv()
    s2[...] = s1[:, :, y] + sy[...]
    va.start()

    cu.wait_recv()
    for k in range(1, 4):
        pb, pc = ranks[k]
        fu[pb, pc] = low(u_ref[a, pb, pc], r3u[pb, pc]).astype(bf16)
        ur[k - 1].start()
    ru[b, c] = low(u_ref[a, b, c], r3u[b, c])

    for s in range(2):
        q2[s, 1].wait_recv()
        o2[s, 1].wait_recv()
        q3[s].wait_recv()
        total = low(*q_terms(s, 1, False), r2q[s, 1], r3q[s])
        fq[s] = total.astype(bf16)
        for j in range(2):
            @pl.when((b == s) & (c == j))
            def _():
                rq[s, j] = total[j]
        o3[s].wait_recv()
        ro[:, halves[s]] = low(*o_terms(s, 1, False), r2o[s, 1], r3o[s])
    for k in (3, 2, 1):
        qr[k - 1].start()
    va.wait_recv()
    s3[...] = s2[a] + sa[...]
    vb.start()
    cd.wait_recv()
    rd[...] = low(d_ref[a], r3d[...])
    vb.wait_recv()
    s4[...] = s3[b] + sb[...]
    vc.start()
    for k in (1, 2, 3):
        pb, pc = ranks[k]
        ur[k - 1].wait_recv()
        ru[pb, pc] = gu[k - 1].astype(f32)
    for k in (1, 2, 3):
        pb, pc = ranks[k]
        qr[k - 1].wait_recv()
        rq[pb, pc] = gq[k - 1].astype(f32)
    for pb in range(2):
        for j in range(4):
            zero, one = rq[pb, 0], rq[pb, 1]
            h = head_of(j // 2, pb, j % 2, 0) * HD
            q, k = slice(j * 128, j * 128 + HD), slice(j * 128 + HD, j * 128 + 128)
            v = slice(512 + j * HD, 512 + j * HD + HD)
            for t, cols in enumerate((q, k, v)):
                out_q[:, t * 1024 + h:t * 1024 + h + 128] = jnp.concatenate([zero[:, cols], one[:, cols]], 1)
            for pc in range(2):
                col = head_of(j // 2, pb, j % 2, pc) * 256
                out_u[:, col:col + 256] = ru[pb, pc, :, j * 256:j * 256 + 256]
    vc.wait_recv()
    rs[...] = s4[c] + sc[...]
    for copy in made:
        copy.wait_send()


def reduce_all(gw_qkv, gw_out, up_sum, down_sum, small, cid):
    f32, bf16 = jnp.float32, jnp.bfloat16
    V = pltpu.VMEM
    vm = pl.BlockSpec(memory_space=V)
    S = jax.ShapeDtypeStruct
    q, o = gw_qkv.shape[5:], (gw_out.shape[3], 512)
    u, d, s = up_sum.shape[1:], down_sum.shape[1:], small.shape[5:]
    scratch = [
        V((2, 2) + q, f32), V(u, f32),
        V((2, 2, 2, 2) + q, bf16), V((2, 2, 2) + q, bf16), V((2, 2, 2) + q, bf16), V((2, 2) + q, bf16), V((2, 2) + q, bf16),
        V((2, 2) + q, bf16), V((3,) + q, bf16),
        V((2, 2, 2) + o, bf16), V((2, 2) + o, bf16), V((2, 2) + o, bf16), V((2,) + o, bf16), V((2,) + o, bf16),
        V(u, bf16), V(u, bf16), V((3,) + u[2:], bf16), V(d, bf16),
        V((2, 2, 2, 2) + s, f32), V((2, 2, 2, 2) + s, f32), V((2, 2, 2) + s, f32), V((2, 2, 2) + s, f32), V((2, 2) + s, f32),
        V((2, 2) + s, f32), V((2,) + s, f32), V((2,) + s, f32), V(s, f32),
        pltpu.SemaphoreType.DMA((33,)), pltpu.SemaphoreType.DMA((33,))]
    return pl.pallas_call(
        reduce_kernel,
        out_shape=(S((q[0], 4 * q[1]), f32), S((o[0], 1024), f32), S((u[2], 4 * u[3]), f32), S(d, f32), S(s, f32)),
        in_specs=[vm] * 5, out_specs=(vm,) * 5, scratch_shapes=scratch,
        compiler_params=pltpu.CompilerParams(collective_id=cid, has_side_effects=True, vmem_limit_bytes=40 << 20),
        name="reduce_all",
    )(gw_qkv, gw_out, up_sum, down_sum, small)


def qk_columns(head):
    return slice(head * HD, head * HD + HD), slice(1024 + head * HD, 1024 + head * HD + HD), slice(2048 + head * HD, 2048 + head * HD + HD)


def head_of(a, b, y, c):
    return a * 8 + b * 4 + y * 2 + c


def start_kernel(q_in, u_in, o_in, t_in, v_in, wq, wo, up, rows, vec, q_src, u_src, send_sem, recv_sem, own_sem):
    a, b, y, c, x = place()
    barrier = pltpu.get_barrier_semaphore()

    def at(pa, pb, py, pc, px):
        return (pa * 8 + pb * 4 + py * 2 + pc, px)

    to_x, to_y, to_a = at(a, b, y, c, 1 - x), at(a, b, 1 - y, c, x), at(1 - a, b, y, c, x)
    ranks = [(lax.rem(b + k // 2, 2), lax.rem(c + k % 2, 2)) for k in range(4)]
    to_rank = [at(a, pb, y, pc, x) for pb, pc in ranks]
    for dev in [to_x, to_y, to_a] + to_rank[1:]:
        pl.semaphore_signal(barrier, inc=1, device_id=dev, device_id_type=MESH)

    for pb in range(2):
        for pc in range(2):
            for j in range(4):
                q, k, v = qk_columns(head_of(j // 2, pb, j % 2, pc))
                q_src[pb, pc, :, j * 128:j * 128 + 128] = jnp.concatenate([q_in[:, q], q_in[:, k]], 1)
            for j in range(2):
                v0 = qk_columns(head_of(j, pb, 0, pc))[2]
                v1 = qk_columns(head_of(j, pb, 1, pc))[2]
                q_src[pb, pc, :, 512 + j * 128:640 + j * 128] = jnp.concatenate([q_in[:, v0], q_in[:, v1]], 1)
            for j in range(4):
                col = (head_of(j // 2, pb, j % 2, pc)) * 256
                u_src[pb, pc, :, j * 256:j * 256 + 256] = u_in[:, col:col + 256]
    own = [pltpu.make_async_copy(src, dst, own_sem.at[k]) for k, (src, dst) in enumerate((
        (q_src.at[b, c], wq.at[a, b, y, c, x]), (u_src.at[b, c], up.at[0, b, c]), (o_in, wo.at[a, y, x]),
        (t_in, rows.at[0]), (v_in, vec.at[a, b, y, c, x])))]
    for copy in own:
        copy.start()
    pl.semaphore_wait(barrier, 6)

    made = []

    def remote(src, dst, dev):
        k = len(made)
        made.append(pltpu.make_async_remote_copy(
            src_ref=src, dst_ref=dst, send_sem=send_sem.at[k], recv_sem=recv_sem.at[k],
            device_id=dev, device_id_type=MESH))
        return made[-1]

    places = [a, 1 - a]
    halves = [slice(0, 512), slice(512, 1024)]
    lateral = [(to_y, to_x), (to_x, to_y)]

    def same(ref, dev):
        return remote(ref, ref, dev)

    q_rank = [remote(q_src.at[ranks[k][0], ranks[k][1]], wq.at[a, b, y, c, x], to_rank[k]) for k in range(1, 4)]
    u_rank = [remote(u_src.at[ranks[k][0], ranks[k][1]], up.at[0, b, c], to_rank[k]) for k in range(1, 4)]
    v_rank = [remote(v_in, vec.at[a, b, y, c, x], to_rank[k]) for k in range(1, 4)]
    t_core, t_near = remote(t_in, rows.at[1], to_rank[1]), remote(t_in, rows.at[2], to_rank[2])
    t_far = remote(rows.at[2], rows.at[3], to_rank[1])
    u_cube = remote(up.at[0], up.at[1], to_a)
    v_cube = [same(vec.at[a, :, y, :, x], to_a), same(vec.at[:, :, y, :, x], to_y), same(vec.at[:, :, :, :, x], to_x)]
    q_cube = [same(wq.at[a, s, y, :, x], to_a) for s in range(2)]
    o_cube = [remote(o_in.at[:, halves[s]], wo.at[a, y, x, :, halves[s]], to_a) for s in range(2)]
    q_side, o_side = {}, {}
    for i in range(2):
        for s in range(2):
            one, two = lateral[s]
            oy, ox = (1 - y, x) if s == 0 else (y, 1 - x)
            p = places[i]
            mine, theirs = wq.at[p, s, y, :, x], wq.at[p, s, oy, :, ox]
            q_side[s, i] = (same(mine, one), same(mine, two), same(theirs, two))
            mine, theirs = wo.at[p, y, x, :, halves[s]], wo.at[p, oy, ox, :, halves[s]]
            first = o_in.at[:, halves[s]] if i == 0 else mine
            o_side[s, i] = (remote(first, mine, one), remote(first, mine, two), same(theirs, two))

    for k in (2, 1, 0):
        q_rank[k].start()
        v_rank[k].start()
    for s in range(2):
        o_cube[s].start()
        o_side[s, 0][0].start()
        o_side[s, 0][1].start()
    t_near.start()
    t_core.start()
    own[0].wait()
    for copy in q_rank:
        copy.wait_recv()
    for s in range(2):
        q_cube[s].start()
        q_side[s, 0][0].start()
        q_side[s, 0][1].start()
    own[4].wait()
    for copy in v_rank:
        copy.wait_recv()
    v_cube[0].start()
    for k in (2, 1, 0):
        u_rank[k].start()
    for s in range(2):
        o_side[s, 0][0].wait_recv()
        o_side[s, 0][2].start()
    for s in range(2):
        o_cube[s].wait_recv()
        o_side[s, 1][0].start()
        o_side[s, 1][1].start()
    t_near.wait_recv()
    t_far.start()
    for s in range(2):
        q_side[s, 0][0].wait_recv()
        q_side[s, 0][2].start()
    for s in range(2):
        q_cube[s].wait_recv()
        q_side[s, 1][0].start()
        q_side[s, 1][1].start()
    v_cube[0].wait_recv()
    v_cube[1].start()
    own[1].wait()
    for copy in u_rank:
        copy.wait_recv()
    u_cube.start()
    for s in range(2):
        o_side[s, 1][0].wait_recv()
        o_side[s, 1][2].start()
    v_cube[1].wait_recv()
    v_cube[2].start()
    for s in range(2):
        q_side[s, 1][0].wait_recv()
        q_side[s, 1][2].start()
    v_cube[2].wait_recv()
    t_core.wait_recv()
    t_far.wait_recv()
    for i in range(2):
        for s in range(2):
            for k in (1, 2):
                q_side[s, i][k].wait_recv()
                o_side[s, i][k].wait_recv()
    u_cube.wait_recv()
    own[2].wait()
    own[3].wait()
    for copy in made:
        copy.wait_send()


def start_gather(w_qkv, w_up, w_out, tokens, vectors, cid):
    bf16 = jnp.bfloat16
    S = lambda *shape: jax.ShapeDtypeStruct(shape, bf16)
    vm, anywhere = pl.BlockSpec(memory_space=pltpu.VMEM), pl.BlockSpec(memory_space=pl.ANY)
    return pl.pallas_call(
        start_kernel,
        out_shape=(S(2, 2, 2, 2, 2, 32, 768), S(2, 2, 2, 32, 1024), S(2, 2, 2, 32, 1024), S(4, 128, 1024),
                   S(2, 2, 2, 2, 2, 16, 128)),
        in_specs=[vm] * 5, out_specs=(anywhere,) * 5,
        scratch_shapes=[
            pltpu.VMEM((2, 2, 32, 768), bf16), pltpu.VMEM((2, 2, 32, 1024), bf16),
            pltpu.SemaphoreType.DMA((48,)), pltpu.SemaphoreType.DMA((48,)), pltpu.SemaphoreType.DMA((5,))],
        compiler_params=pltpu.CompilerParams(collective_id=cid, has_side_effects=True, vmem_limit_bytes=32 << 20),
        cost_estimate=pl.CostEstimate(flops=0, bytes_accessed=100 << 20, transcendentals=0),
        name="start_gather",
    )(w_qkv, w_up, w_out, tokens, vectors)


def pack_heads(block, b, c):
    block = sort_ranks(block.reshape(2, 2, 128, 4, HD), b, c)
    return block.transpose(3, 0, 2, 1, 4).reshape(4, 2, 128, 128)


def unpack_heads(packed):
    return packed.reshape(4, 2, 128, 2, HD).transpose(1, 3, 2, 0, 4).reshape(2, 2, 128, 4 * HD)


def fast_body(tokens, cotangent, lengths, assign, w_qkv, qv_bias, w_out, out_bias, w_up, up_bias, w_down, down_bias,
              norm_gain, norm_shift):
    bf16, f32 = jnp.bfloat16, jnp.float32
    a, b, y, c, x = place()
    spot = jnp.stack([a, y, x]).astype(jnp.int32)
    width = tokens.shape[2]
    valid = lengths[assign[x]].astype(jnp.int32)

    small = jnp.concatenate([qv_bias, out_bias[None], down_bias[None], norm_gain, norm_shift], 0)
    small = jnp.concatenate([jnp.pad(small, ((0, 0), (0, 96))), up_bias[None], jnp.zeros((3, 128), bf16)], 0)
    wqkv, wo, up_one, rows, small = start_gather(w_qkv, w_up, w_out, tokens[0], small, 6)
    wqkv, wo, rows = wqkv.reshape(width, 768), wo.reshape(256, width), rows.reshape(512, width)
    down_one = cube_start(after(w_down, wqkv))

    vectors = small[..., :12, :32].reshape(32, 12, 32).transpose(1, 0, 2).reshape(12, width).astype(f32)
    qv_half = pick(pick(vectors[:2].reshape(2, 2, 2, 2, 2, HD), b, 2), c, 3).reshape(2, 4, HD)
    qk_shift = jnp.concatenate([qv_half[0], jnp.zeros((4, HD), f32)], 1).reshape(512)
    v_shift = qv_half[1].reshape(256)
    out_full, down_full, gains, shifts = vectors[2], vectors[3], vectors[4:8], vectors[8:12]
    up_shift = pick(pick(small[..., 12, :], b, 1), c, 2).reshape(1024).astype(f32)

    hidden = tokens[0].astype(f32)
    first = norm_rows(rows.astype(f32), gains[0], shifts[0]).astype(bf16)
    up_two = cube_one(flip_x, up_one)
    projected = (dot_nn(first, wqkv) + jnp.concatenate([qk_shift, v_shift])).astype(bf16)
    qk, v = projected[:, :512], projected[:, 512:]
    qk = sort_ranks(qk.reshape(2, 2, 128, 4, 128), b, c).transpose(3, 0, 1, 2, 4).reshape(4, 2, 256, 128)
    packed = exchange(after(jnp.concatenate([qk, pack_heads(v, b, c)], 2), up_two, down_one), True, 1).reshape(8, 384, 128)
    down_two = cube_one(flip_y, after(down_one, packed))
    attended = attend(valid[None], packed).reshape(2, 2, 2, 128, 128)
    attended = exchange(after(attended, down_two), False, 2)
    down_all = cube_one(flip_x, down_two)
    attended = sort_ranks(unpack_heads(attended), b, c).reshape(512, 256)

    up_all = cube_one(flip_y, after(up_two, attended))
    branch = scatter_rows(dot_nn(attended, wo)) + out_full
    second, pull_second = jax.vjp(norm_rows, branch, gains[1], shifts[1])
    middle = hidden + second
    third, pull_third = jax.vjp(norm_rows, middle, gains[2], shifts[2])
    third = gather_rows(third.astype(bf16))
    wu, wd = arrange(spot, [(up_all, False), (down_all, True)])
    wu, wd = wu.reshape(width, 1024), wd.reshape(1024, width)
    up_pre = dot_nn(third, wu) + up_shift
    active, pull_gelu = jax.vjp(exact_gelu, up_pre)
    active = active.astype(bf16)
    down_pre = scatter_rows(dot_nn(active, wd)) + down_full
    fourth, pull_fourth = jax.vjp(norm_rows, down_pre, gains[3], shifts[3])
    output = (middle + fourth).astype(bf16)

    own_spot = lax.axis_index("seq") * 128 + jnp.arange(128, dtype=jnp.int32)
    grad_out = cotangent[0].astype(f32) * (own_spot < valid).astype(f32)[:, None]
    grad_down, gain4, shift4 = pull_fourth(grad_out)
    grad_down = grad_down.astype(bf16)
    down_rows = gather_rows(grad_down)
    gw_down = contract_rows(active, down_rows).astype(bf16).reshape(2, 2, 2, 128, width)
    down_term = flip_y(pick(gw_down, 1 - y, 1, True))
    (grad_up,) = pull_gelu(dot_nt(after(down_rows, gw_down), wd))
    grad_up = grad_up.astype(bf16)
    gw_up = contract_rows(third, grad_up).astype(bf16).reshape(2, 2, 2, 2, 2, 32, 1024)
    up_term = flip_x(pick(gw_up, 1 - x, 4, True))
    part, gain3, shift3 = pull_third(scatter_rows(dot_nt(after(grad_up, gw_up), wu)))
    grad_middle = grad_out + part
    grad_branch, gain2, shift2 = pull_second(grad_middle)
    grad_branch = grad_branch.astype(bf16)
    branch_rows = gather_rows(grad_branch)
    grad_att = dot_nt(branch_rows, wo).astype(bf16)
    down_sum = add_low(pick(gw_down, y, 1, True), down_term)
    grad_packed = exchange(after(pack_heads(grad_att, b, c), down_sum), True, 3).reshape(8, 128, 128)
    up_sum = add_low(pick(gw_up, x, 4, True), after(up_term, grad_packed))
    back = attend_back(valid[None], packed, grad_packed)

    up_sum = fold(up_sum, flip_y, y, 2)
    down_sum = fold(down_sum, flip_x, x, 2)
    back = after(back, up_sum)
    gw_out = contract_rows(attended, branch_rows).astype(bf16).reshape(2, 2, 2, 32, width)
    back = exchange(back.reshape(2, 2, 2, 384, 128), False, 4)
    grad_qk = back[:, :, :256].reshape(4, 2, 2, 128, 128).transpose(1, 2, 3, 0, 4).reshape(2, 2, 128, 512)
    grad_qk = sort_ranks(grad_qk, b, c).reshape(512, 512)
    grad_v = sort_ranks(unpack_heads(back[:, :, 256:]), b, c).reshape(512, 256)
    grad_qkv = jnp.concatenate([grad_qk, grad_v], 1)
    gw_qkv = contract_rows(first, grad_qkv).astype(bf16).reshape(2, 2, 2, 2, 2, 32, 768)
    _, pull_first = jax.vjp(norm_rows, hidden, gains[0], shifts[0])
    part, gain1, shift1 = pull_first(scatter_rows(dot_nt(grad_qkv, wqkv)))
    input_grad = (grad_middle + part).astype(bf16)

    def in_ranks(block, axes):
        for axis, flag in axes:
            spots = lax.broadcasted_iota(jnp.int32, [2 if i == axis else 1 for i in range(block.ndim)], axis)
            block = jnp.where(spots == flag, block, 0.0)
        return block

    def head_sums(block):
        sums = jnp.sum(block.astype(f32), 0).reshape(2, 1, 2, 1, -1)[..., :HD]
        sums = jnp.broadcast_to(sums, (2, 2, 2, 2, HD))
        return in_ranks(sums, ((1, b), (3, c))).reshape(1, width)

    whole = jnp.stack([
        jnp.sum(grad_branch.astype(f32), 0), jnp.sum(grad_down.astype(f32), 0),
        gain1, gain2, gain3, gain4, shift1, shift2, shift3, shift4])
    vecs = jnp.concatenate([head_sums(grad_qk), head_sums(grad_v), whole], 0)
    vecs = vecs.reshape(12, 32, 32).transpose(1, 0, 2).reshape(2, 2, 2, 2, 2, 3, 128)
    sums_up = jnp.broadcast_to(jnp.sum(grad_up.astype(f32), 0).reshape(2, 1, 2, 1, 2, 1, 128), (2, 2, 2, 2, 2, 1, 128))
    sums_up = in_ranks(sums_up, ((1, b), (3, c)))
    terms = jnp.concatenate([vecs, sums_up, jnp.zeros((2, 2, 2, 2, 2, 4, 128), f32)], 5)
    r_qkv, r_out, r_up, r_down, small = reduce_all(gw_qkv, gw_out, up_sum[:, :, 0, :, 0], down_sum[:, 0, 0], terms, 5)
    vectors = small[:3].reshape(12, 32)

    return (
        output[None], input_grad[None], r_qkv, vectors[:2], r_out,
        vectors[2], r_up, small[3], r_down, vectors[3], vectors[4:8], vectors[8:12])


def solution(mesh):
    return jax.shard_map(
        fast_body if is_small(mesh) else body,
        mesh=mesh,
        in_specs=(
            P("dp", "seq", None),
            P("dp", "seq", None),
            P(),
            P(),
            P(("seq", "dp"), None),
            P(None, ("seq", "dp")),
            P(("seq", "dp"), None),
            P(("seq", "dp")),
            P(("seq", "dp"), None),
            P(("seq", "dp")),
            P(("seq", "dp"), None),
            P(("seq", "dp")),
            P(None, ("seq", "dp")),
            P(None, ("seq", "dp")),
        ),
        out_specs=(
            P("dp", "seq", None),
            P("dp", "seq", None),
            P(("seq", "dp"), None),
            P(None, ("seq", "dp")),
            P(("seq", "dp"), None),
            P(("seq", "dp")),
            P(("seq", "dp"), None),
            P(("seq", "dp")),
            P(("seq", "dp"), None),
            P(("seq", "dp")),
            P(None, ("seq", "dp")),
            P(None, ("seq", "dp")),
        ),
        check_vma=False,
    )
```

```python
import functools
import math

import jax
import jax.numpy as jnp
from jax import lax
from jax.experimental import pallas as pl
from jax.experimental.pallas import tpu as pltpu
from jax.sharding import PartitionSpec as P


HD = 64


RELAX_SCALE = 32.0
NORM_EPSILON = 1e-05


def norm_rows(values, gain, shift):
    center = values - jnp.mean(values, -1, keepdims=True)
    spread = jnp.mean(center * center, -1, keepdims=True)
    return center * lax.rsqrt(spread + NORM_EPSILON) * gain + shift


def exact_gelu(values):
    return jax.nn.gelu(values, approximate=False)


def contract_rows(left, right):
    return lax.dot_general(
        left, right, (((0,), (0,)), ((), ())), preferred_element_type=jnp.float32
    )


def contract_cols(left, right):
    return lax.dot_general(
        left, right, (((1,), (1,)), ((), ())), preferred_element_type=jnp.float32
    )


def split_heads(block):
    return block.reshape(block.shape[0], 2, HD)


def pair_scores(query_part, key_part):
    factor = 1.0 / (RELAX_SCALE * math.sqrt(HD))
    return (
        jnp.einsum(
            "qhd,khd->hqk",
            split_heads(query_part),
            split_heads(key_part),
            preferred_element_type=jnp.float32,
        )
        * factor
    )


def kept_probs(scores, allowed, row_max, row_total):
    exp_terms = jnp.exp(jnp.where(allowed, RELAX_SCALE * (scores - row_max), -jnp.inf))
    return exp_terms / row_total


def body(
    tokens,
    cotangent,
    lengths,
    assign,
    w_qkv,
    qv_bias,
    w_out,
    out_bias,
    w_up,
    up_bias,
    w_down,
    down_bias,
    norm_gain,
    norm_shift,
):
    gathered = (
        lax.all_gather(w_qkv, ("seq", "dp"), axis=0, tiled=True),
        lax.all_gather(w_out, ("seq", "dp"), axis=0, tiled=True),
        lax.all_gather(w_up, ("seq", "dp"), axis=0, tiled=True),
        lax.all_gather(w_down, ("seq", "dp"), axis=0, tiled=True),
        lax.all_gather(qv_bias, ("seq", "dp"), axis=1, tiled=True),
        lax.all_gather(out_bias, ("seq", "dp"), axis=0, tiled=True),
        lax.all_gather(up_bias, ("seq", "dp"), axis=0, tiled=True),
        lax.all_gather(down_bias, ("seq", "dp"), axis=0, tiled=True),
        lax.all_gather(norm_gain, ("seq", "dp"), axis=1, tiled=True),
        lax.all_gather(norm_shift, ("seq", "dp"), axis=1, tiled=True),
    )
    qkv_full, out_full, up_full, down_full = (gathered[0], gathered[1], gathered[2], gathered[3])
    qv_shift = gathered[4].astype(jnp.float32)
    out_shift = gathered[5].astype(jnp.float32)
    up_shift = gathered[6].astype(jnp.float32)
    down_shift = gathered[7].astype(jnp.float32)
    gains = gathered[8].astype(jnp.float32)
    shifts = gathered[9].astype(jnp.float32)
    row_count = tokens.shape[1]
    model_width = tokens.shape[2]
    pair_cols = 2 * HD
    pair_count = model_width // pair_cols
    slot_rows = row_count * lax.axis_size("seq")
    factor = 1.0 / (RELAX_SCALE * math.sqrt(HD))
    valid = lengths[assign[lax.axis_index("dp")]]
    own_place = lax.axis_index("seq") * row_count + jnp.arange(row_count, dtype=jnp.int32)
    all_place = jnp.arange(slot_rows, dtype=jnp.int32)
    allowed = (all_place[None, :] <= own_place[:, None]) & (all_place[None, :] < valid)
    pair_ids = jnp.arange(pair_count, dtype=jnp.int32)
    hidden = tokens[0].astype(jnp.float32)
    normed_first, pull_first = jax.vjp(norm_rows, hidden, gains[0], shifts[0])
    normed_low = normed_first.astype(jnp.bfloat16)
    projected = jnp.dot(normed_low, qkv_full, preferred_element_type=jnp.float32)
    queries = (projected[:, :model_width] + qv_shift[0]).astype(jnp.bfloat16)
    key_own = projected[:, model_width : 2 * model_width].astype(jnp.bfloat16)
    value_own = (projected[:, 2 * model_width :] + qv_shift[1]).astype(jnp.bfloat16)
    keys, values = (
        lax.all_gather(key_own, "seq", axis=0, tiled=True),
        lax.all_gather(value_own, "seq", axis=0, tiled=True),
    )

    def columns(block, pair_index):
        return lax.dynamic_slice_in_dim(block, pair_index * pair_cols, pair_cols, 1)

    def merge_pairs(stack):
        return stack.transpose(1, 0, 2).reshape(stack.shape[1], model_width)

    def attend(pair_index):
        scores = pair_scores(columns(queries, pair_index), columns(keys, pair_index))
        row_max = jnp.max(jnp.where(allowed, scores, -jnp.inf), -1, keepdims=True)
        exp_terms = jnp.exp(jnp.where(allowed, RELAX_SCALE * (scores - row_max), -jnp.inf))
        row_total = jnp.sum(exp_terms, -1, keepdims=True)
        probs = (exp_terms / row_total).astype(jnp.bfloat16)
        mixed = jnp.einsum(
            "hqk,khd->qhd",
            probs,
            split_heads(columns(values, pair_index)),
            preferred_element_type=jnp.float32,
        )
        return (mixed.reshape(row_count, pair_cols), row_max[..., 0], row_total[..., 0])

    mixed_pairs, max_pairs, total_pairs = lax.map(attend, pair_ids)
    attended = merge_pairs(mixed_pairs).astype(jnp.bfloat16)
    branch = jnp.dot(attended, out_full, preferred_element_type=jnp.float32) + out_shift
    normed_second, pull_second = jax.vjp(norm_rows, branch, gains[1], shifts[1])
    middle = hidden + normed_second
    normed_third, pull_third = jax.vjp(norm_rows, middle, gains[2], shifts[2])
    third_low = normed_third.astype(jnp.bfloat16)
    up_pre = jnp.dot(third_low, up_full, preferred_element_type=jnp.float32) + up_shift
    activated, pull_gelu = jax.vjp(exact_gelu, up_pre)
    active_low = activated.astype(jnp.bfloat16)
    down_pre = jnp.dot(active_low, down_full, preferred_element_type=jnp.float32) + down_shift
    normed_fourth, pull_fourth = jax.vjp(norm_rows, down_pre, gains[3], shifts[3])
    output = (middle + normed_fourth).astype(jnp.bfloat16)[None]
    again = (
        lax.all_gather(w_qkv, ("seq", "dp"), axis=0, tiled=True),
        lax.all_gather(w_out, ("seq", "dp"), axis=0, tiled=True),
        lax.all_gather(w_up, ("seq", "dp"), axis=0, tiled=True),
        lax.all_gather(w_down, ("seq", "dp"), axis=0, tiled=True),
    )
    qkv_back, out_back, up_back, down_back = (again[0], again[1], again[2], again[3])
    keep_rows = (own_place < valid).astype(jnp.float32)[:, None]
    grad_out = cotangent[0].astype(jnp.float32) * keep_rows
    grad_down, grad_gain_four, grad_shift_four = pull_fourth(grad_out)
    grad_down_low = grad_down.astype(jnp.bfloat16)
    grad_w_down = contract_rows(active_low, grad_down_low)
    grad_b_down = jnp.sum(grad_down_low.astype(jnp.float32), 0)
    (grad_up,) = pull_gelu(contract_cols(grad_down_low, down_back))
    grad_up_low = grad_up.astype(jnp.bfloat16)
    grad_w_up = contract_rows(third_low, grad_up_low)
    grad_b_up = jnp.sum(grad_up_low.astype(jnp.float32), 0)
    grad_middle_part, grad_gain_three, grad_shift_three = pull_third(
        contract_cols(grad_up_low, up_back)
    )
    grad_middle = grad_out + grad_middle_part
    grad_branch, grad_gain_two, grad_shift_two = pull_second(grad_middle)
    grad_branch_low = grad_branch.astype(jnp.bfloat16)
    grad_w_out = contract_rows(attended, grad_branch_low)
    grad_b_out = jnp.sum(grad_branch_low.astype(jnp.float32), 0)
    grad_attended = contract_cols(grad_branch_low, out_back).astype(jnp.bfloat16)

    def query_side(pair_index):
        scores = pair_scores(columns(queries, pair_index), columns(keys, pair_index))
        probs = kept_probs(
            scores, allowed, max_pairs[pair_index][..., None], total_pairs[pair_index][..., None]
        )
        grad_part = columns(grad_attended, pair_index)
        grad_probs = jnp.einsum(
            "qhd,khd->hqk",
            split_heads(grad_part),
            split_heads(columns(values, pair_index)),
            preferred_element_type=jnp.float32,
        )
        delta = jnp.sum(probs * grad_probs, -1, keepdims=True)
        grad_scores = (RELAX_SCALE * probs * (grad_probs - delta)).astype(jnp.bfloat16)
        grad_query = (
            jnp.einsum(
                "hqk,khd->qhd",
                grad_scores,
                split_heads(columns(keys, pair_index)),
                preferred_element_type=jnp.float32,
            )
            * factor
        )
        return (grad_query.reshape(row_count, pair_cols), grad_scores, probs, delta)

    def both_sides(pair_index):
        grad_query, grad_scores, probs, delta = query_side(pair_index)
        grad_part = columns(grad_attended, pair_index)
        grad_key = (
            jnp.einsum(
                "hqk,qhd->khd",
                grad_scores,
                split_heads(columns(queries, pair_index)),
                preferred_element_type=jnp.float32,
            )
            * factor
        )
        grad_value = jnp.einsum(
            "hqk,qhd->khd",
            probs.astype(jnp.bfloat16),
            split_heads(grad_part),
            preferred_element_type=jnp.float32,
        )
        return (
            grad_query,
            grad_key.reshape(slot_rows, pair_cols),
            grad_value.reshape(slot_rows, pair_cols),
        )

    query_pairs, key_terms, value_terms = lax.map(both_sides, pair_ids)
    key_pairs, value_pairs = (
        lax.psum_scatter(
            key_terms.astype(jnp.bfloat16), "seq", scatter_dimension=1, tiled=True
        ).astype(jnp.float32),
        lax.psum_scatter(
            value_terms.astype(jnp.bfloat16), "seq", scatter_dimension=1, tiled=True
        ).astype(jnp.float32),
    )
    grad_q_low = merge_pairs(query_pairs).astype(jnp.bfloat16)
    grad_k_low = merge_pairs(key_pairs).astype(jnp.bfloat16)
    grad_v_low = merge_pairs(value_pairs).astype(jnp.bfloat16)
    grad_projected = jnp.concatenate([grad_q_low, grad_k_low, grad_v_low], 1)
    grad_w_qkv = contract_rows(normed_low, grad_projected)
    grad_qv = jnp.stack(
        [jnp.sum(grad_q_low.astype(jnp.float32), 0), jnp.sum(grad_v_low.astype(jnp.float32), 0)]
    )
    grad_hidden_part, grad_gain_one, grad_shift_one = pull_first(
        contract_cols(grad_projected, qkv_back)
    )
    input_grad = (grad_middle + grad_hidden_part).astype(jnp.bfloat16)[None]
    grad_gains = jnp.stack([grad_gain_one, grad_gain_two, grad_gain_three, grad_gain_four])
    grad_shifts = jnp.stack([grad_shift_one, grad_shift_two, grad_shift_three, grad_shift_four])
    owned = (
        lax.psum_scatter(grad_w_qkv, ("seq", "dp"), scatter_dimension=0, tiled=True),
        lax.psum_scatter(grad_w_out, ("seq", "dp"), scatter_dimension=0, tiled=True),
        lax.psum_scatter(grad_w_up, ("seq", "dp"), scatter_dimension=0, tiled=True),
        lax.psum_scatter(grad_w_down, ("seq", "dp"), scatter_dimension=0, tiled=True),
        lax.psum_scatter(grad_qv, ("seq", "dp"), scatter_dimension=1, tiled=True),
        lax.psum_scatter(grad_b_out, ("seq", "dp"), scatter_dimension=0, tiled=True),
        lax.psum_scatter(grad_b_up, ("seq", "dp"), scatter_dimension=0, tiled=True),
        lax.psum_scatter(grad_b_down, ("seq", "dp"), scatter_dimension=0, tiled=True),
        lax.psum_scatter(grad_gains, ("seq", "dp"), scatter_dimension=1, tiled=True),
        lax.psum_scatter(grad_shifts, ("seq", "dp"), scatter_dimension=1, tiled=True),
    )
    return (
        output,
        input_grad,
        owned[0],
        owned[4],
        owned[1],
        owned[5],
        owned[2],
        owned[6],
        owned[3],
        owned[7],
        owned[8],
        owned[9],
    )


MESH = pl.DeviceIdType.MESH


def is_small(mesh):
    return mesh.shape["seq"] == 16 and mesh.shape["dp"] == 2


def place():
    seq = lax.axis_index("seq")
    return seq // 8, (seq // 4) % 2, (seq // 2) % 2, seq % 2, lax.axis_index("dp")


def exchange_copies(scatter, src, out, send_sem, recv_sem, own_sem):
    a, b, y, c, x = place()

    def peer(k):
        return lax.rem(a + k // 2, 2), lax.rem(y + k % 2, 2)

    def device(k):
        pa, py = peer(k)
        return (pa * 8 + b * 4 + py * 2 + c, x)

    def source(k):
        pa, py = peer(k)
        return src.at[pa * 2 + py] if scatter else src.at[pa, :, py]

    def target(k):
        pa, py = peer(k)
        return out.at[pa, :, py] if scatter else out.at[pa * 2 + py]

    def copy(k, dst):
        return pltpu.make_async_remote_copy(
            src_ref=source(k), dst_ref=target(dst), send_sem=send_sem.at[k], recv_sem=recv_sem.at[k],
            device_id=device(k), device_id_type=MESH)

    def greet():
        barrier = pltpu.get_barrier_semaphore()
        for k in range(1, 4):
            pl.semaphore_signal(barrier, inc=1, device_id=device(k), device_id_type=MESH)

    def run():
        own = pltpu.make_async_copy(source(0), target(0), own_sem)
        own.start()
        pl.semaphore_wait(pltpu.get_barrier_semaphore(), 3)
        for k in (3, 2, 1):
            copy(k, 0).start()
        own.wait()
        for k in (3, 2, 1):
            copy(k, k).wait_recv()
        for k in (3, 2, 1):
            copy(k, 0).wait_send()

    return greet, run


def row_block(i, j):
    _, b, _, c, _ = place()
    return pl.ds(pl.multiple_of(lax.rem(b + i, 2) * 256 + lax.rem(c + j, 2) * 128, 128), 128)


def to_heads_kernel(rows_ref, out, src, *sems):
    greet, run = exchange_copies(True, src, out, *sems)
    greet()
    low = src.shape[2] - 128
    for g in range(4):
        values = slice(low * 2 + g * HD, low * 2 + g * HD + HD)
        for i in range(2):
            if low:
                for j in range(2):
                    src[g, i, j * 128:j * 128 + 128] = rows_ref[row_block(i, j), g * 128:g * 128 + 128]
            src[g, i, low:] = jnp.concatenate([rows_ref[row_block(i, j), values] for j in range(2)], 1)
    run()


def from_heads_kernel(heads_ref, out, got, *sems):
    greet, run = exchange_copies(False, heads_ref, got, *sems)
    greet()
    run()
    low = got.shape[2] - 128
    c = place()[3]
    for i in range(2):
        if low:
            for j in range(2):
                for g in range(4):
                    out[row_block(i, j), g * 128:g * 128 + 128] = got[g, i, j * 128:j * 128 + 128]
        for g in (0, 2):
            left, right = got[g, i, low:], got[g + 1, i, low:]
            cols = slice(low * 2 + g * HD, low * 2 + g * HD + 128)
            for j in range(2):
                lanes = slice(j * HD, j * HD + HD)
                out[row_block(i, j), cols] = jnp.concatenate([left[:, lanes], right[:, lanes]], 1)


def exchange(blocks, scatter, cid):
    vm = pl.BlockSpec(memory_space=pltpu.VMEM)
    rows = blocks.shape[-1] // 2 if scatter else blocks.shape[-2]
    shape, held = (2, 2, 2, rows, 128), (4, 2, rows, 128)
    return pl.pallas_call(
        to_heads_kernel if scatter else from_heads_kernel,
        out_shape=jax.ShapeDtypeStruct(shape if scatter else (512, rows * 2), blocks.dtype),
        in_specs=[vm], out_specs=vm,
        scratch_shapes=[pltpu.VMEM(held, blocks.dtype), pltpu.SemaphoreType.DMA((4,)), pltpu.SemaphoreType.DMA((4,)),
                        pltpu.SemaphoreType.DMA],
        compiler_params=pltpu.CompilerParams(collective_id=cid, has_side_effects=True),
        cost_estimate=pl.CostEstimate(flops=0, bytes_accessed=rows * 100000, transcendentals=0),
        name="to_heads" if scatter else "from_heads",
    )(blocks)


def dot_nt(a, b):
    return lax.dot_general(a, b, (((1,), (1,)), ((), ())), preferred_element_type=jnp.float32)


def dot_nn(a, b):
    return jnp.dot(a, b, preferred_element_type=jnp.float32)


BQ = 256
MASKED = -1e30


def load_heads(valid, packed, q_ref, k_ref):
    rows = q_ref.shape[0]
    qk = packed[:, :256].reshape(rows, 128)
    kq = jnp.concatenate([qk[:, 64:], qk[:, :64]], axis=1)
    lane = lax.broadcasted_iota(jnp.int32, (rows, 128), 1)
    spot = lax.broadcasted_iota(jnp.int32, (rows, 128), 0)
    past = jnp.where(spot < valid, 0.0, MASKED)
    q_ref[...] = jnp.where(lane < 64, qk.astype(jnp.float32), jnp.where(lane == 64, 1.0, 0.0)).astype(jnp.bfloat16)
    k_ref[...] = jnp.where(lane < 64, kq.astype(jnp.float32), jnp.where(lane == 64, past, 0.0)).astype(jnp.bfloat16)


def unpack_rows(halves):
    n = halves.shape[0]
    return jnp.concatenate([halves[:, :, :64], halves[:, :, 64:]], axis=1).reshape(n * 256, 64)


def block_probs(q_ref, k_ref, i):
    n = (i + 1) * BQ
    scores = dot_nt(k_ref[:n], q_ref[i * BQ:n])
    key = lax.broadcasted_iota(jnp.int32, (BQ, BQ), 0)
    query = lax.broadcasted_iota(jnp.int32, (BQ, BQ), 1)
    corner = jnp.where(key <= query, scores[n - BQ:], MASKED)
    scores = jnp.concatenate([scores[:n - BQ], corner], axis=0) if i else corner
    top = jnp.max(scores, axis=0, keepdims=True)
    terms = jnp.exp((scores - top) * 0.125)
    return terms, 1.0 / jnp.sum(terms, axis=0, keepdims=True)


def attend_kernel(valid_ref, packed, out_ref, q_ref, k_ref, vt_ref):
    load_heads(valid_ref[0], packed, q_ref, k_ref)
    unit = jnp.where(
        lax.broadcasted_iota(jnp.int32, (64, 64), 0) == lax.broadcasted_iota(jnp.int32, (64, 64), 1), 1.0, 0.0
    ).astype(jnp.bfloat16)
    vt_ref[...] = dot_nt(unit, unpack_rows(packed[:, 256:])).astype(jnp.bfloat16)
    for i in range(q_ref.shape[0] // BQ):
        n = (i + 1) * BQ
        terms, scale = block_probs(q_ref, k_ref, i)
        probs = (terms * scale).astype(jnp.bfloat16)
        mixed = dot_nn(vt_ref[:, :n], probs).T
        out_ref[i] = jnp.concatenate([mixed[:128], mixed[128:]], axis=1).astype(jnp.bfloat16)


def attend_back_kernel(valid_ref, packed, grad, out_ref, q_ref, k_ref, v_ref, g_ref, kt_ref, dk_ref, dv_ref):
    load_heads(valid_ref[0], packed, q_ref, k_ref)
    v_ref[...] = unpack_rows(packed[:, 256:])
    g_ref[...] = unpack_rows(grad[...])
    unit = jnp.where(
        lax.broadcasted_iota(jnp.int32, (64, 128), 0) == lax.broadcasted_iota(jnp.int32, (64, 128), 1), 1.0, 0.0
    ).astype(jnp.bfloat16)
    kt_ref[...] = dot_nt(unit, k_ref[...]).astype(jnp.bfloat16)
    dk_ref[...] = jnp.zeros_like(dk_ref)
    dv_ref[...] = jnp.zeros_like(dv_ref)
    blocks = q_ref.shape[0] // BQ
    for i in range(blocks):
        n = (i + 1) * BQ
        terms, scale = block_probs(q_ref, k_ref, i)
        probs = terms * scale
        grad_probs = dot_nt(v_ref[:n], g_ref[i * BQ:n])
        delta = jnp.sum(probs * grad_probs, axis=0, keepdims=True)
        grad_scores = (probs * (grad_probs - delta)).astype(jnp.bfloat16)
        grad_query = dot_nn(kt_ref[:, :n], grad_scores).T * 0.125
        out_ref[i, :256, :64] = grad_query.astype(jnp.bfloat16)
        dk_ref[:n] += dot_nn(grad_scores, q_ref[i * BQ:n])
        dv_ref[:n] += dot_nn(probs.astype(jnp.bfloat16), g_ref[i * BQ:n])
    for i in range(blocks):
        rows = slice(i * BQ, (i + 1) * BQ)
        out_ref[i, :256, 64:] = (dk_ref[rows, :64] * 0.125).astype(jnp.bfloat16)
        value = dv_ref[rows].astype(jnp.bfloat16)
        out_ref[i, 256:] = jnp.concatenate([value[:128], value[128:]], axis=1)


def attend(valid, packed):
    rows = packed.shape[0] * 256
    vm = pl.BlockSpec(memory_space=pltpu.VMEM)
    return pl.pallas_call(
        attend_kernel,
        out_shape=jax.ShapeDtypeStruct((packed.shape[0], 128, 128), jnp.bfloat16),
        in_specs=[pl.BlockSpec(memory_space=pltpu.SMEM), vm], out_specs=vm,
        scratch_shapes=[pltpu.VMEM((rows, 128), jnp.bfloat16)] * 2 + [pltpu.VMEM((64, rows), jnp.bfloat16)],
        compiler_params=pltpu.CompilerParams(vmem_limit_bytes=48 << 20),
        name="attend",
    )(valid, packed)


def attend_back(valid, packed, grad):
    rows = packed.shape[0] * 256
    vm = pl.BlockSpec(memory_space=pltpu.VMEM)
    return pl.pallas_call(
        attend_back_kernel,
        out_shape=jax.ShapeDtypeStruct(packed.shape, jnp.bfloat16),
        in_specs=[pl.BlockSpec(memory_space=pltpu.SMEM), vm, vm], out_specs=vm,
        scratch_shapes=[pltpu.VMEM((rows, 128), jnp.bfloat16)] * 2 + [pltpu.VMEM((rows, 64), jnp.bfloat16)] * 2
        + [pltpu.VMEM((64, rows), jnp.bfloat16), pltpu.VMEM((rows, 128), jnp.float32), pltpu.VMEM((rows, 64), jnp.float32)],
        compiler_params=pltpu.CompilerParams(vmem_limit_bytes=48 << 20),
        name="attend_back",
    )(valid, packed, grad)


def flip(bits, block):
    return lax.ppermute(block, "seq", [(s, s ^ bits) for s in range(16)])


flip_a, flip_b, flip_y, flip_core, flip_far = (functools.partial(flip, bits) for bits in (8, 4, 2, 1, 5))


def flip_x(block):
    return lax.ppermute(block, "dp", [(0, 1), (1, 0)])


def after(value, *others):
    return lax.optimization_barrier((value,) + others)[0]


def pick(block, index, axis, keepdims=False):
    return lax.dynamic_index_in_dim(block, index, axis, keepdims=keepdims)


def swap_if(flag, block, axis):
    return jnp.where(flag == 0, block, lax.rev(block, (axis,)))


def sort_ranks(block, b, c):
    return swap_if(c, swap_if(b, block, 0), 1)


def to_ranks(block, b, c):
    mine = pick(pick(block, b, 0), c, 0)
    core = flip_core(pick(pick(block, b, 0), 1 - c, 0))
    near = flip_b(pick(pick(block, 1 - b, 0), c, 0))
    far = flip_far(pick(pick(block, 1 - b, 0), 1 - c, 0))
    return jnp.stack([jnp.stack([mine, core]), jnp.stack([near, far])])


def gather_rows(block):
    core, near = flip_core(block), flip_b(block)
    return jnp.concatenate([block, core, near, flip_core(near)], 0)


def scatter_rows(part):
    part = part.reshape(2, 2, part.shape[0] // 4, part.shape[1])
    far = part[1, 0] + flip_core(part[1, 1])
    near = part[0, 0] + flip_core(part[0, 1])
    return near + flip_b(far.astype(jnp.bfloat16)).astype(jnp.float32)


def cube_start(block):
    return jnp.stack([block, flip_a(block)])


def cube_one(flip_one, block):
    return jnp.concatenate([block, flip_one(block)], 0)


def arrange_kernel(count, spot_ref, *refs):
    for k in range(count):
        block, out = refs[k], refs[count + k]
        if len(out.shape) == 7:
            for i in range(2):
                for j in range(2):
                    out[0, i, 0, j, 0] = block[0, i, j]
        else:
            out[0, 0, 0] = block[0]


def arrange(spot, blocks):
    def coords(i, r, y_first):
        second, first, a = i // 4, (i // 2) % 2, i % 2
        y, x = (first, second) if y_first else (second, first)
        return lax.rem(r[0] + a, 2), lax.rem(r[1] + y, 2), lax.rem(r[2] + x, 2)

    def specs(block, y_first):
        shape = block.shape
        if len(shape) == 5:
            def out_place(i, r):
                a, y, x = coords(i, r, y_first)
                return a, 0, y, 0, x, 0, 0
            return (pl.BlockSpec((1,) + shape[1:], lambda i, r: (i, 0, 0, 0, 0)),
                    pl.BlockSpec((1, 2, 1, 2, 1) + shape[3:], out_place),
                    jax.ShapeDtypeStruct((2,) * 5 + shape[3:], block.dtype))

        def out_place(i, r):
            return coords(i, r, y_first) + (0, 0)
        return (pl.BlockSpec((1,) + shape[1:], lambda i, r: (i, 0, 0)),
                pl.BlockSpec((1, 1, 1) + shape[1:], out_place),
                jax.ShapeDtypeStruct((2, 2, 2) + shape[1:], block.dtype))

    made = [specs(*entry) for entry in blocks]
    return pl.pallas_call(
        functools.partial(arrange_kernel, len(blocks)),
        out_shape=tuple(m[2] for m in made),
        grid_spec=pltpu.PrefetchScalarGridSpec(
            num_scalar_prefetch=1, grid=(8,), in_specs=[m[0] for m in made], out_specs=tuple(m[1] for m in made)),
        compiler_params=pltpu.CompilerParams(vmem_limit_bytes=32 << 20),
        cost_estimate=pl.CostEstimate(flops=0, bytes_accessed=8 << 20, transcendentals=0),
        name="arrange",
    )(spot, *[entry[0] for entry in blocks])


def add_low(mine, other):
    return (mine.astype(jnp.float32) + other.astype(jnp.float32)).astype(jnp.bfloat16)


def fold(terms, flip_one, index, axis):
    return add_low(pick(terms, index, axis, True), flip_one(pick(terms, 1 - index, axis, True)))


def reduce_kernel(q_ref, o_ref, u_ref, *refs):
    vec_refs, (out_q, ro, out_u, vec, rq, gu, r1q, t2q, r2q, t3q, r3q, fq, gq, r1o, t2o, r2o, t3o, r3o,
               run, got, send_sem, recv_sem) = refs[:12], refs[12:]
    a, b, y, c, x = place()
    f32, bf16 = jnp.float32, jnp.bfloat16
    barrier = pltpu.get_barrier_semaphore()

    def at(pa, pb, py, pc, px):
        return (pa * 8 + pb * 4 + py * 2 + pc, px)

    to_x, to_y, to_a = at(a, b, y, c, 1 - x), at(a, b, 1 - y, c, x), at(1 - a, b, y, c, x)
    ranks = [(lax.rem(b + k // 2, 2), lax.rem(c + k % 2, 2)) for k in range(4)]
    to_rank = [at(a, ranks[k][0], y, ranks[k][1], x) for k in range(4)]
    to_b, to_c = to_rank[2], to_rank[1]
    for dev in [to_x, to_y, to_a] + to_rank[1:]:
        pl.semaphore_signal(barrier, inc=1, device_id=dev, device_id_type=MESH)
    for pb in range(2):
        for j in range(4):
            for row, cols in ((0, slice(j * 128, j * 128 + HD)), (1, slice(512 + j * HD, 512 + j * HD + HD))):
                piece = vec_refs[0][:, cols]
                pair = [jnp.where((b == pb) & (c == pc), piece, 0.0) for pc in range(2)]
                h = head_of(j // 2, pb, j % 2, 0) * HD
                run[0, row:row + 1, h:h + 128] = jnp.concatenate(pair, 1)
            for pc in range(2):
                col = head_of(j // 2, pb, j % 2, pc) * 256
                piece = vec_refs[1][:, j * 256:j * 256 + 256]
                run[0, 12 + col // 1024:13 + col // 1024, col % 1024:col % 1024 + 256] = jnp.where(
                    (b == pb) & (c == pc), piece, 0.0)
    for k in range(2, 12):
        run[0, k:k + 1] = vec_refs[k][...]
    pl.semaphore_wait(barrier, 6)

    made = []

    def remote(src, dst, dev):
        k = len(made)
        made.append(pltpu.make_async_remote_copy(
            src_ref=src, dst_ref=dst, send_sem=send_sem.at[k], recv_sem=recv_sem.at[k],
            device_id=dev, device_id_type=MESH))
        return made[-1]

    def low(*values):
        return sum(v.astype(f32) for v in values)

    places = [1 - a, a]
    halves = [slice(0, 512), slice(512, 1024)]
    lateral = [(to_x, to_y), (to_y, to_x)]

    q1, q2, o1, o2 = {}, {}, {}, {}
    for i in range(2):
        for s in range(2):
            p = places[i]
            q1[s, i] = remote(q_ref.at[p, 0, :, :, 1 - x] if s == 0 else q_ref.at[p, 1, 1 - y], r1q.at[s, i], lateral[s][0])
            o1[s, i] = remote(o_ref.at[p, :, 1 - x, :, halves[0]] if s == 0 else o_ref.at[p, 1 - y, :, :, halves[1]],
                              r1o.at[s, i], lateral[s][0])
            q2[s, i] = remote(t2q.at[s, i], r2q.at[s, i], lateral[s][1])
            o2[s, i] = remote(t2o.at[s, i], r2o.at[s, i], lateral[s][1])
    q3 = [remote(t3q.at[s], r3q.at[s], to_a) for s in range(2)]
    o3 = [remote(t3o.at[s], r3o.at[s], to_a) for s in range(2)]
    qr = [remote(fq.at[ranks[k][0], ranks[k][1]], gq.at[k - 1], to_rank[k]) for k in range(1, 4)]
    ur = [remote(u_ref.at[ranks[k][0], ranks[k][1]], gu.at[b, c], to_rank[k]) for k in range(1, 4)]
    vs = [remote(run.at[k], got.at[k], dev) for k, dev in enumerate((to_x, to_y, to_a, to_b, to_c))]

    def next_sum(k):
        vs[k].wait_recv()
        if k < 4:
            run[k + 1] = run[k] + got[k]
            vs[k + 1].start()
        else:
            vec[...] = run[k] + got[k]

    vs[0].start()
    for i in range(2):
        for s in range(2):
            q1[s, i].start()
            o1[s, i].start()
    for k in (3, 2, 1):
        ur[k - 1].start()

    def q_terms(s, i, far):
        p = places[i]
        if s == 0:
            v = 1 - y if far else y
            return q_ref[p, 0, v, :, x], r1q[0, i, v]
        v = 1 - x if far else x
        return q_ref[p, 1, y, :, v], r1q[1, i, :, v]

    def o_terms(s, i, far):
        p = places[i]
        if s == 0:
            v = 1 - y if far else y
            return o_ref[p, v, x, :, halves[0]], r1o[0, i, v]
        v = 1 - x if far else x
        return o_ref[p, y, v, :, halves[1]], r1o[1, i, v]

    for i in range(2):
        for s in range(2):
            q1[s, i].wait_recv()
            t2q[s, i] = low(*q_terms(s, i, True)).astype(bf16)
            q2[s, i].start()
            o1[s, i].wait_recv()
            t2o[s, i] = low(*o_terms(s, i, True)).astype(bf16)
            o2[s, i].start()
        if i == 0:
            next_sum(0)
            for s in range(2):
                q2[s, 0].wait_recv()
                t3q[s] = low(*q_terms(s, 0, False), r2q[s, 0]).astype(bf16)
                q3[s].start()
                o2[s, 0].wait_recv()
                t3o[s] = low(*o_terms(s, 0, False), r2o[s, 0]).astype(bf16)
                o3[s].start()
    next_sum(1)
    for s in range(2):
        q2[s, 1].wait_recv()
        o2[s, 1].wait_recv()
        q3[s].wait_recv()
        total = low(*q_terms(s, 1, False), r2q[s, 1], r3q[s])
        fq[s] = total.astype(bf16)
        for j in range(2):
            @pl.when((b == s) & (c == j))
            def _():
                rq[s, j] = total[j]
        o3[s].wait_recv()
        ro[:, halves[s]] = low(*o_terms(s, 1, False), r2o[s, 1], r3o[s])
    for k in (3, 2, 1):
        qr[k - 1].start()
    next_sum(2)
    gu[b, c] = u_ref[b, c]
    for k in (1, 2, 3):
        ur[k - 1].wait_recv()
    next_sum(3)
    for k in (1, 2, 3):
        pb, pc = ranks[k]
        qr[k - 1].wait_recv()
        rq[pb, pc] = gq[k - 1].astype(f32)
    for pb in range(2):
        for j in range(4):
            zero, one = rq[pb, 0], rq[pb, 1]
            h = head_of(j // 2, pb, j % 2, 0) * HD
            q, k = slice(j * 128, j * 128 + HD), slice(j * 128 + HD, j * 128 + 128)
            v = slice(512 + j * HD, 512 + j * HD + HD)
            for t, cols in enumerate((q, k, v)):
                out_q[:, t * 1024 + h:t * 1024 + h + 128] = jnp.concatenate([zero[:, cols], one[:, cols]], 1)
            for pc in range(2):
                col = head_of(j // 2, pb, j % 2, pc) * 256
                out_u[:, col:col + 256] = gu[pb, pc, :, j * 256:j * 256 + 256].astype(f32)
    next_sum(4)
    for copy in made:
        copy.wait_send()


def reduce_all(gw_qkv, gw_out, up_sum, vectors, cid):
    f32, bf16 = jnp.float32, jnp.bfloat16
    V = pltpu.VMEM
    vm = pl.BlockSpec(memory_space=V)
    S = jax.ShapeDtypeStruct
    q, o, u = gw_qkv.shape[5:], (gw_out.shape[3], 512), up_sum.shape
    scratch = [
        V((2, 2) + q, f32), V(u, bf16),
        V((2, 2, 2, 2) + q, bf16), V((2, 2, 2) + q, bf16), V((2, 2, 2) + q, bf16), V((2, 2) + q, bf16), V((2, 2) + q, bf16),
        V((2, 2) + q, bf16), V((3,) + q, bf16),
        V((2, 2, 2) + o, bf16), V((2, 2) + o, bf16), V((2, 2) + o, bf16), V((2,) + o, bf16), V((2,) + o, bf16),
        V((5, 16, 1024), f32), V((5, 16, 1024), f32),
        pltpu.SemaphoreType.DMA((32,)), pltpu.SemaphoreType.DMA((32,))]
    return pl.pallas_call(
        reduce_kernel,
        out_shape=(S((q[0], 4 * q[1]), f32), S((o[0], 1024), f32), S((u[2], 4 * u[3]), f32), S((16, 1024), f32)),
        in_specs=[vm] * 15, out_specs=(vm,) * 4, scratch_shapes=scratch,
        compiler_params=pltpu.CompilerParams(collective_id=cid, has_side_effects=True, vmem_limit_bytes=40 << 20),
        name="reduce_all",
    )(gw_qkv, gw_out, up_sum, *vectors)


def qk_columns(head):
    return slice(head * HD, head * HD + HD), slice(1024 + head * HD, 1024 + head * HD + HD), slice(2048 + head * HD, 2048 + head * HD + HD)


def head_of(a, b, y, c):
    return a * 8 + b * 4 + y * 2 + c


def start_kernel(q_in, u_in, o_in, t_in, v_in, wq, wo, up, rows, vec, q_src, u_src, send_sem, recv_sem, own_sem):
    a, b, y, c, x = place()
    barrier = pltpu.get_barrier_semaphore()

    def at(pa, pb, py, pc, px):
        return (pa * 8 + pb * 4 + py * 2 + pc, px)

    to_x, to_y, to_a = at(a, b, y, c, 1 - x), at(a, b, 1 - y, c, x), at(1 - a, b, y, c, x)
    ranks = [(lax.rem(b + k // 2, 2), lax.rem(c + k % 2, 2)) for k in range(4)]
    to_rank = [at(a, pb, y, pc, x) for pb, pc in ranks]
    for dev in [to_x, to_y, to_a] + to_rank[1:]:
        pl.semaphore_signal(barrier, inc=1, device_id=dev, device_id_type=MESH)

    for pb in range(2):
        for pc in range(2):
            for j in range(4):
                q, k, v = qk_columns(head_of(j // 2, pb, j % 2, pc))
                q_src[pb, pc, :, j * 128:j * 128 + 128] = jnp.concatenate([q_in[:, q], q_in[:, k]], 1)
            for j in range(2):
                v0 = qk_columns(head_of(j, pb, 0, pc))[2]
                v1 = qk_columns(head_of(j, pb, 1, pc))[2]
                q_src[pb, pc, :, 512 + j * 128:640 + j * 128] = jnp.concatenate([q_in[:, v0], q_in[:, v1]], 1)
            for j in range(4):
                col = (head_of(j // 2, pb, j % 2, pc)) * 256
                u_src[pb, pc, :, j * 256:j * 256 + 256] = u_in[:, col:col + 256]
    own = [pltpu.make_async_copy(src, dst, own_sem.at[k]) for k, (src, dst) in enumerate((
        (q_src.at[b, c], wq.at[a, b, y, c, x]), (u_src.at[b, c], up.at[0, b, c]), (o_in, wo.at[a, y, x]),
        (t_in, rows.at[0]), (v_in, vec.at[a, b, y, c, x])))]
    for copy in own:
        copy.start()
    pl.semaphore_wait(barrier, 6)

    made = []

    def remote(src, dst, dev):
        k = len(made)
        made.append(pltpu.make_async_remote_copy(
            src_ref=src, dst_ref=dst, send_sem=send_sem.at[k], recv_sem=recv_sem.at[k],
            device_id=dev, device_id_type=MESH))
        return made[-1]

    places = [a, 1 - a]
    halves = [slice(0, 512), slice(512, 1024)]
    lateral = [(to_y, to_x), (to_x, to_y)]

    def same(ref, dev):
        return remote(ref, ref, dev)

    q_rank = [remote(q_src.at[ranks[k][0], ranks[k][1]], wq.at[a, b, y, c, x], to_rank[k]) for k in range(1, 4)]
    u_rank = [remote(u_src.at[ranks[k][0], ranks[k][1]], up.at[0, b, c], to_rank[k]) for k in range(1, 4)]
    v_rank = [remote(v_in, vec.at[a, b, y, c, x], to_rank[k]) for k in range(1, 4)]
    t_core, t_near = remote(t_in, rows.at[1], to_rank[1]), remote(t_in, rows.at[2], to_rank[2])
    t_far = remote(rows.at[2], rows.at[3], to_rank[1])
    u_cube = remote(up.at[0], up.at[1], to_a)
    v_cube = [same(vec.at[a, :, y, :, x], to_a), same(vec.at[:, :, y, :, x], to_y), same(vec.at[:, :, :, :, x], to_x)]
    q_cube = [same(wq.at[a, s, y, :, x], to_a) for s in range(2)]
    o_cube = [remote(o_in.at[:, halves[s]], wo.at[a, y, x, :, halves[s]], to_a) for s in range(2)]
    q_side, o_side = {}, {}
    for i in range(2):
        for s in range(2):
            one, two = lateral[s]
            oy, ox = (1 - y, x) if s == 0 else (y, 1 - x)
            p = places[i]
            mine, theirs = wq.at[p, s, y, :, x], wq.at[p, s, oy, :, ox]
            q_side[s, i] = (same(mine, one), same(mine, two), same(theirs, two))
            mine, theirs = wo.at[p, y, x, :, halves[s]], wo.at[p, oy, ox, :, halves[s]]
            first = o_in.at[:, halves[s]] if i == 0 else mine
            o_side[s, i] = (remote(first, mine, one), remote(first, mine, two), same(theirs, two))

    for k in (2, 1, 0):
        q_rank[k].start()
        v_rank[k].start()
    for s in range(2):
        o_cube[s].start()
        o_side[s, 0][0].start()
        o_side[s, 0][1].start()
    t_near.start()
    t_core.start()
    own[0].wait()
    for copy in q_rank:
        copy.wait_recv()
    for s in range(2):
        q_cube[s].start()
        q_side[s, 0][0].start()
        q_side[s, 0][1].start()
    own[4].wait()
    for copy in v_rank:
        copy.wait_recv()
    v_cube[0].start()
    for k in (2, 1, 0):
        u_rank[k].start()
    for s in range(2):
        o_side[s, 0][0].wait_recv()
        o_side[s, 0][2].start()
    for s in range(2):
        o_cube[s].wait_recv()
        o_side[s, 1][0].start()
        o_side[s, 1][1].start()
    t_near.wait_recv()
    t_far.start()
    for s in range(2):
        q_side[s, 0][0].wait_recv()
        q_side[s, 0][2].start()
    for s in range(2):
        q_cube[s].wait_recv()
        q_side[s, 1][0].start()
        q_side[s, 1][1].start()
    v_cube[0].wait_recv()
    v_cube[1].start()
    own[1].wait()
    for copy in u_rank:
        copy.wait_recv()
    u_cube.start()
    for s in range(2):
        o_side[s, 1][0].wait_recv()
        o_side[s, 1][2].start()
    v_cube[1].wait_recv()
    v_cube[2].start()
    for s in range(2):
        q_side[s, 1][0].wait_recv()
        q_side[s, 1][2].start()
    v_cube[2].wait_recv()
    t_core.wait_recv()
    t_far.wait_recv()
    for i in range(2):
        for s in range(2):
            for k in (1, 2):
                q_side[s, i][k].wait_recv()
                o_side[s, i][k].wait_recv()
    u_cube.wait_recv()
    own[2].wait()
    own[3].wait()
    for copy in made:
        copy.wait_send()


def start_gather(w_qkv, w_up, w_out, tokens, vectors, cid):
    bf16 = jnp.bfloat16
    S = lambda *shape: jax.ShapeDtypeStruct(shape, bf16)
    vm, anywhere = pl.BlockSpec(memory_space=pltpu.VMEM), pl.BlockSpec(memory_space=pl.ANY)
    return pl.pallas_call(
        start_kernel,
        out_shape=(S(2, 2, 2, 2, 2, 32, 768), S(2, 2, 2, 32, 1024), S(2, 2, 2, 32, 1024), S(4, 128, 1024),
                   S(2, 2, 2, 2, 2, 16, 128)),
        in_specs=[vm] * 5, out_specs=(anywhere,) * 5,
        scratch_shapes=[
            pltpu.VMEM((2, 2, 32, 768), bf16), pltpu.VMEM((2, 2, 32, 1024), bf16),
            pltpu.SemaphoreType.DMA((48,)), pltpu.SemaphoreType.DMA((48,)), pltpu.SemaphoreType.DMA((5,))],
        compiler_params=pltpu.CompilerParams(collective_id=cid, has_side_effects=True, vmem_limit_bytes=32 << 20),
        cost_estimate=pl.CostEstimate(flops=0, bytes_accessed=100 << 20, transcendentals=0),
        name="start_gather",
    )(w_qkv, w_up, w_out, tokens, vectors)


def fast_body(tokens, cotangent, lengths, assign, w_qkv, qv_bias, w_out, out_bias, w_up, up_bias, w_down, down_bias,
              norm_gain, norm_shift):
    bf16, f32 = jnp.bfloat16, jnp.float32
    a, b, y, c, x = place()
    spot = jnp.stack([a, y, x]).astype(jnp.int32)
    width = tokens.shape[2]
    valid = lengths[assign[x]].astype(jnp.int32)

    small = jnp.concatenate([qv_bias, out_bias[None], down_bias[None], norm_gain, norm_shift], 0)
    small = jnp.concatenate([jnp.pad(small, ((0, 0), (0, 96))), up_bias[None], jnp.zeros((3, 128), bf16)], 0)
    wqkv, wo, up_one, rows, small = start_gather(w_qkv, w_up, w_out, tokens[0], small, 6)
    wqkv, wo, rows = wqkv.reshape(width, 768), wo.reshape(256, width), rows.reshape(512, width)
    down_one = cube_start(after(w_down, wqkv))

    vectors = small[..., :12, :32].reshape(32, 12, 32).transpose(1, 0, 2).reshape(12, width).astype(f32)
    qv_half = pick(pick(vectors[:2].reshape(2, 2, 2, 2, 2, HD), b, 2), c, 3).reshape(2, 4, HD)
    qk_shift = jnp.concatenate([qv_half[0], jnp.zeros((4, HD), f32)], 1).reshape(512)
    v_shift = qv_half[1].reshape(256)
    row_of = lambda k: vectors[k:k + 1]
    out_full, down_full = row_of(2), row_of(3)
    gains, shifts = [row_of(4 + k) for k in range(4)], [row_of(8 + k) for k in range(4)]
    up_shift = pick(pick(small[..., 12, :], b, 1), c, 2).reshape(1024).astype(f32)

    hidden = tokens[0].astype(f32)
    first = norm_rows(rows.astype(f32), gains[0], shifts[0]).astype(bf16)
    up_two = cube_one(flip_x, up_one)
    projected = (dot_nn(first, wqkv) + jnp.concatenate([qk_shift, v_shift])).astype(bf16)
    packed = exchange(after(projected, up_two, down_one), True, 1).reshape(8, 384, 128)
    down_two = cube_one(flip_x, down_one)
    up_half = flip_y(after(up_two, packed)[:, 0])
    attended = attend(valid[None], packed).reshape(2, 2, 2, 128, 128)
    attended = exchange(after(attended, down_two, up_half), False, 2)
    up_all = jnp.concatenate([up_two, jnp.stack([up_half, flip_y(after(up_two, attended)[:, 1])], 1)], 0)
    down_all = cube_one(flip_y, after(down_two, attended))
    branch = scatter_rows(dot_nn(attended, wo)) + out_full
    second, pull_second = jax.vjp(norm_rows, branch, gains[1], shifts[1])
    middle = hidden + second
    third, pull_third = jax.vjp(norm_rows, middle, gains[2], shifts[2])
    third = gather_rows(third.astype(bf16))
    wu = arrange(spot, [(up_all, False)])[0].reshape(width, 1024)
    up_pre = dot_nn(third, wu) + up_shift
    active, pull_gelu = jax.vjp(exact_gelu, up_pre)
    active = active.astype(bf16)
    wd = arrange(spot, [(after(down_all, up_pre), False)])[0].reshape(1024, width)
    down_pre = scatter_rows(dot_nn(active, wd)) + down_full
    fourth, pull_fourth = jax.vjp(norm_rows, down_pre, gains[3], shifts[3])
    output = (middle + fourth).astype(bf16)

    own_spot = lax.axis_index("seq") * 128 + jnp.arange(128, dtype=jnp.int32)
    grad_out = cotangent[0].astype(f32) * (own_spot < valid).astype(f32)[:, None]
    grad_down, gain4, shift4 = pull_fourth(grad_out)
    grad_down = grad_down.astype(bf16)
    down_rows = gather_rows(grad_down)
    gw_down = contract_rows(active, down_rows).astype(bf16).reshape(2, 2, 2, 128, width)
    down_term = flip_y(pick(gw_down, 1 - y, 1, True))
    (grad_up,) = pull_gelu(dot_nt(after(down_rows, gw_down), wd))
    grad_up = grad_up.astype(bf16)
    gw_up = contract_rows(third, grad_up).astype(bf16).reshape(2, 2, 2, 2, 2, 32, 1024)
    up_term = flip_x(pick(gw_up, 1 - x, 4, True))
    part, gain3, shift3 = pull_third(scatter_rows(dot_nt(after(grad_up, gw_up), wu)))
    grad_middle = grad_out + part
    grad_branch, gain2, shift2 = pull_second(grad_middle)
    grad_branch = grad_branch.astype(bf16)
    branch_rows = gather_rows(grad_branch)
    grad_att = dot_nt(branch_rows, wo).astype(bf16)
    down_sum = add_low(pick(gw_down, y, 1, True), down_term)
    down_term = flip_x(pick(down_sum, 1 - x, 2, True))
    grad_packed = exchange(after(grad_att, down_sum), True, 3).reshape(8, 128, 128)
    up_sum = add_low(pick(gw_up, x, 4, True), after(up_term, grad_packed))
    up_term = flip_y(pick(up_sum, 1 - y, 2, True))
    down_sum = add_low(pick(down_sum, x, 2, True), after(down_term, grad_packed))
    down_term = flip_a(pick(down_sum, 1 - a, 0))
    back = attend_back(valid[None], packed, grad_packed)

    up_sum = add_low(pick(up_sum, y, 2, True), up_term)
    gw_out = contract_rows(attended, branch_rows).astype(bf16).reshape(2, 2, 2, 32, width)
    grad_qkv = exchange(after(back, up_sum, down_term).reshape(2, 2, 2, 384, 128), False, 4)
    up_term = flip_a(pick(after(up_sum, grad_qkv), 1 - a, 0))
    gw_qkv = contract_rows(first, grad_qkv).astype(bf16).reshape(2, 2, 2, 2, 2, 32, 768)
    _, pull_first = jax.vjp(norm_rows, hidden, gains[0], shifts[0])
    part, gain1, shift1 = pull_first(scatter_rows(dot_nt(grad_qkv, wqkv)))
    input_grad = (grad_middle + part).astype(bf16)

    def sums(block):
        return jnp.sum(block.astype(f32), 0, keepdims=True)

    vectors = [sums(grad_qkv), sums(grad_up), sums(grad_branch), sums(grad_down),
               gain1, gain2, gain3, gain4, shift1, shift2, shift3, shift4]
    up_sum = (pick(up_sum, a, 0).astype(f32) + up_term.astype(f32)).astype(bf16).reshape(2, 2, 32, 1024)
    r_qkv, r_out, r_up, vectors = reduce_all(gw_qkv, gw_out, up_sum, vectors, 5)
    r_down = (pick(down_sum, a, 0).astype(f32) + down_term.astype(f32)).reshape(128, width)
    index = lax.axis_index("seq") * 2 + x
    small_up = lax.dynamic_slice(vectors, (12 + index // 8, index % 8 * 128), (1, 128)).reshape(128)
    vectors = lax.dynamic_slice(vectors, (0, index * 32), (12, 32))

    return (
        output[None], input_grad[None], r_qkv, vectors[:2], r_out,
        vectors[2], r_up, small_up, r_down, vectors[3], vectors[4:8], vectors[8:12])


def solution(mesh):
    return jax.shard_map(
        fast_body if is_small(mesh) else body,
        mesh=mesh,
        in_specs=(
            P("dp", "seq", None),
            P("dp", "seq", None),
            P(),
            P(),
            P(("seq", "dp"), None),
            P(None, ("seq", "dp")),
            P(("seq", "dp"), None),
            P(("seq", "dp")),
            P(("seq", "dp"), None),
            P(("seq", "dp")),
            P(("seq", "dp"), None),
            P(("seq", "dp")),
            P(None, ("seq", "dp")),
            P(None, ("seq", "dp")),
        ),
        out_specs=(
            P("dp", "seq", None),
            P("dp", "seq", None),
            P(("seq", "dp"), None),
            P(None, ("seq", "dp")),
            P(("seq", "dp"), None),
            P(("seq", "dp")),
            P(("seq", "dp"), None),
            P(("seq", "dp")),
            P(("seq", "dp"), None),
            P(("seq", "dp")),
            P(None, ("seq", "dp")),
            P(None, ("seq", "dp")),
        ),
        check_vma=False,
    )
```

```python
import functools
import math

import jax
import jax.numpy as jnp
from jax import lax
from jax.experimental import pallas as pl
from jax.experimental.pallas import tpu as pltpu
from jax.sharding import PartitionSpec as P


HD = 64


RELAX_SCALE = 32.0
NORM_EPSILON = 1e-05


def norm_rows(values, gain, shift):
    center = values - jnp.mean(values, -1, keepdims=True)
    spread = jnp.mean(center * center, -1, keepdims=True)
    return center * lax.rsqrt(spread + NORM_EPSILON) * gain + shift


def exact_gelu(values):
    return jax.nn.gelu(values, approximate=False)


def contract_rows(left, right):
    return lax.dot_general(
        left, right, (((0,), (0,)), ((), ())), preferred_element_type=jnp.float32
    )


def contract_cols(left, right):
    return lax.dot_general(
        left, right, (((1,), (1,)), ((), ())), preferred_element_type=jnp.float32
    )


def split_heads(block):
    return block.reshape(block.shape[0], 2, HD)


def pair_scores(query_part, key_part):
    factor = 1.0 / (RELAX_SCALE * math.sqrt(HD))
    return (
        jnp.einsum(
            "qhd,khd->hqk",
            split_heads(query_part),
            split_heads(key_part),
            preferred_element_type=jnp.float32,
        )
        * factor
    )


def kept_probs(scores, allowed, row_max, row_total):
    exp_terms = jnp.exp(jnp.where(allowed, RELAX_SCALE * (scores - row_max), -jnp.inf))
    return exp_terms / row_total


def body(
    tokens,
    cotangent,
    lengths,
    assign,
    w_qkv,
    qv_bias,
    w_out,
    out_bias,
    w_up,
    up_bias,
    w_down,
    down_bias,
    norm_gain,
    norm_shift,
):
    gathered = (
        lax.all_gather(w_qkv, ("seq", "dp"), axis=0, tiled=True),
        lax.all_gather(w_out, ("seq", "dp"), axis=0, tiled=True),
        lax.all_gather(w_up, ("seq", "dp"), axis=0, tiled=True),
        lax.all_gather(w_down, ("seq", "dp"), axis=0, tiled=True),
        lax.all_gather(qv_bias, ("seq", "dp"), axis=1, tiled=True),
        lax.all_gather(out_bias, ("seq", "dp"), axis=0, tiled=True),
        lax.all_gather(up_bias, ("seq", "dp"), axis=0, tiled=True),
        lax.all_gather(down_bias, ("seq", "dp"), axis=0, tiled=True),
        lax.all_gather(norm_gain, ("seq", "dp"), axis=1, tiled=True),
        lax.all_gather(norm_shift, ("seq", "dp"), axis=1, tiled=True),
    )
    qkv_full, out_full, up_full, down_full = (gathered[0], gathered[1], gathered[2], gathered[3])
    qv_shift = gathered[4].astype(jnp.float32)
    out_shift = gathered[5].astype(jnp.float32)
    up_shift = gathered[6].astype(jnp.float32)
    down_shift = gathered[7].astype(jnp.float32)
    gains = gathered[8].astype(jnp.float32)
    shifts = gathered[9].astype(jnp.float32)
    row_count = tokens.shape[1]
    model_width = tokens.shape[2]
    pair_cols = 2 * HD
    pair_count = model_width // pair_cols
    slot_rows = row_count * lax.axis_size("seq")
    factor = 1.0 / (RELAX_SCALE * math.sqrt(HD))
    valid = lengths[assign[lax.axis_index("dp")]]
    own_place = lax.axis_index("seq") * row_count + jnp.arange(row_count, dtype=jnp.int32)
    all_place = jnp.arange(slot_rows, dtype=jnp.int32)
    allowed = (all_place[None, :] <= own_place[:, None]) & (all_place[None, :] < valid)
    pair_ids = jnp.arange(pair_count, dtype=jnp.int32)
    hidden = tokens[0].astype(jnp.float32)
    normed_first, pull_first = jax.vjp(norm_rows, hidden, gains[0], shifts[0])
    normed_low = normed_first.astype(jnp.bfloat16)
    projected = jnp.dot(normed_low, qkv_full, preferred_element_type=jnp.float32)
    queries = (projected[:, :model_width] + qv_shift[0]).astype(jnp.bfloat16)
    key_own = projected[:, model_width : 2 * model_width].astype(jnp.bfloat16)
    value_own = (projected[:, 2 * model_width :] + qv_shift[1]).astype(jnp.bfloat16)
    keys, values = (
        lax.all_gather(key_own, "seq", axis=0, tiled=True),
        lax.all_gather(value_own, "seq", axis=0, tiled=True),
    )

    def columns(block, pair_index):
        return lax.dynamic_slice_in_dim(block, pair_index * pair_cols, pair_cols, 1)

    def merge_pairs(stack):
        return stack.transpose(1, 0, 2).reshape(stack.shape[1], model_width)

    def attend(pair_index):
        scores = pair_scores(columns(queries, pair_index), columns(keys, pair_index))
        row_max = jnp.max(jnp.where(allowed, scores, -jnp.inf), -1, keepdims=True)
        exp_terms = jnp.exp(jnp.where(allowed, RELAX_SCALE * (scores - row_max), -jnp.inf))
        row_total = jnp.sum(exp_terms, -1, keepdims=True)
        probs = (exp_terms / row_total).astype(jnp.bfloat16)
        mixed = jnp.einsum(
            "hqk,khd->qhd",
            probs,
            split_heads(columns(values, pair_index)),
            preferred_element_type=jnp.float32,
        )
        return (mixed.reshape(row_count, pair_cols), row_max[..., 0], row_total[..., 0])

    mixed_pairs, max_pairs, total_pairs = lax.map(attend, pair_ids)
    attended = merge_pairs(mixed_pairs).astype(jnp.bfloat16)
    branch = jnp.dot(attended, out_full, preferred_element_type=jnp.float32) + out_shift
    normed_second, pull_second = jax.vjp(norm_rows, branch, gains[1], shifts[1])
    middle = hidden + normed_second
    normed_third, pull_third = jax.vjp(norm_rows, middle, gains[2], shifts[2])
    third_low = normed_third.astype(jnp.bfloat16)
    up_pre = jnp.dot(third_low, up_full, preferred_element_type=jnp.float32) + up_shift
    activated, pull_gelu = jax.vjp(exact_gelu, up_pre)
    active_low = activated.astype(jnp.bfloat16)
    down_pre = jnp.dot(active_low, down_full, preferred_element_type=jnp.float32) + down_shift
    normed_fourth, pull_fourth = jax.vjp(norm_rows, down_pre, gains[3], shifts[3])
    output = (middle + normed_fourth).astype(jnp.bfloat16)[None]
    again = (
        lax.all_gather(w_qkv, ("seq", "dp"), axis=0, tiled=True),
        lax.all_gather(w_out, ("seq", "dp"), axis=0, tiled=True),
        lax.all_gather(w_up, ("seq", "dp"), axis=0, tiled=True),
        lax.all_gather(w_down, ("seq", "dp"), axis=0, tiled=True),
    )
    qkv_back, out_back, up_back, down_back = (again[0], again[1], again[2], again[3])
    keep_rows = (own_place < valid).astype(jnp.float32)[:, None]
    grad_out = cotangent[0].astype(jnp.float32) * keep_rows
    grad_down, grad_gain_four, grad_shift_four = pull_fourth(grad_out)
    grad_down_low = grad_down.astype(jnp.bfloat16)
    grad_w_down = contract_rows(active_low, grad_down_low)
    grad_b_down = jnp.sum(grad_down_low.astype(jnp.float32), 0)
    (grad_up,) = pull_gelu(contract_cols(grad_down_low, down_back))
    grad_up_low = grad_up.astype(jnp.bfloat16)
    grad_w_up = contract_rows(third_low, grad_up_low)
    grad_b_up = jnp.sum(grad_up_low.astype(jnp.float32), 0)
    grad_middle_part, grad_gain_three, grad_shift_three = pull_third(
        contract_cols(grad_up_low, up_back)
    )
    grad_middle = grad_out + grad_middle_part
    grad_branch, grad_gain_two, grad_shift_two = pull_second(grad_middle)
    grad_branch_low = grad_branch.astype(jnp.bfloat16)
    grad_w_out = contract_rows(attended, grad_branch_low)
    grad_b_out = jnp.sum(grad_branch_low.astype(jnp.float32), 0)
    grad_attended = contract_cols(grad_branch_low, out_back).astype(jnp.bfloat16)

    def query_side(pair_index):
        scores = pair_scores(columns(queries, pair_index), columns(keys, pair_index))
        probs = kept_probs(
            scores, allowed, max_pairs[pair_index][..., None], total_pairs[pair_index][..., None]
        )
        grad_part = columns(grad_attended, pair_index)
        grad_probs = jnp.einsum(
            "qhd,khd->hqk",
            split_heads(grad_part),
            split_heads(columns(values, pair_index)),
            preferred_element_type=jnp.float32,
        )
        delta = jnp.sum(probs * grad_probs, -1, keepdims=True)
        grad_scores = (RELAX_SCALE * probs * (grad_probs - delta)).astype(jnp.bfloat16)
        grad_query = (
            jnp.einsum(
                "hqk,khd->qhd",
                grad_scores,
                split_heads(columns(keys, pair_index)),
                preferred_element_type=jnp.float32,
            )
            * factor
        )
        return (grad_query.reshape(row_count, pair_cols), grad_scores, probs, delta)

    def both_sides(pair_index):
        grad_query, grad_scores, probs, delta = query_side(pair_index)
        grad_part = columns(grad_attended, pair_index)
        grad_key = (
            jnp.einsum(
                "hqk,qhd->khd",
                grad_scores,
                split_heads(columns(queries, pair_index)),
                preferred_element_type=jnp.float32,
            )
            * factor
        )
        grad_value = jnp.einsum(
            "hqk,qhd->khd",
            probs.astype(jnp.bfloat16),
            split_heads(grad_part),
            preferred_element_type=jnp.float32,
        )
        return (
            grad_query,
            grad_key.reshape(slot_rows, pair_cols),
            grad_value.reshape(slot_rows, pair_cols),
        )

    query_pairs, key_terms, value_terms = lax.map(both_sides, pair_ids)
    key_pairs, value_pairs = (
        lax.psum_scatter(
            key_terms.astype(jnp.bfloat16), "seq", scatter_dimension=1, tiled=True
        ).astype(jnp.float32),
        lax.psum_scatter(
            value_terms.astype(jnp.bfloat16), "seq", scatter_dimension=1, tiled=True
        ).astype(jnp.float32),
    )
    grad_q_low = merge_pairs(query_pairs).astype(jnp.bfloat16)
    grad_k_low = merge_pairs(key_pairs).astype(jnp.bfloat16)
    grad_v_low = merge_pairs(value_pairs).astype(jnp.bfloat16)
    grad_projected = jnp.concatenate([grad_q_low, grad_k_low, grad_v_low], 1)
    grad_w_qkv = contract_rows(normed_low, grad_projected)
    grad_qv = jnp.stack(
        [jnp.sum(grad_q_low.astype(jnp.float32), 0), jnp.sum(grad_v_low.astype(jnp.float32), 0)]
    )
    grad_hidden_part, grad_gain_one, grad_shift_one = pull_first(
        contract_cols(grad_projected, qkv_back)
    )
    input_grad = (grad_middle + grad_hidden_part).astype(jnp.bfloat16)[None]
    grad_gains = jnp.stack([grad_gain_one, grad_gain_two, grad_gain_three, grad_gain_four])
    grad_shifts = jnp.stack([grad_shift_one, grad_shift_two, grad_shift_three, grad_shift_four])
    owned = (
        lax.psum_scatter(grad_w_qkv, ("seq", "dp"), scatter_dimension=0, tiled=True),
        lax.psum_scatter(grad_w_out, ("seq", "dp"), scatter_dimension=0, tiled=True),
        lax.psum_scatter(grad_w_up, ("seq", "dp"), scatter_dimension=0, tiled=True),
        lax.psum_scatter(grad_w_down, ("seq", "dp"), scatter_dimension=0, tiled=True),
        lax.psum_scatter(grad_qv, ("seq", "dp"), scatter_dimension=1, tiled=True),
        lax.psum_scatter(grad_b_out, ("seq", "dp"), scatter_dimension=0, tiled=True),
        lax.psum_scatter(grad_b_up, ("seq", "dp"), scatter_dimension=0, tiled=True),
        lax.psum_scatter(grad_b_down, ("seq", "dp"), scatter_dimension=0, tiled=True),
        lax.psum_scatter(grad_gains, ("seq", "dp"), scatter_dimension=1, tiled=True),
        lax.psum_scatter(grad_shifts, ("seq", "dp"), scatter_dimension=1, tiled=True),
    )
    return (
        output,
        input_grad,
        owned[0],
        owned[4],
        owned[1],
        owned[5],
        owned[2],
        owned[6],
        owned[3],
        owned[7],
        owned[8],
        owned[9],
    )


MESH = pl.DeviceIdType.MESH


def is_small(mesh):
    return mesh.shape["seq"] == 16 and mesh.shape["dp"] == 2


def place():
    seq = lax.axis_index("seq")
    return seq // 8, (seq // 4) % 2, (seq // 2) % 2, seq % 2, lax.axis_index("dp")


def exchange_copies(scatter, src, out, send_sem, recv_sem, own_sem):
    a, b, y, c, x = place()

    def peer(k):
        return lax.rem(a + k // 2, 2), lax.rem(y + k % 2, 2)

    def device(k):
        pa, py = peer(k)
        return (pa * 8 + b * 4 + py * 2 + c, x)

    def source(k):
        pa, py = peer(k)
        return src.at[pa * 2 + py] if scatter else src.at[pa, :, py]

    def target(k):
        pa, py = peer(k)
        return out.at[pa, :, py] if scatter else out.at[pa * 2 + py]

    def copy(k, dst):
        return pltpu.make_async_remote_copy(
            src_ref=source(k), dst_ref=target(dst), send_sem=send_sem.at[k], recv_sem=recv_sem.at[k],
            device_id=device(k), device_id_type=MESH)

    def greet():
        barrier = pltpu.get_barrier_semaphore()
        for k in range(1, 4):
            pl.semaphore_signal(barrier, inc=1, device_id=device(k), device_id_type=MESH)

    def run():
        own = pltpu.make_async_copy(source(0), target(0), own_sem)
        own.start()
        pl.semaphore_wait(pltpu.get_barrier_semaphore(), 3)
        for k in (3, 2, 1):
            copy(k, 0).start()
        own.wait()
        for k in (3, 2, 1):
            copy(k, k).wait_recv()
        for k in (3, 2, 1):
            copy(k, 0).wait_send()

    return greet, run


def row_block(i, j):
    _, b, _, c, _ = place()
    return pl.ds(pl.multiple_of(lax.rem(b + i, 2) * 256 + lax.rem(c + j, 2) * 128, 128), 128)


def to_heads_kernel(rows_ref, out, src, *sems):
    greet, run = exchange_copies(True, src, out, *sems)
    greet()
    low = src.shape[2] - 128
    for g in range(4):
        values = slice(low * 2 + g * HD, low * 2 + g * HD + HD)
        for i in range(2):
            if low:
                for j in range(2):
                    src[g, i, j * 128:j * 128 + 128] = rows_ref[row_block(i, j), g * 128:g * 128 + 128]
            src[g, i, low:] = jnp.concatenate([rows_ref[row_block(i, j), values] for j in range(2)], 1)
    run()


def from_heads_kernel(heads_ref, out, got, *sems):
    greet, run = exchange_copies(False, heads_ref, got, *sems)
    greet()
    run()
    low = got.shape[2] - 128
    c = place()[3]
    for i in range(2):
        if low:
            for j in range(2):
                for g in range(4):
                    out[row_block(i, j), g * 128:g * 128 + 128] = got[g, i, j * 128:j * 128 + 128]
        for g in (0, 2):
            left, right = got[g, i, low:], got[g + 1, i, low:]
            cols = slice(low * 2 + g * HD, low * 2 + g * HD + 128)
            for j in range(2):
                lanes = slice(j * HD, j * HD + HD)
                out[row_block(i, j), cols] = jnp.concatenate([left[:, lanes], right[:, lanes]], 1)


def exchange(blocks, scatter, cid):
    vm = pl.BlockSpec(memory_space=pltpu.VMEM)
    rows = blocks.shape[-1] // 2 if scatter else blocks.shape[-2]
    shape, held = (2, 2, 2, rows, 128), (4, 2, rows, 128)
    return pl.pallas_call(
        to_heads_kernel if scatter else from_heads_kernel,
        out_shape=jax.ShapeDtypeStruct(shape if scatter else (512, rows * 2), blocks.dtype),
        in_specs=[vm], out_specs=vm,
        scratch_shapes=[pltpu.VMEM(held, blocks.dtype), pltpu.SemaphoreType.DMA((4,)), pltpu.SemaphoreType.DMA((4,)),
                        pltpu.SemaphoreType.DMA],
        compiler_params=pltpu.CompilerParams(collective_id=cid, has_side_effects=True),
        cost_estimate=pl.CostEstimate(flops=0, bytes_accessed=rows * 100000, transcendentals=0),
        name="to_heads" if scatter else "from_heads",
    )(blocks)


def dot_nt(a, b):
    return lax.dot_general(a, b, (((1,), (1,)), ((), ())), preferred_element_type=jnp.float32)


def dot_nn(a, b):
    return jnp.dot(a, b, preferred_element_type=jnp.float32)


BQ = 256
MASKED = -1e30


def load_heads(valid, packed, q_ref, k_ref):
    rows = q_ref.shape[0]
    qk = packed[:, :256].reshape(rows, 128)
    kq = jnp.concatenate([qk[:, 64:], qk[:, :64]], axis=1)
    lane = lax.broadcasted_iota(jnp.int32, (rows, 128), 1)
    spot = lax.broadcasted_iota(jnp.int32, (rows, 128), 0)
    past = jnp.where(spot < valid, 0.0, MASKED)
    q_ref[...] = jnp.where(lane < 64, qk.astype(jnp.float32), jnp.where(lane == 64, 1.0, 0.0)).astype(jnp.bfloat16)
    k_ref[...] = jnp.where(lane < 64, kq.astype(jnp.float32), jnp.where(lane == 64, past, 0.0)).astype(jnp.bfloat16)


def unpack_rows(halves):
    n = halves.shape[0]
    return jnp.concatenate([halves[:, :, :64], halves[:, :, 64:]], axis=1).reshape(n * 256, 64)


def block_probs(q_ref, k_ref, i):
    n = (i + 1) * BQ
    scores = dot_nt(k_ref[:n], q_ref[i * BQ:n])
    key = lax.broadcasted_iota(jnp.int32, (BQ, BQ), 0)
    query = lax.broadcasted_iota(jnp.int32, (BQ, BQ), 1)
    corner = jnp.where(key <= query, scores[n - BQ:], MASKED)
    scores = jnp.concatenate([scores[:n - BQ], corner], axis=0) if i else corner
    top = jnp.max(scores, axis=0, keepdims=True)
    terms = jnp.exp((scores - top) * 0.125)
    return terms, 1.0 / jnp.sum(terms, axis=0, keepdims=True)


def attend_kernel(valid_ref, packed, out_ref, q_ref, k_ref, vt_ref):
    load_heads(valid_ref[0], packed, q_ref, k_ref)
    unit = jnp.where(
        lax.broadcasted_iota(jnp.int32, (64, 64), 0) == lax.broadcasted_iota(jnp.int32, (64, 64), 1), 1.0, 0.0
    ).astype(jnp.bfloat16)
    vt_ref[...] = dot_nt(unit, unpack_rows(packed[:, 256:])).astype(jnp.bfloat16)
    for i in range(q_ref.shape[0] // BQ):
        n = (i + 1) * BQ
        terms, scale = block_probs(q_ref, k_ref, i)
        probs = (terms * scale).astype(jnp.bfloat16)
        mixed = dot_nn(vt_ref[:, :n], probs).T
        out_ref[i] = jnp.concatenate([mixed[:128], mixed[128:]], axis=1).astype(jnp.bfloat16)


def attend_back_kernel(valid_ref, packed, grad, out_ref, q_ref, k_ref, v_ref, g_ref, kt_ref, dk_ref, dv_ref):
    load_heads(valid_ref[0], packed, q_ref, k_ref)
    v_ref[...] = unpack_rows(packed[:, 256:])
    g_ref[...] = unpack_rows(grad[...])
    unit = jnp.where(
        lax.broadcasted_iota(jnp.int32, (64, 128), 0) == lax.broadcasted_iota(jnp.int32, (64, 128), 1), 1.0, 0.0
    ).astype(jnp.bfloat16)
    kt_ref[...] = dot_nt(unit, k_ref[...]).astype(jnp.bfloat16)
    dk_ref[...] = jnp.zeros_like(dk_ref)
    dv_ref[...] = jnp.zeros_like(dv_ref)
    blocks = q_ref.shape[0] // BQ
    for i in range(blocks):
        n = (i + 1) * BQ
        terms, scale = block_probs(q_ref, k_ref, i)
        probs = terms * scale
        grad_probs = dot_nt(v_ref[:n], g_ref[i * BQ:n])
        delta = jnp.sum(probs * grad_probs, axis=0, keepdims=True)
        grad_scores = (probs * (grad_probs - delta)).astype(jnp.bfloat16)
        grad_query = dot_nn(kt_ref[:, :n], grad_scores).T * 0.125
        out_ref[i, :256, :64] = grad_query.astype(jnp.bfloat16)
        dk_ref[:n] += dot_nn(grad_scores, q_ref[i * BQ:n])
        dv_ref[:n] += dot_nn(probs.astype(jnp.bfloat16), g_ref[i * BQ:n])
    for i in range(blocks):
        rows = slice(i * BQ, (i + 1) * BQ)
        out_ref[i, :256, 64:] = (dk_ref[rows, :64] * 0.125).astype(jnp.bfloat16)
        value = dv_ref[rows].astype(jnp.bfloat16)
        out_ref[i, 256:] = jnp.concatenate([value[:128], value[128:]], axis=1)


def attend(valid, packed):
    rows = packed.shape[0] * 256
    vm = pl.BlockSpec(memory_space=pltpu.VMEM)
    return pl.pallas_call(
        attend_kernel,
        out_shape=jax.ShapeDtypeStruct((packed.shape[0], 128, 128), jnp.bfloat16),
        in_specs=[pl.BlockSpec(memory_space=pltpu.SMEM), vm], out_specs=vm,
        scratch_shapes=[pltpu.VMEM((rows, 128), jnp.bfloat16)] * 2 + [pltpu.VMEM((64, rows), jnp.bfloat16)],
        compiler_params=pltpu.CompilerParams(vmem_limit_bytes=48 << 20),
        name="attend",
    )(valid, packed)


def attend_back(valid, packed, grad):
    rows = packed.shape[0] * 256
    vm = pl.BlockSpec(memory_space=pltpu.VMEM)
    return pl.pallas_call(
        attend_back_kernel,
        out_shape=jax.ShapeDtypeStruct(packed.shape, jnp.bfloat16),
        in_specs=[pl.BlockSpec(memory_space=pltpu.SMEM), vm, vm], out_specs=vm,
        scratch_shapes=[pltpu.VMEM((rows, 128), jnp.bfloat16)] * 2 + [pltpu.VMEM((rows, 64), jnp.bfloat16)] * 2
        + [pltpu.VMEM((64, rows), jnp.bfloat16), pltpu.VMEM((rows, 128), jnp.float32), pltpu.VMEM((rows, 64), jnp.float32)],
        compiler_params=pltpu.CompilerParams(vmem_limit_bytes=48 << 20),
        name="attend_back",
    )(valid, packed, grad)


def flip(bits, block):
    return lax.ppermute(block, "seq", [(s, s ^ bits) for s in range(16)])


flip_a, flip_b, flip_y, flip_core, flip_far = (functools.partial(flip, bits) for bits in (8, 4, 2, 1, 5))


def flip_x(block):
    return lax.ppermute(block, "dp", [(0, 1), (1, 0)])


def after(value, *others):
    return lax.optimization_barrier((value,) + others)[0]


def pick(block, index, axis, keepdims=False):
    return lax.dynamic_index_in_dim(block, index, axis, keepdims=keepdims)


def swap_if(flag, block, axis):
    return jnp.where(flag == 0, block, lax.rev(block, (axis,)))


def sort_ranks(block, b, c):
    return swap_if(c, swap_if(b, block, 0), 1)


def to_ranks(block, b, c):
    mine = pick(pick(block, b, 0), c, 0)
    core = flip_core(pick(pick(block, b, 0), 1 - c, 0))
    near = flip_b(pick(pick(block, 1 - b, 0), c, 0))
    far = flip_far(pick(pick(block, 1 - b, 0), 1 - c, 0))
    return jnp.stack([jnp.stack([mine, core]), jnp.stack([near, far])])


def cube_start(block):
    return jnp.stack([block, flip_a(block)])


def cube_one(flip_one, block):
    return jnp.concatenate([block, flip_one(block)], 0)


def arrange_kernel(count, spot_ref, *refs):
    for k in range(count):
        block, out = refs[k], refs[count + k]
        if len(out.shape) == 7:
            for i in range(2):
                for j in range(2):
                    out[0, i, 0, j, 0] = block[0, i, j]
        else:
            out[0, 0, 0] = block[0]


def arrange(spot, blocks):
    def coords(i, r, y_first):
        second, first, a = i // 4, (i // 2) % 2, i % 2
        y, x = (first, second) if y_first else (second, first)
        return lax.rem(r[0] + a, 2), lax.rem(r[1] + y, 2), lax.rem(r[2] + x, 2)

    def specs(block, y_first):
        shape = block.shape
        if len(shape) == 5:
            def out_place(i, r):
                a, y, x = coords(i, r, y_first)
                return a, 0, y, 0, x, 0, 0
            return (pl.BlockSpec((1,) + shape[1:], lambda i, r: (i, 0, 0, 0, 0)),
                    pl.BlockSpec((1, 2, 1, 2, 1) + shape[3:], out_place),
                    jax.ShapeDtypeStruct((2,) * 5 + shape[3:], block.dtype))

        def out_place(i, r):
            return coords(i, r, y_first) + (0, 0)
        return (pl.BlockSpec((1,) + shape[1:], lambda i, r: (i, 0, 0)),
                pl.BlockSpec((1, 1, 1) + shape[1:], out_place),
                jax.ShapeDtypeStruct((2, 2, 2) + shape[1:], block.dtype))

    made = [specs(*entry) for entry in blocks]
    return pl.pallas_call(
        functools.partial(arrange_kernel, len(blocks)),
        out_shape=tuple(m[2] for m in made),
        grid_spec=pltpu.PrefetchScalarGridSpec(
            num_scalar_prefetch=1, grid=(8,), in_specs=[m[0] for m in made], out_specs=tuple(m[1] for m in made)),
        compiler_params=pltpu.CompilerParams(vmem_limit_bytes=32 << 20),
        cost_estimate=pl.CostEstimate(flops=0, bytes_accessed=8 << 20, transcendentals=0),
        name="arrange",
    )(spot, *[entry[0] for entry in blocks])


def add_low(mine, other):
    return (mine.astype(jnp.float32) + other.astype(jnp.float32)).astype(jnp.bfloat16)


def fold(terms, flip_one, index, axis):
    return add_low(pick(terms, index, axis, True), flip_one(pick(terms, 1 - index, axis, True)))


def reduce_kernel(q_ref, o_ref, u_ref, *refs):
    vec_refs, (out_q, ro, out_u, vec, rq, gu, r1q, t2q, r2q, t3q, r3q, fq, gq, r1o, t2o, r2o, t3o, r3o,
               run, got, send_sem, recv_sem) = refs[:12], refs[12:]
    a, b, y, c, x = place()
    f32, bf16 = jnp.float32, jnp.bfloat16
    barrier = pltpu.get_barrier_semaphore()

    def at(pa, pb, py, pc, px):
        return (pa * 8 + pb * 4 + py * 2 + pc, px)

    to_x, to_y, to_a = at(a, b, y, c, 1 - x), at(a, b, 1 - y, c, x), at(1 - a, b, y, c, x)
    ranks = [(lax.rem(b + k // 2, 2), lax.rem(c + k % 2, 2)) for k in range(4)]
    to_rank = [at(a, ranks[k][0], y, ranks[k][1], x) for k in range(4)]
    to_b, to_c = to_rank[2], to_rank[1]
    for dev in [to_x, to_y, to_a] + to_rank[1:]:
        pl.semaphore_signal(barrier, inc=1, device_id=dev, device_id_type=MESH)
    for pb in range(2):
        for j in range(4):
            for row, cols in ((0, slice(j * 128, j * 128 + HD)), (1, slice(512 + j * HD, 512 + j * HD + HD))):
                piece = vec_refs[0][:, cols]
                pair = [jnp.where((b == pb) & (c == pc), piece, 0.0) for pc in range(2)]
                h = head_of(j // 2, pb, j % 2, 0) * HD
                run[0, row:row + 1, h:h + 128] = jnp.concatenate(pair, 1)
            for pc in range(2):
                col = head_of(j // 2, pb, j % 2, pc) * 256
                piece = vec_refs[1][:, j * 256:j * 256 + 256]
                run[0, 12 + col // 1024:13 + col // 1024, col % 1024:col % 1024 + 256] = jnp.where(
                    (b == pb) & (c == pc), piece, 0.0)
    for k in range(2, 12):
        run[0, k:k + 1] = vec_refs[k][...]
    pl.semaphore_wait(barrier, 6)

    made = []

    def remote(src, dst, dev):
        k = len(made)
        made.append(pltpu.make_async_remote_copy(
            src_ref=src, dst_ref=dst, send_sem=send_sem.at[k], recv_sem=recv_sem.at[k],
            device_id=dev, device_id_type=MESH))
        return made[-1]

    def low(*values):
        return sum(v.astype(f32) for v in values)

    places = [1 - a, a]
    halves = [slice(0, 512), slice(512, 1024)]
    lateral = [(to_x, to_y), (to_y, to_x)]

    q1, q2, o1, o2 = {}, {}, {}, {}
    for i in range(2):
        for s in range(2):
            p = places[i]
            q1[s, i] = remote(q_ref.at[p, 0, :, :, 1 - x] if s == 0 else q_ref.at[p, 1, 1 - y], r1q.at[s, i], lateral[s][0])
            o1[s, i] = remote(o_ref.at[p, :, 1 - x, :, halves[0]] if s == 0 else o_ref.at[p, 1 - y, :, :, halves[1]],
                              r1o.at[s, i], lateral[s][0])
            q2[s, i] = remote(t2q.at[s, i], r2q.at[s, i], lateral[s][1])
            o2[s, i] = remote(t2o.at[s, i], r2o.at[s, i], lateral[s][1])
    q3 = [remote(t3q.at[s], r3q.at[s], to_a) for s in range(2)]
    o3 = [remote(t3o.at[s], r3o.at[s], to_a) for s in range(2)]
    qr = [remote(fq.at[ranks[k][0], ranks[k][1]], gq.at[k - 1], to_rank[k]) for k in range(1, 4)]
    ur = [remote(u_ref.at[ranks[k][0], ranks[k][1]], gu.at[b, c], to_rank[k]) for k in range(1, 4)]
    vs = [remote(run.at[k], got.at[k], dev) for k, dev in enumerate((to_x, to_y, to_a, to_b, to_c))]

    def next_sum(k):
        vs[k].wait_recv()
        if k < 4:
            run[k + 1] = run[k] + got[k]
            vs[k + 1].start()
        else:
            vec[...] = run[k] + got[k]

    vs[0].start()
    for i in range(2):
        for s in range(2):
            q1[s, i].start()
            o1[s, i].start()
    for k in (3, 2, 1):
        ur[k - 1].start()

    def q_terms(s, i, far):
        p = places[i]
        if s == 0:
            v = 1 - y if far else y
            return q_ref[p, 0, v, :, x], r1q[0, i, v]
        v = 1 - x if far else x
        return q_ref[p, 1, y, :, v], r1q[1, i, :, v]

    def o_terms(s, i, far):
        p = places[i]
        if s == 0:
            v = 1 - y if far else y
            return o_ref[p, v, x, :, halves[0]], r1o[0, i, v]
        v = 1 - x if far else x
        return o_ref[p, y, v, :, halves[1]], r1o[1, i, v]

    for i in range(2):
        for s in range(2):
            q1[s, i].wait_recv()
            t2q[s, i] = low(*q_terms(s, i, True)).astype(bf16)
            q2[s, i].start()
            o1[s, i].wait_recv()
            t2o[s, i] = low(*o_terms(s, i, True)).astype(bf16)
            o2[s, i].start()
        if i == 0:
            next_sum(0)
            for s in range(2):
                q2[s, 0].wait_recv()
                t3q[s] = low(*q_terms(s, 0, False), r2q[s, 0]).astype(bf16)
                q3[s].start()
                o2[s, 0].wait_recv()
                t3o[s] = low(*o_terms(s, 0, False), r2o[s, 0]).astype(bf16)
                o3[s].start()
    next_sum(1)
    for s in range(2):
        q2[s, 1].wait_recv()
        o2[s, 1].wait_recv()
        q3[s].wait_recv()
        total = low(*q_terms(s, 1, False), r2q[s, 1], r3q[s])
        fq[s] = total.astype(bf16)
        for j in range(2):
            @pl.when((b == s) & (c == j))
            def _():
                rq[s, j] = total[j]
        o3[s].wait_recv()
        ro[:, halves[s]] = low(*o_terms(s, 1, False), r2o[s, 1], r3o[s])
    for k in (3, 2, 1):
        qr[k - 1].start()
    next_sum(2)
    gu[b, c] = u_ref[b, c]
    for k in (1, 2, 3):
        ur[k - 1].wait_recv()
    next_sum(3)
    for k in (1, 2, 3):
        pb, pc = ranks[k]
        qr[k - 1].wait_recv()
        rq[pb, pc] = gq[k - 1].astype(f32)
    for pb in range(2):
        for j in range(4):
            zero, one = rq[pb, 0], rq[pb, 1]
            h = head_of(j // 2, pb, j % 2, 0) * HD
            q, k = slice(j * 128, j * 128 + HD), slice(j * 128 + HD, j * 128 + 128)
            v = slice(512 + j * HD, 512 + j * HD + HD)
            for t, cols in enumerate((q, k, v)):
                out_q[:, t * 1024 + h:t * 1024 + h + 128] = jnp.concatenate([zero[:, cols], one[:, cols]], 1)
            for pc in range(2):
                col = head_of(j // 2, pb, j % 2, pc) * 256
                out_u[:, col:col + 256] = gu[pb, pc, :, j * 256:j * 256 + 256].astype(f32)
    next_sum(4)
    for copy in made:
        copy.wait_send()


def reduce_all(gw_qkv, gw_out, up_sum, vectors, cid):
    f32, bf16 = jnp.float32, jnp.bfloat16
    V = pltpu.VMEM
    vm = pl.BlockSpec(memory_space=V)
    S = jax.ShapeDtypeStruct
    q, o, u = gw_qkv.shape[5:], (gw_out.shape[3], 512), up_sum.shape
    scratch = [
        V((2, 2) + q, f32), V(u, bf16),
        V((2, 2, 2, 2) + q, bf16), V((2, 2, 2) + q, bf16), V((2, 2, 2) + q, bf16), V((2, 2) + q, bf16), V((2, 2) + q, bf16),
        V((2, 2) + q, bf16), V((3,) + q, bf16),
        V((2, 2, 2) + o, bf16), V((2, 2) + o, bf16), V((2, 2) + o, bf16), V((2,) + o, bf16), V((2,) + o, bf16),
        V((5, 16, 1024), f32), V((5, 16, 1024), f32),
        pltpu.SemaphoreType.DMA((32,)), pltpu.SemaphoreType.DMA((32,))]
    return pl.pallas_call(
        reduce_kernel,
        out_shape=(S((q[0], 4 * q[1]), f32), S((o[0], 1024), f32), S((u[2], 4 * u[3]), f32), S((16, 1024), f32)),
        in_specs=[vm] * 15, out_specs=(vm,) * 4, scratch_shapes=scratch,
        compiler_params=pltpu.CompilerParams(collective_id=cid, has_side_effects=True, vmem_limit_bytes=40 << 20),
        name="reduce_all",
    )(gw_qkv, gw_out, up_sum, *vectors)


def qk_columns(head):
    return slice(head * HD, head * HD + HD), slice(1024 + head * HD, 1024 + head * HD + HD), slice(2048 + head * HD, 2048 + head * HD + HD)


def head_of(a, b, y, c):
    return a * 8 + b * 4 + y * 2 + c


def start_kernel(q_in, u_in, o_in, t_in, v_in, wq, wo, up, rows, vec, q_src, u_src, send_sem, recv_sem, own_sem):
    a, b, y, c, x = place()
    barrier = pltpu.get_barrier_semaphore()

    def at(pa, pb, py, pc, px):
        return (pa * 8 + pb * 4 + py * 2 + pc, px)

    to_x, to_y, to_a = at(a, b, y, c, 1 - x), at(a, b, 1 - y, c, x), at(1 - a, b, y, c, x)
    ranks = [(lax.rem(b + k // 2, 2), lax.rem(c + k % 2, 2)) for k in range(4)]
    to_rank = [at(a, pb, y, pc, x) for pb, pc in ranks]
    for dev in [to_x, to_y, to_a] + to_rank[1:]:
        pl.semaphore_signal(barrier, inc=1, device_id=dev, device_id_type=MESH)

    for pb in range(2):
        for pc in range(2):
            for j in range(4):
                q, k, v = qk_columns(head_of(j // 2, pb, j % 2, pc))
                q_src[pb, pc, :, j * 128:j * 128 + 128] = jnp.concatenate([q_in[:, q], q_in[:, k]], 1)
            for j in range(2):
                v0 = qk_columns(head_of(j, pb, 0, pc))[2]
                v1 = qk_columns(head_of(j, pb, 1, pc))[2]
                q_src[pb, pc, :, 512 + j * 128:640 + j * 128] = jnp.concatenate([q_in[:, v0], q_in[:, v1]], 1)
            for j in range(4):
                col = (head_of(j // 2, pb, j % 2, pc)) * 256
                u_src[pb, pc, :, j * 256:j * 256 + 256] = u_in[:, col:col + 256]
    own = [pltpu.make_async_copy(src, dst, own_sem.at[k]) for k, (src, dst) in enumerate((
        (q_src.at[b, c], wq.at[a, b, y, c, x]), (u_src.at[b, c], up.at[0, b, c]), (o_in, wo.at[a, y, x]),
        (t_in, rows.at[0]), (v_in, vec.at[a, b, y, c, x])))]
    for copy in own:
        copy.start()
    pl.semaphore_wait(barrier, 6)

    made = []

    def remote(src, dst, dev):
        k = len(made)
        made.append(pltpu.make_async_remote_copy(
            src_ref=src, dst_ref=dst, send_sem=send_sem.at[k], recv_sem=recv_sem.at[k],
            device_id=dev, device_id_type=MESH))
        return made[-1]

    places = [a, 1 - a]
    halves = [slice(0, 512), slice(512, 1024)]
    lateral = [(to_y, to_x), (to_x, to_y)]

    def same(ref, dev):
        return remote(ref, ref, dev)

    q_rank = [remote(q_src.at[ranks[k][0], ranks[k][1]], wq.at[a, b, y, c, x], to_rank[k]) for k in range(1, 4)]
    u_rank = [remote(u_src.at[ranks[k][0], ranks[k][1]], up.at[0, b, c], to_rank[k]) for k in range(1, 4)]
    v_rank = [remote(v_in, vec.at[a, b, y, c, x], to_rank[k]) for k in range(1, 4)]
    t_core, t_near = remote(t_in, rows.at[1], to_rank[1]), remote(t_in, rows.at[2], to_rank[2])
    t_far = remote(rows.at[2], rows.at[3], to_rank[1])
    u_cube = remote(up.at[0], up.at[1], to_a)
    v_cube = [same(vec.at[a, :, y, :, x], to_a), same(vec.at[:, :, y, :, x], to_y), same(vec.at[:, :, :, :, x], to_x)]
    q_cube = [same(wq.at[a, s, y, :, x], to_a) for s in range(2)]
    o_cube = [remote(o_in.at[:, halves[s]], wo.at[a, y, x, :, halves[s]], to_a) for s in range(2)]
    q_side, o_side = {}, {}
    for i in range(2):
        for s in range(2):
            one, two = lateral[s]
            oy, ox = (1 - y, x) if s == 0 else (y, 1 - x)
            p = places[i]
            mine, theirs = wq.at[p, s, y, :, x], wq.at[p, s, oy, :, ox]
            q_side[s, i] = (same(mine, one), same(mine, two), same(theirs, two))
            mine, theirs = wo.at[p, y, x, :, halves[s]], wo.at[p, oy, ox, :, halves[s]]
            first = o_in.at[:, halves[s]] if i == 0 else mine
            o_side[s, i] = (remote(first, mine, one), remote(first, mine, two), same(theirs, two))

    for k in (2, 1, 0):
        q_rank[k].start()
        v_rank[k].start()
    for s in range(2):
        o_cube[s].start()
        o_side[s, 0][0].start()
        o_side[s, 0][1].start()
    t_near.start()
    t_core.start()
    own[0].wait()
    for copy in q_rank:
        copy.wait_recv()
    for s in range(2):
        q_cube[s].start()
        q_side[s, 0][0].start()
        q_side[s, 0][1].start()
    own[4].wait()
    for copy in v_rank:
        copy.wait_recv()
    v_cube[0].start()
    for k in (2, 1, 0):
        u_rank[k].start()
    for s in range(2):
        o_side[s, 0][0].wait_recv()
        o_side[s, 0][2].start()
    for s in range(2):
        o_cube[s].wait_recv()
        o_side[s, 1][0].start()
        o_side[s, 1][1].start()
    t_near.wait_recv()
    t_far.start()
    for s in range(2):
        q_side[s, 0][0].wait_recv()
        q_side[s, 0][2].start()
    for s in range(2):
        q_cube[s].wait_recv()
        q_side[s, 1][0].start()
        q_side[s, 1][1].start()
    v_cube[0].wait_recv()
    v_cube[1].start()
    own[1].wait()
    for copy in u_rank:
        copy.wait_recv()
    u_cube.start()
    for s in range(2):
        o_side[s, 1][0].wait_recv()
        o_side[s, 1][2].start()
    v_cube[1].wait_recv()
    v_cube[2].start()
    for s in range(2):
        q_side[s, 1][0].wait_recv()
        q_side[s, 1][2].start()
    v_cube[2].wait_recv()
    t_core.wait_recv()
    t_far.wait_recv()
    for i in range(2):
        for s in range(2):
            for k in (1, 2):
                q_side[s, i][k].wait_recv()
                o_side[s, i][k].wait_recv()
    u_cube.wait_recv()
    own[2].wait()
    own[3].wait()
    for copy in made:
        copy.wait_send()


def start_gather(w_qkv, w_up, w_out, tokens, vectors, cid):
    bf16 = jnp.bfloat16
    S = lambda *shape: jax.ShapeDtypeStruct(shape, bf16)
    vm, anywhere = pl.BlockSpec(memory_space=pltpu.VMEM), pl.BlockSpec(memory_space=pl.ANY)
    return pl.pallas_call(
        start_kernel,
        out_shape=(S(2, 2, 2, 2, 2, 32, 768), S(2, 2, 2, 32, 1024), S(2, 2, 2, 32, 1024), S(4, 128, 1024),
                   S(2, 2, 2, 2, 2, 16, 128)),
        in_specs=[vm] * 5, out_specs=(anywhere,) * 5,
        scratch_shapes=[
            pltpu.VMEM((2, 2, 32, 768), bf16), pltpu.VMEM((2, 2, 32, 1024), bf16),
            pltpu.SemaphoreType.DMA((48,)), pltpu.SemaphoreType.DMA((48,)), pltpu.SemaphoreType.DMA((5,))],
        compiler_params=pltpu.CompilerParams(collective_id=cid, has_side_effects=True, vmem_limit_bytes=32 << 20),
        cost_estimate=pl.CostEstimate(flops=0, bytes_accessed=100 << 20, transcendentals=0),
        name="start_gather",
    )(w_qkv, w_up, w_out, tokens, vectors)


PIECE = 32


def rows_kernel(step, gather, count_in, count_out, part, *refs):
    ins, outs = refs[:count_in], refs[count_in:count_in + count_out]
    rest = refs[count_in + count_out:]
    rows = rest[0] if gather else None
    got_far, got_near, sums, got_sums, send_sem, recv_sem = rest[-6:]
    a, b, y, c, x = place()

    def at(pb, pc):
        return (a * 8 + pb * 4 + y * 2 + pc, x)

    to_b, to_core = at(1 - b, c), at(b, 1 - c)
    barrier = pltpu.get_barrier_semaphore()
    for dev in (to_b, to_core):
        pl.semaphore_signal(barrier, inc=1, device_id=dev, device_id_type=MESH)
    pl.semaphore_wait(barrier, 2)
    pieces = part.shape[2] // PIECE

    def span(r):
        return pl.ds(pl.multiple_of(r * PIECE, PIECE), PIECE)

    def remote(kind, r, src, dst, dev):
        return pltpu.make_async_remote_copy(
            src_ref=src, dst_ref=dst, send_sem=send_sem.at[kind, r], recv_sem=recv_sem.at[kind, r],
            device_id=dev, device_id_type=MESH)

    def far(r):
        return remote(0, r, part.at[1, 1, span(r)], got_far.at[span(r)], to_core)

    def near(r):
        return remote(1, r, part.at[0, 1, span(r)], got_near.at[span(r)], to_core)

    def across(r):
        return remote(2, r, sums.at[span(r)], got_sums.at[span(r)], to_b)

    def row_near(r):
        return remote(3, r, rows.at[0, span(r)], rows.at[2, span(r)], to_b)

    def row_core(r):
        return remote(4, r, rows.at[0, span(r)], rows.at[1, span(r)], to_core)

    def row_far(r):
        return remote(5, r, rows.at[2, span(r)], rows.at[3, span(r)], to_core)

    for r in range(pieces):
        far(r).start()
    for r in range(pieces):
        near(r).start()

    def send_across(r, _):
        far(r).wait_recv()
        sums[span(r)] = (part[1, 0, span(r)] + got_far[span(r)]).astype(jnp.bfloat16)
        across(r).start()
        return 0

    lax.fori_loop(0, pieces, send_across, 0)
    for ref in outs:
        if ref.shape[0] == 1:
            ref[...] = jnp.zeros_like(ref)

    def take(r, _):
        near(r).wait_recv()
        across(r).wait_recv()
        total = part[0, 0, span(r)] + got_near[span(r)] + got_sums[span(r)].astype(jnp.float32)
        piece = step(span(r), total, ins, outs)
        if gather:
            rows[0, span(r)] = piece
            row_near(r).start()
            row_core(r).start()
        return 0

    lax.fori_loop(0, pieces, take, 0)

    def relay(r, _):
        row_near(r).wait_recv()
        row_far(r).start()
        return 0

    def finish(r, _):
        if gather:
            row_core(r).wait_recv()
            row_far(r).wait_recv()
            row_near(r).wait_send()
            row_core(r).wait_send()
            row_far(r).wait_send()
        far(r).wait_send()
        near(r).wait_send()
        across(r).wait_send()
        return 0

    if gather:
        lax.fori_loop(0, pieces, relay, 0)
    lax.fori_loop(0, pieces, finish, 0)


def sum_rows(step, part, ins, outs, gather, cid):
    rows, n = part.shape[0] // 4, part.shape[1]
    vm = pl.BlockSpec(memory_space=pltpu.VMEM)
    shapes = tuple(outs) + ((jax.ShapeDtypeStruct((4, rows, n), jnp.bfloat16),) if gather else ())
    V = pltpu.VMEM
    return pl.pallas_call(
        functools.partial(rows_kernel, step, gather, len(ins), len(outs)),
        out_shape=shapes, in_specs=[vm] * (1 + len(ins)), out_specs=(vm,) * len(shapes),
        scratch_shapes=[V((rows, n), jnp.float32), V((rows, n), jnp.float32), V((rows, n), jnp.bfloat16), V((rows, n), jnp.bfloat16),
                        pltpu.SemaphoreType.DMA((6, rows // PIECE)), pltpu.SemaphoreType.DMA((6, rows // PIECE))],
        compiler_params=pltpu.CompilerParams(collective_id=cid, has_side_effects=True, vmem_limit_bytes=32 << 20),
        cost_estimate=pl.CostEstimate(flops=0, bytes_accessed=50 << 20, transcendentals=0),
        name="sum_rows",
    )(part.reshape(2, 2, rows, n), *ins)


def attended_step(span, total, ins, outs):
    tokens, bias, gain1, shift1, gain2, shift2 = ins
    branch = total + bias[...]
    middle = tokens[span].astype(jnp.float32) + norm_rows(branch, gain1[...], shift1[...])
    outs[0][span] = branch
    outs[1][span] = middle
    return norm_rows(middle, gain2[...], shift2[...]).astype(jnp.bfloat16)


def output_step(span, total, ins, outs):
    middle, grad_out, bias, gain, shift = ins
    normed, pull = jax.vjp(norm_rows, total + bias[...], gain[...], shift[...])
    outs[0][span] = (middle[span] + normed).astype(jnp.bfloat16)
    grad_down, grad_gain, grad_shift = pull(grad_out[span])
    grad_down = grad_down.astype(jnp.bfloat16)
    outs[1][...] += grad_gain
    outs[2][...] += grad_shift
    outs[3][...] += jnp.sum(grad_down.astype(jnp.float32), 0, keepdims=True)
    return grad_down


def middle_step(span, total, ins, outs):
    middle, branch, grad_out, gain1, shift1, gain2, shift2 = ins
    _, pull = jax.vjp(norm_rows, middle[span], gain2[...], shift2[...])
    part, grad_gain2, grad_shift2 = pull(total)
    grad_middle = grad_out[span] + part
    _, pull = jax.vjp(norm_rows, branch[span], gain1[...], shift1[...])
    grad_branch, grad_gain1, grad_shift1 = pull(grad_middle)
    grad_branch = grad_branch.astype(jnp.bfloat16)
    outs[0][span] = grad_middle
    for ref, value in zip(outs[1:], (grad_gain2, grad_shift2, grad_gain1, grad_shift1,
                                     jnp.sum(grad_branch.astype(jnp.float32), 0, keepdims=True))):
        ref[...] += value
    return grad_branch


def input_step(span, total, ins, outs):
    tokens, grad_middle, gain, shift = ins
    _, pull = jax.vjp(norm_rows, tokens[span].astype(jnp.float32), gain[...], shift[...])
    part, grad_gain, grad_shift = pull(total)
    outs[0][span] = (grad_middle[span] + part).astype(jnp.bfloat16)
    outs[1][...] += grad_gain
    outs[2][...] += grad_shift


def fast_body(tokens, cotangent, lengths, assign, w_qkv, qv_bias, w_out, out_bias, w_up, up_bias, w_down, down_bias,
              norm_gain, norm_shift):
    bf16, f32 = jnp.bfloat16, jnp.float32
    a, b, y, c, x = place()
    spot = jnp.stack([a, y, x]).astype(jnp.int32)
    width = tokens.shape[2]
    valid = lengths[assign[x]].astype(jnp.int32)

    small = jnp.concatenate([qv_bias, out_bias[None], down_bias[None], norm_gain, norm_shift], 0)
    small = jnp.concatenate([jnp.pad(small, ((0, 0), (0, 96))), up_bias[None], jnp.zeros((3, 128), bf16)], 0)
    wqkv, wo, up_one, rows, small = start_gather(w_qkv, w_up, w_out, tokens[0], small, 6)
    wqkv, wo, rows = wqkv.reshape(width, 768), wo.reshape(256, width), rows.reshape(512, width)
    down_one = cube_start(after(w_down, wqkv))

    vectors = small[..., :12, :32].reshape(32, 12, 32).transpose(1, 0, 2).reshape(12, width).astype(f32)
    qv_half = pick(pick(vectors[:2].reshape(2, 2, 2, 2, 2, HD), b, 2), c, 3).reshape(2, 4, HD)
    qk_shift = jnp.concatenate([qv_half[0], jnp.zeros((4, HD), f32)], 1).reshape(512)
    v_shift = qv_half[1].reshape(256)
    row_of = lambda k: vectors[k:k + 1]
    out_full, down_full = row_of(2), row_of(3)
    gains, shifts = [row_of(4 + k) for k in range(4)], [row_of(8 + k) for k in range(4)]
    up_shift = pick(pick(small[..., 12, :], b, 1), c, 2).reshape(1024).astype(f32)

    first = norm_rows(rows.astype(f32), gains[0], shifts[0]).astype(bf16)
    up_two = cube_one(flip_x, up_one)
    projected = (dot_nn(first, wqkv) + jnp.concatenate([qk_shift, v_shift])).astype(bf16)
    packed = exchange(after(projected, up_two, down_one), True, 1).reshape(8, 384, 128)
    down_two = cube_one(flip_x, down_one)
    up_half = flip_y(after(up_two, packed)[:, 0])
    attended = attend(valid[None], packed).reshape(2, 2, 2, 128, 128)
    attended = exchange(after(attended, down_two, up_half), False, 2)
    up_all = jnp.concatenate([up_two, jnp.stack([up_half, flip_y(after(up_two, attended)[:, 1])], 1)], 0)
    down_far = flip_y(after(down_two, attended))
    own_spot = lax.axis_index("seq") * 128 + jnp.arange(128, dtype=jnp.int32)
    grad_out = cotangent[0].astype(f32) * (own_spot < valid).astype(f32)[:, None]
    S = jax.ShapeDtypeStruct
    wide, low, line = S((128, width), f32), S((128, width), bf16), S((1, width), f32)
    branch, middle, third = sum_rows(
        attended_step, dot_nn(attended, wo), (tokens[0], out_full, gains[1], shifts[1], gains[2], shifts[2]),
        (wide, wide), True, 7)
    third = third.reshape(512, width)
    wu = arrange(spot, [(up_all, False)])[0].reshape(width, 1024)
    up_pre = dot_nn(third, wu) + up_shift
    active, pull_gelu = jax.vjp(exact_gelu, up_pre)
    active = active.astype(bf16)
    down_all = jnp.concatenate([down_two, after(down_far, active)], 0)
    wd = arrange(spot, [(down_all, False)])[0].reshape(1024, width)
    output, gain4, shift4, bias_down, down_rows = sum_rows(
        output_step, dot_nn(active, wd), (middle, grad_out, down_full, gains[3], shifts[3]), (low, line, line, line), True, 8)
    down_rows = down_rows.reshape(512, width)
    gw_down = contract_rows(active, down_rows).astype(bf16).reshape(2, 2, 2, 128, width)
    down_term = flip_y(pick(gw_down, 1 - y, 1, True))
    (grad_up,) = pull_gelu(dot_nt(after(down_rows, gw_down), wd))
    grad_up = grad_up.astype(bf16)
    gw_up = contract_rows(third, grad_up).astype(bf16).reshape(2, 2, 2, 2, 2, 32, 1024)
    up_term = flip_x(pick(gw_up, 1 - x, 4, True))
    grad_middle, gain3, shift3, gain2, shift2, bias_out, branch_rows = sum_rows(
        middle_step, dot_nt(after(grad_up, gw_up), wu),
        (middle, branch, grad_out, gains[1], shifts[1], gains[2], shifts[2]), (wide,) + (line,) * 5, True, 9)
    branch_rows = branch_rows.reshape(512, width)
    grad_att = dot_nt(branch_rows, wo).astype(bf16)
    down_sum = add_low(pick(gw_down, y, 1, True), down_term)
    down_term = flip_x(pick(down_sum, 1 - x, 2, True))
    grad_packed = exchange(after(grad_att, down_sum), True, 3).reshape(8, 128, 128)
    up_sum = add_low(pick(gw_up, x, 4, True), after(up_term, grad_packed))
    up_term = flip_y(pick(up_sum, 1 - y, 2, True))
    down_sum = add_low(pick(down_sum, x, 2, True), after(down_term, grad_packed))
    down_term = flip_a(pick(down_sum, 1 - a, 0))
    back = attend_back(valid[None], packed, grad_packed)

    up_sum = add_low(pick(up_sum, y, 2, True), up_term)
    gw_out = contract_rows(attended, branch_rows).astype(bf16).reshape(2, 2, 2, 32, width)
    grad_qkv = exchange(after(back, up_sum, down_term).reshape(2, 2, 2, 384, 128), False, 4)
    up_term = flip_a(pick(after(up_sum, grad_qkv), 1 - a, 0))
    gw_qkv = contract_rows(first, grad_qkv).astype(bf16).reshape(2, 2, 2, 2, 2, 32, 768)
    input_grad, gain1, shift1 = sum_rows(
        input_step, dot_nt(grad_qkv, wqkv), (tokens[0], grad_middle, gains[0], shifts[0]), (low, line, line), False, 10)

    def sums(block):
        return jnp.sum(block.astype(f32), 0, keepdims=True)

    vectors = [sums(grad_qkv), sums(grad_up), bias_out, bias_down,
               gain1, gain2, gain3, gain4, shift1, shift2, shift3, shift4]
    up_sum = (pick(up_sum, a, 0).astype(f32) + up_term.astype(f32)).astype(bf16).reshape(2, 2, 32, 1024)
    r_qkv, r_out, r_up, vectors = reduce_all(gw_qkv, gw_out, up_sum, vectors, 5)
    r_down = (pick(down_sum, a, 0).astype(f32) + down_term.astype(f32)).reshape(128, width)
    index = lax.axis_index("seq") * 2 + x
    small_up = lax.dynamic_slice(vectors, (12 + index // 8, index % 8 * 128), (1, 128)).reshape(128)
    vectors = lax.dynamic_slice(vectors, (0, index * 32), (12, 32))

    return (
        output[None], input_grad[None], r_qkv, vectors[:2], r_out,
        vectors[2], r_up, small_up, r_down, vectors[3], vectors[4:8], vectors[8:12])


def solution(mesh):
    return jax.shard_map(
        fast_body if is_small(mesh) else body,
        mesh=mesh,
        in_specs=(
            P("dp", "seq", None),
            P("dp", "seq", None),
            P(),
            P(),
            P(("seq", "dp"), None),
            P(None, ("seq", "dp")),
            P(("seq", "dp"), None),
            P(("seq", "dp")),
            P(("seq", "dp"), None),
            P(("seq", "dp")),
            P(("seq", "dp"), None),
            P(("seq", "dp")),
            P(None, ("seq", "dp")),
            P(None, ("seq", "dp")),
        ),
        out_specs=(
            P("dp", "seq", None),
            P("dp", "seq", None),
            P(("seq", "dp"), None),
            P(None, ("seq", "dp")),
            P(("seq", "dp"), None),
            P(("seq", "dp")),
            P(("seq", "dp"), None),
            P(("seq", "dp")),
            P(("seq", "dp"), None),
            P(("seq", "dp")),
            P(None, ("seq", "dp")),
            P(None, ("seq", "dp")),
        ),
        check_vma=False,
    )
```

```python
import functools
import math

import jax
import jax.numpy as jnp
from jax import lax
from jax.experimental import pallas as pl
from jax.experimental.pallas import tpu as pltpu
from jax.sharding import PartitionSpec as P


HD = 64


RELAX_SCALE = 32.0
NORM_EPSILON = 1e-05


def norm_rows(values, gain, shift):
    center = values - jnp.mean(values, -1, keepdims=True)
    spread = jnp.mean(center * center, -1, keepdims=True)
    return center * lax.rsqrt(spread + NORM_EPSILON) * gain + shift


def exact_gelu(values):
    return jax.nn.gelu(values, approximate=False)


def contract_rows(left, right):
    return lax.dot_general(
        left, right, (((0,), (0,)), ((), ())), preferred_element_type=jnp.float32
    )


def contract_cols(left, right):
    return lax.dot_general(
        left, right, (((1,), (1,)), ((), ())), preferred_element_type=jnp.float32
    )


def split_heads(block):
    return block.reshape(block.shape[0], 2, HD)


def pair_scores(query_part, key_part):
    factor = 1.0 / (RELAX_SCALE * math.sqrt(HD))
    return (
        jnp.einsum(
            "qhd,khd->hqk",
            split_heads(query_part),
            split_heads(key_part),
            preferred_element_type=jnp.float32,
        )
        * factor
    )


def kept_probs(scores, allowed, row_max, row_total):
    exp_terms = jnp.exp(jnp.where(allowed, RELAX_SCALE * (scores - row_max), -jnp.inf))
    return exp_terms / row_total


def body(
    tokens,
    cotangent,
    lengths,
    assign,
    w_qkv,
    qv_bias,
    w_out,
    out_bias,
    w_up,
    up_bias,
    w_down,
    down_bias,
    norm_gain,
    norm_shift,
):
    gathered = (
        lax.all_gather(w_qkv, ("seq", "dp"), axis=0, tiled=True),
        lax.all_gather(w_out, ("seq", "dp"), axis=0, tiled=True),
        lax.all_gather(w_up, ("seq", "dp"), axis=0, tiled=True),
        lax.all_gather(w_down, ("seq", "dp"), axis=0, tiled=True),
        lax.all_gather(qv_bias, ("seq", "dp"), axis=1, tiled=True),
        lax.all_gather(out_bias, ("seq", "dp"), axis=0, tiled=True),
        lax.all_gather(up_bias, ("seq", "dp"), axis=0, tiled=True),
        lax.all_gather(down_bias, ("seq", "dp"), axis=0, tiled=True),
        lax.all_gather(norm_gain, ("seq", "dp"), axis=1, tiled=True),
        lax.all_gather(norm_shift, ("seq", "dp"), axis=1, tiled=True),
    )
    qkv_full, out_full, up_full, down_full = (gathered[0], gathered[1], gathered[2], gathered[3])
    qv_shift = gathered[4].astype(jnp.float32)
    out_shift = gathered[5].astype(jnp.float32)
    up_shift = gathered[6].astype(jnp.float32)
    down_shift = gathered[7].astype(jnp.float32)
    gains = gathered[8].astype(jnp.float32)
    shifts = gathered[9].astype(jnp.float32)
    row_count = tokens.shape[1]
    model_width = tokens.shape[2]
    pair_cols = 2 * HD
    pair_count = model_width // pair_cols
    slot_rows = row_count * lax.axis_size("seq")
    factor = 1.0 / (RELAX_SCALE * math.sqrt(HD))
    valid = lengths[assign[lax.axis_index("dp")]]
    own_place = lax.axis_index("seq") * row_count + jnp.arange(row_count, dtype=jnp.int32)
    all_place = jnp.arange(slot_rows, dtype=jnp.int32)
    allowed = (all_place[None, :] <= own_place[:, None]) & (all_place[None, :] < valid)
    pair_ids = jnp.arange(pair_count, dtype=jnp.int32)
    hidden = tokens[0].astype(jnp.float32)
    normed_first, pull_first = jax.vjp(norm_rows, hidden, gains[0], shifts[0])
    normed_low = normed_first.astype(jnp.bfloat16)
    projected = jnp.dot(normed_low, qkv_full, preferred_element_type=jnp.float32)
    queries = (projected[:, :model_width] + qv_shift[0]).astype(jnp.bfloat16)
    key_own = projected[:, model_width : 2 * model_width].astype(jnp.bfloat16)
    value_own = (projected[:, 2 * model_width :] + qv_shift[1]).astype(jnp.bfloat16)
    keys, values = (
        lax.all_gather(key_own, "seq", axis=0, tiled=True),
        lax.all_gather(value_own, "seq", axis=0, tiled=True),
    )

    def columns(block, pair_index):
        return lax.dynamic_slice_in_dim(block, pair_index * pair_cols, pair_cols, 1)

    def merge_pairs(stack):
        return stack.transpose(1, 0, 2).reshape(stack.shape[1], model_width)

    def attend(pair_index):
        scores = pair_scores(columns(queries, pair_index), columns(keys, pair_index))
        row_max = jnp.max(jnp.where(allowed, scores, -jnp.inf), -1, keepdims=True)
        exp_terms = jnp.exp(jnp.where(allowed, RELAX_SCALE * (scores - row_max), -jnp.inf))
        row_total = jnp.sum(exp_terms, -1, keepdims=True)
        probs = (exp_terms / row_total).astype(jnp.bfloat16)
        mixed = jnp.einsum(
            "hqk,khd->qhd",
            probs,
            split_heads(columns(values, pair_index)),
            preferred_element_type=jnp.float32,
        )
        return (mixed.reshape(row_count, pair_cols), row_max[..., 0], row_total[..., 0])

    mixed_pairs, max_pairs, total_pairs = lax.map(attend, pair_ids)
    attended = merge_pairs(mixed_pairs).astype(jnp.bfloat16)
    branch = jnp.dot(attended, out_full, preferred_element_type=jnp.float32) + out_shift
    normed_second, pull_second = jax.vjp(norm_rows, branch, gains[1], shifts[1])
    middle = hidden + normed_second
    normed_third, pull_third = jax.vjp(norm_rows, middle, gains[2], shifts[2])
    third_low = normed_third.astype(jnp.bfloat16)
    up_pre = jnp.dot(third_low, up_full, preferred_element_type=jnp.float32) + up_shift
    activated, pull_gelu = jax.vjp(exact_gelu, up_pre)
    active_low = activated.astype(jnp.bfloat16)
    down_pre = jnp.dot(active_low, down_full, preferred_element_type=jnp.float32) + down_shift
    normed_fourth, pull_fourth = jax.vjp(norm_rows, down_pre, gains[3], shifts[3])
    output = (middle + normed_fourth).astype(jnp.bfloat16)[None]
    again = (
        lax.all_gather(w_qkv, ("seq", "dp"), axis=0, tiled=True),
        lax.all_gather(w_out, ("seq", "dp"), axis=0, tiled=True),
        lax.all_gather(w_up, ("seq", "dp"), axis=0, tiled=True),
        lax.all_gather(w_down, ("seq", "dp"), axis=0, tiled=True),
    )
    qkv_back, out_back, up_back, down_back = (again[0], again[1], again[2], again[3])
    keep_rows = (own_place < valid).astype(jnp.float32)[:, None]
    grad_out = cotangent[0].astype(jnp.float32) * keep_rows
    grad_down, grad_gain_four, grad_shift_four = pull_fourth(grad_out)
    grad_down_low = grad_down.astype(jnp.bfloat16)
    grad_w_down = contract_rows(active_low, grad_down_low)
    grad_b_down = jnp.sum(grad_down_low.astype(jnp.float32), 0)
    (grad_up,) = pull_gelu(contract_cols(grad_down_low, down_back))
    grad_up_low = grad_up.astype(jnp.bfloat16)
    grad_w_up = contract_rows(third_low, grad_up_low)
    grad_b_up = jnp.sum(grad_up_low.astype(jnp.float32), 0)
    grad_middle_part, grad_gain_three, grad_shift_three = pull_third(
        contract_cols(grad_up_low, up_back)
    )
    grad_middle = grad_out + grad_middle_part
    grad_branch, grad_gain_two, grad_shift_two = pull_second(grad_middle)
    grad_branch_low = grad_branch.astype(jnp.bfloat16)
    grad_w_out = contract_rows(attended, grad_branch_low)
    grad_b_out = jnp.sum(grad_branch_low.astype(jnp.float32), 0)
    grad_attended = contract_cols(grad_branch_low, out_back).astype(jnp.bfloat16)

    def query_side(pair_index):
        scores = pair_scores(columns(queries, pair_index), columns(keys, pair_index))
        probs = kept_probs(
            scores, allowed, max_pairs[pair_index][..., None], total_pairs[pair_index][..., None]
        )
        grad_part = columns(grad_attended, pair_index)
        grad_probs = jnp.einsum(
            "qhd,khd->hqk",
            split_heads(grad_part),
            split_heads(columns(values, pair_index)),
            preferred_element_type=jnp.float32,
        )
        delta = jnp.sum(probs * grad_probs, -1, keepdims=True)
        grad_scores = (RELAX_SCALE * probs * (grad_probs - delta)).astype(jnp.bfloat16)
        grad_query = (
            jnp.einsum(
                "hqk,khd->qhd",
                grad_scores,
                split_heads(columns(keys, pair_index)),
                preferred_element_type=jnp.float32,
            )
            * factor
        )
        return (grad_query.reshape(row_count, pair_cols), grad_scores, probs, delta)

    def both_sides(pair_index):
        grad_query, grad_scores, probs, delta = query_side(pair_index)
        grad_part = columns(grad_attended, pair_index)
        grad_key = (
            jnp.einsum(
                "hqk,qhd->khd",
                grad_scores,
                split_heads(columns(queries, pair_index)),
                preferred_element_type=jnp.float32,
            )
            * factor
        )
        grad_value = jnp.einsum(
            "hqk,qhd->khd",
            probs.astype(jnp.bfloat16),
            split_heads(grad_part),
            preferred_element_type=jnp.float32,
        )
        return (
            grad_query,
            grad_key.reshape(slot_rows, pair_cols),
            grad_value.reshape(slot_rows, pair_cols),
        )

    query_pairs, key_terms, value_terms = lax.map(both_sides, pair_ids)
    key_pairs, value_pairs = (
        lax.psum_scatter(
            key_terms.astype(jnp.bfloat16), "seq", scatter_dimension=1, tiled=True
        ).astype(jnp.float32),
        lax.psum_scatter(
            value_terms.astype(jnp.bfloat16), "seq", scatter_dimension=1, tiled=True
        ).astype(jnp.float32),
    )
    grad_q_low = merge_pairs(query_pairs).astype(jnp.bfloat16)
    grad_k_low = merge_pairs(key_pairs).astype(jnp.bfloat16)
    grad_v_low = merge_pairs(value_pairs).astype(jnp.bfloat16)
    grad_projected = jnp.concatenate([grad_q_low, grad_k_low, grad_v_low], 1)
    grad_w_qkv = contract_rows(normed_low, grad_projected)
    grad_qv = jnp.stack(
        [jnp.sum(grad_q_low.astype(jnp.float32), 0), jnp.sum(grad_v_low.astype(jnp.float32), 0)]
    )
    grad_hidden_part, grad_gain_one, grad_shift_one = pull_first(
        contract_cols(grad_projected, qkv_back)
    )
    input_grad = (grad_middle + grad_hidden_part).astype(jnp.bfloat16)[None]
    grad_gains = jnp.stack([grad_gain_one, grad_gain_two, grad_gain_three, grad_gain_four])
    grad_shifts = jnp.stack([grad_shift_one, grad_shift_two, grad_shift_three, grad_shift_four])
    owned = (
        lax.psum_scatter(grad_w_qkv, ("seq", "dp"), scatter_dimension=0, tiled=True),
        lax.psum_scatter(grad_w_out, ("seq", "dp"), scatter_dimension=0, tiled=True),
        lax.psum_scatter(grad_w_up, ("seq", "dp"), scatter_dimension=0, tiled=True),
        lax.psum_scatter(grad_w_down, ("seq", "dp"), scatter_dimension=0, tiled=True),
        lax.psum_scatter(grad_qv, ("seq", "dp"), scatter_dimension=1, tiled=True),
        lax.psum_scatter(grad_b_out, ("seq", "dp"), scatter_dimension=0, tiled=True),
        lax.psum_scatter(grad_b_up, ("seq", "dp"), scatter_dimension=0, tiled=True),
        lax.psum_scatter(grad_b_down, ("seq", "dp"), scatter_dimension=0, tiled=True),
        lax.psum_scatter(grad_gains, ("seq", "dp"), scatter_dimension=1, tiled=True),
        lax.psum_scatter(grad_shifts, ("seq", "dp"), scatter_dimension=1, tiled=True),
    )
    return (
        output,
        input_grad,
        owned[0],
        owned[4],
        owned[1],
        owned[5],
        owned[2],
        owned[6],
        owned[3],
        owned[7],
        owned[8],
        owned[9],
    )


MESH = pl.DeviceIdType.MESH


def is_small(mesh):
    return mesh.shape["seq"] == 16 and mesh.shape["dp"] == 2


def place():
    seq = lax.axis_index("seq")
    return seq // 8, (seq // 4) % 2, (seq // 2) % 2, seq % 2, lax.axis_index("dp")


def exchange_copies(scatter, src, out, send_sem, recv_sem, own_sem):
    a, b, y, c, x = place()

    def peer(k):
        return lax.rem(a + k // 2, 2), lax.rem(y + k % 2, 2)

    def device(k):
        pa, py = peer(k)
        return (pa * 8 + b * 4 + py * 2 + c, x)

    def source(k):
        pa, py = peer(k)
        return src.at[pa * 2 + py] if scatter else src.at[pa, :, py]

    def target(k):
        pa, py = peer(k)
        return out.at[pa, :, py] if scatter else out.at[pa * 2 + py]

    def copy(k, dst):
        return pltpu.make_async_remote_copy(
            src_ref=source(k), dst_ref=target(dst), send_sem=send_sem.at[k], recv_sem=recv_sem.at[k],
            device_id=device(k), device_id_type=MESH)

    def greet():
        barrier = pltpu.get_barrier_semaphore()
        for k in range(1, 4):
            pl.semaphore_signal(barrier, inc=1, device_id=device(k), device_id_type=MESH)

    def run():
        own = pltpu.make_async_copy(source(0), target(0), own_sem)
        own.start()
        pl.semaphore_wait(pltpu.get_barrier_semaphore(), 3)
        for k in (3, 2, 1):
            copy(k, 0).start()
        own.wait()
        for k in (3, 2, 1):
            copy(k, k).wait_recv()
        for k in (3, 2, 1):
            copy(k, 0).wait_send()

    return greet, run


def row_block(i, j):
    _, b, _, c, _ = place()
    return pl.ds(pl.multiple_of(lax.rem(b + i, 2) * 256 + lax.rem(c + j, 2) * 128, 128), 128)


def to_heads_kernel(rows_ref, out, src, *sems):
    greet, run = exchange_copies(True, src, out, *sems)
    greet()
    low = src.shape[2] - 128
    for g in range(4):
        values = slice(low * 2 + g * HD, low * 2 + g * HD + HD)
        for i in range(2):
            if low:
                for j in range(2):
                    src[g, i, j * 128:j * 128 + 128] = rows_ref[row_block(i, j), g * 128:g * 128 + 128]
            src[g, i, low:] = jnp.concatenate([rows_ref[row_block(i, j), values] for j in range(2)], 1)
    run()


def from_heads_kernel(heads_ref, out, got, *sems):
    greet, run = exchange_copies(False, heads_ref, got, *sems)
    greet()
    run()
    low = got.shape[2] - 128
    c = place()[3]
    for i in range(2):
        if low:
            for j in range(2):
                for g in range(4):
                    out[row_block(i, j), g * 128:g * 128 + 128] = got[g, i, j * 128:j * 128 + 128]
        for g in (0, 2):
            left, right = got[g, i, low:], got[g + 1, i, low:]
            cols = slice(low * 2 + g * HD, low * 2 + g * HD + 128)
            for j in range(2):
                lanes = slice(j * HD, j * HD + HD)
                out[row_block(i, j), cols] = jnp.concatenate([left[:, lanes], right[:, lanes]], 1)


def exchange(blocks, scatter, cid):
    vm = pl.BlockSpec(memory_space=pltpu.VMEM)
    rows = blocks.shape[-1] // 2 if scatter else blocks.shape[-2]
    shape, held = (2, 2, 2, rows, 128), (4, 2, rows, 128)
    return pl.pallas_call(
        to_heads_kernel if scatter else from_heads_kernel,
        out_shape=jax.ShapeDtypeStruct(shape if scatter else (512, rows * 2), blocks.dtype),
        in_specs=[vm], out_specs=vm,
        scratch_shapes=[pltpu.VMEM(held, blocks.dtype), pltpu.SemaphoreType.DMA((4,)), pltpu.SemaphoreType.DMA((4,)),
                        pltpu.SemaphoreType.DMA],
        compiler_params=pltpu.CompilerParams(collective_id=cid, has_side_effects=True),
        cost_estimate=pl.CostEstimate(flops=0, bytes_accessed=rows * 100000, transcendentals=0),
        name="to_heads" if scatter else "from_heads",
    )(blocks)


def dot_nt(a, b):
    return lax.dot_general(a, b, (((1,), (1,)), ((), ())), preferred_element_type=jnp.float32)


def dot_nn(a, b):
    return jnp.dot(a, b, preferred_element_type=jnp.float32)


BQ = 256
MASKED = -1e30


def load_heads(valid, packed, q_ref, k_ref):
    rows = q_ref.shape[0]
    qk = packed[:, :256].reshape(rows, 128)
    kq = jnp.concatenate([qk[:, 64:], qk[:, :64]], axis=1)
    lane = lax.broadcasted_iota(jnp.int32, (rows, 128), 1)
    spot = lax.broadcasted_iota(jnp.int32, (rows, 128), 0)
    past = jnp.where(spot < valid, 0.0, MASKED)
    q_ref[...] = jnp.where(lane < 64, qk.astype(jnp.float32), jnp.where(lane == 64, 1.0, 0.0)).astype(jnp.bfloat16)
    k_ref[...] = jnp.where(lane < 64, kq.astype(jnp.float32), jnp.where(lane == 64, past, 0.0)).astype(jnp.bfloat16)


def unpack_rows(halves):
    n = halves.shape[0]
    return jnp.concatenate([halves[:, :, :64], halves[:, :, 64:]], axis=1).reshape(n * 256, 64)


def block_probs(q_ref, k_ref, i):
    n = (i + 1) * BQ
    scores = dot_nt(k_ref[:n], q_ref[i * BQ:n])
    key = lax.broadcasted_iota(jnp.int32, (BQ, BQ), 0)
    query = lax.broadcasted_iota(jnp.int32, (BQ, BQ), 1)
    corner = jnp.where(key <= query, scores[n - BQ:], MASKED)
    scores = jnp.concatenate([scores[:n - BQ], corner], axis=0) if i else corner
    top = jnp.max(scores, axis=0, keepdims=True)
    terms = jnp.exp((scores - top) * 0.125)
    return terms, 1.0 / jnp.sum(terms, axis=0, keepdims=True)


def attend_kernel(valid_ref, packed, out_ref, q_ref, k_ref, vt_ref):
    load_heads(valid_ref[0], packed, q_ref, k_ref)
    unit = jnp.where(
        lax.broadcasted_iota(jnp.int32, (64, 64), 0) == lax.broadcasted_iota(jnp.int32, (64, 64), 1), 1.0, 0.0
    ).astype(jnp.bfloat16)
    vt_ref[...] = dot_nt(unit, unpack_rows(packed[:, 256:])).astype(jnp.bfloat16)
    for i in range(q_ref.shape[0] // BQ):
        n = (i + 1) * BQ
        terms, scale = block_probs(q_ref, k_ref, i)
        probs = (terms * scale).astype(jnp.bfloat16)
        mixed = dot_nn(vt_ref[:, :n], probs).T
        out_ref[i] = jnp.concatenate([mixed[:128], mixed[128:]], axis=1).astype(jnp.bfloat16)


def attend_back_kernel(valid_ref, packed, grad, out_ref, q_ref, k_ref, v_ref, g_ref, kt_ref, dk_ref, dv_ref):
    load_heads(valid_ref[0], packed, q_ref, k_ref)
    v_ref[...] = unpack_rows(packed[:, 256:])
    g_ref[...] = unpack_rows(grad[...])
    unit = jnp.where(
        lax.broadcasted_iota(jnp.int32, (64, 128), 0) == lax.broadcasted_iota(jnp.int32, (64, 128), 1), 1.0, 0.0
    ).astype(jnp.bfloat16)
    kt_ref[...] = dot_nt(unit, k_ref[...]).astype(jnp.bfloat16)
    dk_ref[...] = jnp.zeros_like(dk_ref)
    dv_ref[...] = jnp.zeros_like(dv_ref)
    blocks = q_ref.shape[0] // BQ
    for i in range(blocks):
        n = (i + 1) * BQ
        terms, scale = block_probs(q_ref, k_ref, i)
        probs = terms * scale
        grad_probs = dot_nt(v_ref[:n], g_ref[i * BQ:n])
        delta = jnp.sum(probs * grad_probs, axis=0, keepdims=True)
        grad_scores = (probs * (grad_probs - delta)).astype(jnp.bfloat16)
        grad_query = dot_nn(kt_ref[:, :n], grad_scores).T * 0.125
        out_ref[i, :256, :64] = grad_query.astype(jnp.bfloat16)
        dk_ref[:n] += dot_nn(grad_scores, q_ref[i * BQ:n])
        dv_ref[:n] += dot_nn(probs.astype(jnp.bfloat16), g_ref[i * BQ:n])
    for i in range(blocks):
        rows = slice(i * BQ, (i + 1) * BQ)
        out_ref[i, :256, 64:] = (dk_ref[rows, :64] * 0.125).astype(jnp.bfloat16)
        value = dv_ref[rows].astype(jnp.bfloat16)
        out_ref[i, 256:] = jnp.concatenate([value[:128], value[128:]], axis=1)


def attend(valid, packed):
    rows = packed.shape[0] * 256
    vm = pl.BlockSpec(memory_space=pltpu.VMEM)
    return pl.pallas_call(
        attend_kernel,
        out_shape=jax.ShapeDtypeStruct((packed.shape[0], 128, 128), jnp.bfloat16),
        in_specs=[pl.BlockSpec(memory_space=pltpu.SMEM), vm], out_specs=vm,
        scratch_shapes=[pltpu.VMEM((rows, 128), jnp.bfloat16)] * 2 + [pltpu.VMEM((64, rows), jnp.bfloat16)],
        compiler_params=pltpu.CompilerParams(vmem_limit_bytes=48 << 20),
        name="attend",
    )(valid, packed)


def attend_back(valid, packed, grad):
    rows = packed.shape[0] * 256
    vm = pl.BlockSpec(memory_space=pltpu.VMEM)
    return pl.pallas_call(
        attend_back_kernel,
        out_shape=jax.ShapeDtypeStruct(packed.shape, jnp.bfloat16),
        in_specs=[pl.BlockSpec(memory_space=pltpu.SMEM), vm, vm], out_specs=vm,
        scratch_shapes=[pltpu.VMEM((rows, 128), jnp.bfloat16)] * 2 + [pltpu.VMEM((rows, 64), jnp.bfloat16)] * 2
        + [pltpu.VMEM((64, rows), jnp.bfloat16), pltpu.VMEM((rows, 128), jnp.float32), pltpu.VMEM((rows, 64), jnp.float32)],
        compiler_params=pltpu.CompilerParams(vmem_limit_bytes=48 << 20),
        name="attend_back",
    )(valid, packed, grad)


def flip(bits, block):
    return lax.ppermute(block, "seq", [(s, s ^ bits) for s in range(16)])


flip_a, flip_y = (functools.partial(flip, bits) for bits in (8, 2))


def flip_x(block):
    return lax.ppermute(block, "dp", [(0, 1), (1, 0)])


def after(value, *others):
    return lax.optimization_barrier((value,) + others)[0]


def pick(block, index, axis, keepdims=False):
    return lax.dynamic_index_in_dim(block, index, axis, keepdims=keepdims)


def cube_one(flip_one, block):
    return jnp.concatenate([block, flip_one(block)], 0)


def arrange_kernel(count, spot_ref, *refs):
    for k in range(count):
        block, out = refs[k], refs[count + k]
        if len(out.shape) == 7:
            for i in range(2):
                for j in range(2):
                    out[0, i, 0, j, 0] = block[0, i, j]
        else:
            out[0, 0, 0] = block[0]


def arrange(spot, blocks):
    def coords(i, r, y_first):
        second, first, a = i // 4, (i // 2) % 2, i % 2
        y, x = (first, second) if y_first else (second, first)
        return lax.rem(r[0] + a, 2), lax.rem(r[1] + y, 2), lax.rem(r[2] + x, 2)

    def specs(block, y_first):
        shape = block.shape
        if len(shape) == 5:
            def out_place(i, r):
                a, y, x = coords(i, r, y_first)
                return a, 0, y, 0, x, 0, 0
            return (pl.BlockSpec((1,) + shape[1:], lambda i, r: (i, 0, 0, 0, 0)),
                    pl.BlockSpec((1, 2, 1, 2, 1) + shape[3:], out_place),
                    jax.ShapeDtypeStruct((2,) * 5 + shape[3:], block.dtype))

        def out_place(i, r):
            return coords(i, r, y_first) + (0, 0)
        return (pl.BlockSpec((1,) + shape[1:], lambda i, r: (i, 0, 0)),
                pl.BlockSpec((1, 1, 1) + shape[1:], out_place),
                jax.ShapeDtypeStruct((2, 2, 2) + shape[1:], block.dtype))

    made = [specs(*entry) for entry in blocks]
    return pl.pallas_call(
        functools.partial(arrange_kernel, len(blocks)),
        out_shape=tuple(m[2] for m in made),
        grid_spec=pltpu.PrefetchScalarGridSpec(
            num_scalar_prefetch=1, grid=(8,), in_specs=[m[0] for m in made], out_specs=tuple(m[1] for m in made)),
        compiler_params=pltpu.CompilerParams(vmem_limit_bytes=32 << 20),
        cost_estimate=pl.CostEstimate(flops=0, bytes_accessed=8 << 20, transcendentals=0),
        name="arrange",
    )(spot, *[entry[0] for entry in blocks])


def add_low(mine, other):
    return (mine.astype(jnp.float32) + other.astype(jnp.float32)).astype(jnp.bfloat16)


def fold(terms, flip_one, index, axis):
    return add_low(pick(terms, index, axis, True), flip_one(pick(terms, 1 - index, axis, True)))


def reduce_kernel(q_ref, o_ref, u_ref, *refs):
    vec_refs, (out_q, ro, out_u, vec, rq, gu, r1q, t2q, r2q, t3q, r3q, fq, gq, r1o, t2o, r2o, t3o, r3o,
               run, got, send_sem, recv_sem) = refs[:12], refs[12:]
    a, b, y, c, x = place()
    f32, bf16 = jnp.float32, jnp.bfloat16
    barrier = pltpu.get_barrier_semaphore()

    def at(pa, pb, py, pc, px):
        return (pa * 8 + pb * 4 + py * 2 + pc, px)

    to_x, to_y, to_a = at(a, b, y, c, 1 - x), at(a, b, 1 - y, c, x), at(1 - a, b, y, c, x)
    ranks = [(lax.rem(b + k // 2, 2), lax.rem(c + k % 2, 2)) for k in range(4)]
    to_rank = [at(a, ranks[k][0], y, ranks[k][1], x) for k in range(4)]
    to_b, to_c = to_rank[2], to_rank[1]
    for dev in [to_x, to_y, to_a] + to_rank[1:]:
        pl.semaphore_signal(barrier, inc=1, device_id=dev, device_id_type=MESH)
    for pb in range(2):
        for j in range(4):
            for row, cols in ((0, slice(j * 128, j * 128 + HD)), (1, slice(512 + j * HD, 512 + j * HD + HD))):
                piece = vec_refs[0][:, cols]
                pair = [jnp.where((b == pb) & (c == pc), piece, 0.0) for pc in range(2)]
                h = head_of(j // 2, pb, j % 2, 0) * HD
                run[0, row:row + 1, h:h + 128] = jnp.concatenate(pair, 1)
            for pc in range(2):
                col = head_of(j // 2, pb, j % 2, pc) * 256
                piece = vec_refs[1][:, j * 256:j * 256 + 256]
                run[0, 12 + col // 1024:13 + col // 1024, col % 1024:col % 1024 + 256] = jnp.where(
                    (b == pb) & (c == pc), piece, 0.0)
    for k in range(2, 12):
        run[0, k:k + 1] = vec_refs[k][...]
    pl.semaphore_wait(barrier, 6)

    made = []

    def remote(src, dst, dev):
        k = len(made)
        made.append(pltpu.make_async_remote_copy(
            src_ref=src, dst_ref=dst, send_sem=send_sem.at[k], recv_sem=recv_sem.at[k],
            device_id=dev, device_id_type=MESH))
        return made[-1]

    def low(*values):
        return sum(v.astype(f32) for v in values)

    places = [1 - a, a]
    halves = [slice(0, 512), slice(512, 1024)]
    lateral = [(to_x, to_y), (to_y, to_x)]

    q1, q2, o1, o2 = {}, {}, {}, {}
    for i in range(2):
        for s in range(2):
            p = places[i]
            q1[s, i] = remote(q_ref.at[p, 0, :, :, 1 - x] if s == 0 else q_ref.at[p, 1, 1 - y], r1q.at[s, i], lateral[s][0])
            o1[s, i] = remote(o_ref.at[p, :, 1 - x, :, halves[0]] if s == 0 else o_ref.at[p, 1 - y, :, :, halves[1]],
                              r1o.at[s, i], lateral[s][0])
            q2[s, i] = remote(t2q.at[s, i], r2q.at[s, i], lateral[s][1])
            o2[s, i] = remote(t2o.at[s, i], r2o.at[s, i], lateral[s][1])
    q3 = [remote(t3q.at[s], r3q.at[s], to_a) for s in range(2)]
    o3 = [remote(t3o.at[s], r3o.at[s], to_a) for s in range(2)]
    qr = [remote(fq.at[ranks[k][0], ranks[k][1]], gq.at[k - 1], to_rank[k]) for k in range(1, 4)]
    ur = [remote(u_ref.at[ranks[k][0], ranks[k][1]], gu.at[b, c], to_rank[k]) for k in range(1, 4)]
    vs = [remote(run.at[k], got.at[k], dev) for k, dev in enumerate((to_x, to_y, to_a, to_b, to_c))]

    def next_sum(k):
        vs[k].wait_recv()
        if k < 4:
            run[k + 1] = run[k] + got[k]
            vs[k + 1].start()
        else:
            vec[...] = run[k] + got[k]

    vs[0].start()
    for s in range(2):
        q1[s, 0].start()
        o1[s, 0].start()
    for k in (3, 2, 1):
        ur[k - 1].start()
    for s in range(2):
        o1[s, 1].start()

    def q_terms(s, i, far):
        p = places[i]
        if s == 0:
            v = 1 - y if far else y
            return q_ref[p, 0, v, :, x], r1q[0, i, v]
        v = 1 - x if far else x
        return q_ref[p, 1, y, :, v], r1q[1, i, :, v]

    def o_terms(s, i, far):
        p = places[i]
        if s == 0:
            v = 1 - y if far else y
            return o_ref[p, v, x, :, halves[0]], r1o[0, i, v]
        v = 1 - x if far else x
        return o_ref[p, y, v, :, halves[1]], r1o[1, i, v]

    for i in range(2):
        for s in range(2):
            q1[s, i].wait_recv()
            t2q[s, i] = low(*q_terms(s, i, True)).astype(bf16)
            q2[s, i].start()
            o1[s, i].wait_recv()
            t2o[s, i] = low(*o_terms(s, i, True)).astype(bf16)
            o2[s, i].start()
        if i == 0:
            for s in range(2):
                q1[s, 1].start()
            next_sum(0)
            for s in range(2):
                q2[s, 0].wait_recv()
                t3q[s] = low(*q_terms(s, 0, False), r2q[s, 0]).astype(bf16)
                q3[s].start()
                o2[s, 0].wait_recv()
                t3o[s] = low(*o_terms(s, 0, False), r2o[s, 0]).astype(bf16)
                o3[s].start()
    next_sum(1)
    for s in range(2):
        q2[s, 1].wait_recv()
        o2[s, 1].wait_recv()
        q3[s].wait_recv()
        total = low(*q_terms(s, 1, False), r2q[s, 1], r3q[s])
        fq[s] = total.astype(bf16)
        for j in range(2):
            @pl.when((b == s) & (c == j))
            def _():
                rq[s, j] = total[j]
        o3[s].wait_recv()
        ro[:, halves[s]] = low(*o_terms(s, 1, False), r2o[s, 1], r3o[s])
    for k in (3, 2, 1):
        qr[k - 1].start()
    next_sum(2)
    gu[b, c] = u_ref[b, c]
    for k in (1, 2, 3):
        ur[k - 1].wait_recv()
    next_sum(3)
    for k in (1, 2, 3):
        pb, pc = ranks[k]
        qr[k - 1].wait_recv()
        rq[pb, pc] = gq[k - 1].astype(f32)
    for pb in range(2):
        for j in range(4):
            zero, one = rq[pb, 0], rq[pb, 1]
            h = head_of(j // 2, pb, j % 2, 0) * HD
            q, k = slice(j * 128, j * 128 + HD), slice(j * 128 + HD, j * 128 + 128)
            v = slice(512 + j * HD, 512 + j * HD + HD)
            for t, cols in enumerate((q, k, v)):
                out_q[:, t * 1024 + h:t * 1024 + h + 128] = jnp.concatenate([zero[:, cols], one[:, cols]], 1)
            for pc in range(2):
                col = head_of(j // 2, pb, j % 2, pc) * 256
                out_u[:, col:col + 256] = gu[pb, pc, :, j * 256:j * 256 + 256].astype(f32)
    next_sum(4)
    for copy in made:
        copy.wait_send()


def reduce_all(gw_qkv, gw_out, up_sum, vectors, cid):
    f32, bf16 = jnp.float32, jnp.bfloat16
    V = pltpu.VMEM
    vm = pl.BlockSpec(memory_space=V)
    S = jax.ShapeDtypeStruct
    q, o, u = gw_qkv.shape[5:], (gw_out.shape[3], 512), up_sum.shape
    scratch = [
        V((2, 2) + q, f32), V(u, bf16),
        V((2, 2, 2, 2) + q, bf16), V((2, 2, 2) + q, bf16), V((2, 2, 2) + q, bf16), V((2, 2) + q, bf16), V((2, 2) + q, bf16),
        V((2, 2) + q, bf16), V((3,) + q, bf16),
        V((2, 2, 2) + o, bf16), V((2, 2) + o, bf16), V((2, 2) + o, bf16), V((2,) + o, bf16), V((2,) + o, bf16),
        V((5, 16, 1024), f32), V((5, 16, 1024), f32),
        pltpu.SemaphoreType.DMA((32,)), pltpu.SemaphoreType.DMA((32,))]
    return pl.pallas_call(
        reduce_kernel,
        out_shape=(S((q[0], 4 * q[1]), f32), S((o[0], 1024), f32), S((u[2], 4 * u[3]), f32), S((16, 1024), f32)),
        in_specs=[vm] * 15, out_specs=(vm,) * 4, scratch_shapes=scratch,
        compiler_params=pltpu.CompilerParams(collective_id=cid, has_side_effects=True, vmem_limit_bytes=40 << 20),
        name="reduce_all",
    )(gw_qkv, gw_out, up_sum, *vectors)


def qk_columns(head):
    return slice(head * HD, head * HD + HD), slice(1024 + head * HD, 1024 + head * HD + HD), slice(2048 + head * HD, 2048 + head * HD + HD)


def head_of(a, b, y, c):
    return a * 8 + b * 4 + y * 2 + c


def start_kernel(q_hbm, u_hbm, o_in, t_in, d_in, v_in, wq, wo, up, rows, vec, down, q_in, u_in, q_src, u_src, send_sem, recv_sem, own_sem):
    a, b, y, c, x = place()
    barrier = pltpu.get_barrier_semaphore()

    def at(pa, pb, py, pc, px):
        return (pa * 8 + pb * 4 + py * 2 + pc, px)

    to_x, to_y, to_a = at(a, b, y, c, 1 - x), at(a, b, 1 - y, c, x), at(1 - a, b, y, c, x)
    ranks = [(lax.rem(b + k // 2, 2), lax.rem(c + k % 2, 2)) for k in range(4)]
    to_rank = [at(a, pb, y, pc, x) for pb, pc in ranks]
    for dev in [to_x, to_y, to_a] + to_rank[1:]:
        pl.semaphore_signal(barrier, inc=1, device_id=dev, device_id_type=MESH)

    loads = [pltpu.make_async_copy(q_hbm, q_in, own_sem.at[6]), pltpu.make_async_copy(u_hbm, u_in, own_sem.at[7])]
    for copy in loads:
        copy.start()
    for copy in loads:
        copy.wait()

    for pb in range(2):
        for pc in range(2):
            for j in range(4):
                q, k, v = qk_columns(head_of(j // 2, pb, j % 2, pc))
                q_src[pb, pc, :, j * 128:j * 128 + 128] = jnp.concatenate([q_in[:, q], q_in[:, k]], 1)
            for j in range(2):
                v0 = qk_columns(head_of(j, pb, 0, pc))[2]
                v1 = qk_columns(head_of(j, pb, 1, pc))[2]
                q_src[pb, pc, :, 512 + j * 128:640 + j * 128] = jnp.concatenate([q_in[:, v0], q_in[:, v1]], 1)
            for j in range(4):
                col = (head_of(j // 2, pb, j % 2, pc)) * 256
                u_src[pb, pc, :, j * 256:j * 256 + 256] = u_in[:, col:col + 256]
    own = [pltpu.make_async_copy(src, dst, own_sem.at[k]) for k, (src, dst) in enumerate((
        (q_src.at[b, c], wq.at[a, b, y, c, x]), (u_src.at[b, c], up.at[0, b, c]), (o_in, wo.at[a, y, x]),
        (t_in, rows.at[0]), (v_in, vec.at[a, b, y, c, x]), (d_in, down.at[0])))]
    for copy in own:
        copy.start()
    pl.semaphore_wait(barrier, 6)

    made = []

    def remote(src, dst, dev):
        k = len(made)
        made.append(pltpu.make_async_remote_copy(
            src_ref=src, dst_ref=dst, send_sem=send_sem.at[k], recv_sem=recv_sem.at[k],
            device_id=dev, device_id_type=MESH))
        return made[-1]

    places = [a, 1 - a]
    halves = [slice(0, 512), slice(512, 1024)]
    lateral = [(to_y, to_x), (to_x, to_y)]

    def same(ref, dev):
        return remote(ref, ref, dev)

    q_rank = [remote(q_src.at[ranks[k][0], ranks[k][1]], wq.at[a, b, y, c, x], to_rank[k]) for k in range(1, 4)]
    u_rank = [remote(u_src.at[ranks[k][0], ranks[k][1]], up.at[0, b, c], to_rank[k]) for k in range(1, 4)]
    v_rank = [remote(v_in, vec.at[a, b, y, c, x], to_rank[k]) for k in range(1, 4)]
    t_core, t_near = remote(t_in, rows.at[1], to_rank[1]), remote(t_in, rows.at[2], to_rank[2])
    t_far = remote(rows.at[2], rows.at[3], to_rank[1])
    u_cube, d_cube = remote(up.at[0], up.at[1], to_a), remote(d_in, down.at[1], to_a)
    v_cube = [same(vec.at[a, :, y, :, x], to_a), same(vec.at[:, :, y, :, x], to_y), same(vec.at[:, :, :, :, x], to_x)]
    q_cube = [same(wq.at[a, s, y, :, x], to_a) for s in range(2)]
    o_cube = [remote(o_in.at[:, halves[s]], wo.at[a, y, x, :, halves[s]], to_a) for s in range(2)]
    q_side, o_side = {}, {}
    for i in range(2):
        for s in range(2):
            one, two = lateral[s]
            oy, ox = (1 - y, x) if s == 0 else (y, 1 - x)
            p = places[i]
            mine, theirs = wq.at[p, s, y, :, x], wq.at[p, s, oy, :, ox]
            q_side[s, i] = (same(mine, one), same(mine, two), same(theirs, two))
            mine, theirs = wo.at[p, y, x, :, halves[s]], wo.at[p, oy, ox, :, halves[s]]
            first = o_in.at[:, halves[s]] if i == 0 else mine
            o_side[s, i] = (remote(first, mine, one), remote(first, mine, two), same(theirs, two))

    for k in (2, 1, 0):
        q_rank[k].start()
        v_rank[k].start()
    for s in range(2):
        o_cube[s].start()
        o_side[s, 0][0].start()
        o_side[s, 0][1].start()
    t_near.start()
    t_core.start()
    own[0].wait()
    for copy in q_rank:
        copy.wait_recv()
    for s in range(2):
        q_cube[s].start()
        q_side[s, 0][0].start()
        q_side[s, 0][1].start()
    own[4].wait()
    for copy in v_rank:
        copy.wait_recv()
    v_cube[0].start()
    for k in (2, 1, 0):
        u_rank[k].start()
    for s in range(2):
        o_side[s, 0][0].wait_recv()
        o_side[s, 0][2].start()
    for s in range(2):
        o_cube[s].wait_recv()
        o_side[s, 1][0].start()
        o_side[s, 1][1].start()
    t_near.wait_recv()
    t_far.start()
    for s in range(2):
        q_side[s, 0][0].wait_recv()
        q_side[s, 0][2].start()
    for s in range(2):
        q_cube[s].wait_recv()
        q_side[s, 1][0].start()
        q_side[s, 1][1].start()
    v_cube[0].wait_recv()
    v_cube[1].start()
    own[1].wait()
    for copy in u_rank:
        copy.wait_recv()
    u_cube.start()
    d_cube.start()
    for s in range(2):
        o_side[s, 1][0].wait_recv()
        o_side[s, 1][2].start()
    v_cube[1].wait_recv()
    v_cube[2].start()
    for s in range(2):
        q_side[s, 1][0].wait_recv()
        q_side[s, 1][2].start()
    v_cube[2].wait_recv()
    t_core.wait_recv()
    t_far.wait_recv()
    for i in range(2):
        for s in range(2):
            for k in (1, 2):
                q_side[s, i][k].wait_recv()
                o_side[s, i][k].wait_recv()
    u_cube.wait_recv()
    d_cube.wait_recv()
    for k in (2, 3, 5):
        own[k].wait()
    for copy in made:
        copy.wait_send()


def start_gather(w_qkv, w_up, w_out, tokens, w_down, vectors, cid):
    bf16 = jnp.bfloat16
    S = lambda *shape: jax.ShapeDtypeStruct(shape, bf16)
    vm, anywhere = pl.BlockSpec(memory_space=pltpu.VMEM), pl.BlockSpec(memory_space=pl.ANY)
    return pl.pallas_call(
        start_kernel,
        out_shape=(S(2, 2, 2, 2, 2, 32, 768), S(2, 2, 2, 32, 1024), S(2, 2, 2, 32, 1024), S(4, 128, 1024),
                   S(2, 2, 2, 2, 2, 16, 128), S(2, 128, 1024)),
        in_specs=[anywhere] * 5 + [vm], out_specs=(anywhere,) * 6,
        scratch_shapes=[
            pltpu.VMEM(w_qkv.shape, bf16), pltpu.VMEM(w_up.shape, bf16),
            pltpu.VMEM((2, 2, 32, 768), bf16), pltpu.VMEM((2, 2, 32, 1024), bf16),
            pltpu.SemaphoreType.DMA((48,)), pltpu.SemaphoreType.DMA((48,)), pltpu.SemaphoreType.DMA((8,))],
        compiler_params=pltpu.CompilerParams(collective_id=cid, has_side_effects=True, vmem_limit_bytes=32 << 20),
        cost_estimate=pl.CostEstimate(flops=0, bytes_accessed=100 << 20, transcendentals=0),
        name="start_gather",
    )(w_qkv, w_up, w_out, tokens, w_down, vectors)


PIECE = 32


def rows_kernel(step, gather, count_in, count_out, part, *refs):
    ins, outs = refs[:count_in], refs[count_in:count_in + count_out]
    rest = refs[count_in + count_out:]
    rows = rest[0] if gather else None
    got_far, got_near, sums, got_sums, send_sem, recv_sem = rest[-6:]
    a, b, y, c, x = place()

    def at(pb, pc):
        return (a * 8 + pb * 4 + y * 2 + pc, x)

    to_b, to_core = at(1 - b, c), at(b, 1 - c)
    barrier = pltpu.get_barrier_semaphore()
    for dev in (to_b, to_core):
        pl.semaphore_signal(barrier, inc=1, device_id=dev, device_id_type=MESH)
    pl.semaphore_wait(barrier, 2)
    pieces = part.shape[2] // PIECE

    def span(r):
        return pl.ds(pl.multiple_of(r * PIECE, PIECE), PIECE)

    def remote(kind, r, src, dst, dev):
        return pltpu.make_async_remote_copy(
            src_ref=src, dst_ref=dst, send_sem=send_sem.at[kind, r], recv_sem=recv_sem.at[kind, r],
            device_id=dev, device_id_type=MESH)

    def far(r):
        return remote(0, r, part.at[1, 1, span(r)], got_far.at[span(r)], to_core)

    def near(r):
        return remote(1, r, part.at[0, 1, span(r)], got_near.at[span(r)], to_core)

    def across(r):
        return remote(2, r, sums.at[span(r)], got_sums.at[span(r)], to_b)

    def row_near(r):
        return remote(3, r, rows.at[0, span(r)], rows.at[2, span(r)], to_b)

    def row_core(r):
        return remote(4, r, rows.at[0, span(r)], rows.at[1, span(r)], to_core)

    def row_far(r):
        return remote(5, r, rows.at[2, span(r)], rows.at[3, span(r)], to_core)

    for r in range(pieces):
        far(r).start()
    for r in range(pieces):
        near(r).start()

    def send_across(r, _):
        far(r).wait_recv()
        sums[span(r)] = (part[1, 0, span(r)] + got_far[span(r)]).astype(jnp.bfloat16)
        across(r).start()
        return 0

    lax.fori_loop(0, pieces, send_across, 0)
    for ref in outs:
        if ref.shape[0] == 1:
            ref[...] = jnp.zeros_like(ref)

    def take(r, _):
        near(r).wait_recv()
        across(r).wait_recv()
        total = part[0, 0, span(r)] + got_near[span(r)] + got_sums[span(r)].astype(jnp.float32)
        piece = step(span(r), total, ins, outs)
        if gather:
            rows[0, span(r)] = piece
            row_near(r).start()
            row_core(r).start()
        return 0

    lax.fori_loop(0, pieces, take, 0)

    def relay(r, _):
        row_near(r).wait_recv()
        row_far(r).start()
        return 0

    def finish(r, _):
        if gather:
            row_core(r).wait_recv()
            row_far(r).wait_recv()
            row_near(r).wait_send()
            row_core(r).wait_send()
            row_far(r).wait_send()
        far(r).wait_send()
        near(r).wait_send()
        across(r).wait_send()
        return 0

    if gather:
        lax.fori_loop(0, pieces, relay, 0)
    lax.fori_loop(0, pieces, finish, 0)


def sum_rows(step, part, ins, outs, gather, cid):
    rows, n = part.shape[0] // 4, part.shape[1]
    vm = pl.BlockSpec(memory_space=pltpu.VMEM)
    shapes = tuple(outs) + ((jax.ShapeDtypeStruct((4, rows, n), jnp.bfloat16),) if gather else ())
    V = pltpu.VMEM
    return pl.pallas_call(
        functools.partial(rows_kernel, step, gather, len(ins), len(outs)),
        out_shape=shapes, in_specs=[vm] * (1 + len(ins)), out_specs=(vm,) * len(shapes),
        scratch_shapes=[V((rows, n), jnp.float32), V((rows, n), jnp.float32), V((rows, n), jnp.bfloat16), V((rows, n), jnp.bfloat16),
                        pltpu.SemaphoreType.DMA((6, rows // PIECE)), pltpu.SemaphoreType.DMA((6, rows // PIECE))],
        compiler_params=pltpu.CompilerParams(collective_id=cid, has_side_effects=True, vmem_limit_bytes=32 << 20),
        cost_estimate=pl.CostEstimate(flops=0, bytes_accessed=50 << 20, transcendentals=0),
        name="sum_rows",
    )(part.reshape(2, 2, rows, n), *ins)


def norm_vectors(vectors, k):
    return vectors[4 + k:5 + k], vectors[8 + k:9 + k]


def attended_step(span, total, ins, outs):
    tokens, vectors = ins
    branch = total + vectors[2:3]
    middle = tokens[span].astype(jnp.float32) + norm_rows(branch, *norm_vectors(vectors, 1))
    outs[0][span] = branch
    outs[1][span] = middle
    return norm_rows(middle, *norm_vectors(vectors, 2)).astype(jnp.bfloat16)


def output_step(span, total, ins, outs):
    middle, grad_out, vectors = ins
    normed, pull = jax.vjp(norm_rows, total + vectors[3:4], *norm_vectors(vectors, 3))
    outs[0][span] = (middle[span] + normed).astype(jnp.bfloat16)
    grad_down, grad_gain, grad_shift = pull(grad_out[span])
    grad_down = grad_down.astype(jnp.bfloat16)
    outs[1][...] += grad_gain
    outs[2][...] += grad_shift
    outs[3][...] += jnp.sum(grad_down.astype(jnp.float32), 0, keepdims=True)
    return grad_down


def middle_step(span, total, ins, outs):
    middle, branch, grad_out, vectors = ins
    _, pull = jax.vjp(norm_rows, middle[span], *norm_vectors(vectors, 2))
    part, grad_gain2, grad_shift2 = pull(total)
    grad_middle = grad_out[span] + part
    _, pull = jax.vjp(norm_rows, branch[span], *norm_vectors(vectors, 1))
    grad_branch, grad_gain1, grad_shift1 = pull(grad_middle)
    grad_branch = grad_branch.astype(jnp.bfloat16)
    outs[0][span] = grad_middle
    for ref, value in zip(outs[1:], (grad_gain2, grad_shift2, grad_gain1, grad_shift1,
                                     jnp.sum(grad_branch.astype(jnp.float32), 0, keepdims=True))):
        ref[...] += value
    return grad_branch


def input_step(span, total, ins, outs):
    tokens, grad_middle, vectors = ins
    _, pull = jax.vjp(norm_rows, tokens[span].astype(jnp.float32), *norm_vectors(vectors, 0))
    part, grad_gain, grad_shift = pull(total)
    outs[0][span] = (grad_middle[span] + part).astype(jnp.bfloat16)
    outs[1][...] += grad_gain
    outs[2][...] += grad_shift


def fast_body(tokens, cotangent, lengths, assign, w_qkv, qv_bias, w_out, out_bias, w_up, up_bias, w_down, down_bias,
              norm_gain, norm_shift):
    bf16, f32 = jnp.bfloat16, jnp.float32
    a, b, y, c, x = place()
    spot = jnp.stack([a, y, x]).astype(jnp.int32)
    width = tokens.shape[2]
    place_two = jnp.arange(2, dtype=jnp.int32)
    sequence = jnp.sum(jnp.where(place_two == x, assign.astype(jnp.int32), 0))
    valid = jnp.sum(jnp.where(place_two == sequence, lengths.astype(jnp.int32), 0))

    small = jnp.concatenate([qv_bias, out_bias[None], down_bias[None], norm_gain, norm_shift], 0)
    small = jnp.concatenate([jnp.pad(small, ((0, 0), (0, 96))), up_bias[None], jnp.zeros((3, 128), bf16)], 0)
    wqkv, wo, up_one, rows, small, down_one = start_gather(w_qkv, w_up, w_out, tokens[0], w_down, small, 6)
    wqkv, wo, rows = wqkv.reshape(width, 768), wo.reshape(256, width), rows.reshape(512, width)

    vectors = small[..., :12, :32].reshape(32, 12, 32).transpose(1, 0, 2).reshape(12, width).astype(f32)
    qv_half = pick(pick(vectors[:2].reshape(2, 2, 2, 2, 2, HD), b, 2), c, 3).reshape(2, 4, HD)
    qk_shift = jnp.concatenate([qv_half[0], jnp.zeros((4, HD), f32)], 1).reshape(512)
    v_shift = qv_half[1].reshape(256)
    up_shift = pick(pick(small[..., 12, :], b, 1), c, 2).reshape(1024).astype(f32)

    first = norm_rows(rows.astype(f32), vectors[4:5], vectors[8:9]).astype(bf16)
    up_two = cube_one(flip_x, up_one)
    projected = (dot_nn(first, wqkv) + jnp.concatenate([qk_shift, v_shift])).astype(bf16)
    packed = exchange(after(projected, up_two), True, 1).reshape(8, 384, 128)
    down_two = cube_one(flip_x, down_one)
    up_half = flip_y(after(up_two, packed)[:, 0])
    attended = attend(valid[None], packed).reshape(2, 2, 2, 128, 128)
    attended = exchange(after(attended, down_two, up_half), False, 2)
    up_all = jnp.concatenate([up_two, jnp.stack([up_half, flip_y(after(up_two, attended)[:, 1])], 1)], 0)
    down_far = flip_y(after(down_two, attended))
    own_spot = lax.axis_index("seq") * 128 + jnp.arange(128, dtype=jnp.int32)
    grad_out = cotangent[0].astype(f32) * (own_spot < valid).astype(f32)[:, None]
    S = jax.ShapeDtypeStruct
    wide, low, line = S((128, width), f32), S((128, width), bf16), S((1, width), f32)
    branch, middle, third = sum_rows(
        attended_step, dot_nn(attended, wo), (tokens[0], vectors),
        (wide, wide), True, 7)
    third = third.reshape(512, width)
    wu = arrange(spot, [(up_all, False)])[0].reshape(width, 1024)
    up_pre = dot_nn(third, wu) + up_shift
    active, pull_gelu = jax.vjp(exact_gelu, up_pre)
    active = active.astype(bf16)
    down_all = jnp.concatenate([down_two, after(down_far, active)], 0)
    wd = arrange(spot, [(down_all, False)])[0].reshape(1024, width)
    output, gain4, shift4, bias_down, down_rows = sum_rows(
        output_step, dot_nn(active, wd), (middle, grad_out, vectors), (low, line, line, line), True, 8)
    down_rows = down_rows.reshape(512, width)
    gw_down = contract_rows(active, down_rows).astype(bf16).reshape(2, 2, 2, 128, width)
    down_term = flip_y(pick(gw_down, 1 - y, 1, True))
    (grad_up,) = pull_gelu(dot_nt(after(down_rows, gw_down), wd))
    grad_up = grad_up.astype(bf16)
    gw_up = contract_rows(third, grad_up).astype(bf16).reshape(2, 2, 2, 2, 2, 32, 1024)
    up_term = flip_x(pick(gw_up, 1 - x, 4, True))
    grad_middle, gain3, shift3, gain2, shift2, bias_out, branch_rows = sum_rows(
        middle_step, dot_nt(after(grad_up, gw_up), wu),
        (middle, branch, grad_out, vectors), (wide,) + (line,) * 5, True, 9)
    branch_rows = branch_rows.reshape(512, width)
    grad_att = dot_nt(branch_rows, wo).astype(bf16)
    down_sum = add_low(pick(gw_down, y, 1, True), down_term)
    down_term = flip_x(pick(down_sum, 1 - x, 2, True))
    grad_packed = exchange(after(grad_att, down_sum), True, 3).reshape(8, 128, 128)
    up_sum = add_low(pick(gw_up, x, 4, True), after(up_term, grad_packed))
    up_term = flip_y(pick(up_sum, 1 - y, 2, True))
    down_sum = add_low(pick(down_sum, x, 2, True), after(down_term, grad_packed))
    down_term = flip_a(pick(down_sum, 1 - a, 0))
    back = attend_back(valid[None], packed, grad_packed)

    up_sum = add_low(pick(up_sum, y, 2, True), up_term)
    gw_out = contract_rows(attended, branch_rows).astype(bf16).reshape(2, 2, 2, 32, width)
    grad_qkv = exchange(after(back, up_sum, down_term).reshape(2, 2, 2, 384, 128), False, 4)
    up_term = flip_a(pick(after(up_sum, grad_qkv), 1 - a, 0))
    gw_qkv = contract_rows(first, grad_qkv).astype(bf16).reshape(2, 2, 2, 2, 2, 32, 768)
    input_grad, gain1, shift1 = sum_rows(
        input_step, dot_nt(grad_qkv, wqkv), (tokens[0], grad_middle, vectors), (low, line, line), False, 10)

    def sums(block):
        return jnp.sum(block.astype(f32), 0, keepdims=True)

    vectors = [sums(grad_qkv), sums(grad_up), bias_out, bias_down,
               gain1, gain2, gain3, gain4, shift1, shift2, shift3, shift4]
    up_sum = (pick(up_sum, a, 0).astype(f32) + up_term.astype(f32)).astype(bf16).reshape(2, 2, 32, 1024)
    r_qkv, r_out, r_up, vectors = reduce_all(gw_qkv, gw_out, up_sum, vectors, 5)
    r_down = (pick(down_sum, a, 0).astype(f32) + down_term.astype(f32)).reshape(128, width)
    index = lax.axis_index("seq") * 2 + x
    small_up = lax.dynamic_slice(vectors, (12 + index // 8, index % 8 * 128), (1, 128)).reshape(128)
    vectors = lax.dynamic_slice(vectors, (0, index * 32), (12, 32))

    return (
        output[None], input_grad[None], r_qkv, vectors[:2], r_out,
        vectors[2], r_up, small_up, r_down, vectors[3], vectors[4:8], vectors[8:12])


def solution(mesh):
    return jax.shard_map(
        fast_body if is_small(mesh) else body,
        mesh=mesh,
        in_specs=(
            P("dp", "seq", None),
            P("dp", "seq", None),
            P(),
            P(),
            P(("seq", "dp"), None),
            P(None, ("seq", "dp")),
            P(("seq", "dp"), None),
            P(("seq", "dp")),
            P(("seq", "dp"), None),
            P(("seq", "dp")),
            P(("seq", "dp"), None),
            P(("seq", "dp")),
            P(None, ("seq", "dp")),
            P(None, ("seq", "dp")),
        ),
        out_specs=(
            P("dp", "seq", None),
            P("dp", "seq", None),
            P(("seq", "dp"), None),
            P(None, ("seq", "dp")),
            P(("seq", "dp"), None),
            P(("seq", "dp")),
            P(("seq", "dp"), None),
            P(("seq", "dp")),
            P(("seq", "dp"), None),
            P(("seq", "dp")),
            P(None, ("seq", "dp")),
            P(None, ("seq", "dp")),
        ),
        check_vma=False,
    )
```

```python
import functools
import math

import jax
import jax.numpy as jnp
from jax import lax
from jax.experimental import pallas as pl
from jax.experimental.pallas import tpu as pltpu
from jax.sharding import PartitionSpec as P


HD = 64


RELAX_SCALE = 32.0
NORM_EPSILON = 1e-05


def norm_rows(values, gain, shift):
    center = values - jnp.mean(values, -1, keepdims=True)
    spread = jnp.mean(center * center, -1, keepdims=True)
    return center * lax.rsqrt(spread + NORM_EPSILON) * gain + shift


def exact_gelu(values):
    return jax.nn.gelu(values, approximate=False)


def contract_rows(left, right):
    return lax.dot_general(
        left, right, (((0,), (0,)), ((), ())), preferred_element_type=jnp.float32
    )


def contract_cols(left, right):
    return lax.dot_general(
        left, right, (((1,), (1,)), ((), ())), preferred_element_type=jnp.float32
    )


def split_heads(block):
    return block.reshape(block.shape[0], 2, HD)


def pair_scores(query_part, key_part):
    factor = 1.0 / (RELAX_SCALE * math.sqrt(HD))
    return (
        jnp.einsum(
            "qhd,khd->hqk",
            split_heads(query_part),
            split_heads(key_part),
            preferred_element_type=jnp.float32,
        )
        * factor
    )


def kept_probs(scores, allowed, row_max, row_total):
    exp_terms = jnp.exp(jnp.where(allowed, RELAX_SCALE * (scores - row_max), -jnp.inf))
    return exp_terms / row_total


def body(
    tokens,
    cotangent,
    lengths,
    assign,
    w_qkv,
    qv_bias,
    w_out,
    out_bias,
    w_up,
    up_bias,
    w_down,
    down_bias,
    norm_gain,
    norm_shift,
):
    gathered = (
        lax.all_gather(w_qkv, ("seq", "dp"), axis=0, tiled=True),
        lax.all_gather(w_out, ("seq", "dp"), axis=0, tiled=True),
        lax.all_gather(w_up, ("seq", "dp"), axis=0, tiled=True),
        lax.all_gather(w_down, ("seq", "dp"), axis=0, tiled=True),
        lax.all_gather(qv_bias, ("seq", "dp"), axis=1, tiled=True),
        lax.all_gather(out_bias, ("seq", "dp"), axis=0, tiled=True),
        lax.all_gather(up_bias, ("seq", "dp"), axis=0, tiled=True),
        lax.all_gather(down_bias, ("seq", "dp"), axis=0, tiled=True),
        lax.all_gather(norm_gain, ("seq", "dp"), axis=1, tiled=True),
        lax.all_gather(norm_shift, ("seq", "dp"), axis=1, tiled=True),
    )
    qkv_full, out_full, up_full, down_full = (gathered[0], gathered[1], gathered[2], gathered[3])
    qv_shift = gathered[4].astype(jnp.float32)
    out_shift = gathered[5].astype(jnp.float32)
    up_shift = gathered[6].astype(jnp.float32)
    down_shift = gathered[7].astype(jnp.float32)
    gains = gathered[8].astype(jnp.float32)
    shifts = gathered[9].astype(jnp.float32)
    row_count = tokens.shape[1]
    model_width = tokens.shape[2]
    pair_cols = 2 * HD
    pair_count = model_width // pair_cols
    slot_rows = row_count * lax.axis_size("seq")
    factor = 1.0 / (RELAX_SCALE * math.sqrt(HD))
    valid = lengths[assign[lax.axis_index("dp")]]
    own_place = lax.axis_index("seq") * row_count + jnp.arange(row_count, dtype=jnp.int32)
    all_place = jnp.arange(slot_rows, dtype=jnp.int32)
    allowed = (all_place[None, :] <= own_place[:, None]) & (all_place[None, :] < valid)
    pair_ids = jnp.arange(pair_count, dtype=jnp.int32)
    hidden = tokens[0].astype(jnp.float32)
    normed_first, pull_first = jax.vjp(norm_rows, hidden, gains[0], shifts[0])
    normed_low = normed_first.astype(jnp.bfloat16)
    projected = jnp.dot(normed_low, qkv_full, preferred_element_type=jnp.float32)
    queries = (projected[:, :model_width] + qv_shift[0]).astype(jnp.bfloat16)
    key_own = projected[:, model_width : 2 * model_width].astype(jnp.bfloat16)
    value_own = (projected[:, 2 * model_width :] + qv_shift[1]).astype(jnp.bfloat16)
    keys, values = (
        lax.all_gather(key_own, "seq", axis=0, tiled=True),
        lax.all_gather(value_own, "seq", axis=0, tiled=True),
    )

    def columns(block, pair_index):
        return lax.dynamic_slice_in_dim(block, pair_index * pair_cols, pair_cols, 1)

    def merge_pairs(stack):
        return stack.transpose(1, 0, 2).reshape(stack.shape[1], model_width)

    def attend(pair_index):
        scores = pair_scores(columns(queries, pair_index), columns(keys, pair_index))
        row_max = jnp.max(jnp.where(allowed, scores, -jnp.inf), -1, keepdims=True)
        exp_terms = jnp.exp(jnp.where(allowed, RELAX_SCALE * (scores - row_max), -jnp.inf))
        row_total = jnp.sum(exp_terms, -1, keepdims=True)
        probs = (exp_terms / row_total).astype(jnp.bfloat16)
        mixed = jnp.einsum(
            "hqk,khd->qhd",
            probs,
            split_heads(columns(values, pair_index)),
            preferred_element_type=jnp.float32,
        )
        return (mixed.reshape(row_count, pair_cols), row_max[..., 0], row_total[..., 0])

    mixed_pairs, max_pairs, total_pairs = lax.map(attend, pair_ids)
    attended = merge_pairs(mixed_pairs).astype(jnp.bfloat16)
    branch = jnp.dot(attended, out_full, preferred_element_type=jnp.float32) + out_shift
    normed_second, pull_second = jax.vjp(norm_rows, branch, gains[1], shifts[1])
    middle = hidden + normed_second
    normed_third, pull_third = jax.vjp(norm_rows, middle, gains[2], shifts[2])
    third_low = normed_third.astype(jnp.bfloat16)
    up_pre = jnp.dot(third_low, up_full, preferred_element_type=jnp.float32) + up_shift
    activated, pull_gelu = jax.vjp(exact_gelu, up_pre)
    active_low = activated.astype(jnp.bfloat16)
    down_pre = jnp.dot(active_low, down_full, preferred_element_type=jnp.float32) + down_shift
    normed_fourth, pull_fourth = jax.vjp(norm_rows, down_pre, gains[3], shifts[3])
    output = (middle + normed_fourth).astype(jnp.bfloat16)[None]
    again = (
        lax.all_gather(w_qkv, ("seq", "dp"), axis=0, tiled=True),
        lax.all_gather(w_out, ("seq", "dp"), axis=0, tiled=True),
        lax.all_gather(w_up, ("seq", "dp"), axis=0, tiled=True),
        lax.all_gather(w_down, ("seq", "dp"), axis=0, tiled=True),
    )
    qkv_back, out_back, up_back, down_back = (again[0], again[1], again[2], again[3])
    keep_rows = (own_place < valid).astype(jnp.float32)[:, None]
    grad_out = cotangent[0].astype(jnp.float32) * keep_rows
    grad_down, grad_gain_four, grad_shift_four = pull_fourth(grad_out)
    grad_down_low = grad_down.astype(jnp.bfloat16)
    grad_w_down = contract_rows(active_low, grad_down_low)
    grad_b_down = jnp.sum(grad_down_low.astype(jnp.float32), 0)
    (grad_up,) = pull_gelu(contract_cols(grad_down_low, down_back))
    grad_up_low = grad_up.astype(jnp.bfloat16)
    grad_w_up = contract_rows(third_low, grad_up_low)
    grad_b_up = jnp.sum(grad_up_low.astype(jnp.float32), 0)
    grad_middle_part, grad_gain_three, grad_shift_three = pull_third(
        contract_cols(grad_up_low, up_back)
    )
    grad_middle = grad_out + grad_middle_part
    grad_branch, grad_gain_two, grad_shift_two = pull_second(grad_middle)
    grad_branch_low = grad_branch.astype(jnp.bfloat16)
    grad_w_out = contract_rows(attended, grad_branch_low)
    grad_b_out = jnp.sum(grad_branch_low.astype(jnp.float32), 0)
    grad_attended = contract_cols(grad_branch_low, out_back).astype(jnp.bfloat16)

    def query_side(pair_index):
        scores = pair_scores(columns(queries, pair_index), columns(keys, pair_index))
        probs = kept_probs(
            scores, allowed, max_pairs[pair_index][..., None], total_pairs[pair_index][..., None]
        )
        grad_part = columns(grad_attended, pair_index)
        grad_probs = jnp.einsum(
            "qhd,khd->hqk",
            split_heads(grad_part),
            split_heads(columns(values, pair_index)),
            preferred_element_type=jnp.float32,
        )
        delta = jnp.sum(probs * grad_probs, -1, keepdims=True)
        grad_scores = (RELAX_SCALE * probs * (grad_probs - delta)).astype(jnp.bfloat16)
        grad_query = (
            jnp.einsum(
                "hqk,khd->qhd",
                grad_scores,
                split_heads(columns(keys, pair_index)),
                preferred_element_type=jnp.float32,
            )
            * factor
        )
        return (grad_query.reshape(row_count, pair_cols), grad_scores, probs, delta)

    def both_sides(pair_index):
        grad_query, grad_scores, probs, delta = query_side(pair_index)
        grad_part = columns(grad_attended, pair_index)
        grad_key = (
            jnp.einsum(
                "hqk,qhd->khd",
                grad_scores,
                split_heads(columns(queries, pair_index)),
                preferred_element_type=jnp.float32,
            )
            * factor
        )
        grad_value = jnp.einsum(
            "hqk,qhd->khd",
            probs.astype(jnp.bfloat16),
            split_heads(grad_part),
            preferred_element_type=jnp.float32,
        )
        return (
            grad_query,
            grad_key.reshape(slot_rows, pair_cols),
            grad_value.reshape(slot_rows, pair_cols),
        )

    query_pairs, key_terms, value_terms = lax.map(both_sides, pair_ids)
    key_pairs, value_pairs = (
        lax.psum_scatter(
            key_terms.astype(jnp.bfloat16), "seq", scatter_dimension=1, tiled=True
        ).astype(jnp.float32),
        lax.psum_scatter(
            value_terms.astype(jnp.bfloat16), "seq", scatter_dimension=1, tiled=True
        ).astype(jnp.float32),
    )
    grad_q_low = merge_pairs(query_pairs).astype(jnp.bfloat16)
    grad_k_low = merge_pairs(key_pairs).astype(jnp.bfloat16)
    grad_v_low = merge_pairs(value_pairs).astype(jnp.bfloat16)
    grad_projected = jnp.concatenate([grad_q_low, grad_k_low, grad_v_low], 1)
    grad_w_qkv = contract_rows(normed_low, grad_projected)
    grad_qv = jnp.stack(
        [jnp.sum(grad_q_low.astype(jnp.float32), 0), jnp.sum(grad_v_low.astype(jnp.float32), 0)]
    )
    grad_hidden_part, grad_gain_one, grad_shift_one = pull_first(
        contract_cols(grad_projected, qkv_back)
    )
    input_grad = (grad_middle + grad_hidden_part).astype(jnp.bfloat16)[None]
    grad_gains = jnp.stack([grad_gain_one, grad_gain_two, grad_gain_three, grad_gain_four])
    grad_shifts = jnp.stack([grad_shift_one, grad_shift_two, grad_shift_three, grad_shift_four])
    owned = (
        lax.psum_scatter(grad_w_qkv, ("seq", "dp"), scatter_dimension=0, tiled=True),
        lax.psum_scatter(grad_w_out, ("seq", "dp"), scatter_dimension=0, tiled=True),
        lax.psum_scatter(grad_w_up, ("seq", "dp"), scatter_dimension=0, tiled=True),
        lax.psum_scatter(grad_w_down, ("seq", "dp"), scatter_dimension=0, tiled=True),
        lax.psum_scatter(grad_qv, ("seq", "dp"), scatter_dimension=1, tiled=True),
        lax.psum_scatter(grad_b_out, ("seq", "dp"), scatter_dimension=0, tiled=True),
        lax.psum_scatter(grad_b_up, ("seq", "dp"), scatter_dimension=0, tiled=True),
        lax.psum_scatter(grad_b_down, ("seq", "dp"), scatter_dimension=0, tiled=True),
        lax.psum_scatter(grad_gains, ("seq", "dp"), scatter_dimension=1, tiled=True),
        lax.psum_scatter(grad_shifts, ("seq", "dp"), scatter_dimension=1, tiled=True),
    )
    return (
        output,
        input_grad,
        owned[0],
        owned[4],
        owned[1],
        owned[5],
        owned[2],
        owned[6],
        owned[3],
        owned[7],
        owned[8],
        owned[9],
    )


MESH = pl.DeviceIdType.MESH


def is_small(mesh):
    return mesh.shape["seq"] == 16 and mesh.shape["dp"] == 2


def place():
    seq = lax.axis_index("seq")
    return seq // 8, (seq // 4) % 2, (seq // 2) % 2, seq % 2, lax.axis_index("dp")


def exchange_copies(scatter, src, out, send_sem, recv_sem, own_sem):
    a, b, y, c, x = place()

    def peer(k):
        return lax.rem(a + k // 2, 2), lax.rem(y + k % 2, 2)

    def device(k):
        pa, py = peer(k)
        return (pa * 8 + b * 4 + py * 2 + c, x)

    def source(k):
        pa, py = peer(k)
        return src.at[pa * 2 + py] if scatter else src.at[pa, :, py]

    def target(k):
        pa, py = peer(k)
        return out.at[pa, :, py] if scatter else out.at[pa * 2 + py]

    def copy(k, dst):
        return pltpu.make_async_remote_copy(
            src_ref=source(k), dst_ref=target(dst), send_sem=send_sem.at[k], recv_sem=recv_sem.at[k],
            device_id=device(k), device_id_type=MESH)

    def greet():
        barrier = pltpu.get_barrier_semaphore()
        for k in range(1, 4):
            pl.semaphore_signal(barrier, inc=1, device_id=device(k), device_id_type=MESH)

    def run():
        own = pltpu.make_async_copy(source(0), target(0), own_sem)
        own.start()
        pl.semaphore_wait(pltpu.get_barrier_semaphore(), 3)
        for k in (3, 2, 1):
            copy(k, 0).start()
        own.wait()
        for k in (3, 2, 1):
            copy(k, k).wait_recv()
        for k in (3, 2, 1):
            copy(k, 0).wait_send()

    return greet, run


def row_block(i, j):
    _, b, _, c, _ = place()
    return pl.ds(pl.multiple_of(lax.rem(b + i, 2) * 256 + lax.rem(c + j, 2) * 128, 128), 128)


def to_heads_kernel(rows_ref, out, src, *sems):
    greet, run = exchange_copies(True, src, out, *sems)
    greet()
    low = src.shape[2] - 128
    for g in range(4):
        values = slice(low * 2 + g * HD, low * 2 + g * HD + HD)
        for i in range(2):
            if low:
                for j in range(2):
                    src[g, i, j * 128:j * 128 + 128] = rows_ref[row_block(i, j), g * 128:g * 128 + 128]
            src[g, i, low:] = jnp.concatenate([rows_ref[row_block(i, j), values] for j in range(2)], 1)
    run()


def from_heads_kernel(heads_ref, out, got, *sems):
    greet, run = exchange_copies(False, heads_ref, got, *sems)
    greet()
    run()
    low = got.shape[2] - 128
    c = place()[3]
    for i in range(2):
        if low:
            for j in range(2):
                for g in range(4):
                    out[row_block(i, j), g * 128:g * 128 + 128] = got[g, i, j * 128:j * 128 + 128]
        for g in (0, 2):
            left, right = got[g, i, low:], got[g + 1, i, low:]
            cols = slice(low * 2 + g * HD, low * 2 + g * HD + 128)
            for j in range(2):
                lanes = slice(j * HD, j * HD + HD)
                out[row_block(i, j), cols] = jnp.concatenate([left[:, lanes], right[:, lanes]], 1)


def exchange(blocks, scatter, cid):
    vm = pl.BlockSpec(memory_space=pltpu.VMEM)
    rows = blocks.shape[-1] // 2 if scatter else blocks.shape[-2]
    shape, held = (2, 2, 2, rows, 128), (4, 2, rows, 128)
    return pl.pallas_call(
        to_heads_kernel if scatter else from_heads_kernel,
        out_shape=jax.ShapeDtypeStruct(shape if scatter else (512, rows * 2), blocks.dtype),
        in_specs=[vm], out_specs=vm,
        scratch_shapes=[pltpu.VMEM(held, blocks.dtype), pltpu.SemaphoreType.DMA((4,)), pltpu.SemaphoreType.DMA((4,)),
                        pltpu.SemaphoreType.DMA],
        compiler_params=pltpu.CompilerParams(collective_id=cid, has_side_effects=True),
        cost_estimate=pl.CostEstimate(flops=0, bytes_accessed=rows * 100000, transcendentals=0),
        name="to_heads" if scatter else "from_heads",
    )(blocks)


def dot_nt(a, b):
    return lax.dot_general(a, b, (((1,), (1,)), ((), ())), preferred_element_type=jnp.float32)


def dot_nn(a, b):
    return jnp.dot(a, b, preferred_element_type=jnp.float32)


BQ = 256
MASKED = -1e30


def load_heads(valid, packed, q_ref, k_ref):
    rows = q_ref.shape[0]
    qk = packed[:, :256].reshape(rows, 128)
    kq = jnp.concatenate([qk[:, 64:], qk[:, :64]], axis=1)
    lane = lax.broadcasted_iota(jnp.int32, (rows, 128), 1)
    spot = lax.broadcasted_iota(jnp.int32, (rows, 128), 0)
    past = jnp.where(spot < valid, 0.0, MASKED)
    q_ref[...] = jnp.where(lane < 64, qk.astype(jnp.float32), jnp.where(lane == 64, 1.0, 0.0)).astype(jnp.bfloat16)
    k_ref[...] = jnp.where(lane < 64, kq.astype(jnp.float32), jnp.where(lane == 64, past, 0.0)).astype(jnp.bfloat16)


def unpack_rows(halves):
    n = halves.shape[0]
    return jnp.concatenate([halves[:, :, :64], halves[:, :, 64:]], axis=1).reshape(n * 256, 64)


def block_probs(q_ref, k_ref, i):
    n = (i + 1) * BQ
    scores = dot_nt(k_ref[:n], q_ref[i * BQ:n])
    key = lax.broadcasted_iota(jnp.int32, (BQ, BQ), 0)
    query = lax.broadcasted_iota(jnp.int32, (BQ, BQ), 1)
    corner = jnp.where(key <= query, scores[n - BQ:], MASKED)
    scores = jnp.concatenate([scores[:n - BQ], corner], axis=0) if i else corner
    top = jnp.max(scores, axis=0, keepdims=True)
    terms = jnp.exp((scores - top) * 0.125)
    return terms, 1.0 / jnp.sum(terms, axis=0, keepdims=True)


def attend_kernel(valid_ref, packed, out_ref, q_ref, k_ref, vt_ref):
    load_heads(valid_ref[0], packed, q_ref, k_ref)
    unit = jnp.where(
        lax.broadcasted_iota(jnp.int32, (64, 64), 0) == lax.broadcasted_iota(jnp.int32, (64, 64), 1), 1.0, 0.0
    ).astype(jnp.bfloat16)
    vt_ref[...] = dot_nt(unit, unpack_rows(packed[:, 256:])).astype(jnp.bfloat16)
    for i in range(q_ref.shape[0] // BQ):
        n = (i + 1) * BQ
        terms, scale = block_probs(q_ref, k_ref, i)
        probs = (terms * scale).astype(jnp.bfloat16)
        mixed = dot_nn(vt_ref[:, :n], probs).T
        out_ref[i] = jnp.concatenate([mixed[:128], mixed[128:]], axis=1).astype(jnp.bfloat16)


def attend_back_kernel(valid_ref, packed, grad, out_ref, q_ref, k_ref, v_ref, g_ref, kt_ref, dk_ref, dv_ref):
    load_heads(valid_ref[0], packed, q_ref, k_ref)
    v_ref[...] = unpack_rows(packed[:, 256:])
    g_ref[...] = unpack_rows(grad[...])
    unit = jnp.where(
        lax.broadcasted_iota(jnp.int32, (64, 128), 0) == lax.broadcasted_iota(jnp.int32, (64, 128), 1), 1.0, 0.0
    ).astype(jnp.bfloat16)
    kt_ref[...] = dot_nt(unit, k_ref[...]).astype(jnp.bfloat16)
    dk_ref[...] = jnp.zeros_like(dk_ref)
    dv_ref[...] = jnp.zeros_like(dv_ref)
    blocks = q_ref.shape[0] // BQ
    for i in range(blocks):
        n = (i + 1) * BQ
        terms, scale = block_probs(q_ref, k_ref, i)
        probs = terms * scale
        grad_probs = dot_nt(v_ref[:n], g_ref[i * BQ:n])
        delta = jnp.sum(probs * grad_probs, axis=0, keepdims=True)
        grad_scores = (probs * (grad_probs - delta)).astype(jnp.bfloat16)
        grad_query = dot_nn(kt_ref[:, :n], grad_scores).T * 0.125
        out_ref[i, :256, :64] = grad_query.astype(jnp.bfloat16)
        dk_ref[:n] += dot_nn(grad_scores, q_ref[i * BQ:n])
        dv_ref[:n] += dot_nn(probs.astype(jnp.bfloat16), g_ref[i * BQ:n])
    for i in range(blocks):
        rows = slice(i * BQ, (i + 1) * BQ)
        out_ref[i, :256, 64:] = (dk_ref[rows, :64] * 0.125).astype(jnp.bfloat16)
        value = dv_ref[rows].astype(jnp.bfloat16)
        out_ref[i, 256:] = jnp.concatenate([value[:128], value[128:]], axis=1)


def attend(valid, packed):
    rows = packed.shape[0] * 256
    vm = pl.BlockSpec(memory_space=pltpu.VMEM)
    return pl.pallas_call(
        attend_kernel,
        out_shape=jax.ShapeDtypeStruct((packed.shape[0], 128, 128), jnp.bfloat16),
        in_specs=[pl.BlockSpec(memory_space=pltpu.SMEM), vm], out_specs=vm,
        scratch_shapes=[pltpu.VMEM((rows, 128), jnp.bfloat16)] * 2 + [pltpu.VMEM((64, rows), jnp.bfloat16)],
        compiler_params=pltpu.CompilerParams(vmem_limit_bytes=48 << 20),
        name="attend",
    )(valid, packed)


def attend_back(valid, packed, grad):
    rows = packed.shape[0] * 256
    vm = pl.BlockSpec(memory_space=pltpu.VMEM)
    return pl.pallas_call(
        attend_back_kernel,
        out_shape=jax.ShapeDtypeStruct(packed.shape, jnp.bfloat16),
        in_specs=[pl.BlockSpec(memory_space=pltpu.SMEM), vm, vm], out_specs=vm,
        scratch_shapes=[pltpu.VMEM((rows, 128), jnp.bfloat16)] * 2 + [pltpu.VMEM((rows, 64), jnp.bfloat16)] * 2
        + [pltpu.VMEM((64, rows), jnp.bfloat16), pltpu.VMEM((rows, 128), jnp.float32), pltpu.VMEM((rows, 64), jnp.float32)],
        compiler_params=pltpu.CompilerParams(vmem_limit_bytes=48 << 20),
        name="attend_back",
    )(valid, packed, grad)


def flip(bits, block):
    return lax.ppermute(block, "seq", [(s, s ^ bits) for s in range(16)])


flip_a, flip_y = (functools.partial(flip, bits) for bits in (8, 2))


def flip_x(block):
    return lax.ppermute(block, "dp", [(0, 1), (1, 0)])


def after(value, *others):
    return lax.optimization_barrier((value,) + others)[0]


def pick(block, index, axis, keepdims=False):
    return lax.dynamic_index_in_dim(block, index, axis, keepdims=keepdims)


def cube_one(flip_one, block):
    return jnp.concatenate([block, flip_one(block)], 0)


def arrange_kernel(count, spot_ref, *refs):
    for k in range(count):
        block, out = refs[k], refs[count + k]
        if len(out.shape) == 7:
            for i in range(2):
                for j in range(2):
                    out[0, i, 0, j, 0] = block[0, i, j]
        else:
            out[0, 0, 0] = block[0]


def arrange(spot, blocks):
    def coords(i, r, y_first):
        second, first, a = i // 4, (i // 2) % 2, i % 2
        y, x = (first, second) if y_first else (second, first)
        return lax.rem(r[0] + a, 2), lax.rem(r[1] + y, 2), lax.rem(r[2] + x, 2)

    def specs(block, y_first):
        shape = block.shape
        if len(shape) == 5:
            def out_place(i, r):
                a, y, x = coords(i, r, y_first)
                return a, 0, y, 0, x, 0, 0
            return (pl.BlockSpec((1,) + shape[1:], lambda i, r: (i, 0, 0, 0, 0)),
                    pl.BlockSpec((1, 2, 1, 2, 1) + shape[3:], out_place),
                    jax.ShapeDtypeStruct((2,) * 5 + shape[3:], block.dtype))

        def out_place(i, r):
            return coords(i, r, y_first) + (0, 0)
        return (pl.BlockSpec((1,) + shape[1:], lambda i, r: (i, 0, 0)),
                pl.BlockSpec((1, 1, 1) + shape[1:], out_place),
                jax.ShapeDtypeStruct((2, 2, 2) + shape[1:], block.dtype))

    made = [specs(*entry) for entry in blocks]
    return pl.pallas_call(
        functools.partial(arrange_kernel, len(blocks)),
        out_shape=tuple(m[2] for m in made),
        grid_spec=pltpu.PrefetchScalarGridSpec(
            num_scalar_prefetch=1, grid=(8,), in_specs=[m[0] for m in made], out_specs=tuple(m[1] for m in made)),
        compiler_params=pltpu.CompilerParams(vmem_limit_bytes=32 << 20),
        cost_estimate=pl.CostEstimate(flops=0, bytes_accessed=8 << 20, transcendentals=0),
        name="arrange",
    )(spot, *[entry[0] for entry in blocks])


def add_low(mine, other):
    return (mine.astype(jnp.float32) + other.astype(jnp.float32)).astype(jnp.bfloat16)


def fold(terms, flip_one, index, axis):
    return add_low(pick(terms, index, axis, True), flip_one(pick(terms, 1 - index, axis, True)))


def reduce_kernel(q_ref, o_ref, u_ref, part, tokens, grad_middle, vectors, *refs):
    vec_refs, (out_q, ro, out_u, vec, input_grad, got_far, got_near, low_sums, got_sums, row_send, row_recv, rq, gu, r1q, t2q, r2q, t3q, r3q, fq, gq, r1o, t2o, r2o, t3o, r3o,
               run, got, send_sem, recv_sem) = refs[:10], refs[10:]
    a, b, y, c, x = place()
    f32, bf16 = jnp.float32, jnp.bfloat16
    barrier = pltpu.get_barrier_semaphore()

    def at(pa, pb, py, pc, px):
        return (pa * 8 + pb * 4 + py * 2 + pc, px)

    to_x, to_y, to_a = at(a, b, y, c, 1 - x), at(a, b, 1 - y, c, x), at(1 - a, b, y, c, x)
    ranks = [(lax.rem(b + k // 2, 2), lax.rem(c + k % 2, 2)) for k in range(4)]
    to_rank = [at(a, ranks[k][0], y, ranks[k][1], x) for k in range(4)]
    to_b, to_c = to_rank[2], to_rank[1]
    for dev in [to_x, to_y, to_a] + to_rank[1:]:
        pl.semaphore_signal(barrier, inc=1, device_id=dev, device_id_type=MESH)
    for pb in range(2):
        for j in range(4):
            for row, cols in ((0, slice(j * 128, j * 128 + HD)), (1, slice(512 + j * HD, 512 + j * HD + HD))):
                piece = vec_refs[0][:, cols]
                pair = [jnp.where((b == pb) & (c == pc), piece, 0.0) for pc in range(2)]
                h = head_of(j // 2, pb, j % 2, 0) * HD
                run[0, row:row + 1, h:h + 128] = jnp.concatenate(pair, 1)
            for pc in range(2):
                col = head_of(j // 2, pb, j % 2, pc) * 256
                piece = vec_refs[1][:, j * 256:j * 256 + 256]
                run[0, 12 + col // 1024:13 + col // 1024, col % 1024:col % 1024 + 256] = jnp.where(
                    (b == pb) & (c == pc), piece, 0.0)
    for k, row in enumerate((2, 3, 5, 6, 7, 9, 10, 11)):
        run[0, row:row + 1] = vec_refs[2 + k][...]
    for row in (4, 8):
        run[0, row:row + 1] = jnp.zeros((1, 1024), f32)
    pl.semaphore_wait(barrier, 6)

    made = []

    def remote(src, dst, dev):
        k = len(made)
        made.append(pltpu.make_async_remote_copy(
            src_ref=src, dst_ref=dst, send_sem=send_sem.at[k], recv_sem=recv_sem.at[k],
            device_id=dev, device_id_type=MESH))
        return made[-1]

    def low(*values):
        return sum(v.astype(f32) for v in values)

    places = [1 - a, a]
    halves = [slice(0, 512), slice(512, 1024)]
    lateral = [(to_x, to_y), (to_y, to_x)]

    q1, q2, o1, o2 = {}, {}, {}, {}
    for i in range(2):
        for s in range(2):
            p = places[i]
            q1[s, i] = remote(q_ref.at[p, 0, :, :, 1 - x] if s == 0 else q_ref.at[p, 1, 1 - y], r1q.at[s, i], lateral[s][0])
            o1[s, i] = remote(o_ref.at[p, :, 1 - x, :, halves[0]] if s == 0 else o_ref.at[p, 1 - y, :, :, halves[1]],
                              r1o.at[s, i], lateral[s][0])
            q2[s, i] = remote(t2q.at[s, i], r2q.at[s, i], lateral[s][1])
            o2[s, i] = remote(t2o.at[s, i], r2o.at[s, i], lateral[s][1])
    q3 = [remote(t3q.at[s], r3q.at[s], to_a) for s in range(2)]
    o3 = [remote(t3o.at[s], r3o.at[s], to_a) for s in range(2)]
    qr = [remote(fq.at[ranks[k][0], ranks[k][1]], gq.at[k - 1], to_rank[k]) for k in range(1, 4)]
    ur = [remote(u_ref.at[ranks[k][0], ranks[k][1]], gu.at[b, c], to_rank[k]) for k in range(1, 4)]
    vs = [remote(run.at[k], got.at[k], dev) for k, dev in enumerate((to_x, to_y, to_a, to_b, to_c))]

    def next_sum(k):
        vs[k].wait_recv()
        if k < 4:
            run[k + 1] = run[k] + got[k]
            vs[k + 1].start()
        else:
            vec[...] = run[k] + got[k]

    pieces = part.shape[2] // PIECE

    def span(r):
        return pl.ds(pl.multiple_of(r * PIECE, PIECE), PIECE)

    def row_copy(kind, r):
        src, dst, dev = ((part.at[1, 1, span(r)], got_far.at[span(r)], to_c), (part.at[0, 1, span(r)], got_near.at[span(r)], to_c),
                         (low_sums.at[span(r)], got_sums.at[span(r)], to_b))[kind]
        return pltpu.make_async_remote_copy(
            src_ref=src, dst_ref=dst, send_sem=row_send.at[kind, r], recv_sem=row_recv.at[kind, r],
            device_id=dev, device_id_type=MESH)

    def send_across(r, _):
        row_copy(0, r).wait_recv()
        low_sums[span(r)] = (part[1, 0, span(r)] + got_far[span(r)]).astype(bf16)
        row_copy(2, r).start()
        return 0

    def take(r, _):
        row_copy(1, r).wait_recv()
        row_copy(2, r).wait_recv()
        total = part[0, 0, span(r)] + got_near[span(r)] + got_sums[span(r)].astype(f32)
        _, pull = jax.vjp(norm_rows, tokens[span(r)].astype(f32), *norm_vectors(vectors, 0))
        term, grad_gain, grad_shift = pull(total)
        input_grad[span(r)] = (grad_middle[span(r)] + term).astype(bf16)
        run[0, 4:5] += grad_gain
        run[0, 8:9] += grad_shift
        for kind in range(3):
            row_copy(kind, r).wait_send()
        return 0

    for kind in range(2):
        for r in range(pieces):
            row_copy(kind, r).start()
    for s in range(2):
        q1[s, 0].start()
        o1[s, 0].start()
    for k in (3, 2, 1):
        ur[k - 1].start()
    for s in range(2):
        o1[s, 1].start()
    lax.fori_loop(0, pieces, send_across, 0)

    def q_terms(s, i, far):
        p = places[i]
        if s == 0:
            v = 1 - y if far else y
            return q_ref[p, 0, v, :, x], r1q[0, i, v]
        v = 1 - x if far else x
        return q_ref[p, 1, y, :, v], r1q[1, i, :, v]

    def o_terms(s, i, far):
        p = places[i]
        if s == 0:
            v = 1 - y if far else y
            return o_ref[p, v, x, :, halves[0]], r1o[0, i, v]
        v = 1 - x if far else x
        return o_ref[p, y, v, :, halves[1]], r1o[1, i, v]

    for i in range(2):
        for s in range(2):
            q1[s, i].wait_recv()
            t2q[s, i] = low(*q_terms(s, i, True)).astype(bf16)
            q2[s, i].start()
            o1[s, i].wait_recv()
            t2o[s, i] = low(*o_terms(s, i, True)).astype(bf16)
            o2[s, i].start()
        if i == 0:
            for s in range(2):
                q1[s, 1].start()
            lax.fori_loop(0, pieces, take, 0)
            vs[0].start()
            for s in range(2):
                q2[s, 0].wait_recv()
                t3q[s] = low(*q_terms(s, 0, False), r2q[s, 0]).astype(bf16)
                q3[s].start()
                o2[s, 0].wait_recv()
                t3o[s] = low(*o_terms(s, 0, False), r2o[s, 0]).astype(bf16)
                o3[s].start()
    next_sum(0)
    for s in range(2):
        q2[s, 1].wait_recv()
        o2[s, 1].wait_recv()
        q3[s].wait_recv()
        total = low(*q_terms(s, 1, False), r2q[s, 1], r3q[s])
        fq[s] = total.astype(bf16)
        for j in range(2):
            @pl.when((b == s) & (c == j))
            def _():
                rq[s, j] = total[j]
        o3[s].wait_recv()
        ro[:, halves[s]] = low(*o_terms(s, 1, False), r2o[s, 1], r3o[s])
        next_sum(1 + s)
    for k in (3, 2, 1):
        qr[k - 1].start()
    gu[b, c] = u_ref[b, c]
    for k in (1, 2, 3):
        ur[k - 1].wait_recv()
    next_sum(3)
    for k in (1, 2, 3):
        pb, pc = ranks[k]
        qr[k - 1].wait_recv()
        rq[pb, pc] = gq[k - 1].astype(f32)
    for pb in range(2):
        for j in range(4):
            zero, one = rq[pb, 0], rq[pb, 1]
            h = head_of(j // 2, pb, j % 2, 0) * HD
            q, k = slice(j * 128, j * 128 + HD), slice(j * 128 + HD, j * 128 + 128)
            v = slice(512 + j * HD, 512 + j * HD + HD)
            for t, cols in enumerate((q, k, v)):
                out_q[:, t * 1024 + h:t * 1024 + h + 128] = jnp.concatenate([zero[:, cols], one[:, cols]], 1)
            for pc in range(2):
                col = head_of(j // 2, pb, j % 2, pc) * 256
                out_u[:, col:col + 256] = gu[pb, pc, :, j * 256:j * 256 + 256].astype(f32)
    next_sum(4)
    for copy in made:
        copy.wait_send()


def reduce_all(gw_qkv, gw_out, up_sum, part, tokens, grad_middle, params, vectors, cid):
    f32, bf16 = jnp.float32, jnp.bfloat16
    V = pltpu.VMEM
    vm = pl.BlockSpec(memory_space=V)
    S = jax.ShapeDtypeStruct
    q, o, u = gw_qkv.shape[5:], (gw_out.shape[3], 512), up_sum.shape
    rows, n = grad_middle.shape
    scratch = [
        V((rows, n), f32), V((rows, n), f32), V((rows, n), bf16), V((rows, n), bf16),
        pltpu.SemaphoreType.DMA((3, rows // PIECE)), pltpu.SemaphoreType.DMA((3, rows // PIECE)),
        V((2, 2) + q, f32), V(u, bf16),
        V((2, 2, 2, 2) + q, bf16), V((2, 2, 2) + q, bf16), V((2, 2, 2) + q, bf16), V((2, 2) + q, bf16), V((2, 2) + q, bf16),
        V((2, 2) + q, bf16), V((3,) + q, bf16),
        V((2, 2, 2) + o, bf16), V((2, 2) + o, bf16), V((2, 2) + o, bf16), V((2,) + o, bf16), V((2,) + o, bf16),
        V((5, 16, 1024), f32), V((5, 16, 1024), f32),
        pltpu.SemaphoreType.DMA((32,)), pltpu.SemaphoreType.DMA((32,))]
    return pl.pallas_call(
        reduce_kernel,
        out_shape=(S((q[0], 4 * q[1]), f32), S((o[0], 1024), f32), S((u[2], 4 * u[3]), f32), S((16, 1024), f32), S((rows, n), bf16)),
        in_specs=[vm] * 17, out_specs=(vm,) * 5, scratch_shapes=scratch,
        compiler_params=pltpu.CompilerParams(collective_id=cid, has_side_effects=True, vmem_limit_bytes=48 << 20),
        name="reduce_all",
    )(gw_qkv, gw_out, up_sum, part.reshape(2, 2, rows, n), tokens, grad_middle, params, *vectors)


def qk_columns(head):
    return slice(head * HD, head * HD + HD), slice(1024 + head * HD, 1024 + head * HD + HD), slice(2048 + head * HD, 2048 + head * HD + HD)


def head_of(a, b, y, c):
    return a * 8 + b * 4 + y * 2 + c


def start_kernel(q_hbm, u_hbm, o_in, t_in, v_in, wq, wo, up, rows, vec, q_in, u_in, q_src, u_src, send_sem, recv_sem, own_sem):
    a, b, y, c, x = place()
    barrier = pltpu.get_barrier_semaphore()

    def at(pa, pb, py, pc, px):
        return (pa * 8 + pb * 4 + py * 2 + pc, px)

    to_x, to_y, to_a = at(a, b, y, c, 1 - x), at(a, b, 1 - y, c, x), at(1 - a, b, y, c, x)
    ranks = [(lax.rem(b + k // 2, 2), lax.rem(c + k % 2, 2)) for k in range(4)]
    to_rank = [at(a, pb, y, pc, x) for pb, pc in ranks]
    for dev in [to_x, to_y, to_a] + to_rank[1:]:
        pl.semaphore_signal(barrier, inc=1, device_id=dev, device_id_type=MESH)

    loads = [pltpu.make_async_copy(q_hbm, q_in, own_sem.at[5]), pltpu.make_async_copy(u_hbm, u_in, own_sem.at[6])]
    for copy in loads:
        copy.start()
    for copy in loads:
        copy.wait()

    for pb in range(2):
        for pc in range(2):
            for j in range(4):
                q, k, v = qk_columns(head_of(j // 2, pb, j % 2, pc))
                q_src[pb, pc, :, j * 128:j * 128 + 128] = jnp.concatenate([q_in[:, q], q_in[:, k]], 1)
            for j in range(2):
                v0 = qk_columns(head_of(j, pb, 0, pc))[2]
                v1 = qk_columns(head_of(j, pb, 1, pc))[2]
                q_src[pb, pc, :, 512 + j * 128:640 + j * 128] = jnp.concatenate([q_in[:, v0], q_in[:, v1]], 1)
            for j in range(4):
                col = (head_of(j // 2, pb, j % 2, pc)) * 256
                u_src[pb, pc, :, j * 256:j * 256 + 256] = u_in[:, col:col + 256]
    own = [pltpu.make_async_copy(src, dst, own_sem.at[k]) for k, (src, dst) in enumerate((
        (q_src.at[b, c], wq.at[a, b, y, c, x]), (u_src.at[b, c], up.at[0, b, c]), (o_in, wo.at[a, y, x]),
        (t_in, rows.at[0]), (v_in, vec.at[a, b, y, c, x])))]
    for copy in own:
        copy.start()
    pl.semaphore_wait(barrier, 6)

    made = []

    def remote(src, dst, dev):
        k = len(made)
        made.append(pltpu.make_async_remote_copy(
            src_ref=src, dst_ref=dst, send_sem=send_sem.at[k], recv_sem=recv_sem.at[k],
            device_id=dev, device_id_type=MESH))
        return made[-1]

    places = [a, 1 - a]
    halves = [slice(0, 512), slice(512, 1024)]
    lateral = [(to_y, to_x), (to_x, to_y)]

    def same(ref, dev):
        return remote(ref, ref, dev)

    q_rank = [remote(q_src.at[ranks[k][0], ranks[k][1]], wq.at[a, b, y, c, x], to_rank[k]) for k in range(1, 4)]
    u_rank = [remote(u_src.at[ranks[k][0], ranks[k][1]], up.at[0, b, c], to_rank[k]) for k in range(1, 4)]
    v_rank = [remote(v_in, vec.at[a, b, y, c, x], to_rank[k]) for k in range(1, 4)]
    t_core, t_near = remote(t_in, rows.at[1], to_rank[1]), remote(t_in, rows.at[2], to_rank[2])
    t_far = remote(rows.at[2], rows.at[3], to_rank[1])
    u_cube = remote(up.at[0], up.at[1], to_a)
    v_cube = [same(vec.at[a, :, y, :, x], to_a), same(vec.at[:, :, y, :, x], to_y), same(vec.at[:, :, :, :, x], to_x)]
    q_cube = [same(wq.at[a, s, y, :, x], to_a) for s in range(2)]
    o_cube = [remote(o_in.at[:, halves[s]], wo.at[a, y, x, :, halves[s]], to_a) for s in range(2)]
    q_side, o_side = {}, {}
    for i in range(2):
        for s in range(2):
            one, two = lateral[s]
            oy, ox = (1 - y, x) if s == 0 else (y, 1 - x)
            p = places[i]
            mine, theirs = wq.at[p, s, y, :, x], wq.at[p, s, oy, :, ox]
            q_side[s, i] = (same(mine, one), same(mine, two), same(theirs, two))
            mine, theirs = wo.at[p, y, x, :, halves[s]], wo.at[p, oy, ox, :, halves[s]]
            first = o_in.at[:, halves[s]] if i == 0 else mine
            o_side[s, i] = (remote(first, mine, one), remote(first, mine, two), same(theirs, two))

    for k in (2, 1, 0):
        q_rank[k].start()
        v_rank[k].start()
    for s in range(2):
        o_cube[s].start()
        o_side[s, 0][0].start()
        o_side[s, 0][1].start()
    t_near.start()
    t_core.start()
    own[0].wait()
    for copy in q_rank:
        copy.wait_recv()
    for s in range(2):
        q_cube[s].start()
        q_side[s, 0][0].start()
        q_side[s, 0][1].start()
    own[4].wait()
    for copy in v_rank:
        copy.wait_recv()
    v_cube[0].start()
    for k in (2, 1, 0):
        u_rank[k].start()
    for s in range(2):
        o_side[s, 0][0].wait_recv()
        o_side[s, 0][2].start()
    for s in range(2):
        o_cube[s].wait_recv()
        o_side[s, 1][0].start()
        o_side[s, 1][1].start()
    t_near.wait_recv()
    t_far.start()
    for s in range(2):
        q_side[s, 0][0].wait_recv()
        q_side[s, 0][2].start()
    for s in range(2):
        q_cube[s].wait_recv()
        q_side[s, 1][0].start()
        q_side[s, 1][1].start()
    v_cube[0].wait_recv()
    v_cube[1].start()
    own[1].wait()
    for copy in u_rank:
        copy.wait_recv()
    u_cube.start()
    for s in range(2):
        o_side[s, 1][0].wait_recv()
        o_side[s, 1][2].start()
    v_cube[1].wait_recv()
    v_cube[2].start()
    for s in range(2):
        q_side[s, 1][0].wait_recv()
        q_side[s, 1][2].start()
    v_cube[2].wait_recv()
    t_core.wait_recv()
    t_far.wait_recv()
    for i in range(2):
        for s in range(2):
            for k in (1, 2):
                q_side[s, i][k].wait_recv()
                o_side[s, i][k].wait_recv()
    u_cube.wait_recv()
    for k in (2, 3):
        own[k].wait()
    for copy in made:
        copy.wait_send()


def start_gather(w_qkv, w_up, w_out, tokens, vectors, cid):
    bf16 = jnp.bfloat16
    S = lambda *shape: jax.ShapeDtypeStruct(shape, bf16)
    vm, anywhere = pl.BlockSpec(memory_space=pltpu.VMEM), pl.BlockSpec(memory_space=pl.ANY)
    return pl.pallas_call(
        start_kernel,
        out_shape=(S(2, 2, 2, 2, 2, 32, 768), S(2, 2, 2, 32, 1024), S(2, 2, 2, 32, 1024), S(4, 128, 1024),
                   S(2, 2, 2, 2, 2, 16, 128)),
        in_specs=[pl.BlockSpec(memory_space=pltpu.HBM)] * 4 + [vm], out_specs=(anywhere,) * 5,
        scratch_shapes=[
            pltpu.VMEM(w_qkv.shape, bf16), pltpu.VMEM(w_up.shape, bf16),
            pltpu.VMEM((2, 2, 32, 768), bf16), pltpu.VMEM((2, 2, 32, 1024), bf16),
            pltpu.SemaphoreType.DMA((48,)), pltpu.SemaphoreType.DMA((48,)), pltpu.SemaphoreType.DMA((7,))],
        compiler_params=pltpu.CompilerParams(collective_id=cid, has_side_effects=True, vmem_limit_bytes=32 << 20),
        cost_estimate=pl.CostEstimate(flops=0, bytes_accessed=100 << 20, transcendentals=0),
        name="start_gather",
    )(w_qkv, w_up, w_out, tokens, vectors)


PIECE = 32


def rows_kernel(step, gather, count_in, count_out, part, *refs):
    ins, outs = refs[:count_in], refs[count_in:count_in + count_out]
    rest = refs[count_in + count_out:]
    rows = rest[0] if gather else None
    got_far, got_near, sums, got_sums, send_sem, recv_sem = rest[-6:]
    a, b, y, c, x = place()

    def at(pb, pc):
        return (a * 8 + pb * 4 + y * 2 + pc, x)

    to_b, to_core = at(1 - b, c), at(b, 1 - c)
    barrier = pltpu.get_barrier_semaphore()
    for dev in (to_b, to_core):
        pl.semaphore_signal(barrier, inc=1, device_id=dev, device_id_type=MESH)
    pl.semaphore_wait(barrier, 2)
    pieces = part.shape[2] // PIECE

    def span(r):
        return pl.ds(pl.multiple_of(r * PIECE, PIECE), PIECE)

    def remote(kind, r, src, dst, dev):
        return pltpu.make_async_remote_copy(
            src_ref=src, dst_ref=dst, send_sem=send_sem.at[kind, r], recv_sem=recv_sem.at[kind, r],
            device_id=dev, device_id_type=MESH)

    def far(r):
        return remote(0, r, part.at[1, 1, span(r)], got_far.at[span(r)], to_core)

    def near(r):
        return remote(1, r, part.at[0, 1, span(r)], got_near.at[span(r)], to_core)

    def across(r):
        return remote(2, r, sums.at[span(r)], got_sums.at[span(r)], to_b)

    def row_near(r):
        return remote(3, r, rows.at[0, span(r)], rows.at[2, span(r)], to_b)

    def row_core(r):
        return remote(4, r, rows.at[0, span(r)], rows.at[1, span(r)], to_core)

    def row_far(r):
        return remote(5, r, rows.at[2, span(r)], rows.at[3, span(r)], to_core)

    for r in range(pieces):
        far(r).start()
    for r in range(pieces):
        near(r).start()

    def send_across(r, _):
        far(r).wait_recv()
        sums[span(r)] = (part[1, 0, span(r)] + got_far[span(r)]).astype(jnp.bfloat16)
        across(r).start()
        return 0

    lax.fori_loop(0, pieces, send_across, 0)
    for ref in outs:
        if ref.shape[0] == 1:
            ref[...] = jnp.zeros_like(ref)

    def take(r, _):
        near(r).wait_recv()
        across(r).wait_recv()
        total = part[0, 0, span(r)] + got_near[span(r)] + got_sums[span(r)].astype(jnp.float32)
        piece = step(span(r), total, ins, outs)
        if gather:
            rows[0, span(r)] = piece
            row_near(r).start()
            row_core(r).start()
        return 0

    lax.fori_loop(0, pieces, take, 0)

    def relay(r, _):
        row_near(r).wait_recv()
        row_far(r).start()
        return 0

    def finish(r, _):
        if gather:
            row_core(r).wait_recv()
            row_far(r).wait_recv()
            row_near(r).wait_send()
            row_core(r).wait_send()
            row_far(r).wait_send()
        far(r).wait_send()
        near(r).wait_send()
        across(r).wait_send()
        return 0

    if gather:
        lax.fori_loop(0, pieces, relay, 0)
    lax.fori_loop(0, pieces, finish, 0)


def sum_rows(step, part, ins, outs, gather, cid):
    rows, n = part.shape[0] // 4, part.shape[1]
    vm = pl.BlockSpec(memory_space=pltpu.VMEM)
    shapes = tuple(outs) + ((jax.ShapeDtypeStruct((4, rows, n), jnp.bfloat16),) if gather else ())
    V = pltpu.VMEM
    return pl.pallas_call(
        functools.partial(rows_kernel, step, gather, len(ins), len(outs)),
        out_shape=shapes, in_specs=[vm] * (1 + len(ins)), out_specs=(vm,) * len(shapes),
        scratch_shapes=[V((rows, n), jnp.float32), V((rows, n), jnp.float32), V((rows, n), jnp.bfloat16), V((rows, n), jnp.bfloat16),
                        pltpu.SemaphoreType.DMA((6, rows // PIECE)), pltpu.SemaphoreType.DMA((6, rows // PIECE))],
        compiler_params=pltpu.CompilerParams(collective_id=cid, has_side_effects=True, vmem_limit_bytes=32 << 20),
        cost_estimate=pl.CostEstimate(flops=0, bytes_accessed=50 << 20, transcendentals=0),
        name="sum_rows",
    )(part.reshape(2, 2, rows, n), *ins)


def norm_vectors(vectors, k):
    return vectors[4 + k:5 + k], vectors[8 + k:9 + k]


def attended_step(span, total, ins, outs):
    tokens, vectors = ins
    branch = total + vectors[2:3]
    middle = tokens[span].astype(jnp.float32) + norm_rows(branch, *norm_vectors(vectors, 1))
    outs[0][span] = branch
    outs[1][span] = middle
    return norm_rows(middle, *norm_vectors(vectors, 2)).astype(jnp.bfloat16)


def output_step(span, total, ins, outs):
    middle, grad_out, vectors = ins
    normed, pull = jax.vjp(norm_rows, total + vectors[3:4], *norm_vectors(vectors, 3))
    outs[0][span] = (middle[span] + normed).astype(jnp.bfloat16)
    grad_down, grad_gain, grad_shift = pull(grad_out[span])
    grad_down = grad_down.astype(jnp.bfloat16)
    outs[1][...] += grad_gain
    outs[2][...] += grad_shift
    outs[3][...] += jnp.sum(grad_down.astype(jnp.float32), 0, keepdims=True)
    return grad_down


def middle_step(span, total, ins, outs):
    middle, branch, grad_out, vectors = ins
    _, pull = jax.vjp(norm_rows, middle[span], *norm_vectors(vectors, 2))
    part, grad_gain2, grad_shift2 = pull(total)
    grad_middle = grad_out[span] + part
    _, pull = jax.vjp(norm_rows, branch[span], *norm_vectors(vectors, 1))
    grad_branch, grad_gain1, grad_shift1 = pull(grad_middle)
    grad_branch = grad_branch.astype(jnp.bfloat16)
    outs[0][span] = grad_middle
    for ref, value in zip(outs[1:], (grad_gain2, grad_shift2, grad_gain1, grad_shift1,
                                     jnp.sum(grad_branch.astype(jnp.float32), 0, keepdims=True))):
        ref[...] += value
    return grad_branch


def fast_body(tokens, cotangent, lengths, assign, w_qkv, qv_bias, w_out, out_bias, w_up, up_bias, w_down, down_bias,
              norm_gain, norm_shift):
    bf16, f32 = jnp.bfloat16, jnp.float32
    a, b, y, c, x = place()
    spot = jnp.stack([a, y, x]).astype(jnp.int32)
    width = tokens.shape[2]
    place_two = jnp.arange(2, dtype=jnp.int32)
    sequence = jnp.sum(jnp.where(place_two == x, assign.astype(jnp.int32), 0))
    valid = jnp.sum(jnp.where(place_two == sequence, lengths.astype(jnp.int32), 0))

    small = jnp.concatenate([qv_bias, out_bias[None], down_bias[None], norm_gain, norm_shift], 0)
    small = jnp.concatenate([jnp.pad(small, ((0, 0), (0, 96))), up_bias[None], jnp.zeros((3, 128), bf16)], 0)
    wqkv, wo, up_one, rows, small = start_gather(w_qkv, w_up, w_out, tokens[0], small, 6)
    down_one = after(w_down, wqkv)
    down_one = jnp.stack([down_one, flip_a(down_one)])
    wqkv, wo, rows = wqkv.reshape(width, 768), wo.reshape(256, width), rows.reshape(512, width)

    vectors = small[..., :12, :32].reshape(32, 12, 32).transpose(1, 0, 2).reshape(12, width).astype(f32)
    qv_half = pick(pick(vectors[:2].reshape(2, 2, 2, 2, 2, HD), b, 2), c, 3).reshape(2, 4, HD)
    qk_shift = jnp.concatenate([qv_half[0], jnp.zeros((4, HD), f32)], 1).reshape(512)
    v_shift = qv_half[1].reshape(256)
    up_shift = pick(pick(small[..., 12, :], b, 1), c, 2).reshape(1024).astype(f32)

    first = norm_rows(rows.astype(f32), vectors[4:5], vectors[8:9]).astype(bf16)
    up_two = cube_one(flip_x, up_one)
    projected = (dot_nn(first, wqkv) + jnp.concatenate([qk_shift, v_shift])).astype(bf16)
    packed = exchange(after(projected, up_two, down_one), True, 1).reshape(8, 384, 128)
    down_two = cube_one(flip_x, down_one)
    up_half = flip_y(after(up_two, packed)[:, 0])
    attended = attend(valid[None], packed).reshape(2, 2, 2, 128, 128)
    attended = exchange(after(attended, down_two, up_half), False, 2)
    up_all = jnp.concatenate([up_two, jnp.stack([up_half, flip_y(after(up_two, attended)[:, 1])], 1)], 0)
    down_far = flip_y(after(down_two, attended))
    own_spot = lax.axis_index("seq") * 128 + jnp.arange(128, dtype=jnp.int32)
    grad_out = cotangent[0].astype(f32) * (own_spot < valid).astype(f32)[:, None]
    S = jax.ShapeDtypeStruct
    wide, low, line = S((128, width), f32), S((128, width), bf16), S((1, width), f32)
    branch, middle, third = sum_rows(
        attended_step, dot_nn(attended, wo), (tokens[0], vectors),
        (wide, wide), True, 7)
    third = third.reshape(512, width)
    wu = arrange(spot, [(up_all, False)])[0].reshape(width, 1024)
    up_pre = dot_nn(third, wu) + up_shift
    active, pull_gelu = jax.vjp(exact_gelu, up_pre)
    active = active.astype(bf16)
    down_all = jnp.concatenate([down_two, after(down_far, active)], 0)
    wd = arrange(spot, [(down_all, False)])[0].reshape(1024, width)
    output, gain4, shift4, bias_down, down_rows = sum_rows(
        output_step, dot_nn(active, wd), (middle, grad_out, vectors), (low, line, line, line), True, 8)
    down_rows = down_rows.reshape(512, width)
    gw_down = contract_rows(active, down_rows).astype(bf16).reshape(2, 2, 2, 128, width)
    down_term = flip_y(pick(gw_down, 1 - y, 1, True))
    (grad_up,) = pull_gelu(dot_nt(after(down_rows, gw_down), wd))
    grad_up = grad_up.astype(bf16)
    gw_up = contract_rows(third, grad_up).astype(bf16).reshape(2, 2, 2, 2, 2, 32, 1024)
    up_term = flip_x(pick(gw_up, 1 - x, 4, True))
    grad_middle, gain3, shift3, gain2, shift2, bias_out, branch_rows = sum_rows(
        middle_step, after(dot_nt(grad_up, wu), gw_up),
        (middle, branch, grad_out, vectors), (wide,) + (line,) * 5, True, 9)
    branch_rows = branch_rows.reshape(512, width)
    grad_att = dot_nt(branch_rows, wo).astype(bf16)
    down_sum = add_low(pick(gw_down, y, 1, True), down_term)
    down_term = flip_x(pick(down_sum, 1 - x, 2, True))
    grad_packed = exchange(after(grad_att, down_sum), True, 3).reshape(8, 128, 128)
    up_sum = add_low(pick(gw_up, x, 4, True), after(up_term, grad_packed))
    up_term = flip_y(pick(up_sum, 1 - y, 2, True))
    down_sum = add_low(pick(down_sum, x, 2, True), after(down_term, grad_packed))
    down_term = flip_a(pick(down_sum, 1 - a, 0))
    back = attend_back(valid[None], packed, grad_packed)

    up_sum = add_low(pick(up_sum, y, 2, True), up_term)
    gw_out = contract_rows(attended, branch_rows).astype(bf16).reshape(2, 2, 2, 32, width)
    grad_qkv = exchange(after(back, up_sum, down_term).reshape(2, 2, 2, 384, 128), False, 4)
    up_term = flip_a(pick(after(up_sum, grad_qkv), 1 - a, 0))
    gw_qkv = contract_rows(first, grad_qkv).astype(bf16).reshape(2, 2, 2, 2, 2, 32, 768)
    def sums(block):
        return jnp.sum(block.astype(f32), 0, keepdims=True)

    sums_of = [sums(grad_qkv), sums(grad_up), bias_out, bias_down, gain2, gain3, gain4, shift2, shift3, shift4]
    up_sum = (pick(up_sum, a, 0).astype(f32) + up_term.astype(f32)).astype(bf16).reshape(2, 2, 32, 1024)
    r_qkv, r_out, r_up, vectors, input_grad = reduce_all(
        gw_qkv, gw_out, up_sum, dot_nt(grad_qkv, wqkv), tokens[0], grad_middle, vectors, sums_of, 5)
    r_down = (pick(down_sum, a, 0).astype(f32) + down_term.astype(f32)).reshape(128, width)
    index = lax.axis_index("seq") * 2 + x
    small_up = lax.dynamic_slice(vectors, (12 + index // 8, index % 8 * 128), (1, 128)).reshape(128)
    vectors = lax.dynamic_slice(vectors, (0, index * 32), (12, 32))

    return (
        output[None], input_grad[None], r_qkv, vectors[:2], r_out,
        vectors[2], r_up, small_up, r_down, vectors[3], vectors[4:8], vectors[8:12])


def solution(mesh):
    return jax.shard_map(
        fast_body if is_small(mesh) else body,
        mesh=mesh,
        in_specs=(
            P("dp", "seq", None),
            P("dp", "seq", None),
            P(),
            P(),
            P(("seq", "dp"), None),
            P(None, ("seq", "dp")),
            P(("seq", "dp"), None),
            P(("seq", "dp")),
            P(("seq", "dp"), None),
            P(("seq", "dp")),
            P(("seq", "dp"), None),
            P(("seq", "dp")),
            P(None, ("seq", "dp")),
            P(None, ("seq", "dp")),
        ),
        out_specs=(
            P("dp", "seq", None),
            P("dp", "seq", None),
            P(("seq", "dp"), None),
            P(None, ("seq", "dp")),
            P(("seq", "dp"), None),
            P(("seq", "dp")),
            P(("seq", "dp"), None),
            P(("seq", "dp")),
            P(("seq", "dp"), None),
            P(("seq", "dp")),
            P(None, ("seq", "dp")),
            P(None, ("seq", "dp")),
        ),
        check_vma=False,
    )
```

```python
import functools
import math

import jax
import jax.numpy as jnp
from jax import lax
from jax.experimental import pallas as pl
from jax.experimental.pallas import tpu as pltpu
from jax.sharding import PartitionSpec as P


HD = 64


RELAX_SCALE = 32.0
NORM_EPSILON = 1e-05


def norm_rows(values, gain, shift):
    center = values - jnp.mean(values, -1, keepdims=True)
    spread = jnp.mean(center * center, -1, keepdims=True)
    return center * lax.rsqrt(spread + NORM_EPSILON) * gain + shift


def exact_gelu(values):
    return jax.nn.gelu(values, approximate=False)


def contract_rows(left, right):
    return lax.dot_general(
        left, right, (((0,), (0,)), ((), ())), preferred_element_type=jnp.float32
    )


def contract_cols(left, right):
    return lax.dot_general(
        left, right, (((1,), (1,)), ((), ())), preferred_element_type=jnp.float32
    )


def split_heads(block):
    return block.reshape(block.shape[0], 2, HD)


def pair_scores(query_part, key_part):
    factor = 1.0 / (RELAX_SCALE * math.sqrt(HD))
    return (
        jnp.einsum(
            "qhd,khd->hqk",
            split_heads(query_part),
            split_heads(key_part),
            preferred_element_type=jnp.float32,
        )
        * factor
    )


def kept_probs(scores, allowed, row_max, row_total):
    exp_terms = jnp.exp(jnp.where(allowed, RELAX_SCALE * (scores - row_max), -jnp.inf))
    return exp_terms / row_total


def body(
    tokens,
    cotangent,
    lengths,
    assign,
    w_qkv,
    qv_bias,
    w_out,
    out_bias,
    w_up,
    up_bias,
    w_down,
    down_bias,
    norm_gain,
    norm_shift,
):
    gathered = (
        lax.all_gather(w_qkv, ("seq", "dp"), axis=0, tiled=True),
        lax.all_gather(w_out, ("seq", "dp"), axis=0, tiled=True),
        lax.all_gather(w_up, ("seq", "dp"), axis=0, tiled=True),
        lax.all_gather(w_down, ("seq", "dp"), axis=0, tiled=True),
        lax.all_gather(qv_bias, ("seq", "dp"), axis=1, tiled=True),
        lax.all_gather(out_bias, ("seq", "dp"), axis=0, tiled=True),
        lax.all_gather(up_bias, ("seq", "dp"), axis=0, tiled=True),
        lax.all_gather(down_bias, ("seq", "dp"), axis=0, tiled=True),
        lax.all_gather(norm_gain, ("seq", "dp"), axis=1, tiled=True),
        lax.all_gather(norm_shift, ("seq", "dp"), axis=1, tiled=True),
    )
    qkv_full, out_full, up_full, down_full = (gathered[0], gathered[1], gathered[2], gathered[3])
    qv_shift = gathered[4].astype(jnp.float32)
    out_shift = gathered[5].astype(jnp.float32)
    up_shift = gathered[6].astype(jnp.float32)
    down_shift = gathered[7].astype(jnp.float32)
    gains = gathered[8].astype(jnp.float32)
    shifts = gathered[9].astype(jnp.float32)
    row_count = tokens.shape[1]
    model_width = tokens.shape[2]
    pair_cols = 2 * HD
    pair_count = model_width // pair_cols
    slot_rows = row_count * lax.axis_size("seq")
    factor = 1.0 / (RELAX_SCALE * math.sqrt(HD))
    valid = lengths[assign[lax.axis_index("dp")]]
    own_place = lax.axis_index("seq") * row_count + jnp.arange(row_count, dtype=jnp.int32)
    all_place = jnp.arange(slot_rows, dtype=jnp.int32)
    allowed = (all_place[None, :] <= own_place[:, None]) & (all_place[None, :] < valid)
    pair_ids = jnp.arange(pair_count, dtype=jnp.int32)
    hidden = tokens[0].astype(jnp.float32)
    normed_first, pull_first = jax.vjp(norm_rows, hidden, gains[0], shifts[0])
    normed_low = normed_first.astype(jnp.bfloat16)
    projected = jnp.dot(normed_low, qkv_full, preferred_element_type=jnp.float32)
    queries = (projected[:, :model_width] + qv_shift[0]).astype(jnp.bfloat16)
    key_own = projected[:, model_width : 2 * model_width].astype(jnp.bfloat16)
    value_own = (projected[:, 2 * model_width :] + qv_shift[1]).astype(jnp.bfloat16)
    keys, values = (
        lax.all_gather(key_own, "seq", axis=0, tiled=True),
        lax.all_gather(value_own, "seq", axis=0, tiled=True),
    )

    def columns(block, pair_index):
        return lax.dynamic_slice_in_dim(block, pair_index * pair_cols, pair_cols, 1)

    def merge_pairs(stack):
        return stack.transpose(1, 0, 2).reshape(stack.shape[1], model_width)

    def attend(pair_index):
        scores = pair_scores(columns(queries, pair_index), columns(keys, pair_index))
        row_max = jnp.max(jnp.where(allowed, scores, -jnp.inf), -1, keepdims=True)
        exp_terms = jnp.exp(jnp.where(allowed, RELAX_SCALE * (scores - row_max), -jnp.inf))
        row_total = jnp.sum(exp_terms, -1, keepdims=True)
        probs = (exp_terms / row_total).astype(jnp.bfloat16)
        mixed = jnp.einsum(
            "hqk,khd->qhd",
            probs,
            split_heads(columns(values, pair_index)),
            preferred_element_type=jnp.float32,
        )
        return (mixed.reshape(row_count, pair_cols), row_max[..., 0], row_total[..., 0])

    mixed_pairs, max_pairs, total_pairs = lax.map(attend, pair_ids)
    attended = merge_pairs(mixed_pairs).astype(jnp.bfloat16)
    branch = jnp.dot(attended, out_full, preferred_element_type=jnp.float32) + out_shift
    normed_second, pull_second = jax.vjp(norm_rows, branch, gains[1], shifts[1])
    middle = hidden + normed_second
    normed_third, pull_third = jax.vjp(norm_rows, middle, gains[2], shifts[2])
    third_low = normed_third.astype(jnp.bfloat16)
    up_pre = jnp.dot(third_low, up_full, preferred_element_type=jnp.float32) + up_shift
    activated, pull_gelu = jax.vjp(exact_gelu, up_pre)
    active_low = activated.astype(jnp.bfloat16)
    down_pre = jnp.dot(active_low, down_full, preferred_element_type=jnp.float32) + down_shift
    normed_fourth, pull_fourth = jax.vjp(norm_rows, down_pre, gains[3], shifts[3])
    output = (middle + normed_fourth).astype(jnp.bfloat16)[None]
    again = (
        lax.all_gather(w_qkv, ("seq", "dp"), axis=0, tiled=True),
        lax.all_gather(w_out, ("seq", "dp"), axis=0, tiled=True),
        lax.all_gather(w_up, ("seq", "dp"), axis=0, tiled=True),
        lax.all_gather(w_down, ("seq", "dp"), axis=0, tiled=True),
    )
    qkv_back, out_back, up_back, down_back = (again[0], again[1], again[2], again[3])
    keep_rows = (own_place < valid).astype(jnp.float32)[:, None]
    grad_out = cotangent[0].astype(jnp.float32) * keep_rows
    grad_down, grad_gain_four, grad_shift_four = pull_fourth(grad_out)
    grad_down_low = grad_down.astype(jnp.bfloat16)
    grad_w_down = contract_rows(active_low, grad_down_low)
    grad_b_down = jnp.sum(grad_down_low.astype(jnp.float32), 0)
    (grad_up,) = pull_gelu(contract_cols(grad_down_low, down_back))
    grad_up_low = grad_up.astype(jnp.bfloat16)
    grad_w_up = contract_rows(third_low, grad_up_low)
    grad_b_up = jnp.sum(grad_up_low.astype(jnp.float32), 0)
    grad_middle_part, grad_gain_three, grad_shift_three = pull_third(
        contract_cols(grad_up_low, up_back)
    )
    grad_middle = grad_out + grad_middle_part
    grad_branch, grad_gain_two, grad_shift_two = pull_second(grad_middle)
    grad_branch_low = grad_branch.astype(jnp.bfloat16)
    grad_w_out = contract_rows(attended, grad_branch_low)
    grad_b_out = jnp.sum(grad_branch_low.astype(jnp.float32), 0)
    grad_attended = contract_cols(grad_branch_low, out_back).astype(jnp.bfloat16)

    def query_side(pair_index):
        scores = pair_scores(columns(queries, pair_index), columns(keys, pair_index))
        probs = kept_probs(
            scores, allowed, max_pairs[pair_index][..., None], total_pairs[pair_index][..., None]
        )
        grad_part = columns(grad_attended, pair_index)
        grad_probs = jnp.einsum(
            "qhd,khd->hqk",
            split_heads(grad_part),
            split_heads(columns(values, pair_index)),
            preferred_element_type=jnp.float32,
        )
        delta = jnp.sum(probs * grad_probs, -1, keepdims=True)
        grad_scores = (RELAX_SCALE * probs * (grad_probs - delta)).astype(jnp.bfloat16)
        grad_query = (
            jnp.einsum(
                "hqk,khd->qhd",
                grad_scores,
                split_heads(columns(keys, pair_index)),
                preferred_element_type=jnp.float32,
            )
            * factor
        )
        return (grad_query.reshape(row_count, pair_cols), grad_scores, probs, delta)

    def both_sides(pair_index):
        grad_query, grad_scores, probs, delta = query_side(pair_index)
        grad_part = columns(grad_attended, pair_index)
        grad_key = (
            jnp.einsum(
                "hqk,qhd->khd",
                grad_scores,
                split_heads(columns(queries, pair_index)),
                preferred_element_type=jnp.float32,
            )
            * factor
        )
        grad_value = jnp.einsum(
            "hqk,qhd->khd",
            probs.astype(jnp.bfloat16),
            split_heads(grad_part),
            preferred_element_type=jnp.float32,
        )
        return (
            grad_query,
            grad_key.reshape(slot_rows, pair_cols),
            grad_value.reshape(slot_rows, pair_cols),
        )

    query_pairs, key_terms, value_terms = lax.map(both_sides, pair_ids)
    key_pairs, value_pairs = (
        lax.psum_scatter(
            key_terms.astype(jnp.bfloat16), "seq", scatter_dimension=1, tiled=True
        ).astype(jnp.float32),
        lax.psum_scatter(
            value_terms.astype(jnp.bfloat16), "seq", scatter_dimension=1, tiled=True
        ).astype(jnp.float32),
    )
    grad_q_low = merge_pairs(query_pairs).astype(jnp.bfloat16)
    grad_k_low = merge_pairs(key_pairs).astype(jnp.bfloat16)
    grad_v_low = merge_pairs(value_pairs).astype(jnp.bfloat16)
    grad_projected = jnp.concatenate([grad_q_low, grad_k_low, grad_v_low], 1)
    grad_w_qkv = contract_rows(normed_low, grad_projected)
    grad_qv = jnp.stack(
        [jnp.sum(grad_q_low.astype(jnp.float32), 0), jnp.sum(grad_v_low.astype(jnp.float32), 0)]
    )
    grad_hidden_part, grad_gain_one, grad_shift_one = pull_first(
        contract_cols(grad_projected, qkv_back)
    )
    input_grad = (grad_middle + grad_hidden_part).astype(jnp.bfloat16)[None]
    grad_gains = jnp.stack([grad_gain_one, grad_gain_two, grad_gain_three, grad_gain_four])
    grad_shifts = jnp.stack([grad_shift_one, grad_shift_two, grad_shift_three, grad_shift_four])
    owned = (
        lax.psum_scatter(grad_w_qkv, ("seq", "dp"), scatter_dimension=0, tiled=True),
        lax.psum_scatter(grad_w_out, ("seq", "dp"), scatter_dimension=0, tiled=True),
        lax.psum_scatter(grad_w_up, ("seq", "dp"), scatter_dimension=0, tiled=True),
        lax.psum_scatter(grad_w_down, ("seq", "dp"), scatter_dimension=0, tiled=True),
        lax.psum_scatter(grad_qv, ("seq", "dp"), scatter_dimension=1, tiled=True),
        lax.psum_scatter(grad_b_out, ("seq", "dp"), scatter_dimension=0, tiled=True),
        lax.psum_scatter(grad_b_up, ("seq", "dp"), scatter_dimension=0, tiled=True),
        lax.psum_scatter(grad_b_down, ("seq", "dp"), scatter_dimension=0, tiled=True),
        lax.psum_scatter(grad_gains, ("seq", "dp"), scatter_dimension=1, tiled=True),
        lax.psum_scatter(grad_shifts, ("seq", "dp"), scatter_dimension=1, tiled=True),
    )
    return (
        output,
        input_grad,
        owned[0],
        owned[4],
        owned[1],
        owned[5],
        owned[2],
        owned[6],
        owned[3],
        owned[7],
        owned[8],
        owned[9],
    )


MESH = pl.DeviceIdType.MESH


def is_small(mesh):
    return mesh.shape["seq"] == 16 and mesh.shape["dp"] == 2


def place():
    seq = lax.axis_index("seq")
    return seq // 8, (seq // 4) % 2, (seq // 2) % 2, seq % 2, lax.axis_index("dp")


def exchange_copies(scatter, src, out, send_sem, recv_sem, own_sem):
    a, b, y, c, x = place()

    def peer(k):
        return lax.rem(a + k // 2, 2), lax.rem(y + k % 2, 2)

    def device(k):
        pa, py = peer(k)
        return (pa * 8 + b * 4 + py * 2 + c, x)

    def source(k):
        pa, py = peer(k)
        return src.at[pa * 2 + py] if scatter else src.at[pa, :, py]

    def target(k):
        pa, py = peer(k)
        return out.at[pa, :, py] if scatter else out.at[pa * 2 + py]

    def copy(k, dst):
        return pltpu.make_async_remote_copy(
            src_ref=source(k), dst_ref=target(dst), send_sem=send_sem.at[k], recv_sem=recv_sem.at[k],
            device_id=device(k), device_id_type=MESH)

    def greet():
        barrier = pltpu.get_barrier_semaphore()
        for k in range(1, 4):
            pl.semaphore_signal(barrier, inc=1, device_id=device(k), device_id_type=MESH)

    def run():
        own = pltpu.make_async_copy(source(0), target(0), own_sem)
        own.start()
        pl.semaphore_wait(pltpu.get_barrier_semaphore(), 3)
        for k in (3, 2, 1):
            copy(k, 0).start()
        own.wait()
        for k in (3, 2, 1):
            copy(k, k).wait_recv()
        for k in (3, 2, 1):
            copy(k, 0).wait_send()

    return greet, run


def row_block(i, j):
    _, b, _, c, _ = place()
    return pl.ds(pl.multiple_of(lax.rem(b + i, 2) * 256 + lax.rem(c + j, 2) * 128, 128), 128)


def to_heads_kernel(rows_ref, out, src, *sems):
    greet, run = exchange_copies(True, src, out, *sems)
    greet()
    low = src.shape[2] - 128
    for g in range(4):
        values = slice(low * 2 + g * HD, low * 2 + g * HD + HD)
        for i in range(2):
            if low:
                for j in range(2):
                    src[g, i, j * 128:j * 128 + 128] = rows_ref[row_block(i, j), g * 128:g * 128 + 128]
            src[g, i, low:] = jnp.concatenate([rows_ref[row_block(i, j), values] for j in range(2)], 1)
    run()


def from_heads_kernel(heads_ref, out, got, *sems):
    greet, run = exchange_copies(False, heads_ref, got, *sems)
    greet()
    run()
    low = got.shape[2] - 128
    c = place()[3]
    for i in range(2):
        if low:
            for j in range(2):
                for g in range(4):
                    out[row_block(i, j), g * 128:g * 128 + 128] = got[g, i, j * 128:j * 128 + 128]
        for g in (0, 2):
            left, right = got[g, i, low:], got[g + 1, i, low:]
            cols = slice(low * 2 + g * HD, low * 2 + g * HD + 128)
            for j in range(2):
                lanes = slice(j * HD, j * HD + HD)
                out[row_block(i, j), cols] = jnp.concatenate([left[:, lanes], right[:, lanes]], 1)


def exchange(blocks, scatter, cid):
    vm = pl.BlockSpec(memory_space=pltpu.VMEM)
    rows = blocks.shape[-1] // 2 if scatter else blocks.shape[-2]
    shape, held = (2, 2, 2, rows, 128), (4, 2, rows, 128)
    return pl.pallas_call(
        to_heads_kernel if scatter else from_heads_kernel,
        out_shape=jax.ShapeDtypeStruct(shape if scatter else (512, rows * 2), blocks.dtype),
        in_specs=[vm], out_specs=vm,
        scratch_shapes=[pltpu.VMEM(held, blocks.dtype), pltpu.SemaphoreType.DMA((4,)), pltpu.SemaphoreType.DMA((4,)),
                        pltpu.SemaphoreType.DMA],
        compiler_params=pltpu.CompilerParams(collective_id=cid, has_side_effects=True),
        cost_estimate=pl.CostEstimate(flops=0, bytes_accessed=rows * 100000, transcendentals=0),
        name="to_heads" if scatter else "from_heads",
    )(blocks)


def dot_nt(a, b):
    return lax.dot_general(a, b, (((1,), (1,)), ((), ())), preferred_element_type=jnp.float32)


def dot_nn(a, b):
    return jnp.dot(a, b, preferred_element_type=jnp.float32)


BQ = 256
MASKED = -1e30


def load_heads(valid, packed, q_ref, k_ref):
    rows = q_ref.shape[0]
    qk = packed[:, :256].reshape(rows, 128)
    kq = jnp.concatenate([qk[:, 64:], qk[:, :64]], axis=1)
    lane = lax.broadcasted_iota(jnp.int32, (rows, 128), 1)
    spot = lax.broadcasted_iota(jnp.int32, (rows, 128), 0)
    past = jnp.where(spot < valid, 0.0, MASKED)
    q_ref[...] = jnp.where(lane < 64, qk.astype(jnp.float32), jnp.where(lane == 64, 1.0, 0.0)).astype(jnp.bfloat16)
    k_ref[...] = jnp.where(lane < 64, kq.astype(jnp.float32), jnp.where(lane == 64, past, 0.0)).astype(jnp.bfloat16)


def unpack_rows(halves):
    n = halves.shape[0]
    return jnp.concatenate([halves[:, :, :64], halves[:, :, 64:]], axis=1).reshape(n * 256, 64)


def block_probs(q_ref, k_ref, i):
    n = (i + 1) * BQ
    scores = dot_nt(k_ref[:n], q_ref[i * BQ:n])
    key = lax.broadcasted_iota(jnp.int32, (BQ, BQ), 0)
    query = lax.broadcasted_iota(jnp.int32, (BQ, BQ), 1)
    corner = jnp.where(key <= query, scores[n - BQ:], MASKED)
    scores = jnp.concatenate([scores[:n - BQ], corner], axis=0) if i else corner
    top = jnp.max(scores, axis=0, keepdims=True)
    terms = jnp.exp((scores - top) * 0.125)
    return terms, 1.0 / jnp.sum(terms, axis=0, keepdims=True)


def attend_kernel(valid_ref, packed, out_ref, q_ref, k_ref, vt_ref):
    load_heads(valid_ref[0], packed, q_ref, k_ref)
    unit = jnp.where(
        lax.broadcasted_iota(jnp.int32, (64, 64), 0) == lax.broadcasted_iota(jnp.int32, (64, 64), 1), 1.0, 0.0
    ).astype(jnp.bfloat16)
    vt_ref[...] = dot_nt(unit, unpack_rows(packed[:, 256:])).astype(jnp.bfloat16)
    for i in range(q_ref.shape[0] // BQ):
        n = (i + 1) * BQ
        terms, scale = block_probs(q_ref, k_ref, i)
        probs = (terms * scale).astype(jnp.bfloat16)
        mixed = dot_nn(vt_ref[:, :n], probs).T
        out_ref[i] = jnp.concatenate([mixed[:128], mixed[128:]], axis=1).astype(jnp.bfloat16)


def attend_back_kernel(valid_ref, packed, grad, out_ref, q_ref, k_ref, v_ref, g_ref, kt_ref, dk_ref, dv_ref):
    load_heads(valid_ref[0], packed, q_ref, k_ref)
    v_ref[...] = unpack_rows(packed[:, 256:])
    g_ref[...] = unpack_rows(grad[...])
    unit = jnp.where(
        lax.broadcasted_iota(jnp.int32, (64, 128), 0) == lax.broadcasted_iota(jnp.int32, (64, 128), 1), 1.0, 0.0
    ).astype(jnp.bfloat16)
    kt_ref[...] = dot_nt(unit, k_ref[...]).astype(jnp.bfloat16)
    dk_ref[...] = jnp.zeros_like(dk_ref)
    dv_ref[...] = jnp.zeros_like(dv_ref)
    blocks = q_ref.shape[0] // BQ
    for i in range(blocks):
        n = (i + 1) * BQ
        terms, scale = block_probs(q_ref, k_ref, i)
        probs = terms * scale
        grad_probs = dot_nt(v_ref[:n], g_ref[i * BQ:n])
        delta = jnp.sum(probs * grad_probs, axis=0, keepdims=True)
        grad_scores = (probs * (grad_probs - delta)).astype(jnp.bfloat16)
        grad_query = dot_nn(kt_ref[:, :n], grad_scores).T * 0.125
        out_ref[i, :256, :64] = grad_query.astype(jnp.bfloat16)
        dk_ref[:n] += dot_nn(grad_scores, q_ref[i * BQ:n])
        dv_ref[:n] += dot_nn(probs.astype(jnp.bfloat16), g_ref[i * BQ:n])
    for i in range(blocks):
        rows = slice(i * BQ, (i + 1) * BQ)
        out_ref[i, :256, 64:] = (dk_ref[rows, :64] * 0.125).astype(jnp.bfloat16)
        value = dv_ref[rows].astype(jnp.bfloat16)
        out_ref[i, 256:] = jnp.concatenate([value[:128], value[128:]], axis=1)


def attend(valid, packed):
    rows = packed.shape[0] * 256
    vm = pl.BlockSpec(memory_space=pltpu.VMEM)
    return pl.pallas_call(
        attend_kernel,
        out_shape=jax.ShapeDtypeStruct((packed.shape[0], 128, 128), jnp.bfloat16),
        in_specs=[pl.BlockSpec(memory_space=pltpu.SMEM), vm], out_specs=vm,
        scratch_shapes=[pltpu.VMEM((rows, 128), jnp.bfloat16)] * 2 + [pltpu.VMEM((64, rows), jnp.bfloat16)],
        compiler_params=pltpu.CompilerParams(vmem_limit_bytes=48 << 20),
        name="attend",
    )(valid, packed)


def attend_back(valid, packed, grad):
    rows = packed.shape[0] * 256
    vm = pl.BlockSpec(memory_space=pltpu.VMEM)
    return pl.pallas_call(
        attend_back_kernel,
        out_shape=jax.ShapeDtypeStruct(packed.shape, jnp.bfloat16),
        in_specs=[pl.BlockSpec(memory_space=pltpu.SMEM), vm, vm], out_specs=vm,
        scratch_shapes=[pltpu.VMEM((rows, 128), jnp.bfloat16)] * 2 + [pltpu.VMEM((rows, 64), jnp.bfloat16)] * 2
        + [pltpu.VMEM((64, rows), jnp.bfloat16), pltpu.VMEM((rows, 128), jnp.float32), pltpu.VMEM((rows, 64), jnp.float32)],
        compiler_params=pltpu.CompilerParams(vmem_limit_bytes=48 << 20),
        name="attend_back",
    )(valid, packed, grad)


def flip(bits, block):
    return lax.ppermute(block, "seq", [(s, s ^ bits) for s in range(16)])


flip_a, flip_y = (functools.partial(flip, bits) for bits in (8, 2))


def flip_x(block):
    return lax.ppermute(block, "dp", [(0, 1), (1, 0)])


def after(value, *others):
    return lax.optimization_barrier((value,) + others)[0]


def pick(block, index, axis, keepdims=False):
    return lax.dynamic_index_in_dim(block, index, axis, keepdims=keepdims)


def cube_one(flip_one, block):
    return jnp.concatenate([block, flip_one(block)], 0)


def arrange_kernel(spot_ref, kept, *refs):
    out = refs[-1]
    i = pl.program_id(0)
    wide = len(out.shape) == 7

    @pl.when(i < 4)
    def _():
        if wide:
            for j in range(2):
                for k in range(2):
                    out[0, j, 0, k, 0] = kept[0, j, k]
        else:
            out[0, 0, 0] = kept[0]

    @pl.when(i >= 4)
    def _():
        if wide:
            for j in range(2):
                for k in range(2):
                    out[0, j, 0, k, 0] = refs[j][0, k]
        else:
            out[0, 0, 0] = refs[0][0]


def arrange(spot, kept, *received):
    def coords(i, r):
        return lax.rem(r[0] + i % 2, 2), lax.rem(r[1] + i // 4, 2), lax.rem(r[2] + (i // 2) % 2, 2)

    shape = kept.shape

    def spec(block, low):
        rest = (0,) * (block.ndim - 1)
        return pl.BlockSpec((1,) + block.shape[1:], lambda i, r: (jnp.clip(i - low, 0, 3),) + rest)

    if len(shape) == 5:
        def out_place(i, r):
            a, y, x = coords(i, r)
            return a, 0, y, 0, x, 0, 0
        out_block, out_shape = (1, 2, 1, 2, 1) + shape[3:], (2,) * 5 + shape[3:]
    else:
        def out_place(i, r):
            return coords(i, r) + (0, 0)
        out_block, out_shape = (1, 1, 1) + shape[1:], (2, 2, 2) + shape[1:]
    return pl.pallas_call(
        arrange_kernel,
        out_shape=jax.ShapeDtypeStruct(out_shape, kept.dtype),
        grid_spec=pltpu.PrefetchScalarGridSpec(
            num_scalar_prefetch=1, grid=(8,), in_specs=[spec(kept, 0)] + [spec(block, 4) for block in received],
            out_specs=pl.BlockSpec(out_block, out_place)),
        compiler_params=pltpu.CompilerParams(vmem_limit_bytes=32 << 20),
        cost_estimate=pl.CostEstimate(flops=0, bytes_accessed=8 << 20, transcendentals=0),
        name="arrange",
    )(spot, kept, *received)


def up_kernel(rows_ref, w_ref, shift_ref, active_ref, slope_ref):
    for r in range(0, rows_ref.shape[0], 128):
        span = slice(r, r + 128)
        t = dot_nn(rows_ref[span], w_ref[...]) + shift_ref[...]
        half = 0.5 + 0.5 * lax.erf(t * math.sqrt(0.5))
        active_ref[span] = (t * half).astype(jnp.bfloat16)
        slope_ref[span] = half + t * jnp.exp(t * t * -0.5) * (1.0 / math.sqrt(2.0 * math.pi))


def up_gelu(rows, w, shift):
    m, k = rows.shape
    n, block = w.shape[1], 256
    return pl.pallas_call(
        up_kernel, grid=(n // block,),
        out_shape=(jax.ShapeDtypeStruct((m, n), jnp.bfloat16), jax.ShapeDtypeStruct((m, n), jnp.float32)),
        in_specs=[pl.BlockSpec((m, k), lambda i: (0, 0)), pl.BlockSpec((k, block), lambda i: (0, i)),
                  pl.BlockSpec((1, block), lambda i: (0, i))],
        out_specs=(pl.BlockSpec((m, block), lambda i: (0, i)),) * 2,
        compiler_params=pltpu.CompilerParams(vmem_limit_bytes=32 << 20),
        cost_estimate=pl.CostEstimate(flops=2 * m * n * k, bytes_accessed=24 << 20, transcendentals=2 * m * n),
        name="up_gelu",
    )(rows, w, shift)


def add_low(mine, other):
    return (mine.astype(jnp.float32) + other.astype(jnp.float32)).astype(jnp.bfloat16)


def fold(terms, flip_one, index, axis):
    return add_low(pick(terms, index, axis, True), flip_one(pick(terms, 1 - index, axis, True)))


def reduce_kernel(q_ref, o_ref, u_ref, part, tokens, grad_middle, vectors, *refs):
    vec_refs, (out_q, ro, out_u, vec, input_grad, got_far, got_near, low_sums, got_sums, row_send, row_recv, rq, gu, r1q, t2q, r2q, t3q, r3q, fq, gq, r1o, t2o, r2o, t3o, r3o,
               run, got, send_sem, recv_sem) = refs[:10], refs[10:]
    a, b, y, c, x = place()
    f32, bf16 = jnp.float32, jnp.bfloat16
    barrier = pltpu.get_barrier_semaphore()

    def at(pa, pb, py, pc, px):
        return (pa * 8 + pb * 4 + py * 2 + pc, px)

    to_x, to_y, to_a = at(a, b, y, c, 1 - x), at(a, b, 1 - y, c, x), at(1 - a, b, y, c, x)
    ranks = [(lax.rem(b + k // 2, 2), lax.rem(c + k % 2, 2)) for k in range(4)]
    to_rank = [at(a, ranks[k][0], y, ranks[k][1], x) for k in range(4)]
    to_b, to_c = to_rank[2], to_rank[1]
    for dev in [to_x, to_y, to_a] + to_rank[1:]:
        pl.semaphore_signal(barrier, inc=1, device_id=dev, device_id_type=MESH)
    for pb in range(2):
        for j in range(4):
            for row, cols in ((0, slice(j * 128, j * 128 + HD)), (1, slice(512 + j * HD, 512 + j * HD + HD))):
                piece = vec_refs[0][:, cols]
                pair = [jnp.where((b == pb) & (c == pc), piece, 0.0) for pc in range(2)]
                h = head_of(j // 2, pb, j % 2, 0) * HD
                run[0, row:row + 1, h:h + 128] = jnp.concatenate(pair, 1)
            for pc in range(2):
                col = head_of(j // 2, pb, j % 2, pc) * 256
                piece = vec_refs[1][:, j * 256:j * 256 + 256]
                run[0, 12 + col // 1024:13 + col // 1024, col % 1024:col % 1024 + 256] = jnp.where(
                    (b == pb) & (c == pc), piece, 0.0)
    for k, row in enumerate((2, 3, 5, 6, 7, 9, 10, 11)):
        run[0, row:row + 1] = vec_refs[2 + k][...]
    for row in (4, 8):
        run[0, row:row + 1] = jnp.zeros((1, 1024), f32)
    pl.semaphore_wait(barrier, 6)

    made = []

    def remote(src, dst, dev):
        k = len(made)
        made.append(pltpu.make_async_remote_copy(
            src_ref=src, dst_ref=dst, send_sem=send_sem.at[k], recv_sem=recv_sem.at[k],
            device_id=dev, device_id_type=MESH))
        return made[-1]

    def low(*values):
        return sum(v.astype(f32) for v in values)

    places = [1 - a, a]
    halves = [slice(0, 512), slice(512, 1024)]
    lateral = [(to_x, to_y), (to_y, to_x)]

    q1, q2, o1, o2 = {}, {}, {}, {}
    for i in range(2):
        for s in range(2):
            p = places[i]
            q1[s, i] = remote(q_ref.at[p, 0, :, :, 1 - x] if s == 0 else q_ref.at[p, 1, 1 - y], r1q.at[s, i], lateral[s][0])
            o1[s, i] = remote(o_ref.at[p, :, 1 - x, :, halves[0]] if s == 0 else o_ref.at[p, 1 - y, :, :, halves[1]],
                              r1o.at[s, i], lateral[s][0])
            q2[s, i] = remote(t2q.at[s, i], r2q.at[s, i], lateral[s][1])
            o2[s, i] = remote(t2o.at[s, i], r2o.at[s, i], lateral[s][1])
    q3 = [remote(t3q.at[s], r3q.at[s], to_a) for s in range(2)]
    o3 = [remote(t3o.at[s], r3o.at[s], to_a) for s in range(2)]
    qr = [remote(fq.at[ranks[k][0], ranks[k][1]], gq.at[k - 1], to_rank[k]) for k in range(1, 4)]
    ur = [remote(u_ref.at[ranks[k][0], ranks[k][1]], gu.at[b, c], to_rank[k]) for k in range(1, 4)]
    vs = [remote(run.at[k], got.at[k], dev) for k, dev in enumerate((to_x, to_y, to_a, to_b, to_c))]

    def next_sum(k):
        vs[k].wait_recv()
        if k < 4:
            run[k + 1] = run[k] + got[k]
            vs[k + 1].start()
        else:
            vec[...] = run[k] + got[k]

    pieces = part.shape[2] // PIECE

    def span(r):
        return pl.ds(pl.multiple_of(r * PIECE, PIECE), PIECE)

    def row_copy(kind, r):
        src, dst, dev = ((part.at[1, 1, span(r)], got_far.at[span(r)], to_c), (part.at[0, 1, span(r)], got_near.at[span(r)], to_c),
                         (low_sums.at[span(r)], got_sums.at[span(r)], to_b))[kind]
        return pltpu.make_async_remote_copy(
            src_ref=src, dst_ref=dst, send_sem=row_send.at[kind, r], recv_sem=row_recv.at[kind, r],
            device_id=dev, device_id_type=MESH)

    def send_across(r, _):
        row_copy(0, r).wait_recv()
        low_sums[span(r)] = (part[1, 0, span(r)] + got_far[span(r)]).astype(bf16)
        row_copy(2, r).start()
        return 0

    def take(r, _):
        row_copy(1, r).wait_recv()
        row_copy(2, r).wait_recv()
        total = part[0, 0, span(r)] + got_near[span(r)] + got_sums[span(r)].astype(f32)
        _, pull = jax.vjp(norm_rows, tokens[span(r)].astype(f32), *norm_vectors(vectors, 0))
        term, grad_gain, grad_shift = pull(total)
        input_grad[span(r)] = (grad_middle[span(r)] + term).astype(bf16)
        run[0, 4:5] += grad_gain
        run[0, 8:9] += grad_shift
        for kind in range(3):
            row_copy(kind, r).wait_send()
        return 0

    for kind in range(2):
        for r in range(pieces):
            row_copy(kind, r).start()
    for s in range(2):
        q1[s, 0].start()
        o1[s, 0].start()
    for k in (3, 2, 1):
        ur[k - 1].start()
    for s in range(2):
        o1[s, 1].start()
    lax.fori_loop(0, pieces, send_across, 0)

    def q_terms(s, i, far):
        p = places[i]
        if s == 0:
            v = 1 - y if far else y
            return q_ref[p, 0, v, :, x], r1q[0, i, v]
        v = 1 - x if far else x
        return q_ref[p, 1, y, :, v], r1q[1, i, :, v]

    def o_terms(s, i, far):
        p = places[i]
        if s == 0:
            v = 1 - y if far else y
            return o_ref[p, v, x, :, halves[0]], r1o[0, i, v]
        v = 1 - x if far else x
        return o_ref[p, y, v, :, halves[1]], r1o[1, i, v]

    for i in range(2):
        for s in range(2):
            q1[s, i].wait_recv()
            t2q[s, i] = low(*q_terms(s, i, True)).astype(bf16)
            q2[s, i].start()
            o1[s, i].wait_recv()
            t2o[s, i] = low(*o_terms(s, i, True)).astype(bf16)
            o2[s, i].start()
        if i == 0:
            for s in range(2):
                q1[s, 1].start()
            lax.fori_loop(0, pieces, take, 0)
            vs[0].start()
            for s in range(2):
                q2[s, 0].wait_recv()
                t3q[s] = low(*q_terms(s, 0, False), r2q[s, 0]).astype(bf16)
                q3[s].start()
                o2[s, 0].wait_recv()
                t3o[s] = low(*o_terms(s, 0, False), r2o[s, 0]).astype(bf16)
                o3[s].start()
    next_sum(0)
    for s in range(2):
        q2[s, 1].wait_recv()
        o2[s, 1].wait_recv()
        q3[s].wait_recv()
        total = low(*q_terms(s, 1, False), r2q[s, 1], r3q[s])
        fq[s] = total.astype(bf16)
        for j in range(2):
            @pl.when((b == s) & (c == j))
            def _():
                rq[s, j] = total[j]
        o3[s].wait_recv()
        ro[:, halves[s]] = low(*o_terms(s, 1, False), r2o[s, 1], r3o[s])
        next_sum(1 + s)
    for k in (3, 2, 1):
        qr[k - 1].start()
    gu[b, c] = u_ref[b, c]
    for k in (1, 2, 3):
        ur[k - 1].wait_recv()
    next_sum(3)
    for k in (1, 2, 3):
        pb, pc = ranks[k]
        qr[k - 1].wait_recv()
        rq[pb, pc] = gq[k - 1].astype(f32)
    for pb in range(2):
        for j in range(4):
            zero, one = rq[pb, 0], rq[pb, 1]
            h = head_of(j // 2, pb, j % 2, 0) * HD
            q, k = slice(j * 128, j * 128 + HD), slice(j * 128 + HD, j * 128 + 128)
            v = slice(512 + j * HD, 512 + j * HD + HD)
            for t, cols in enumerate((q, k, v)):
                out_q[:, t * 1024 + h:t * 1024 + h + 128] = jnp.concatenate([zero[:, cols], one[:, cols]], 1)
            for pc in range(2):
                col = head_of(j // 2, pb, j % 2, pc) * 256
                out_u[:, col:col + 256] = gu[pb, pc, :, j * 256:j * 256 + 256].astype(f32)
    next_sum(4)
    for copy in made:
        copy.wait_send()


def reduce_all(gw_qkv, gw_out, up_sum, part, tokens, grad_middle, params, vectors, cid):
    f32, bf16 = jnp.float32, jnp.bfloat16
    V = pltpu.VMEM
    vm = pl.BlockSpec(memory_space=V)
    S = jax.ShapeDtypeStruct
    q, o, u = gw_qkv.shape[5:], (gw_out.shape[3], 512), up_sum.shape
    rows, n = grad_middle.shape
    scratch = [
        V((rows, n), f32), V((rows, n), f32), V((rows, n), bf16), V((rows, n), bf16),
        pltpu.SemaphoreType.DMA((3, rows // PIECE)), pltpu.SemaphoreType.DMA((3, rows // PIECE)),
        V((2, 2) + q, f32), V(u, bf16),
        V((2, 2, 2, 2) + q, bf16), V((2, 2, 2) + q, bf16), V((2, 2, 2) + q, bf16), V((2, 2) + q, bf16), V((2, 2) + q, bf16),
        V((2, 2) + q, bf16), V((3,) + q, bf16),
        V((2, 2, 2) + o, bf16), V((2, 2) + o, bf16), V((2, 2) + o, bf16), V((2,) + o, bf16), V((2,) + o, bf16),
        V((5, 16, 1024), f32), V((5, 16, 1024), f32),
        pltpu.SemaphoreType.DMA((32,)), pltpu.SemaphoreType.DMA((32,))]
    return pl.pallas_call(
        reduce_kernel,
        out_shape=(S((q[0], 4 * q[1]), f32), S((o[0], 1024), f32), S((u[2], 4 * u[3]), f32), S((16, 1024), f32), S((rows, n), bf16)),
        in_specs=[vm] * 17, out_specs=(vm,) * 5, scratch_shapes=scratch,
        compiler_params=pltpu.CompilerParams(collective_id=cid, has_side_effects=True, vmem_limit_bytes=48 << 20),
        name="reduce_all",
    )(gw_qkv, gw_out, up_sum, part.reshape(2, 2, rows, n), tokens, grad_middle, params, *vectors)


def qk_columns(head):
    return slice(head * HD, head * HD + HD), slice(1024 + head * HD, 1024 + head * HD + HD), slice(2048 + head * HD, 2048 + head * HD + HD)


def head_of(a, b, y, c):
    return a * 8 + b * 4 + y * 2 + c


def start_kernel(q_hbm, u_hbm, o_in, t_in, v_in, wq, wo, up, rows, vec, q_in, u_in, q_src, u_src, send_sem, recv_sem, own_sem):
    a, b, y, c, x = place()
    barrier = pltpu.get_barrier_semaphore()

    def at(pa, pb, py, pc, px):
        return (pa * 8 + pb * 4 + py * 2 + pc, px)

    to_x, to_y, to_a = at(a, b, y, c, 1 - x), at(a, b, 1 - y, c, x), at(1 - a, b, y, c, x)
    ranks = [(lax.rem(b + k // 2, 2), lax.rem(c + k % 2, 2)) for k in range(4)]
    to_rank = [at(a, pb, y, pc, x) for pb, pc in ranks]
    for dev in [to_x, to_y, to_a] + to_rank[1:]:
        pl.semaphore_signal(barrier, inc=1, device_id=dev, device_id_type=MESH)

    loads = [pltpu.make_async_copy(q_hbm, q_in, own_sem.at[5]), pltpu.make_async_copy(u_hbm, u_in, own_sem.at[6])]
    for copy in loads:
        copy.start()
    for copy in loads:
        copy.wait()

    for pb in range(2):
        for pc in range(2):
            for j in range(4):
                q, k, v = qk_columns(head_of(j // 2, pb, j % 2, pc))
                q_src[pb, pc, :, j * 128:j * 128 + 128] = jnp.concatenate([q_in[:, q], q_in[:, k]], 1)
            for j in range(2):
                v0 = qk_columns(head_of(j, pb, 0, pc))[2]
                v1 = qk_columns(head_of(j, pb, 1, pc))[2]
                q_src[pb, pc, :, 512 + j * 128:640 + j * 128] = jnp.concatenate([q_in[:, v0], q_in[:, v1]], 1)
            for j in range(4):
                col = (head_of(j // 2, pb, j % 2, pc)) * 256
                u_src[pb, pc, :, j * 256:j * 256 + 256] = u_in[:, col:col + 256]
    own = [pltpu.make_async_copy(src, dst, own_sem.at[k]) for k, (src, dst) in enumerate((
        (q_src.at[b, c], wq.at[a, b, y, c, x]), (u_src.at[b, c], up.at[0, b, c]), (o_in, wo.at[a, y, x]),
        (t_in, rows.at[0]), (v_in, vec.at[a, b, y, c, x])))]
    for copy in own:
        copy.start()
    pl.semaphore_wait(barrier, 6)

    made = []

    def remote(src, dst, dev):
        k = len(made)
        made.append(pltpu.make_async_remote_copy(
            src_ref=src, dst_ref=dst, send_sem=send_sem.at[k], recv_sem=recv_sem.at[k],
            device_id=dev, device_id_type=MESH))
        return made[-1]

    places = [a, 1 - a]
    halves = [slice(0, 512), slice(512, 1024)]
    lateral = [(to_y, to_x), (to_x, to_y)]

    def same(ref, dev):
        return remote(ref, ref, dev)

    q_rank = [remote(q_src.at[ranks[k][0], ranks[k][1]], wq.at[a, b, y, c, x], to_rank[k]) for k in range(1, 4)]
    u_rank = [remote(u_src.at[ranks[k][0], ranks[k][1]], up.at[0, b, c], to_rank[k]) for k in range(1, 4)]
    v_rank = [remote(v_in, vec.at[a, b, y, c, x], to_rank[k]) for k in range(1, 4)]
    t_core, t_near = remote(t_in, rows.at[1], to_rank[1]), remote(t_in, rows.at[2], to_rank[2])
    t_far = remote(rows.at[2], rows.at[3], to_rank[1])
    u_cube = remote(up.at[0], up.at[1], to_a)
    v_cube = [same(vec.at[a, :, y, :, x], to_a), same(vec.at[:, :, y, :, x], to_y), same(vec.at[:, :, :, :, x], to_x)]
    q_cube = [same(wq.at[a, s, y, :, x], to_a) for s in range(2)]
    o_cube = [remote(o_in.at[:, halves[s]], wo.at[a, y, x, :, halves[s]], to_a) for s in range(2)]
    q_side, o_side = {}, {}
    for i in range(2):
        for s in range(2):
            one, two = lateral[s]
            oy, ox = (1 - y, x) if s == 0 else (y, 1 - x)
            p = places[i]
            mine, theirs = wq.at[p, s, y, :, x], wq.at[p, s, oy, :, ox]
            q_side[s, i] = (same(mine, one), same(mine, two), same(theirs, two))
            mine, theirs = wo.at[p, y, x, :, halves[s]], wo.at[p, oy, ox, :, halves[s]]
            first = o_in.at[:, halves[s]] if i == 0 else mine
            o_side[s, i] = (remote(first, mine, one), remote(first, mine, two), same(theirs, two))

    for k in (2, 1, 0):
        q_rank[k].start()
        v_rank[k].start()
    for s in range(2):
        o_cube[s].start()
        o_side[s, 0][0].start()
        o_side[s, 0][1].start()
    t_near.start()
    t_core.start()
    own[0].wait()
    for copy in q_rank:
        copy.wait_recv()
    for s in range(2):
        q_cube[s].start()
        q_side[s, 0][0].start()
        q_side[s, 0][1].start()
    own[4].wait()
    for copy in v_rank:
        copy.wait_recv()
    v_cube[0].start()
    for k in (2, 1, 0):
        u_rank[k].start()
    for s in range(2):
        o_side[s, 0][0].wait_recv()
        o_side[s, 0][2].start()
    for s in range(2):
        o_cube[s].wait_recv()
        o_side[s, 1][0].start()
        o_side[s, 1][1].start()
    t_near.wait_recv()
    t_far.start()
    for s in range(2):
        q_side[s, 0][0].wait_recv()
        q_side[s, 0][2].start()
    for s in range(2):
        q_cube[s].wait_recv()
        q_side[s, 1][0].start()
        q_side[s, 1][1].start()
    v_cube[0].wait_recv()
    v_cube[1].start()
    own[1].wait()
    for copy in u_rank:
        copy.wait_recv()
    u_cube.start()
    for s in range(2):
        o_side[s, 1][0].wait_recv()
        o_side[s, 1][2].start()
    v_cube[1].wait_recv()
    v_cube[2].start()
    for s in range(2):
        q_side[s, 1][0].wait_recv()
        q_side[s, 1][2].start()
    v_cube[2].wait_recv()
    t_core.wait_recv()
    t_far.wait_recv()
    for i in range(2):
        for s in range(2):
            for k in (1, 2):
                q_side[s, i][k].wait_recv()
                o_side[s, i][k].wait_recv()
    u_cube.wait_recv()
    for k in (2, 3):
        own[k].wait()
    for copy in made:
        copy.wait_send()


def start_gather(w_qkv, w_up, w_out, tokens, vectors, cid):
    bf16 = jnp.bfloat16
    S = lambda *shape: jax.ShapeDtypeStruct(shape, bf16)
    vm, anywhere = pl.BlockSpec(memory_space=pltpu.VMEM), pl.BlockSpec(memory_space=pl.ANY)
    return pl.pallas_call(
        start_kernel,
        out_shape=(S(2, 2, 2, 2, 2, 32, 768), S(2, 2, 2, 32, 1024), S(2, 2, 2, 32, 1024), S(4, 128, 1024),
                   S(2, 2, 2, 2, 2, 16, 128)),
        in_specs=[pl.BlockSpec(memory_space=pltpu.HBM)] * 4 + [vm], out_specs=(anywhere,) * 5,
        scratch_shapes=[
            pltpu.VMEM(w_qkv.shape, bf16), pltpu.VMEM(w_up.shape, bf16),
            pltpu.VMEM((2, 2, 32, 768), bf16), pltpu.VMEM((2, 2, 32, 1024), bf16),
            pltpu.SemaphoreType.DMA((48,)), pltpu.SemaphoreType.DMA((48,)), pltpu.SemaphoreType.DMA((7,))],
        compiler_params=pltpu.CompilerParams(collective_id=cid, has_side_effects=True, vmem_limit_bytes=63 << 20),
        cost_estimate=pl.CostEstimate(flops=0, bytes_accessed=100 << 20, transcendentals=0),
        name="start_gather",
    )(w_qkv, w_up, w_out, tokens, vectors)


PIECE = 32


def rows_kernel(step, gather, count_in, count_out, part, *refs):
    ins, outs = refs[:count_in], refs[count_in:count_in + count_out]
    rest = refs[count_in + count_out:]
    rows = rest[0] if gather else None
    got_far, got_near, sums, got_sums, send_sem, recv_sem = rest[-6:]
    a, b, y, c, x = place()

    def at(pb, pc):
        return (a * 8 + pb * 4 + y * 2 + pc, x)

    to_b, to_core = at(1 - b, c), at(b, 1 - c)
    barrier = pltpu.get_barrier_semaphore()
    for dev in (to_b, to_core):
        pl.semaphore_signal(barrier, inc=1, device_id=dev, device_id_type=MESH)
    pl.semaphore_wait(barrier, 2)
    pieces = part.shape[2] // PIECE

    def span(r):
        return pl.ds(pl.multiple_of(r * PIECE, PIECE), PIECE)

    def remote(kind, r, src, dst, dev):
        return pltpu.make_async_remote_copy(
            src_ref=src, dst_ref=dst, send_sem=send_sem.at[kind, r], recv_sem=recv_sem.at[kind, r],
            device_id=dev, device_id_type=MESH)

    def far(r):
        return remote(0, r, part.at[1, 1, span(r)], got_far.at[span(r)], to_core)

    def near(r):
        return remote(1, r, part.at[0, 1, span(r)], got_near.at[span(r)], to_core)

    def across(r):
        return remote(2, r, sums.at[span(r)], got_sums.at[span(r)], to_b)

    def row_near(r):
        return remote(3, r, rows.at[0, span(r)], rows.at[2, span(r)], to_b)

    def row_core(r):
        return remote(4, r, rows.at[0, span(r)], rows.at[1, span(r)], to_core)

    def row_far(r):
        return remote(5, r, rows.at[2, span(r)], rows.at[3, span(r)], to_core)

    for r in range(pieces):
        far(r).start()
    for r in range(pieces):
        near(r).start()

    def send_across(r, _):
        far(r).wait_recv()
        sums[span(r)] = (part[1, 0, span(r)] + got_far[span(r)]).astype(jnp.bfloat16)
        across(r).start()
        return 0

    lax.fori_loop(0, pieces, send_across, 0)
    for ref in outs:
        if ref.shape[0] == 1:
            ref[...] = jnp.zeros_like(ref)

    def take(r, _):
        near(r).wait_recv()
        across(r).wait_recv()
        total = part[0, 0, span(r)] + got_near[span(r)] + got_sums[span(r)].astype(jnp.float32)
        piece = step(span(r), total, ins, outs)
        if gather:
            rows[0, span(r)] = piece
            row_near(r).start()
            row_core(r).start()
        return 0

    lax.fori_loop(0, pieces, take, 0)

    def relay(r, _):
        row_near(r).wait_recv()
        row_far(r).start()
        return 0

    def finish(r, _):
        if gather:
            row_core(r).wait_recv()
            row_far(r).wait_recv()
            row_near(r).wait_send()
            row_core(r).wait_send()
            row_far(r).wait_send()
        far(r).wait_send()
        near(r).wait_send()
        across(r).wait_send()
        return 0

    if gather:
        lax.fori_loop(0, pieces, relay, 0)
    lax.fori_loop(0, pieces, finish, 0)


def sum_rows(step, part, ins, outs, gather, cid):
    rows, n = part.shape[0] // 4, part.shape[1]
    vm = pl.BlockSpec(memory_space=pltpu.VMEM)
    shapes = tuple(outs) + ((jax.ShapeDtypeStruct((4, rows, n), jnp.bfloat16),) if gather else ())
    V = pltpu.VMEM
    return pl.pallas_call(
        functools.partial(rows_kernel, step, gather, len(ins), len(outs)),
        out_shape=shapes, in_specs=[vm] * (1 + len(ins)), out_specs=(vm,) * len(shapes),
        scratch_shapes=[V((rows, n), jnp.float32), V((rows, n), jnp.float32), V((rows, n), jnp.bfloat16), V((rows, n), jnp.bfloat16),
                        pltpu.SemaphoreType.DMA((6, rows // PIECE)), pltpu.SemaphoreType.DMA((6, rows // PIECE))],
        compiler_params=pltpu.CompilerParams(collective_id=cid, has_side_effects=True, vmem_limit_bytes=32 << 20),
        cost_estimate=pl.CostEstimate(flops=0, bytes_accessed=50 << 20, transcendentals=0),
        name="sum_rows",
    )(part.reshape(2, 2, rows, n), *ins)


def norm_vectors(vectors, k):
    return vectors[4 + k:5 + k], vectors[8 + k:9 + k]


def attended_step(span, total, ins, outs):
    tokens, vectors = ins
    branch = total + vectors[2:3]
    middle = tokens[span].astype(jnp.float32) + norm_rows(branch, *norm_vectors(vectors, 1))
    outs[0][span] = branch
    outs[1][span] = middle
    return norm_rows(middle, *norm_vectors(vectors, 2)).astype(jnp.bfloat16)


def output_step(span, total, ins, outs):
    middle, grad_out, vectors = ins
    normed, pull = jax.vjp(norm_rows, total + vectors[3:4], *norm_vectors(vectors, 3))
    outs[0][span] = (middle[span] + normed).astype(jnp.bfloat16)
    grad_down, grad_gain, grad_shift = pull(grad_out[span])
    grad_down = grad_down.astype(jnp.bfloat16)
    outs[1][...] += grad_gain
    outs[2][...] += grad_shift
    outs[3][...] += jnp.sum(grad_down.astype(jnp.float32), 0, keepdims=True)
    return grad_down


def middle_step(span, total, ins, outs):
    middle, branch, grad_out, vectors = ins
    _, pull = jax.vjp(norm_rows, middle[span], *norm_vectors(vectors, 2))
    part, grad_gain2, grad_shift2 = pull(total)
    grad_middle = grad_out[span] + part
    _, pull = jax.vjp(norm_rows, branch[span], *norm_vectors(vectors, 1))
    grad_branch, grad_gain1, grad_shift1 = pull(grad_middle)
    grad_branch = grad_branch.astype(jnp.bfloat16)
    outs[0][span] = grad_middle
    for ref, value in zip(outs[1:], (grad_gain2, grad_shift2, grad_gain1, grad_shift1,
                                     jnp.sum(grad_branch.astype(jnp.float32), 0, keepdims=True))):
        ref[...] += value
    return grad_branch


def fast_body(tokens, cotangent, lengths, assign, w_qkv, qv_bias, w_out, out_bias, w_up, up_bias, w_down, down_bias,
              norm_gain, norm_shift):
    bf16, f32 = jnp.bfloat16, jnp.float32
    a, b, y, c, x = place()
    spot = jnp.stack([a, y, x]).astype(jnp.int32)
    width = tokens.shape[2]
    place_two = jnp.arange(2, dtype=jnp.int32)
    sequence = jnp.sum(jnp.where(place_two == x, assign.astype(jnp.int32), 0))
    valid = jnp.sum(jnp.where(place_two == sequence, lengths.astype(jnp.int32), 0))

    small, row = jnp.zeros((16, 128), bf16), 0
    for block in (qv_bias, out_bias[None], down_bias[None], norm_gain, norm_shift, up_bias[None]):
        small += jnp.pad(block, ((row, 16 - row - block.shape[0]), (0, 128 - block.shape[1])))
        row += block.shape[0]
    wqkv, wo, up_one, rows, small = start_gather(w_qkv, w_up, w_out, tokens[0], small, 6)
    down_one = after(w_down, wqkv)
    down_one = jnp.stack([down_one, flip_a(down_one)])
    wqkv, wo, rows = wqkv.reshape(width, 768), wo.reshape(256, width), rows.reshape(512, width)

    vectors = small[..., :12, :32].reshape(32, 12, 32).transpose(1, 0, 2).reshape(12, width).astype(f32)
    qv_half = pick(pick(vectors[:2].reshape(2, 2, 2, 2, 2, HD), b, 2), c, 3).reshape(2, 4, HD)
    qk_shift = jnp.concatenate([qv_half[0], jnp.zeros((4, HD), f32)], 1).reshape(512)
    v_shift = qv_half[1].reshape(256)
    up_shift = pick(pick(small[..., 12, :], b, 1), c, 2).reshape(1024).astype(f32)

    first = norm_rows(rows.astype(f32), vectors[4:5], vectors[8:9]).astype(bf16)
    up_two = cube_one(flip_x, up_one)
    projected = (dot_nn(first, wqkv) + jnp.concatenate([qk_shift, v_shift])).astype(bf16)
    packed = exchange(after(projected, up_two, down_one), True, 1).reshape(8, 384, 128)
    down_two = cube_one(flip_x, down_one)
    up_half = flip_y(after(up_two, packed)[:, 0])
    attended = attend(valid[None], packed).reshape(2, 2, 2, 128, 128)
    attended = exchange(after(attended, down_two, up_half), False, 2)
    up_rest = flip_y(after(up_two, attended)[:, 1])
    down_far = flip_y(after(down_two, attended))
    own_spot = lax.axis_index("seq") * 128 + jnp.arange(128, dtype=jnp.int32)
    grad_out = cotangent[0].astype(f32) * (own_spot < valid).astype(f32)[:, None]
    S = jax.ShapeDtypeStruct
    wide, low, line = S((128, width), f32), S((128, width), bf16), S((1, width), f32)
    branch, middle, third = sum_rows(
        attended_step, dot_nn(attended, wo), (tokens[0], vectors),
        (wide, wide), True, 7)
    third = third.reshape(512, width)
    wu = arrange(spot, up_two, up_half, up_rest).reshape(width, 1024)
    active, slope = up_gelu(third, wu, up_shift.reshape(1, 1024))
    wd = arrange(spot, down_two, after(down_far, active)).reshape(1024, width)
    output, gain4, shift4, bias_down, down_rows = sum_rows(
        output_step, dot_nn(active, wd), (middle, grad_out, vectors), (low, line, line, line), True, 8)
    down_rows = down_rows.reshape(512, width)
    gw_down = contract_rows(active, down_rows).astype(bf16).reshape(2, 2, 2, 128, width)
    down_term = flip_y(pick(gw_down, 1 - y, 1, True))
    grad_up = (dot_nt(after(down_rows, gw_down), wd) * slope).astype(bf16)
    gw_up = contract_rows(third, grad_up).astype(bf16).reshape(2, 2, 2, 2, 2, 32, 1024)
    up_term = flip_x(pick(gw_up, 1 - x, 4, True))
    grad_middle, gain3, shift3, gain2, shift2, bias_out, branch_rows = sum_rows(
        middle_step, after(dot_nt(grad_up, wu), gw_up),
        (middle, branch, grad_out, vectors), (wide,) + (line,) * 5, True, 9)
    branch_rows = branch_rows.reshape(512, width)
    grad_att = dot_nt(branch_rows, wo).astype(bf16)
    down_sum = add_low(pick(gw_down, y, 1, True), down_term)
    down_term = flip_x(pick(down_sum, 1 - x, 2, True))
    grad_packed = exchange(after(grad_att, down_sum), True, 3).reshape(8, 128, 128)
    up_sum = add_low(pick(gw_up, x, 4, True), after(up_term, grad_packed))
    up_term = flip_y(pick(up_sum, 1 - y, 2, True))
    down_sum = add_low(pick(down_sum, x, 2, True), after(down_term, grad_packed))
    down_term = flip_a(pick(down_sum, 1 - a, 0))
    back = attend_back(valid[None], packed, grad_packed)

    up_sum = add_low(pick(up_sum, y, 2, True), up_term)
    gw_out = contract_rows(attended, branch_rows).astype(bf16).reshape(2, 2, 2, 32, width)
    grad_qkv = exchange(after(back, up_sum, down_term).reshape(2, 2, 2, 384, 128), False, 4)
    up_term = flip_a(pick(after(up_sum, grad_qkv), 1 - a, 0))
    gw_qkv = contract_rows(first, grad_qkv).astype(bf16).reshape(2, 2, 2, 2, 2, 32, 768)
    def sums(block):
        return jnp.sum(block.astype(f32), 0, keepdims=True)

    sums_of = [sums(grad_qkv), sums(grad_up), bias_out, bias_down, gain2, gain3, gain4, shift2, shift3, shift4]
    up_sum = (pick(up_sum, a, 0).astype(f32) + up_term.astype(f32)).astype(bf16).reshape(2, 2, 32, 1024)
    r_qkv, r_out, r_up, vectors, input_grad = reduce_all(
        gw_qkv, gw_out, up_sum, dot_nt(grad_qkv, wqkv), tokens[0], grad_middle, vectors, sums_of, 5)
    r_down = (pick(down_sum, a, 0).astype(f32) + down_term.astype(f32)).reshape(128, width)
    index = lax.axis_index("seq") * 2 + x
    small_up = lax.dynamic_slice(vectors, (12 + index // 8, index % 8 * 128), (1, 128)).reshape(128)
    vectors = lax.dynamic_slice(vectors, (0, index * 32), (12, 32))

    return (
        output[None], input_grad[None], r_qkv, vectors[:2], r_out,
        vectors[2], r_up, small_up, r_down, vectors[3], vectors[4:8], vectors[8:12])


def solution(mesh):
    return jax.shard_map(
        fast_body if is_small(mesh) else body,
        mesh=mesh,
        in_specs=(
            P("dp", "seq", None),
            P("dp", "seq", None),
            P(),
            P(),
            P(("seq", "dp"), None),
            P(None, ("seq", "dp")),
            P(("seq", "dp"), None),
            P(("seq", "dp")),
            P(("seq", "dp"), None),
            P(("seq", "dp")),
            P(("seq", "dp"), None),
            P(("seq", "dp")),
            P(None, ("seq", "dp")),
            P(None, ("seq", "dp")),
        ),
        out_specs=(
            P("dp", "seq", None),
            P("dp", "seq", None),
            P(("seq", "dp"), None),
            P(None, ("seq", "dp")),
            P(("seq", "dp"), None),
            P(("seq", "dp")),
            P(("seq", "dp"), None),
            P(("seq", "dp")),
            P(("seq", "dp"), None),
            P(("seq", "dp")),
            P(None, ("seq", "dp")),
            P(None, ("seq", "dp")),
        ),
        check_vma=False,
    )
```

```python
import functools
import math

import jax
import jax.numpy as jnp
from jax import lax
from jax.experimental import pallas as pl
from jax.experimental.pallas import tpu as pltpu
from jax.sharding import PartitionSpec as P


HD = 64


RELAX_SCALE = 32.0
NORM_EPSILON = 1e-05


def norm_rows(values, gain, shift):
    center = values - jnp.mean(values, -1, keepdims=True)
    spread = jnp.mean(center * center, -1, keepdims=True)
    return center * lax.rsqrt(spread + NORM_EPSILON) * gain + shift


def exact_gelu(values):
    return jax.nn.gelu(values, approximate=False)


def contract_rows(left, right):
    return lax.dot_general(
        left, right, (((0,), (0,)), ((), ())), preferred_element_type=jnp.float32
    )


def contract_cols(left, right):
    return lax.dot_general(
        left, right, (((1,), (1,)), ((), ())), preferred_element_type=jnp.float32
    )


def split_heads(block):
    return block.reshape(block.shape[0], 2, HD)


def pair_scores(query_part, key_part):
    factor = 1.0 / (RELAX_SCALE * math.sqrt(HD))
    return (
        jnp.einsum(
            "qhd,khd->hqk",
            split_heads(query_part),
            split_heads(key_part),
            preferred_element_type=jnp.float32,
        )
        * factor
    )


def kept_probs(scores, allowed, row_max, row_total):
    exp_terms = jnp.exp(jnp.where(allowed, RELAX_SCALE * (scores - row_max), -jnp.inf))
    return exp_terms / row_total


def body(
    tokens,
    cotangent,
    lengths,
    assign,
    w_qkv,
    qv_bias,
    w_out,
    out_bias,
    w_up,
    up_bias,
    w_down,
    down_bias,
    norm_gain,
    norm_shift,
):
    gathered = (
        lax.all_gather(w_qkv, ("seq", "dp"), axis=0, tiled=True),
        lax.all_gather(w_out, ("seq", "dp"), axis=0, tiled=True),
        lax.all_gather(w_up, ("seq", "dp"), axis=0, tiled=True),
        lax.all_gather(w_down, ("seq", "dp"), axis=0, tiled=True),
        lax.all_gather(qv_bias, ("seq", "dp"), axis=1, tiled=True),
        lax.all_gather(out_bias, ("seq", "dp"), axis=0, tiled=True),
        lax.all_gather(up_bias, ("seq", "dp"), axis=0, tiled=True),
        lax.all_gather(down_bias, ("seq", "dp"), axis=0, tiled=True),
        lax.all_gather(norm_gain, ("seq", "dp"), axis=1, tiled=True),
        lax.all_gather(norm_shift, ("seq", "dp"), axis=1, tiled=True),
    )
    qkv_full, out_full, up_full, down_full = (gathered[0], gathered[1], gathered[2], gathered[3])
    qv_shift = gathered[4].astype(jnp.float32)
    out_shift = gathered[5].astype(jnp.float32)
    up_shift = gathered[6].astype(jnp.float32)
    down_shift = gathered[7].astype(jnp.float32)
    gains = gathered[8].astype(jnp.float32)
    shifts = gathered[9].astype(jnp.float32)
    row_count = tokens.shape[1]
    model_width = tokens.shape[2]
    pair_cols = 2 * HD
    pair_count = model_width // pair_cols
    slot_rows = row_count * lax.axis_size("seq")
    factor = 1.0 / (RELAX_SCALE * math.sqrt(HD))
    valid = lengths[assign[lax.axis_index("dp")]]
    own_place = lax.axis_index("seq") * row_count + jnp.arange(row_count, dtype=jnp.int32)
    all_place = jnp.arange(slot_rows, dtype=jnp.int32)
    allowed = (all_place[None, :] <= own_place[:, None]) & (all_place[None, :] < valid)
    pair_ids = jnp.arange(pair_count, dtype=jnp.int32)
    hidden = tokens[0].astype(jnp.float32)
    normed_first, pull_first = jax.vjp(norm_rows, hidden, gains[0], shifts[0])
    normed_low = normed_first.astype(jnp.bfloat16)
    projected = jnp.dot(normed_low, qkv_full, preferred_element_type=jnp.float32)
    queries = (projected[:, :model_width] + qv_shift[0]).astype(jnp.bfloat16)
    key_own = projected[:, model_width : 2 * model_width].astype(jnp.bfloat16)
    value_own = (projected[:, 2 * model_width :] + qv_shift[1]).astype(jnp.bfloat16)
    keys, values = (
        lax.all_gather(key_own, "seq", axis=0, tiled=True),
        lax.all_gather(value_own, "seq", axis=0, tiled=True),
    )

    def columns(block, pair_index):
        return lax.dynamic_slice_in_dim(block, pair_index * pair_cols, pair_cols, 1)

    def merge_pairs(stack):
        return stack.transpose(1, 0, 2).reshape(stack.shape[1], model_width)

    def attend(pair_index):
        scores = pair_scores(columns(queries, pair_index), columns(keys, pair_index))
        row_max = jnp.max(jnp.where(allowed, scores, -jnp.inf), -1, keepdims=True)
        exp_terms = jnp.exp(jnp.where(allowed, RELAX_SCALE * (scores - row_max), -jnp.inf))
        row_total = jnp.sum(exp_terms, -1, keepdims=True)
        probs = (exp_terms / row_total).astype(jnp.bfloat16)
        mixed = jnp.einsum(
            "hqk,khd->qhd",
            probs,
            split_heads(columns(values, pair_index)),
            preferred_element_type=jnp.float32,
        )
        return (mixed.reshape(row_count, pair_cols), row_max[..., 0], row_total[..., 0])

    mixed_pairs, max_pairs, total_pairs = lax.map(attend, pair_ids)
    attended = merge_pairs(mixed_pairs).astype(jnp.bfloat16)
    branch = jnp.dot(attended, out_full, preferred_element_type=jnp.float32) + out_shift
    normed_second, pull_second = jax.vjp(norm_rows, branch, gains[1], shifts[1])
    middle = hidden + normed_second
    normed_third, pull_third = jax.vjp(norm_rows, middle, gains[2], shifts[2])
    third_low = normed_third.astype(jnp.bfloat16)
    up_pre = jnp.dot(third_low, up_full, preferred_element_type=jnp.float32) + up_shift
    activated, pull_gelu = jax.vjp(exact_gelu, up_pre)
    active_low = activated.astype(jnp.bfloat16)
    down_pre = jnp.dot(active_low, down_full, preferred_element_type=jnp.float32) + down_shift
    normed_fourth, pull_fourth = jax.vjp(norm_rows, down_pre, gains[3], shifts[3])
    output = (middle + normed_fourth).astype(jnp.bfloat16)[None]
    again = (
        lax.all_gather(w_qkv, ("seq", "dp"), axis=0, tiled=True),
        lax.all_gather(w_out, ("seq", "dp"), axis=0, tiled=True),
        lax.all_gather(w_up, ("seq", "dp"), axis=0, tiled=True),
        lax.all_gather(w_down, ("seq", "dp"), axis=0, tiled=True),
    )
    qkv_back, out_back, up_back, down_back = (again[0], again[1], again[2], again[3])
    keep_rows = (own_place < valid).astype(jnp.float32)[:, None]
    grad_out = cotangent[0].astype(jnp.float32) * keep_rows
    grad_down, grad_gain_four, grad_shift_four = pull_fourth(grad_out)
    grad_down_low = grad_down.astype(jnp.bfloat16)
    grad_w_down = contract_rows(active_low, grad_down_low)
    grad_b_down = jnp.sum(grad_down_low.astype(jnp.float32), 0)
    (grad_up,) = pull_gelu(contract_cols(grad_down_low, down_back))
    grad_up_low = grad_up.astype(jnp.bfloat16)
    grad_w_up = contract_rows(third_low, grad_up_low)
    grad_b_up = jnp.sum(grad_up_low.astype(jnp.float32), 0)
    grad_middle_part, grad_gain_three, grad_shift_three = pull_third(
        contract_cols(grad_up_low, up_back)
    )
    grad_middle = grad_out + grad_middle_part
    grad_branch, grad_gain_two, grad_shift_two = pull_second(grad_middle)
    grad_branch_low = grad_branch.astype(jnp.bfloat16)
    grad_w_out = contract_rows(attended, grad_branch_low)
    grad_b_out = jnp.sum(grad_branch_low.astype(jnp.float32), 0)
    grad_attended = contract_cols(grad_branch_low, out_back).astype(jnp.bfloat16)

    def query_side(pair_index):
        scores = pair_scores(columns(queries, pair_index), columns(keys, pair_index))
        probs = kept_probs(
            scores, allowed, max_pairs[pair_index][..., None], total_pairs[pair_index][..., None]
        )
        grad_part = columns(grad_attended, pair_index)
        grad_probs = jnp.einsum(
            "qhd,khd->hqk",
            split_heads(grad_part),
            split_heads(columns(values, pair_index)),
            preferred_element_type=jnp.float32,
        )
        delta = jnp.sum(probs * grad_probs, -1, keepdims=True)
        grad_scores = (RELAX_SCALE * probs * (grad_probs - delta)).astype(jnp.bfloat16)
        grad_query = (
            jnp.einsum(
                "hqk,khd->qhd",
                grad_scores,
                split_heads(columns(keys, pair_index)),
                preferred_element_type=jnp.float32,
            )
            * factor
        )
        return (grad_query.reshape(row_count, pair_cols), grad_scores, probs, delta)

    def both_sides(pair_index):
        grad_query, grad_scores, probs, delta = query_side(pair_index)
        grad_part = columns(grad_attended, pair_index)
        grad_key = (
            jnp.einsum(
                "hqk,qhd->khd",
                grad_scores,
                split_heads(columns(queries, pair_index)),
                preferred_element_type=jnp.float32,
            )
            * factor
        )
        grad_value = jnp.einsum(
            "hqk,qhd->khd",
            probs.astype(jnp.bfloat16),
            split_heads(grad_part),
            preferred_element_type=jnp.float32,
        )
        return (
            grad_query,
            grad_key.reshape(slot_rows, pair_cols),
            grad_value.reshape(slot_rows, pair_cols),
        )

    query_pairs, key_terms, value_terms = lax.map(both_sides, pair_ids)
    key_pairs, value_pairs = (
        lax.psum_scatter(
            key_terms.astype(jnp.bfloat16), "seq", scatter_dimension=1, tiled=True
        ).astype(jnp.float32),
        lax.psum_scatter(
            value_terms.astype(jnp.bfloat16), "seq", scatter_dimension=1, tiled=True
        ).astype(jnp.float32),
    )
    grad_q_low = merge_pairs(query_pairs).astype(jnp.bfloat16)
    grad_k_low = merge_pairs(key_pairs).astype(jnp.bfloat16)
    grad_v_low = merge_pairs(value_pairs).astype(jnp.bfloat16)
    grad_projected = jnp.concatenate([grad_q_low, grad_k_low, grad_v_low], 1)
    grad_w_qkv = contract_rows(normed_low, grad_projected)
    grad_qv = jnp.stack(
        [jnp.sum(grad_q_low.astype(jnp.float32), 0), jnp.sum(grad_v_low.astype(jnp.float32), 0)]
    )
    grad_hidden_part, grad_gain_one, grad_shift_one = pull_first(
        contract_cols(grad_projected, qkv_back)
    )
    input_grad = (grad_middle + grad_hidden_part).astype(jnp.bfloat16)[None]
    grad_gains = jnp.stack([grad_gain_one, grad_gain_two, grad_gain_three, grad_gain_four])
    grad_shifts = jnp.stack([grad_shift_one, grad_shift_two, grad_shift_three, grad_shift_four])
    owned = (
        lax.psum_scatter(grad_w_qkv, ("seq", "dp"), scatter_dimension=0, tiled=True),
        lax.psum_scatter(grad_w_out, ("seq", "dp"), scatter_dimension=0, tiled=True),
        lax.psum_scatter(grad_w_up, ("seq", "dp"), scatter_dimension=0, tiled=True),
        lax.psum_scatter(grad_w_down, ("seq", "dp"), scatter_dimension=0, tiled=True),
        lax.psum_scatter(grad_qv, ("seq", "dp"), scatter_dimension=1, tiled=True),
        lax.psum_scatter(grad_b_out, ("seq", "dp"), scatter_dimension=0, tiled=True),
        lax.psum_scatter(grad_b_up, ("seq", "dp"), scatter_dimension=0, tiled=True),
        lax.psum_scatter(grad_b_down, ("seq", "dp"), scatter_dimension=0, tiled=True),
        lax.psum_scatter(grad_gains, ("seq", "dp"), scatter_dimension=1, tiled=True),
        lax.psum_scatter(grad_shifts, ("seq", "dp"), scatter_dimension=1, tiled=True),
    )
    return (
        output,
        input_grad,
        owned[0],
        owned[4],
        owned[1],
        owned[5],
        owned[2],
        owned[6],
        owned[3],
        owned[7],
        owned[8],
        owned[9],
    )


MESH = pl.DeviceIdType.MESH


def is_small(mesh):
    return mesh.shape["seq"] == 16 and mesh.shape["dp"] == 2


def place():
    seq = lax.axis_index("seq")
    return seq // 8, (seq // 4) % 2, (seq // 2) % 2, seq % 2, lax.axis_index("dp")


def exchange_copies(scatter, src, out, send_sem, recv_sem, own_sem):
    a, b, y, c, x = place()

    def peer(k):
        return lax.rem(a + k // 2, 2), lax.rem(y + k % 2, 2)

    def device(k):
        pa, py = peer(k)
        return (pa * 8 + b * 4 + py * 2 + c, x)

    def source(k):
        pa, py = peer(k)
        return src.at[pa * 2 + py] if scatter else src.at[pa, :, py]

    def target(k):
        pa, py = peer(k)
        return out.at[pa, :, py] if scatter else out.at[pa * 2 + py]

    def copy(k, dst):
        return pltpu.make_async_remote_copy(
            src_ref=source(k), dst_ref=target(dst), send_sem=send_sem.at[k], recv_sem=recv_sem.at[k],
            device_id=device(k), device_id_type=MESH)

    def greet():
        barrier = pltpu.get_barrier_semaphore()
        for k in range(1, 4):
            pl.semaphore_signal(barrier, inc=1, device_id=device(k), device_id_type=MESH)

    def run():
        own = pltpu.make_async_copy(source(0), target(0), own_sem)
        own.start()
        pl.semaphore_wait(pltpu.get_barrier_semaphore(), 3)
        for k in (3, 2, 1):
            copy(k, 0).start()
        own.wait()
        for k in (3, 2, 1):
            copy(k, k).wait_recv()
        for k in (3, 2, 1):
            copy(k, 0).wait_send()

    return greet, run


def row_block(i, j):
    _, b, _, c, _ = place()
    return pl.ds(pl.multiple_of(lax.rem(b + i, 2) * 256 + lax.rem(c + j, 2) * 128, 128), 128)


def to_heads_kernel(rows_ref, out, src, *sems):
    greet, run = exchange_copies(True, src, out, *sems)
    greet()
    low = src.shape[2] - 128
    for g in range(4):
        values = slice(low * 2 + g * HD, low * 2 + g * HD + HD)
        for i in range(2):
            if low:
                for j in range(2):
                    src[g, i, j * 128:j * 128 + 128] = rows_ref[row_block(i, j), g * 128:g * 128 + 128]
            src[g, i, low:] = jnp.concatenate([rows_ref[row_block(i, j), values] for j in range(2)], 1)
    run()


def from_heads_kernel(heads_ref, out, got, *sems):
    greet, run = exchange_copies(False, heads_ref, got, *sems)
    greet()
    run()
    low = got.shape[2] - 128
    c = place()[3]
    for i in range(2):
        if low:
            for j in range(2):
                for g in range(4):
                    out[row_block(i, j), g * 128:g * 128 + 128] = got[g, i, j * 128:j * 128 + 128]
        for g in (0, 2):
            left, right = got[g, i, low:], got[g + 1, i, low:]
            cols = slice(low * 2 + g * HD, low * 2 + g * HD + 128)
            for j in range(2):
                lanes = slice(j * HD, j * HD + HD)
                out[row_block(i, j), cols] = jnp.concatenate([left[:, lanes], right[:, lanes]], 1)


def exchange(blocks, scatter, cid):
    vm = pl.BlockSpec(memory_space=pltpu.VMEM)
    rows = blocks.shape[-1] // 2 if scatter else blocks.shape[-2]
    shape, held = (2, 2, 2, rows, 128), (4, 2, rows, 128)
    return pl.pallas_call(
        to_heads_kernel if scatter else from_heads_kernel,
        out_shape=jax.ShapeDtypeStruct(shape if scatter else (512, rows * 2), blocks.dtype),
        in_specs=[vm], out_specs=vm,
        scratch_shapes=[pltpu.VMEM(held, blocks.dtype), pltpu.SemaphoreType.DMA((4,)), pltpu.SemaphoreType.DMA((4,)),
                        pltpu.SemaphoreType.DMA],
        compiler_params=pltpu.CompilerParams(collective_id=cid, has_side_effects=True),
        cost_estimate=pl.CostEstimate(flops=0, bytes_accessed=rows * 100000, transcendentals=0),
        name="to_heads" if scatter else "from_heads",
    )(blocks)


def dot_nt(a, b):
    return lax.dot_general(a, b, (((1,), (1,)), ((), ())), preferred_element_type=jnp.float32)


def dot_nn(a, b):
    return jnp.dot(a, b, preferred_element_type=jnp.float32)


BQ = 256
MASKED = -1e30


def load_heads(valid, packed, q_ref, k_ref):
    rows = q_ref.shape[0]
    qk = packed[:, :256].reshape(rows, 128)
    kq = jnp.concatenate([qk[:, 64:], qk[:, :64]], axis=1)
    lane = lax.broadcasted_iota(jnp.int32, (rows, 128), 1)
    spot = lax.broadcasted_iota(jnp.int32, (rows, 128), 0)
    past = jnp.where(spot < valid, 0.0, MASKED)
    q_ref[...] = jnp.where(lane < 64, qk.astype(jnp.float32), jnp.where(lane == 64, 1.0, 0.0)).astype(jnp.bfloat16)
    k_ref[...] = jnp.where(lane < 64, kq.astype(jnp.float32), jnp.where(lane == 64, past, 0.0)).astype(jnp.bfloat16)


def unpack_rows(halves):
    n = halves.shape[0]
    return jnp.concatenate([halves[:, :, :64], halves[:, :, 64:]], axis=1).reshape(n * 256, 64)


def block_probs(q_ref, k_ref, i):
    n = (i + 1) * BQ
    scores = dot_nt(k_ref[:n], q_ref[i * BQ:n])
    key = lax.broadcasted_iota(jnp.int32, (BQ, BQ), 0)
    query = lax.broadcasted_iota(jnp.int32, (BQ, BQ), 1)
    corner = jnp.where(key <= query, scores[n - BQ:], MASKED)
    scores = jnp.concatenate([scores[:n - BQ], corner], axis=0) if i else corner
    top = jnp.max(scores, axis=0, keepdims=True)
    terms = jnp.exp((scores - top) * 0.125)
    return terms, 1.0 / jnp.sum(terms, axis=0, keepdims=True)


def attend_kernel(valid_ref, packed, out_ref, q_ref, k_ref, vt_ref):
    load_heads(valid_ref[0], packed, q_ref, k_ref)
    unit = jnp.where(
        lax.broadcasted_iota(jnp.int32, (64, 64), 0) == lax.broadcasted_iota(jnp.int32, (64, 64), 1), 1.0, 0.0
    ).astype(jnp.bfloat16)
    vt_ref[...] = dot_nt(unit, unpack_rows(packed[:, 256:])).astype(jnp.bfloat16)
    for i in range(q_ref.shape[0] // BQ):
        n = (i + 1) * BQ
        terms, scale = block_probs(q_ref, k_ref, i)
        probs = (terms * scale).astype(jnp.bfloat16)
        mixed = dot_nn(vt_ref[:, :n], probs).T
        out_ref[i] = jnp.concatenate([mixed[:128], mixed[128:]], axis=1).astype(jnp.bfloat16)


def attend_back_kernel(valid_ref, packed, grad, out_ref, q_ref, k_ref, v_ref, g_ref, kt_ref, dk_ref, dv_ref):
    load_heads(valid_ref[0], packed, q_ref, k_ref)
    v_ref[...] = unpack_rows(packed[:, 256:])
    g_ref[...] = unpack_rows(grad[...])
    unit = jnp.where(
        lax.broadcasted_iota(jnp.int32, (64, 128), 0) == lax.broadcasted_iota(jnp.int32, (64, 128), 1), 1.0, 0.0
    ).astype(jnp.bfloat16)
    kt_ref[...] = dot_nt(unit, k_ref[...]).astype(jnp.bfloat16)
    dk_ref[...] = jnp.zeros_like(dk_ref)
    dv_ref[...] = jnp.zeros_like(dv_ref)
    blocks = q_ref.shape[0] // BQ
    for i in range(blocks):
        n = (i + 1) * BQ
        terms, scale = block_probs(q_ref, k_ref, i)
        probs = terms * scale
        grad_probs = dot_nt(v_ref[:n], g_ref[i * BQ:n])
        delta = jnp.sum(probs * grad_probs, axis=0, keepdims=True)
        grad_scores = (probs * (grad_probs - delta)).astype(jnp.bfloat16)
        grad_query = dot_nn(kt_ref[:, :n], grad_scores).T * 0.125
        out_ref[i, :256, :64] = grad_query.astype(jnp.bfloat16)
        dk_ref[:n] += dot_nn(grad_scores, q_ref[i * BQ:n])
        dv_ref[:n] += dot_nn(probs.astype(jnp.bfloat16), g_ref[i * BQ:n])
    for i in range(blocks):
        rows = slice(i * BQ, (i + 1) * BQ)
        out_ref[i, :256, 64:] = (dk_ref[rows, :64] * 0.125).astype(jnp.bfloat16)
        value = dv_ref[rows].astype(jnp.bfloat16)
        out_ref[i, 256:] = jnp.concatenate([value[:128], value[128:]], axis=1)


def attend(valid, packed):
    rows = packed.shape[0] * 256
    vm = pl.BlockSpec(memory_space=pltpu.VMEM)
    return pl.pallas_call(
        attend_kernel,
        out_shape=jax.ShapeDtypeStruct((packed.shape[0], 128, 128), jnp.bfloat16),
        in_specs=[pl.BlockSpec(memory_space=pltpu.SMEM), vm], out_specs=vm,
        scratch_shapes=[pltpu.VMEM((rows, 128), jnp.bfloat16)] * 2 + [pltpu.VMEM((64, rows), jnp.bfloat16)],
        compiler_params=pltpu.CompilerParams(vmem_limit_bytes=48 << 20),
        name="attend",
    )(valid, packed)


def attend_back(valid, packed, grad):
    rows = packed.shape[0] * 256
    vm = pl.BlockSpec(memory_space=pltpu.VMEM)
    return pl.pallas_call(
        attend_back_kernel,
        out_shape=jax.ShapeDtypeStruct(packed.shape, jnp.bfloat16),
        in_specs=[pl.BlockSpec(memory_space=pltpu.SMEM), vm, vm], out_specs=vm,
        scratch_shapes=[pltpu.VMEM((rows, 128), jnp.bfloat16)] * 2 + [pltpu.VMEM((rows, 64), jnp.bfloat16)] * 2
        + [pltpu.VMEM((64, rows), jnp.bfloat16), pltpu.VMEM((rows, 128), jnp.float32), pltpu.VMEM((rows, 64), jnp.float32)],
        compiler_params=pltpu.CompilerParams(vmem_limit_bytes=48 << 20),
        name="attend_back",
    )(valid, packed, grad)


def flip(bits, block):
    return lax.ppermute(block, "seq", [(s, s ^ bits) for s in range(16)])


flip_a, flip_y = (functools.partial(flip, bits) for bits in (8, 2))


def flip_x(block):
    return lax.ppermute(block, "dp", [(0, 1), (1, 0)])


def after(value, *others):
    return lax.optimization_barrier((value,) + others)[0]


def pick(block, index, axis, keepdims=False):
    return lax.dynamic_index_in_dim(block, index, axis, keepdims=keepdims)


def cube_one(flip_one, block):
    return jnp.concatenate([block, flip_one(block)], 0)


def arrange_kernel(spot_ref, kept, *refs):
    out = refs[-1]
    i = pl.program_id(0)
    wide = len(out.shape) == 7

    @pl.when(i < 4)
    def _():
        if wide:
            for j in range(2):
                for k in range(2):
                    out[0, j, 0, k, 0] = kept[0, j, k]
        else:
            out[0, 0, 0] = kept[0]

    @pl.when(i >= 4)
    def _():
        if wide:
            for j in range(2):
                for k in range(2):
                    out[0, j, 0, k, 0] = refs[j][0, k]
        else:
            out[0, 0, 0] = refs[0][0]


def arrange(spot, kept, *received):
    def coords(i, r):
        return lax.rem(r[0] + i % 2, 2), lax.rem(r[1] + i // 4, 2), lax.rem(r[2] + (i // 2) % 2, 2)

    shape = kept.shape

    def spec(block, low):
        rest = (0,) * (block.ndim - 1)
        return pl.BlockSpec((1,) + block.shape[1:], lambda i, r: (jnp.clip(i - low, 0, 3),) + rest)

    if len(shape) == 5:
        def out_place(i, r):
            a, y, x = coords(i, r)
            return a, 0, y, 0, x, 0, 0
        out_block, out_shape = (1, 2, 1, 2, 1) + shape[3:], (2,) * 5 + shape[3:]
    else:
        def out_place(i, r):
            return coords(i, r) + (0, 0)
        out_block, out_shape = (1, 1, 1) + shape[1:], (2, 2, 2) + shape[1:]
    return pl.pallas_call(
        arrange_kernel,
        out_shape=jax.ShapeDtypeStruct(out_shape, kept.dtype),
        grid_spec=pltpu.PrefetchScalarGridSpec(
            num_scalar_prefetch=1, grid=(8,), in_specs=[spec(kept, 0)] + [spec(block, 4) for block in received],
            out_specs=pl.BlockSpec(out_block, out_place)),
        compiler_params=pltpu.CompilerParams(vmem_limit_bytes=32 << 20),
        cost_estimate=pl.CostEstimate(flops=0, bytes_accessed=8 << 20, transcendentals=0),
        name="arrange",
    )(spot, kept, *received)


def up_kernel(rows_ref, w_ref, shift_ref, active_ref, slope_ref):
    for r in range(0, rows_ref.shape[0], 128):
        span = slice(r, r + 128)
        t = dot_nn(rows_ref[span], w_ref[...]) + shift_ref[...]
        half = 0.5 + 0.5 * lax.erf(t * math.sqrt(0.5))
        active_ref[span] = (t * half).astype(jnp.bfloat16)
        slope_ref[span] = half + t * jnp.exp(t * t * -0.5) * (1.0 / math.sqrt(2.0 * math.pi))


def up_gelu(rows, w, shift):
    m, k = rows.shape
    n, block = w.shape[1], 256
    return pl.pallas_call(
        up_kernel, grid=(n // block,),
        out_shape=(jax.ShapeDtypeStruct((m, n), jnp.bfloat16), jax.ShapeDtypeStruct((m, n), jnp.float32)),
        in_specs=[pl.BlockSpec((m, k), lambda i: (0, 0)), pl.BlockSpec((k, block), lambda i: (0, i)),
                  pl.BlockSpec((1, block), lambda i: (0, i))],
        out_specs=(pl.BlockSpec((m, block), lambda i: (0, i)),) * 2,
        compiler_params=pltpu.CompilerParams(vmem_limit_bytes=32 << 20),
        cost_estimate=pl.CostEstimate(flops=2 * m * n * k, bytes_accessed=24 << 20, transcendentals=2 * m * n),
        name="up_gelu",
    )(rows, w, shift)


def add_low(mine, other):
    return (mine.astype(jnp.float32) + other.astype(jnp.float32)).astype(jnp.bfloat16)


def fold(terms, flip_one, index, axis):
    return add_low(pick(terms, index, axis, True), flip_one(pick(terms, 1 - index, axis, True)))


def reduce_kernel(q_ref, o_ref, u_ref, part, tokens, grad_middle, vectors, *refs):
    vec_refs, (out_q, ro, out_u, vec, input_grad, got_far, got_near, low_sums, got_sums, row_send, row_recv, rq, gu, r1q, t2q, r2q, t3q, r3q, fq, gq, r1o, t2o, r2o, t3o, r3o,
               run, got, send_sem, recv_sem) = refs[:10], refs[10:]
    a, b, y, c, x = place()
    f32, bf16 = jnp.float32, jnp.bfloat16
    barrier = pltpu.get_barrier_semaphore()

    def at(pa, pb, py, pc, px):
        return (pa * 8 + pb * 4 + py * 2 + pc, px)

    to_x, to_y, to_a = at(a, b, y, c, 1 - x), at(a, b, 1 - y, c, x), at(1 - a, b, y, c, x)
    ranks = [(lax.rem(b + k // 2, 2), lax.rem(c + k % 2, 2)) for k in range(4)]
    to_rank = [at(a, ranks[k][0], y, ranks[k][1], x) for k in range(4)]
    to_b, to_c = to_rank[2], to_rank[1]
    for dev in [to_x, to_y, to_a] + to_rank[1:]:
        pl.semaphore_signal(barrier, inc=1, device_id=dev, device_id_type=MESH)
    for pb in range(2):
        for j in range(4):
            for row, cols in ((0, slice(j * 128, j * 128 + HD)), (1, slice(512 + j * HD, 512 + j * HD + HD))):
                piece = vec_refs[0][:, cols]
                pair = [jnp.where((b == pb) & (c == pc), piece, 0.0) for pc in range(2)]
                h = head_of(j // 2, pb, j % 2, 0) * HD
                run[0, row:row + 1, h:h + 128] = jnp.concatenate(pair, 1)
            for pc in range(2):
                col = head_of(j // 2, pb, j % 2, pc) * 256
                piece = vec_refs[1][:, j * 256:j * 256 + 256]
                run[0, 12 + col // 1024:13 + col // 1024, col % 1024:col % 1024 + 256] = jnp.where(
                    (b == pb) & (c == pc), piece, 0.0)
    for k, row in enumerate((2, 3, 5, 6, 7, 9, 10, 11)):
        run[0, row:row + 1] = vec_refs[2 + k][...]
    for row in (4, 8):
        run[0, row:row + 1] = jnp.zeros((1, 1024), f32)
    pl.semaphore_wait(barrier, 6)

    made = []

    def remote(src, dst, dev):
        k = len(made)
        made.append(pltpu.make_async_remote_copy(
            src_ref=src, dst_ref=dst, send_sem=send_sem.at[k], recv_sem=recv_sem.at[k],
            device_id=dev, device_id_type=MESH))
        return made[-1]

    def low(*values):
        return sum(v.astype(f32) for v in values)

    places = [1 - a, a]
    halves = [slice(0, 512), slice(512, 1024)]
    lateral = [(to_x, to_y), (to_y, to_x)]

    q1, q2, o1, o2 = {}, {}, {}, {}
    for i in range(2):
        for s in range(2):
            p = places[i]
            q1[s, i] = remote(q_ref.at[p, 0, :, :, 1 - x] if s == 0 else q_ref.at[p, 1, 1 - y], r1q.at[s, i], lateral[s][0])
            o1[s, i] = remote(o_ref.at[p, :, 1 - x, :, halves[0]] if s == 0 else o_ref.at[p, 1 - y, :, :, halves[1]],
                              r1o.at[s, i], lateral[s][0])
            q2[s, i] = remote(t2q.at[s, i], r2q.at[s, i], lateral[s][1])
            o2[s, i] = remote(t2o.at[s, i], r2o.at[s, i], lateral[s][1])
    q3 = [remote(t3q.at[s], r3q.at[s], to_a) for s in range(2)]
    o3 = [remote(t3o.at[s], r3o.at[s], to_a) for s in range(2)]
    qr = [remote(fq.at[ranks[k][0], ranks[k][1]], gq.at[k - 1], to_rank[k]) for k in range(1, 4)]
    ur = [remote(u_ref.at[ranks[k][0], ranks[k][1]], gu.at[b, c], to_rank[k]) for k in range(1, 4)]
    vs = [remote(run.at[k], got.at[k], dev) for k, dev in enumerate((to_x, to_y, to_a, to_b, to_c))]

    def next_sum(k):
        vs[k].wait_recv()
        if k < 4:
            run[k + 1] = run[k] + got[k]
            vs[k + 1].start()
        else:
            vec[...] = run[k] + got[k]

    pieces = part.shape[2] // PIECE

    def span(r):
        return pl.ds(pl.multiple_of(r * PIECE, PIECE), PIECE)

    def row_copy(kind, r):
        src, dst, dev = ((part.at[1, 1, span(r)], got_far.at[span(r)], to_c), (part.at[0, 1, span(r)], got_near.at[span(r)], to_c),
                         (low_sums.at[span(r)], got_sums.at[span(r)], to_b))[kind]
        return pltpu.make_async_remote_copy(
            src_ref=src, dst_ref=dst, send_sem=row_send.at[kind, r], recv_sem=row_recv.at[kind, r],
            device_id=dev, device_id_type=MESH)

    def send_across(r, _):
        row_copy(0, r).wait_recv()
        low_sums[span(r)] = (part[1, 0, span(r)] + got_far[span(r)]).astype(bf16)
        row_copy(2, r).start()
        return 0

    def take(r, _):
        row_copy(1, r).wait_recv()
        row_copy(2, r).wait_recv()
        total = part[0, 0, span(r)] + got_near[span(r)] + got_sums[span(r)].astype(f32)
        _, pull = jax.vjp(norm_rows, tokens[span(r)].astype(f32), *norm_vectors(vectors, 0))
        term, grad_gain, grad_shift = pull(total)
        input_grad[span(r)] = (grad_middle[span(r)] + term).astype(bf16)
        run[0, 4:5] += grad_gain
        run[0, 8:9] += grad_shift
        for kind in range(3):
            row_copy(kind, r).wait_send()
        return 0

    for kind in range(2):
        for r in range(pieces):
            row_copy(kind, r).start()
    for s in range(2):
        q1[s, 0].start()
        o1[s, 0].start()
    for k in (3, 2, 1):
        ur[k - 1].start()
    for s in range(2):
        o1[s, 1].start()
    lax.fori_loop(0, pieces, send_across, 0)

    def q_terms(s, i, far):
        p = places[i]
        if s == 0:
            v = 1 - y if far else y
            return q_ref[p, 0, v, :, x], r1q[0, i, v]
        v = 1 - x if far else x
        return q_ref[p, 1, y, :, v], r1q[1, i, :, v]

    def o_terms(s, i, far):
        p = places[i]
        if s == 0:
            v = 1 - y if far else y
            return o_ref[p, v, x, :, halves[0]], r1o[0, i, v]
        v = 1 - x if far else x
        return o_ref[p, y, v, :, halves[1]], r1o[1, i, v]

    for i in range(2):
        for s in range(2):
            q1[s, i].wait_recv()
            t2q[s, i] = low(*q_terms(s, i, True)).astype(bf16)
            q2[s, i].start()
            o1[s, i].wait_recv()
            t2o[s, i] = low(*o_terms(s, i, True)).astype(bf16)
            o2[s, i].start()
        if i == 0:
            for s in range(2):
                q1[s, 1].start()
            lax.fori_loop(0, pieces, take, 0)
            vs[0].start()
            for s in range(2):
                q2[s, 0].wait_recv()
                t3q[s] = low(*q_terms(s, 0, False), r2q[s, 0]).astype(bf16)
                q3[s].start()
                o2[s, 0].wait_recv()
                t3o[s] = low(*o_terms(s, 0, False), r2o[s, 0]).astype(bf16)
                o3[s].start()
    next_sum(0)
    for s in range(2):
        q2[s, 1].wait_recv()
        o2[s, 1].wait_recv()
        q3[s].wait_recv()
        total = low(*q_terms(s, 1, False), r2q[s, 1], r3q[s])
        fq[s] = total.astype(bf16)
        for j in range(2):
            @pl.when((b == s) & (c == j))
            def _():
                rq[s, j] = total[j]
        o3[s].wait_recv()
        ro[:, halves[s]] = low(*o_terms(s, 1, False), r2o[s, 1], r3o[s])
        next_sum(1 + s)
    for k in (3, 2, 1):
        qr[k - 1].start()
    gu[b, c] = u_ref[b, c]
    for k in (1, 2, 3):
        ur[k - 1].wait_recv()
    next_sum(3)
    for k in (1, 2, 3):
        pb, pc = ranks[k]
        qr[k - 1].wait_recv()
        rq[pb, pc] = gq[k - 1].astype(f32)
    for pb in range(2):
        for j in range(4):
            zero, one = rq[pb, 0], rq[pb, 1]
            h = head_of(j // 2, pb, j % 2, 0) * HD
            q, k = slice(j * 128, j * 128 + HD), slice(j * 128 + HD, j * 128 + 128)
            v = slice(512 + j * HD, 512 + j * HD + HD)
            for t, cols in enumerate((q, k, v)):
                out_q[:, t * 1024 + h:t * 1024 + h + 128] = jnp.concatenate([zero[:, cols], one[:, cols]], 1)
            for pc in range(2):
                col = head_of(j // 2, pb, j % 2, pc) * 256
                out_u[:, col:col + 256] = gu[pb, pc, :, j * 256:j * 256 + 256].astype(f32)
    next_sum(4)
    for copy in made:
        copy.wait_send()


def reduce_all(gw_qkv, gw_out, up_sum, part, tokens, grad_middle, params, vectors, cid):
    f32, bf16 = jnp.float32, jnp.bfloat16
    V = pltpu.VMEM
    vm = pl.BlockSpec(memory_space=V)
    S = jax.ShapeDtypeStruct
    q, o, u = gw_qkv.shape[5:], (gw_out.shape[3], 512), up_sum.shape
    rows, n = grad_middle.shape
    scratch = [
        V((rows, n), f32), V((rows, n), f32), V((rows, n), bf16), V((rows, n), bf16),
        pltpu.SemaphoreType.DMA((3, rows // PIECE)), pltpu.SemaphoreType.DMA((3, rows // PIECE)),
        V((2, 2) + q, f32), V(u, bf16),
        V((2, 2, 2, 2) + q, bf16), V((2, 2, 2) + q, bf16), V((2, 2, 2) + q, bf16), V((2, 2) + q, bf16), V((2, 2) + q, bf16),
        V((2, 2) + q, bf16), V((3,) + q, bf16),
        V((2, 2, 2) + o, bf16), V((2, 2) + o, bf16), V((2, 2) + o, bf16), V((2,) + o, bf16), V((2,) + o, bf16),
        V((5, 16, 1024), f32), V((5, 16, 1024), f32),
        pltpu.SemaphoreType.DMA((32,)), pltpu.SemaphoreType.DMA((32,))]
    return pl.pallas_call(
        reduce_kernel,
        out_shape=(S((q[0], 4 * q[1]), f32), S((o[0], 1024), f32), S((u[2], 4 * u[3]), f32), S((16, 1024), f32), S((rows, n), bf16)),
        in_specs=[vm] * 17, out_specs=(vm,) * 5, scratch_shapes=scratch,
        compiler_params=pltpu.CompilerParams(collective_id=cid, has_side_effects=True, vmem_limit_bytes=48 << 20),
        name="reduce_all",
    )(gw_qkv, gw_out, up_sum, part.reshape(2, 2, rows, n), tokens, grad_middle, params, *vectors)


def qk_columns(head):
    return slice(head * HD, head * HD + HD), slice(1024 + head * HD, 1024 + head * HD + HD), slice(2048 + head * HD, 2048 + head * HD + HD)


def head_of(a, b, y, c):
    return a * 8 + b * 4 + y * 2 + c


def start_kernel(q_hbm, u_hbm, o_in, t_in, v_in, wq, wo, up, rows, vec, q_in, u_in, q_src, u_src, send_sem, recv_sem, own_sem):
    a, b, y, c, x = place()
    barrier = pltpu.get_barrier_semaphore()

    def at(pa, pb, py, pc, px):
        return (pa * 8 + pb * 4 + py * 2 + pc, px)

    to_x, to_y, to_a = at(a, b, y, c, 1 - x), at(a, b, 1 - y, c, x), at(1 - a, b, y, c, x)
    ranks = [(lax.rem(b + k // 2, 2), lax.rem(c + k % 2, 2)) for k in range(4)]
    to_rank = [at(a, pb, y, pc, x) for pb, pc in ranks]
    for dev in [to_x, to_y, to_a] + to_rank[1:]:
        pl.semaphore_signal(barrier, inc=1, device_id=dev, device_id_type=MESH)

    loads = [pltpu.make_async_copy(q_hbm, q_in, own_sem.at[5]), pltpu.make_async_copy(u_hbm, u_in, own_sem.at[6])]
    for copy in loads:
        copy.start()
    for copy in loads:
        copy.wait()

    for pb in range(2):
        for pc in range(2):
            for j in range(4):
                q, k, v = qk_columns(head_of(j // 2, pb, j % 2, pc))
                q_src[pb, pc, :, j * 128:j * 128 + 128] = jnp.concatenate([q_in[:, q], q_in[:, k]], 1)
            for j in range(2):
                v0 = qk_columns(head_of(j, pb, 0, pc))[2]
                v1 = qk_columns(head_of(j, pb, 1, pc))[2]
                q_src[pb, pc, :, 512 + j * 128:640 + j * 128] = jnp.concatenate([q_in[:, v0], q_in[:, v1]], 1)
            for j in range(4):
                col = (head_of(j // 2, pb, j % 2, pc)) * 256
                u_src[pb, pc, :, j * 256:j * 256 + 256] = u_in[:, col:col + 256]
    own = [pltpu.make_async_copy(src, dst, own_sem.at[k]) for k, (src, dst) in enumerate((
        (q_src.at[b, c], wq.at[a, b, y, c, x]), (u_src.at[b, c], up.at[0, b, c]), (o_in, wo.at[a, y, x]),
        (t_in, rows.at[0]), (v_in, vec.at[a, b, y, c, x])))]
    for copy in own:
        copy.start()
    pl.semaphore_wait(barrier, 6)

    made = []

    def remote(src, dst, dev):
        k = len(made)
        made.append(pltpu.make_async_remote_copy(
            src_ref=src, dst_ref=dst, send_sem=send_sem.at[k], recv_sem=recv_sem.at[k],
            device_id=dev, device_id_type=MESH))
        return made[-1]

    places = [a, 1 - a]
    halves = [slice(0, 512), slice(512, 1024)]
    lateral = [(to_y, to_x), (to_x, to_y)]

    def same(ref, dev):
        return remote(ref, ref, dev)

    q_rank = [remote(q_src.at[ranks[k][0], ranks[k][1]], wq.at[a, b, y, c, x], to_rank[k]) for k in range(1, 4)]
    u_rank = [remote(u_src.at[ranks[k][0], ranks[k][1]], up.at[0, b, c], to_rank[k]) for k in range(1, 4)]
    v_rank = [remote(v_in, vec.at[a, b, y, c, x], to_rank[k]) for k in range(1, 4)]
    t_core, t_near = remote(t_in, rows.at[1], to_rank[1]), remote(t_in, rows.at[2], to_rank[2])
    t_far = remote(rows.at[2], rows.at[3], to_rank[1])
    u_cube = remote(up.at[0], up.at[1], to_a)
    v_cube = [same(vec.at[a, :, y, :, x], to_a), same(vec.at[:, :, y, :, x], to_y), same(vec.at[:, :, :, :, x], to_x)]
    q_cube = [same(wq.at[a, s, y, :, x], to_a) for s in range(2)]
    o_cube = [remote(o_in.at[:, halves[s]], wo.at[a, y, x, :, halves[s]], to_a) for s in range(2)]
    q_side, o_side = {}, {}
    for i in range(2):
        for s in range(2):
            one, two = lateral[s]
            oy, ox = (1 - y, x) if s == 0 else (y, 1 - x)
            p = places[i]
            mine, theirs = wq.at[p, s, y, :, x], wq.at[p, s, oy, :, ox]
            q_side[s, i] = (same(mine, one), same(mine, two), same(theirs, two))
            mine, theirs = wo.at[p, y, x, :, halves[s]], wo.at[p, oy, ox, :, halves[s]]
            first = o_in.at[:, halves[s]] if i == 0 else mine
            o_side[s, i] = (remote(first, mine, one), remote(first, mine, two), same(theirs, two))

    for k in (2, 1, 0):
        q_rank[k].start()
        v_rank[k].start()
    for s in range(2):
        o_cube[s].start()
        o_side[s, 0][0].start()
        o_side[s, 0][1].start()
    t_near.start()
    t_core.start()
    own[0].wait()
    for copy in q_rank:
        copy.wait_recv()
    for s in range(2):
        q_cube[s].start()
        q_side[s, 0][0].start()
        q_side[s, 0][1].start()
    own[4].wait()
    for copy in v_rank:
        copy.wait_recv()
    v_cube[0].start()
    for k in (2, 1, 0):
        u_rank[k].start()
    for s in range(2):
        o_side[s, 0][0].wait_recv()
        o_side[s, 0][2].start()
    for s in range(2):
        o_cube[s].wait_recv()
        o_side[s, 1][0].start()
        o_side[s, 1][1].start()
    t_near.wait_recv()
    t_far.start()
    for s in range(2):
        q_side[s, 0][0].wait_recv()
        q_side[s, 0][2].start()
    for s in range(2):
        q_cube[s].wait_recv()
        q_side[s, 1][0].start()
        q_side[s, 1][1].start()
    v_cube[0].wait_recv()
    v_cube[1].start()
    own[1].wait()
    for copy in u_rank:
        copy.wait_recv()
    u_cube.start()
    for s in range(2):
        o_side[s, 1][0].wait_recv()
        o_side[s, 1][2].start()
    v_cube[1].wait_recv()
    v_cube[2].start()
    for s in range(2):
        q_side[s, 1][0].wait_recv()
        q_side[s, 1][2].start()
    v_cube[2].wait_recv()
    t_core.wait_recv()
    t_far.wait_recv()
    for i in range(2):
        for s in range(2):
            for k in (1, 2):
                q_side[s, i][k].wait_recv()
                o_side[s, i][k].wait_recv()
    u_cube.wait_recv()
    for k in (2, 3):
        own[k].wait()
    for copy in made:
        copy.wait_send()


def start_gather(w_qkv, w_up, w_out, tokens, vectors, cid):
    bf16 = jnp.bfloat16
    S = lambda *shape: jax.ShapeDtypeStruct(shape, bf16)
    vm, anywhere = pl.BlockSpec(memory_space=pltpu.VMEM), pl.BlockSpec(memory_space=pl.ANY)
    return pl.pallas_call(
        start_kernel,
        out_shape=(S(2, 2, 2, 2, 2, 32, 768), S(2, 2, 2, 32, 1024), S(2, 2, 2, 32, 1024), S(4, 128, 1024),
                   S(2, 2, 2, 2, 2, 16, 128)),
        in_specs=[pl.BlockSpec(memory_space=pltpu.HBM)] * 4 + [vm], out_specs=(anywhere,) * 5,
        scratch_shapes=[
            pltpu.VMEM(w_qkv.shape, bf16), pltpu.VMEM(w_up.shape, bf16),
            pltpu.VMEM((2, 2, 32, 768), bf16), pltpu.VMEM((2, 2, 32, 1024), bf16),
            pltpu.SemaphoreType.DMA((48,)), pltpu.SemaphoreType.DMA((48,)), pltpu.SemaphoreType.DMA((7,))],
        compiler_params=pltpu.CompilerParams(collective_id=cid, has_side_effects=True, vmem_limit_bytes=63 << 20),
        cost_estimate=pl.CostEstimate(flops=0, bytes_accessed=100 << 20, transcendentals=0),
        name="start_gather",
    )(w_qkv, w_up, w_out, tokens, vectors)


PIECE = 32


def rows_kernel(step, gather, count_in, count_out, part, *refs):
    ins, outs = refs[:count_in], refs[count_in:count_in + count_out]
    rest = refs[count_in + count_out:]
    rows = rest[0] if gather else None
    got_far, got_near, sums, got_sums, send_sem, recv_sem = rest[-6:]
    a, b, y, c, x = place()

    def at(pb, pc):
        return (a * 8 + pb * 4 + y * 2 + pc, x)

    to_b, to_core = at(1 - b, c), at(b, 1 - c)
    barrier = pltpu.get_barrier_semaphore()
    for dev in (to_b, to_core):
        pl.semaphore_signal(barrier, inc=1, device_id=dev, device_id_type=MESH)
    pl.semaphore_wait(barrier, 2)
    pieces = part.shape[2] // PIECE

    def span(r):
        return pl.ds(pl.multiple_of(r * PIECE, PIECE), PIECE)

    def remote(kind, r, src, dst, dev):
        return pltpu.make_async_remote_copy(
            src_ref=src, dst_ref=dst, send_sem=send_sem.at[kind, r], recv_sem=recv_sem.at[kind, r],
            device_id=dev, device_id_type=MESH)

    def far(r):
        return remote(0, r, part.at[1, 1, span(r)], got_far.at[span(r)], to_core)

    def near(r):
        return remote(1, r, part.at[0, 1, span(r)], got_near.at[span(r)], to_core)

    def across(r):
        return remote(2, r, sums.at[span(r)], got_sums.at[span(r)], to_b)

    def row_near(r):
        return remote(3, r, rows.at[0, span(r)], rows.at[2, span(r)], to_b)

    def row_core(r):
        return remote(4, r, rows.at[0, span(r)], rows.at[1, span(r)], to_core)

    def row_far(r):
        return remote(5, r, rows.at[2, span(r)], rows.at[3, span(r)], to_core)

    for r in range(pieces):
        far(r).start()
    for r in range(pieces):
        near(r).start()

    def send_across(r, _):
        far(r).wait_recv()
        sums[span(r)] = (part[1, 0, span(r)] + got_far[span(r)]).astype(jnp.bfloat16)
        across(r).start()
        return 0

    lax.fori_loop(0, pieces, send_across, 0)
    for ref in outs:
        if ref.shape[0] == 1:
            ref[...] = jnp.zeros_like(ref)

    def take(r, _):
        near(r).wait_recv()
        across(r).wait_recv()
        total = part[0, 0, span(r)] + got_near[span(r)] + got_sums[span(r)].astype(jnp.float32)
        piece = step(span(r), total, ins, outs)
        if gather:
            rows[0, span(r)] = piece
            row_near(r).start()
            row_core(r).start()
        return 0

    lax.fori_loop(0, pieces, take, 0)

    def relay(r, _):
        row_near(r).wait_recv()
        row_far(r).start()
        return 0

    def finish(r, _):
        if gather:
            row_core(r).wait_recv()
            row_far(r).wait_recv()
            row_near(r).wait_send()
            row_core(r).wait_send()
            row_far(r).wait_send()
        far(r).wait_send()
        near(r).wait_send()
        across(r).wait_send()
        return 0

    if gather:
        lax.fori_loop(0, pieces, relay, 0)
    lax.fori_loop(0, pieces, finish, 0)


def sum_rows(step, part, ins, outs, gather, cid):
    rows, n = part.shape[0] // 4, part.shape[1]
    vm = pl.BlockSpec(memory_space=pltpu.VMEM)
    shapes = tuple(outs) + ((jax.ShapeDtypeStruct((4, rows, n), jnp.bfloat16),) if gather else ())
    V = pltpu.VMEM
    return pl.pallas_call(
        functools.partial(rows_kernel, step, gather, len(ins), len(outs)),
        out_shape=shapes, in_specs=[vm] * (1 + len(ins)), out_specs=(vm,) * len(shapes),
        scratch_shapes=[V((rows, n), jnp.float32), V((rows, n), jnp.float32), V((rows, n), jnp.bfloat16), V((rows, n), jnp.bfloat16),
                        pltpu.SemaphoreType.DMA((6, rows // PIECE)), pltpu.SemaphoreType.DMA((6, rows // PIECE))],
        compiler_params=pltpu.CompilerParams(collective_id=cid, has_side_effects=True, vmem_limit_bytes=32 << 20),
        cost_estimate=pl.CostEstimate(flops=0, bytes_accessed=50 << 20, transcendentals=0),
        name="sum_rows",
    )(part.reshape(2, 2, rows, n), *ins)


def norm_vectors(vectors, k):
    return vectors[4 + k:5 + k], vectors[8 + k:9 + k]


def attended_step(span, total, ins, outs):
    tokens, vectors = ins
    branch = total + vectors[2:3]
    middle = tokens[span].astype(jnp.float32) + norm_rows(branch, *norm_vectors(vectors, 1))
    outs[0][span] = branch
    outs[1][span] = middle
    return norm_rows(middle, *norm_vectors(vectors, 2)).astype(jnp.bfloat16)


def output_step(span, total, ins, outs):
    middle, grad_out, vectors = ins
    normed, pull = jax.vjp(norm_rows, total + vectors[3:4], *norm_vectors(vectors, 3))
    outs[0][span] = (middle[span] + normed).astype(jnp.bfloat16)
    grad_down, grad_gain, grad_shift = pull(grad_out[span])
    grad_down = grad_down.astype(jnp.bfloat16)
    outs[1][...] += grad_gain
    outs[2][...] += grad_shift
    outs[3][...] += jnp.sum(grad_down.astype(jnp.float32), 0, keepdims=True)
    return grad_down


def middle_step(span, total, ins, outs):
    middle, branch, grad_out, vectors = ins
    _, pull = jax.vjp(norm_rows, middle[span], *norm_vectors(vectors, 2))
    part, grad_gain2, grad_shift2 = pull(total)
    grad_middle = grad_out[span] + part
    _, pull = jax.vjp(norm_rows, branch[span], *norm_vectors(vectors, 1))
    grad_branch, grad_gain1, grad_shift1 = pull(grad_middle)
    grad_branch = grad_branch.astype(jnp.bfloat16)
    outs[0][span] = grad_middle
    for ref, value in zip(outs[1:], (grad_gain2, grad_shift2, grad_gain1, grad_shift1,
                                     jnp.sum(grad_branch.astype(jnp.float32), 0, keepdims=True))):
        ref[...] += value
    return grad_branch


def fast_body(tokens, cotangent, lengths, assign, w_qkv, qv_bias, w_out, out_bias, w_up, up_bias, w_down, down_bias,
              norm_gain, norm_shift):
    bf16, f32 = jnp.bfloat16, jnp.float32
    a, b, y, c, x = place()
    spot = jnp.stack([a, y, x]).astype(jnp.int32)
    width = tokens.shape[2]
    place_two = jnp.arange(2, dtype=jnp.int32)
    sequence = jnp.sum(jnp.where(place_two == x, assign.astype(jnp.int32), 0))
    valid = jnp.sum(jnp.where(place_two == sequence, lengths.astype(jnp.int32), 0))

    small, row = jnp.zeros((16, 128), bf16), 0
    for block in (qv_bias, out_bias[None], down_bias[None], norm_gain, norm_shift, up_bias[None]):
        small += jnp.pad(block, ((row, 16 - row - block.shape[0]), (0, 128 - block.shape[1])))
        row += block.shape[0]
    wqkv, wo, up_one, rows, small = start_gather(w_qkv, w_up, w_out, tokens[0], small, 6)
    down_one = after(w_down, wqkv)
    down_one = jnp.stack([down_one, flip_a(down_one)])
    wqkv, wo, rows = wqkv.reshape(width, 768), wo.reshape(256, width), rows.reshape(512, width)

    vectors = small[..., :12, :32].reshape(32, 12, 32).transpose(1, 0, 2).reshape(12, width).astype(f32)
    qv_half = pick(pick(vectors[:2].reshape(2, 2, 2, 2, 2, HD), b, 2), c, 3).reshape(2, 4, HD)
    qk_shift = jnp.concatenate([qv_half[0], jnp.zeros((4, HD), f32)], 1).reshape(512)
    v_shift = qv_half[1].reshape(256)
    up_shift = pick(pick(small[..., 12, :], b, 1), c, 2).reshape(1024).astype(f32)

    first = norm_rows(rows.astype(f32), vectors[4:5], vectors[8:9]).astype(bf16)
    up_two = cube_one(flip_x, up_one)
    projected = (dot_nn(first, wqkv) + jnp.concatenate([qk_shift, v_shift])).astype(bf16)
    up_half = flip_y(up_two[:, 0])
    packed = exchange(after(projected, up_two, down_one), True, 1).reshape(8, 384, 128)
    packed = after(packed, up_half)
    down_two = cube_one(flip_x, down_one)
    up_rest = flip_y(after(up_two, packed)[:, 1])
    attended = attend(valid[None], packed).reshape(2, 2, 2, 128, 128)
    attended = exchange(after(attended, down_two, up_rest), False, 2)
    down_far = flip_y(after(down_two, attended))
    own_spot = lax.axis_index("seq") * 128 + jnp.arange(128, dtype=jnp.int32)
    grad_out = cotangent[0].astype(f32) * (own_spot < valid).astype(f32)[:, None]
    S = jax.ShapeDtypeStruct
    wide, low, line = S((128, width), f32), S((128, width), bf16), S((1, width), f32)
    branch, middle, third = sum_rows(
        attended_step, dot_nn(attended, wo), (tokens[0], vectors),
        (wide, wide), True, 7)
    third = third.reshape(512, width)
    wu = arrange(spot, up_two, up_half, up_rest).reshape(width, 1024)
    active, slope = up_gelu(third, wu, up_shift.reshape(1, 1024))
    wd = arrange(spot, down_two, after(down_far, active)).reshape(1024, width)
    output, gain4, shift4, bias_down, down_rows = sum_rows(
        output_step, dot_nn(active, wd), (middle, grad_out, vectors), (low, line, line, line), True, 8)
    down_rows = down_rows.reshape(512, width)
    gw_down = contract_rows(active, down_rows).astype(bf16).reshape(2, 2, 2, 128, width)
    down_send = pick(gw_down, 1 - y, 1, True)
    down_term = flip_y(down_send)
    grad_up = (dot_nt(after(down_rows, down_send), wd) * slope).astype(bf16)
    gw_up = contract_rows(third, grad_up).astype(bf16).reshape(2, 2, 2, 2, 2, 32, 1024)
    up_term = flip_x(pick(gw_up, 1 - x, 4, True))
    grad_middle, gain3, shift3, gain2, shift2, bias_out, branch_rows = sum_rows(
        middle_step, after(dot_nt(grad_up, wu), gw_up),
        (middle, branch, grad_out, vectors), (wide,) + (line,) * 5, True, 9)
    branch_rows = branch_rows.reshape(512, width)
    grad_att = dot_nt(branch_rows, wo).astype(bf16)
    down_sum = add_low(pick(gw_down, y, 1, True), down_term)
    up_sum = add_low(pick(gw_up, x, 4, True), up_term)
    down_term = flip_x(pick(down_sum, 1 - x, 2, True))
    up_term = flip_y(pick(up_sum, 1 - y, 2, True))
    grad_packed = exchange(after(grad_att, down_sum, up_sum), True, 3).reshape(8, 128, 128)
    up_sum = add_low(pick(up_sum, y, 2, True), after(up_term, grad_packed))
    up_term = flip_a(pick(up_sum, 1 - a, 0))
    back = attend_back(valid[None], packed, grad_packed)

    down_sum = add_low(pick(down_sum, x, 2, True), after(down_term, grad_packed))
    gw_out = contract_rows(attended, branch_rows).astype(bf16).reshape(2, 2, 2, 32, width)
    grad_qkv = exchange(after(back, up_term, down_sum).reshape(2, 2, 2, 384, 128), False, 4)
    down_term = flip_a(pick(after(down_sum, grad_qkv), 1 - a, 0))
    gw_qkv = contract_rows(first, grad_qkv).astype(bf16).reshape(2, 2, 2, 2, 2, 32, 768)
    def sums(block):
        return jnp.sum(block.astype(f32), 0, keepdims=True)

    sums_of = [sums(grad_qkv), sums(grad_up), bias_out, bias_down, gain2, gain3, gain4, shift2, shift3, shift4]
    up_sum = (pick(up_sum, a, 0).astype(f32) + up_term.astype(f32)).astype(bf16).reshape(2, 2, 32, 1024)
    r_qkv, r_out, r_up, vectors, input_grad = reduce_all(
        gw_qkv, gw_out, up_sum, dot_nt(grad_qkv, wqkv), tokens[0], grad_middle, vectors, sums_of, 5)
    r_down = (pick(down_sum, a, 0).astype(f32) + after(down_term, vectors).astype(f32)).reshape(128, width)
    index = lax.axis_index("seq") * 2 + x
    small_up = lax.dynamic_slice(vectors, (12 + index // 8, index % 8 * 128), (1, 128)).reshape(128)
    vectors = lax.dynamic_slice(vectors, (0, index * 32), (12, 32))

    return (
        output[None], input_grad[None], r_qkv, vectors[:2], r_out,
        vectors[2], r_up, small_up, r_down, vectors[3], vectors[4:8], vectors[8:12])


def solution(mesh):
    return jax.shard_map(
        fast_body if is_small(mesh) else body,
        mesh=mesh,
        in_specs=(
            P("dp", "seq", None),
            P("dp", "seq", None),
            P(),
            P(),
            P(("seq", "dp"), None),
            P(None, ("seq", "dp")),
            P(("seq", "dp"), None),
            P(("seq", "dp")),
            P(("seq", "dp"), None),
            P(("seq", "dp")),
            P(("seq", "dp"), None),
            P(("seq", "dp")),
            P(None, ("seq", "dp")),
            P(None, ("seq", "dp")),
        ),
        out_specs=(
            P("dp", "seq", None),
            P("dp", "seq", None),
            P(("seq", "dp"), None),
            P(None, ("seq", "dp")),
            P(("seq", "dp"), None),
            P(("seq", "dp")),
            P(("seq", "dp"), None),
            P(("seq", "dp")),
            P(("seq", "dp"), None),
            P(("seq", "dp")),
            P(None, ("seq", "dp")),
            P(None, ("seq", "dp")),
        ),
        check_vma=False,
    )
```

```python
import functools
import math

import jax
import jax.numpy as jnp
from jax import lax
from jax.experimental import pallas as pl
from jax.experimental.pallas import tpu as pltpu
from jax.sharding import PartitionSpec as P


HD = 64


RELAX_SCALE = 32.0
NORM_EPSILON = 1e-05


def norm_rows(values, gain, shift):
    center = values - jnp.mean(values, -1, keepdims=True)
    spread = jnp.mean(center * center, -1, keepdims=True)
    return center * lax.rsqrt(spread + NORM_EPSILON) * gain + shift


def exact_gelu(values):
    return jax.nn.gelu(values, approximate=False)


def contract_rows(left, right):
    return lax.dot_general(
        left, right, (((0,), (0,)), ((), ())), preferred_element_type=jnp.float32
    )


def contract_cols(left, right):
    return lax.dot_general(
        left, right, (((1,), (1,)), ((), ())), preferred_element_type=jnp.float32
    )


def split_heads(block):
    return block.reshape(block.shape[0], 2, HD)


def pair_scores(query_part, key_part):
    factor = 1.0 / (RELAX_SCALE * math.sqrt(HD))
    return (
        jnp.einsum(
            "qhd,khd->hqk",
            split_heads(query_part),
            split_heads(key_part),
            preferred_element_type=jnp.float32,
        )
        * factor
    )


def kept_probs(scores, allowed, row_max, row_total):
    exp_terms = jnp.exp(jnp.where(allowed, RELAX_SCALE * (scores - row_max), -jnp.inf))
    return exp_terms / row_total


def body(
    tokens,
    cotangent,
    lengths,
    assign,
    w_qkv,
    qv_bias,
    w_out,
    out_bias,
    w_up,
    up_bias,
    w_down,
    down_bias,
    norm_gain,
    norm_shift,
):
    gathered = (
        lax.all_gather(w_qkv, ("seq", "dp"), axis=0, tiled=True),
        lax.all_gather(w_out, ("seq", "dp"), axis=0, tiled=True),
        lax.all_gather(w_up, ("seq", "dp"), axis=0, tiled=True),
        lax.all_gather(w_down, ("seq", "dp"), axis=0, tiled=True),
        lax.all_gather(qv_bias, ("seq", "dp"), axis=1, tiled=True),
        lax.all_gather(out_bias, ("seq", "dp"), axis=0, tiled=True),
        lax.all_gather(up_bias, ("seq", "dp"), axis=0, tiled=True),
        lax.all_gather(down_bias, ("seq", "dp"), axis=0, tiled=True),
        lax.all_gather(norm_gain, ("seq", "dp"), axis=1, tiled=True),
        lax.all_gather(norm_shift, ("seq", "dp"), axis=1, tiled=True),
    )
    qkv_full, out_full, up_full, down_full = (gathered[0], gathered[1], gathered[2], gathered[3])
    qv_shift = gathered[4].astype(jnp.float32)
    out_shift = gathered[5].astype(jnp.float32)
    up_shift = gathered[6].astype(jnp.float32)
    down_shift = gathered[7].astype(jnp.float32)
    gains = gathered[8].astype(jnp.float32)
    shifts = gathered[9].astype(jnp.float32)
    row_count = tokens.shape[1]
    model_width = tokens.shape[2]
    pair_cols = 2 * HD
    pair_count = model_width // pair_cols
    slot_rows = row_count * lax.axis_size("seq")
    factor = 1.0 / (RELAX_SCALE * math.sqrt(HD))
    valid = lengths[assign[lax.axis_index("dp")]]
    own_place = lax.axis_index("seq") * row_count + jnp.arange(row_count, dtype=jnp.int32)
    all_place = jnp.arange(slot_rows, dtype=jnp.int32)
    allowed = (all_place[None, :] <= own_place[:, None]) & (all_place[None, :] < valid)
    pair_ids = jnp.arange(pair_count, dtype=jnp.int32)
    hidden = tokens[0].astype(jnp.float32)
    normed_first, pull_first = jax.vjp(norm_rows, hidden, gains[0], shifts[0])
    normed_low = normed_first.astype(jnp.bfloat16)
    projected = jnp.dot(normed_low, qkv_full, preferred_element_type=jnp.float32)
    queries = (projected[:, :model_width] + qv_shift[0]).astype(jnp.bfloat16)
    key_own = projected[:, model_width : 2 * model_width].astype(jnp.bfloat16)
    value_own = (projected[:, 2 * model_width :] + qv_shift[1]).astype(jnp.bfloat16)
    keys, values = (
        lax.all_gather(key_own, "seq", axis=0, tiled=True),
        lax.all_gather(value_own, "seq", axis=0, tiled=True),
    )

    def columns(block, pair_index):
        return lax.dynamic_slice_in_dim(block, pair_index * pair_cols, pair_cols, 1)

    def merge_pairs(stack):
        return stack.transpose(1, 0, 2).reshape(stack.shape[1], model_width)

    def attend(pair_index):
        scores = pair_scores(columns(queries, pair_index), columns(keys, pair_index))
        row_max = jnp.max(jnp.where(allowed, scores, -jnp.inf), -1, keepdims=True)
        exp_terms = jnp.exp(jnp.where(allowed, RELAX_SCALE * (scores - row_max), -jnp.inf))
        row_total = jnp.sum(exp_terms, -1, keepdims=True)
        probs = (exp_terms / row_total).astype(jnp.bfloat16)
        mixed = jnp.einsum(
            "hqk,khd->qhd",
            probs,
            split_heads(columns(values, pair_index)),
            preferred_element_type=jnp.float32,
        )
        return (mixed.reshape(row_count, pair_cols), row_max[..., 0], row_total[..., 0])

    mixed_pairs, max_pairs, total_pairs = lax.map(attend, pair_ids)
    attended = merge_pairs(mixed_pairs).astype(jnp.bfloat16)
    branch = jnp.dot(attended, out_full, preferred_element_type=jnp.float32) + out_shift
    normed_second, pull_second = jax.vjp(norm_rows, branch, gains[1], shifts[1])
    middle = hidden + normed_second
    normed_third, pull_third = jax.vjp(norm_rows, middle, gains[2], shifts[2])
    third_low = normed_third.astype(jnp.bfloat16)
    up_pre = jnp.dot(third_low, up_full, preferred_element_type=jnp.float32) + up_shift
    activated, pull_gelu = jax.vjp(exact_gelu, up_pre)
    active_low = activated.astype(jnp.bfloat16)
    down_pre = jnp.dot(active_low, down_full, preferred_element_type=jnp.float32) + down_shift
    normed_fourth, pull_fourth = jax.vjp(norm_rows, down_pre, gains[3], shifts[3])
    output = (middle + normed_fourth).astype(jnp.bfloat16)[None]
    again = (
        lax.all_gather(w_qkv, ("seq", "dp"), axis=0, tiled=True),
        lax.all_gather(w_out, ("seq", "dp"), axis=0, tiled=True),
        lax.all_gather(w_up, ("seq", "dp"), axis=0, tiled=True),
        lax.all_gather(w_down, ("seq", "dp"), axis=0, tiled=True),
    )
    qkv_back, out_back, up_back, down_back = (again[0], again[1], again[2], again[3])
    keep_rows = (own_place < valid).astype(jnp.float32)[:, None]
    grad_out = cotangent[0].astype(jnp.float32) * keep_rows
    grad_down, grad_gain_four, grad_shift_four = pull_fourth(grad_out)
    grad_down_low = grad_down.astype(jnp.bfloat16)
    grad_w_down = contract_rows(active_low, grad_down_low)
    grad_b_down = jnp.sum(grad_down_low.astype(jnp.float32), 0)
    (grad_up,) = pull_gelu(contract_cols(grad_down_low, down_back))
    grad_up_low = grad_up.astype(jnp.bfloat16)
    grad_w_up = contract_rows(third_low, grad_up_low)
    grad_b_up = jnp.sum(grad_up_low.astype(jnp.float32), 0)
    grad_middle_part, grad_gain_three, grad_shift_three = pull_third(
        contract_cols(grad_up_low, up_back)
    )
    grad_middle = grad_out + grad_middle_part
    grad_branch, grad_gain_two, grad_shift_two = pull_second(grad_middle)
    grad_branch_low = grad_branch.astype(jnp.bfloat16)
    grad_w_out = contract_rows(attended, grad_branch_low)
    grad_b_out = jnp.sum(grad_branch_low.astype(jnp.float32), 0)
    grad_attended = contract_cols(grad_branch_low, out_back).astype(jnp.bfloat16)

    def query_side(pair_index):
        scores = pair_scores(columns(queries, pair_index), columns(keys, pair_index))
        probs = kept_probs(
            scores, allowed, max_pairs[pair_index][..., None], total_pairs[pair_index][..., None]
        )
        grad_part = columns(grad_attended, pair_index)
        grad_probs = jnp.einsum(
            "qhd,khd->hqk",
            split_heads(grad_part),
            split_heads(columns(values, pair_index)),
            preferred_element_type=jnp.float32,
        )
        delta = jnp.sum(probs * grad_probs, -1, keepdims=True)
        grad_scores = (RELAX_SCALE * probs * (grad_probs - delta)).astype(jnp.bfloat16)
        grad_query = (
            jnp.einsum(
                "hqk,khd->qhd",
                grad_scores,
                split_heads(columns(keys, pair_index)),
                preferred_element_type=jnp.float32,
            )
            * factor
        )
        return (grad_query.reshape(row_count, pair_cols), grad_scores, probs, delta)

    def both_sides(pair_index):
        grad_query, grad_scores, probs, delta = query_side(pair_index)
        grad_part = columns(grad_attended, pair_index)
        grad_key = (
            jnp.einsum(
                "hqk,qhd->khd",
                grad_scores,
                split_heads(columns(queries, pair_index)),
                preferred_element_type=jnp.float32,
            )
            * factor
        )
        grad_value = jnp.einsum(
            "hqk,qhd->khd",
            probs.astype(jnp.bfloat16),
            split_heads(grad_part),
            preferred_element_type=jnp.float32,
        )
        return (
            grad_query,
            grad_key.reshape(slot_rows, pair_cols),
            grad_value.reshape(slot_rows, pair_cols),
        )

    query_pairs, key_terms, value_terms = lax.map(both_sides, pair_ids)
    key_pairs, value_pairs = (
        lax.psum_scatter(
            key_terms.astype(jnp.bfloat16), "seq", scatter_dimension=1, tiled=True
        ).astype(jnp.float32),
        lax.psum_scatter(
            value_terms.astype(jnp.bfloat16), "seq", scatter_dimension=1, tiled=True
        ).astype(jnp.float32),
    )
    grad_q_low = merge_pairs(query_pairs).astype(jnp.bfloat16)
    grad_k_low = merge_pairs(key_pairs).astype(jnp.bfloat16)
    grad_v_low = merge_pairs(value_pairs).astype(jnp.bfloat16)
    grad_projected = jnp.concatenate([grad_q_low, grad_k_low, grad_v_low], 1)
    grad_w_qkv = contract_rows(normed_low, grad_projected)
    grad_qv = jnp.stack(
        [jnp.sum(grad_q_low.astype(jnp.float32), 0), jnp.sum(grad_v_low.astype(jnp.float32), 0)]
    )
    grad_hidden_part, grad_gain_one, grad_shift_one = pull_first(
        contract_cols(grad_projected, qkv_back)
    )
    input_grad = (grad_middle + grad_hidden_part).astype(jnp.bfloat16)[None]
    grad_gains = jnp.stack([grad_gain_one, grad_gain_two, grad_gain_three, grad_gain_four])
    grad_shifts = jnp.stack([grad_shift_one, grad_shift_two, grad_shift_three, grad_shift_four])
    owned = (
        lax.psum_scatter(grad_w_qkv, ("seq", "dp"), scatter_dimension=0, tiled=True),
        lax.psum_scatter(grad_w_out, ("seq", "dp"), scatter_dimension=0, tiled=True),
        lax.psum_scatter(grad_w_up, ("seq", "dp"), scatter_dimension=0, tiled=True),
        lax.psum_scatter(grad_w_down, ("seq", "dp"), scatter_dimension=0, tiled=True),
        lax.psum_scatter(grad_qv, ("seq", "dp"), scatter_dimension=1, tiled=True),
        lax.psum_scatter(grad_b_out, ("seq", "dp"), scatter_dimension=0, tiled=True),
        lax.psum_scatter(grad_b_up, ("seq", "dp"), scatter_dimension=0, tiled=True),
        lax.psum_scatter(grad_b_down, ("seq", "dp"), scatter_dimension=0, tiled=True),
        lax.psum_scatter(grad_gains, ("seq", "dp"), scatter_dimension=1, tiled=True),
        lax.psum_scatter(grad_shifts, ("seq", "dp"), scatter_dimension=1, tiled=True),
    )
    return (
        output,
        input_grad,
        owned[0],
        owned[4],
        owned[1],
        owned[5],
        owned[2],
        owned[6],
        owned[3],
        owned[7],
        owned[8],
        owned[9],
    )


MESH = pl.DeviceIdType.MESH


def is_small(mesh):
    return mesh.shape["seq"] == 16 and mesh.shape["dp"] == 2


def place():
    seq = lax.axis_index("seq")
    return seq // 8, (seq // 4) % 2, (seq // 2) % 2, seq % 2, lax.axis_index("dp")


def exchange_copies(scatter, src, out, send_sem, recv_sem, own_sem):
    a, b, y, c, x = place()

    def peer(k):
        return lax.rem(a + k // 2, 2), lax.rem(y + k % 2, 2)

    def device(k):
        pa, py = peer(k)
        return (pa * 8 + b * 4 + py * 2 + c, x)

    def source(k):
        pa, py = peer(k)
        return src.at[pa * 2 + py] if scatter else src.at[pa, :, py]

    def target(k):
        pa, py = peer(k)
        return out.at[pa, :, py] if scatter else out.at[pa * 2 + py]

    def copy(k, dst):
        return pltpu.make_async_remote_copy(
            src_ref=source(k), dst_ref=target(dst), send_sem=send_sem.at[k], recv_sem=recv_sem.at[k],
            device_id=device(k), device_id_type=MESH)

    def greet():
        barrier = pltpu.get_barrier_semaphore()
        for k in range(1, 4):
            pl.semaphore_signal(barrier, inc=1, device_id=device(k), device_id_type=MESH)

    def run():
        own = pltpu.make_async_copy(source(0), target(0), own_sem)
        own.start()
        pl.semaphore_wait(pltpu.get_barrier_semaphore(), 3)
        for k in (3, 2, 1):
            copy(k, 0).start()
        own.wait()
        for k in (3, 2, 1):
            copy(k, k).wait_recv()
        for k in (3, 2, 1):
            copy(k, 0).wait_send()

    return greet, run


def row_block(i, j):
    _, b, _, c, _ = place()
    return pl.ds(pl.multiple_of(lax.rem(b + i, 2) * 256 + lax.rem(c + j, 2) * 128, 128), 128)


def to_heads_kernel(rows_ref, out, src, *sems):
    greet, run = exchange_copies(True, src, out, *sems)
    greet()
    low = src.shape[2] - 128
    for g in range(4):
        values = slice(low * 2 + g * HD, low * 2 + g * HD + HD)
        for i in range(2):
            if low:
                for j in range(2):
                    src[g, i, j * 128:j * 128 + 128] = rows_ref[row_block(i, j), g * 128:g * 128 + 128]
            src[g, i, low:] = jnp.concatenate([rows_ref[row_block(i, j), values] for j in range(2)], 1)
    run()


def from_heads_kernel(heads_ref, out, got, *sems):
    greet, run = exchange_copies(False, heads_ref, got, *sems)
    greet()
    run()
    low = got.shape[2] - 128
    c = place()[3]
    for i in range(2):
        if low:
            for j in range(2):
                for g in range(4):
                    out[row_block(i, j), g * 128:g * 128 + 128] = got[g, i, j * 128:j * 128 + 128]
        for g in (0, 2):
            left, right = got[g, i, low:], got[g + 1, i, low:]
            cols = slice(low * 2 + g * HD, low * 2 + g * HD + 128)
            for j in range(2):
                lanes = slice(j * HD, j * HD + HD)
                out[row_block(i, j), cols] = jnp.concatenate([left[:, lanes], right[:, lanes]], 1)


def exchange(blocks, scatter, cid):
    vm = pl.BlockSpec(memory_space=pltpu.VMEM)
    rows = blocks.shape[-1] // 2 if scatter else blocks.shape[-2]
    shape, held = (2, 2, 2, rows, 128), (4, 2, rows, 128)
    return pl.pallas_call(
        to_heads_kernel if scatter else from_heads_kernel,
        out_shape=jax.ShapeDtypeStruct(shape if scatter else (512, rows * 2), blocks.dtype),
        in_specs=[vm], out_specs=vm,
        scratch_shapes=[pltpu.VMEM(held, blocks.dtype), pltpu.SemaphoreType.DMA((4,)), pltpu.SemaphoreType.DMA((4,)),
                        pltpu.SemaphoreType.DMA],
        compiler_params=pltpu.CompilerParams(collective_id=cid, has_side_effects=True),
        cost_estimate=pl.CostEstimate(flops=0, bytes_accessed=rows * 100000, transcendentals=0),
        name="to_heads" if scatter else "from_heads",
    )(blocks)


def dot_nt(a, b):
    return lax.dot_general(a, b, (((1,), (1,)), ((), ())), preferred_element_type=jnp.float32)


def dot_nn(a, b):
    return jnp.dot(a, b, preferred_element_type=jnp.float32)


BQ = 256
MASKED = -1e30


def load_heads(valid, packed, q_ref, k_ref):
    rows = q_ref.shape[0]
    qk = packed[:, :256].reshape(rows, 128)
    kq = jnp.concatenate([qk[:, 64:], qk[:, :64]], axis=1)
    lane = lax.broadcasted_iota(jnp.int32, (rows, 128), 1)
    spot = lax.broadcasted_iota(jnp.int32, (rows, 128), 0)
    past = jnp.where(spot < valid, 0.0, MASKED)
    q_ref[...] = jnp.where(lane < 64, qk.astype(jnp.float32), jnp.where(lane == 64, 1.0, 0.0)).astype(jnp.bfloat16)
    k_ref[...] = jnp.where(lane < 64, kq.astype(jnp.float32), jnp.where(lane == 64, past, 0.0)).astype(jnp.bfloat16)


def unpack_rows(halves):
    n = halves.shape[0]
    return jnp.concatenate([halves[:, :, :64], halves[:, :, 64:]], axis=1).reshape(n * 256, 64)


def block_probs(q_ref, k_ref, i):
    n = (i + 1) * BQ
    scores = dot_nt(k_ref[:n], q_ref[i * BQ:n])
    key = lax.broadcasted_iota(jnp.int32, (BQ, BQ), 0)
    query = lax.broadcasted_iota(jnp.int32, (BQ, BQ), 1)
    corner = jnp.where(key <= query, scores[n - BQ:], MASKED)
    scores = jnp.concatenate([scores[:n - BQ], corner], axis=0) if i else corner
    top = jnp.max(scores, axis=0, keepdims=True)
    terms = jnp.exp((scores - top) * 0.125)
    return terms, 1.0 / jnp.sum(terms, axis=0, keepdims=True)


def attend_kernel(valid_ref, packed, out_ref, q_ref, k_ref, vt_ref):
    load_heads(valid_ref[0], packed, q_ref, k_ref)
    unit = jnp.where(
        lax.broadcasted_iota(jnp.int32, (64, 64), 0) == lax.broadcasted_iota(jnp.int32, (64, 64), 1), 1.0, 0.0
    ).astype(jnp.bfloat16)
    vt_ref[...] = dot_nt(unit, unpack_rows(packed[:, 256:])).astype(jnp.bfloat16)
    for i in range(q_ref.shape[0] // BQ):
        n = (i + 1) * BQ
        terms, scale = block_probs(q_ref, k_ref, i)
        probs = (terms * scale).astype(jnp.bfloat16)
        mixed = dot_nn(vt_ref[:, :n], probs).T
        out_ref[i] = jnp.concatenate([mixed[:128], mixed[128:]], axis=1).astype(jnp.bfloat16)


def attend_back_kernel(valid_ref, packed, grad, out_ref, q_ref, k_ref, v_ref, g_ref, kt_ref, dk_ref, dv_ref):
    load_heads(valid_ref[0], packed, q_ref, k_ref)
    v_ref[...] = unpack_rows(packed[:, 256:])
    g_ref[...] = unpack_rows(grad[...])
    unit = jnp.where(
        lax.broadcasted_iota(jnp.int32, (64, 128), 0) == lax.broadcasted_iota(jnp.int32, (64, 128), 1), 1.0, 0.0
    ).astype(jnp.bfloat16)
    kt_ref[...] = dot_nt(unit, k_ref[...]).astype(jnp.bfloat16)
    dk_ref[...] = jnp.zeros_like(dk_ref)
    dv_ref[...] = jnp.zeros_like(dv_ref)
    blocks = q_ref.shape[0] // BQ
    for i in range(blocks):
        n = (i + 1) * BQ
        terms, scale = block_probs(q_ref, k_ref, i)
        probs = terms * scale
        grad_probs = dot_nt(v_ref[:n], g_ref[i * BQ:n])
        delta = jnp.sum(probs * grad_probs, axis=0, keepdims=True)
        grad_scores = (probs * (grad_probs - delta)).astype(jnp.bfloat16)
        grad_query = dot_nn(kt_ref[:, :n], grad_scores).T * 0.125
        out_ref[i, :256, :64] = grad_query.astype(jnp.bfloat16)
        dk_ref[:n] += dot_nn(grad_scores, q_ref[i * BQ:n])
        dv_ref[:n] += dot_nn(probs.astype(jnp.bfloat16), g_ref[i * BQ:n])
    for i in range(blocks):
        rows = slice(i * BQ, (i + 1) * BQ)
        out_ref[i, :256, 64:] = (dk_ref[rows, :64] * 0.125).astype(jnp.bfloat16)
        value = dv_ref[rows].astype(jnp.bfloat16)
        out_ref[i, 256:] = jnp.concatenate([value[:128], value[128:]], axis=1)


def attend(valid, packed):
    rows = packed.shape[0] * 256
    vm = pl.BlockSpec(memory_space=pltpu.VMEM)
    return pl.pallas_call(
        attend_kernel,
        out_shape=jax.ShapeDtypeStruct((packed.shape[0], 128, 128), jnp.bfloat16),
        in_specs=[pl.BlockSpec(memory_space=pltpu.SMEM), vm], out_specs=vm,
        scratch_shapes=[pltpu.VMEM((rows, 128), jnp.bfloat16)] * 2 + [pltpu.VMEM((64, rows), jnp.bfloat16)],
        compiler_params=pltpu.CompilerParams(vmem_limit_bytes=48 << 20),
        name="attend",
    )(valid, packed)


def attend_back(valid, packed, grad):
    rows = packed.shape[0] * 256
    vm = pl.BlockSpec(memory_space=pltpu.VMEM)
    return pl.pallas_call(
        attend_back_kernel,
        out_shape=jax.ShapeDtypeStruct(packed.shape, jnp.bfloat16),
        in_specs=[pl.BlockSpec(memory_space=pltpu.SMEM), vm, vm], out_specs=vm,
        scratch_shapes=[pltpu.VMEM((rows, 128), jnp.bfloat16)] * 2 + [pltpu.VMEM((rows, 64), jnp.bfloat16)] * 2
        + [pltpu.VMEM((64, rows), jnp.bfloat16), pltpu.VMEM((rows, 128), jnp.float32), pltpu.VMEM((rows, 64), jnp.float32)],
        compiler_params=pltpu.CompilerParams(vmem_limit_bytes=48 << 20),
        name="attend_back",
    )(valid, packed, grad)


def flip(bits, block):
    return lax.ppermute(block, "seq", [(s, s ^ bits) for s in range(16)])


flip_a, flip_y = (functools.partial(flip, bits) for bits in (8, 2))


def flip_x(block):
    return lax.ppermute(block, "dp", [(0, 1), (1, 0)])


def after(value, *others):
    return lax.optimization_barrier((value,) + others)[0]


def pick(block, index, axis, keepdims=False):
    return lax.dynamic_index_in_dim(block, index, axis, keepdims=keepdims)


def cube_one(flip_one, block):
    return jnp.concatenate([block, flip_one(block)], 0)


def arrange_kernel(spot_ref, kept, received, out):
    def put(block):
        if len(out.shape) == 7:
            for j in range(2):
                for k in range(2):
                    out[0, j, 0, k, 0] = block[0, j, k]
        else:
            out[0, 0, 0] = block[0]

    @pl.when(pl.program_id(0) < 4)
    def _():
        put(kept)

    @pl.when(pl.program_id(0) >= 4)
    def _():
        put(received)


def arrange(spot, y_first, kept, received):
    def coords(i, r):
        second, first = i // 4, (i // 2) % 2
        y, x = (first, second) if y_first else (second, first)
        return lax.rem(r[0] + i % 2, 2), lax.rem(r[1] + y, 2), lax.rem(r[2] + x, 2)

    shape = kept.shape

    def spec(block, low):
        rest = (0,) * (block.ndim - 1)
        return pl.BlockSpec((1,) + block.shape[1:], lambda i, r: (jnp.clip(i - low, 0, 3),) + rest)

    if len(shape) == 5:
        def out_place(i, r):
            a, y, x = coords(i, r)
            return a, 0, y, 0, x, 0, 0
        out_block, out_shape = (1, 2, 1, 2, 1) + shape[3:], (2,) * 5 + shape[3:]
    else:
        def out_place(i, r):
            return coords(i, r) + (0, 0)
        out_block, out_shape = (1, 1, 1) + shape[1:], (2, 2, 2) + shape[1:]
    return pl.pallas_call(
        arrange_kernel,
        out_shape=jax.ShapeDtypeStruct(out_shape, kept.dtype),
        grid_spec=pltpu.PrefetchScalarGridSpec(
            num_scalar_prefetch=1, grid=(8,), in_specs=[spec(kept, 0), spec(received, 4)],
            out_specs=pl.BlockSpec(out_block, out_place)),
        compiler_params=pltpu.CompilerParams(vmem_limit_bytes=32 << 20),
        cost_estimate=pl.CostEstimate(flops=0, bytes_accessed=8 << 20, transcendentals=0),
        name="arrange",
    )(spot, kept, received)


def up_kernel(rows_ref, w_ref, shift_ref, active_ref, slope_ref):
    for r in range(0, rows_ref.shape[0], 128):
        span = slice(r, r + 128)
        t = dot_nn(rows_ref[span], w_ref[...]) + shift_ref[...]
        half = 0.5 + 0.5 * lax.erf(t * math.sqrt(0.5))
        active_ref[span] = (t * half).astype(jnp.bfloat16)
        slope_ref[span] = half + t * jnp.exp(t * t * -0.5) * (1.0 / math.sqrt(2.0 * math.pi))


def up_gelu(rows, w, shift):
    m, k = rows.shape
    n, block = w.shape[1], 256
    return pl.pallas_call(
        up_kernel, grid=(n // block,),
        out_shape=(jax.ShapeDtypeStruct((m, n), jnp.bfloat16), jax.ShapeDtypeStruct((m, n), jnp.float32)),
        in_specs=[pl.BlockSpec((m, k), lambda i: (0, 0)), pl.BlockSpec((k, block), lambda i: (0, i)),
                  pl.BlockSpec((1, block), lambda i: (0, i))],
        out_specs=(pl.BlockSpec((m, block), lambda i: (0, i)),) * 2,
        compiler_params=pltpu.CompilerParams(vmem_limit_bytes=32 << 20),
        cost_estimate=pl.CostEstimate(flops=2 * m * n * k, bytes_accessed=24 << 20, transcendentals=2 * m * n),
        name="up_gelu",
    )(rows, w, shift)


def add_low(mine, other):
    return (mine.astype(jnp.float32) + other.astype(jnp.float32)).astype(jnp.bfloat16)


def fold(terms, flip_one, index, axis):
    return add_low(pick(terms, index, axis, True), flip_one(pick(terms, 1 - index, axis, True)))


def reduce_kernel(q_ref, o_ref, u_ref, part, tokens, grad_middle, vectors, *refs):
    vec_refs, (out_q, ro, out_u, vec, input_grad, got_far, got_near, low_sums, got_sums, row_send, row_recv, rq, gu, r1q, t2q, r2q, t3q, r3q, fq, gq, r1o, t2o, r2o, t3o, r3o,
               run, got, send_sem, recv_sem) = refs[:10], refs[10:]
    a, b, y, c, x = place()
    f32, bf16 = jnp.float32, jnp.bfloat16
    barrier = pltpu.get_barrier_semaphore()

    def at(pa, pb, py, pc, px):
        return (pa * 8 + pb * 4 + py * 2 + pc, px)

    to_x, to_y, to_a = at(a, b, y, c, 1 - x), at(a, b, 1 - y, c, x), at(1 - a, b, y, c, x)
    ranks = [(lax.rem(b + k // 2, 2), lax.rem(c + k % 2, 2)) for k in range(4)]
    to_rank = [at(a, ranks[k][0], y, ranks[k][1], x) for k in range(4)]
    to_b, to_c = to_rank[2], to_rank[1]
    for dev in [to_x, to_y, to_a] + to_rank[1:]:
        pl.semaphore_signal(barrier, inc=1, device_id=dev, device_id_type=MESH)
    for pb in range(2):
        for j in range(4):
            for row, cols in ((0, slice(j * 128, j * 128 + HD)), (1, slice(512 + j * HD, 512 + j * HD + HD))):
                piece = vec_refs[0][:, cols]
                pair = [jnp.where((b == pb) & (c == pc), piece, 0.0) for pc in range(2)]
                h = head_of(j // 2, pb, j % 2, 0) * HD
                run[0, row:row + 1, h:h + 128] = jnp.concatenate(pair, 1)
            for pc in range(2):
                col = head_of(j // 2, pb, j % 2, pc) * 256
                piece = vec_refs[1][:, j * 256:j * 256 + 256]
                run[0, 12 + col // 1024:13 + col // 1024, col % 1024:col % 1024 + 256] = jnp.where(
                    (b == pb) & (c == pc), piece, 0.0)
    for k, row in enumerate((2, 3, 5, 6, 7, 9, 10, 11)):
        run[0, row:row + 1] = vec_refs[2 + k][...]
    for row in (4, 8):
        run[0, row:row + 1] = jnp.zeros((1, 1024), f32)
    pl.semaphore_wait(barrier, 6)

    made = []

    def remote(src, dst, dev):
        k = len(made)
        made.append(pltpu.make_async_remote_copy(
            src_ref=src, dst_ref=dst, send_sem=send_sem.at[k], recv_sem=recv_sem.at[k],
            device_id=dev, device_id_type=MESH))
        return made[-1]

    def low(*values):
        return sum(v.astype(f32) for v in values)

    places = [1 - a, a]
    halves = [slice(0, 512), slice(512, 1024)]
    lateral = [(to_x, to_y), (to_y, to_x)]

    q1, q2, o1, o2 = {}, {}, {}, {}
    for i in range(2):
        for s in range(2):
            p = places[i]
            q1[s, i] = remote(q_ref.at[p, 0, :, :, 1 - x] if s == 0 else q_ref.at[p, 1, 1 - y], r1q.at[s, i], lateral[s][0])
            o1[s, i] = remote(o_ref.at[p, :, 1 - x, :, halves[0]] if s == 0 else o_ref.at[p, 1 - y, :, :, halves[1]],
                              r1o.at[s, i], lateral[s][0])
            q2[s, i] = remote(t2q.at[s, i], r2q.at[s, i], lateral[s][1])
            o2[s, i] = remote(t2o.at[s, i], r2o.at[s, i], lateral[s][1])
    q3 = [remote(t3q.at[s], r3q.at[s], to_a) for s in range(2)]
    o3 = [remote(t3o.at[s], r3o.at[s], to_a) for s in range(2)]
    qr = [remote(fq.at[ranks[k][0], ranks[k][1]], gq.at[k - 1], to_rank[k]) for k in range(1, 4)]
    ur = [remote(u_ref.at[ranks[k][0], ranks[k][1]], gu.at[b, c], to_rank[k]) for k in range(1, 4)]
    vs = [remote(run.at[k], got.at[k], dev) for k, dev in enumerate((to_x, to_y, to_a, to_b, to_c))]

    def next_sum(k):
        vs[k].wait_recv()
        if k < 4:
            run[k + 1] = run[k] + got[k]
            vs[k + 1].start()
        else:
            vec[...] = run[k] + got[k]

    pieces = part.shape[2] // PIECE

    def span(r):
        return pl.ds(pl.multiple_of(r * PIECE, PIECE), PIECE)

    def row_copy(kind, r):
        src, dst, dev = ((part.at[1, 1, span(r)], got_far.at[span(r)], to_c), (part.at[0, 1, span(r)], got_near.at[span(r)], to_c),
                         (low_sums.at[span(r)], got_sums.at[span(r)], to_b))[kind]
        return pltpu.make_async_remote_copy(
            src_ref=src, dst_ref=dst, send_sem=row_send.at[kind, r], recv_sem=row_recv.at[kind, r],
            device_id=dev, device_id_type=MESH)

    def send_across(r, _):
        row_copy(0, r).wait_recv()
        low_sums[span(r)] = (part[1, 0, span(r)] + got_far[span(r)]).astype(bf16)
        row_copy(2, r).start()
        return 0

    def take(r, _):
        row_copy(1, r).wait_recv()
        row_copy(2, r).wait_recv()
        total = part[0, 0, span(r)] + got_near[span(r)] + got_sums[span(r)].astype(f32)
        _, pull = jax.vjp(norm_rows, tokens[span(r)].astype(f32), *norm_vectors(vectors, 0))
        term, grad_gain, grad_shift = pull(total)
        input_grad[span(r)] = (grad_middle[span(r)] + term).astype(bf16)
        run[0, 4:5] += grad_gain
        run[0, 8:9] += grad_shift
        for kind in range(3):
            row_copy(kind, r).wait_send()
        return 0

    for kind in range(2):
        for r in range(pieces):
            row_copy(kind, r).start()
    for s in range(2):
        q1[s, 0].start()
        o1[s, 0].start()
    for k in (3, 2, 1):
        ur[k - 1].start()
    for s in range(2):
        o1[s, 1].start()
    lax.fori_loop(0, pieces, send_across, 0)

    def q_terms(s, i, far):
        p = places[i]
        if s == 0:
            v = 1 - y if far else y
            return q_ref[p, 0, v, :, x], r1q[0, i, v]
        v = 1 - x if far else x
        return q_ref[p, 1, y, :, v], r1q[1, i, :, v]

    def o_terms(s, i, far):
        p = places[i]
        if s == 0:
            v = 1 - y if far else y
            return o_ref[p, v, x, :, halves[0]], r1o[0, i, v]
        v = 1 - x if far else x
        return o_ref[p, y, v, :, halves[1]], r1o[1, i, v]

    for i in range(2):
        for s in range(2):
            q1[s, i].wait_recv()
            t2q[s, i] = low(*q_terms(s, i, True)).astype(bf16)
            q2[s, i].start()
            o1[s, i].wait_recv()
            t2o[s, i] = low(*o_terms(s, i, True)).astype(bf16)
            o2[s, i].start()
        if i == 0:
            for s in range(2):
                q1[s, 1].start()
            lax.fori_loop(0, pieces, take, 0)
            vs[0].start()
            for s in range(2):
                q2[s, 0].wait_recv()
                t3q[s] = low(*q_terms(s, 0, False), r2q[s, 0]).astype(bf16)
                q3[s].start()
                o2[s, 0].wait_recv()
                t3o[s] = low(*o_terms(s, 0, False), r2o[s, 0]).astype(bf16)
                o3[s].start()
    next_sum(0)
    for s in range(2):
        q2[s, 1].wait_recv()
        o2[s, 1].wait_recv()
        q3[s].wait_recv()
        total = low(*q_terms(s, 1, False), r2q[s, 1], r3q[s])
        fq[s] = total.astype(bf16)
        for j in range(2):
            @pl.when((b == s) & (c == j))
            def _():
                rq[s, j] = total[j]
        o3[s].wait_recv()
        ro[:, halves[s]] = low(*o_terms(s, 1, False), r2o[s, 1], r3o[s])
        next_sum(1 + s)
    for k in (3, 2, 1):
        qr[k - 1].start()
    gu[b, c] = u_ref[b, c]
    for k in (1, 2, 3):
        ur[k - 1].wait_recv()
    next_sum(3)
    for k in (1, 2, 3):
        pb, pc = ranks[k]
        qr[k - 1].wait_recv()
        rq[pb, pc] = gq[k - 1].astype(f32)
    for pb in range(2):
        for j in range(4):
            zero, one = rq[pb, 0], rq[pb, 1]
            h = head_of(j // 2, pb, j % 2, 0) * HD
            q, k = slice(j * 128, j * 128 + HD), slice(j * 128 + HD, j * 128 + 128)
            v = slice(512 + j * HD, 512 + j * HD + HD)
            for t, cols in enumerate((q, k, v)):
                out_q[:, t * 1024 + h:t * 1024 + h + 128] = jnp.concatenate([zero[:, cols], one[:, cols]], 1)
            for pc in range(2):
                col = head_of(j // 2, pb, j % 2, pc) * 256
                out_u[:, col:col + 256] = gu[pb, pc, :, j * 256:j * 256 + 256].astype(f32)
    next_sum(4)
    for copy in made:
        copy.wait_send()


def reduce_all(gw_qkv, gw_out, up_sum, part, tokens, grad_middle, params, vectors, cid):
    f32, bf16 = jnp.float32, jnp.bfloat16
    V = pltpu.VMEM
    vm = pl.BlockSpec(memory_space=V)
    S = jax.ShapeDtypeStruct
    q, o, u = gw_qkv.shape[5:], (gw_out.shape[3], 512), up_sum.shape
    rows, n = grad_middle.shape
    scratch = [
        V((rows, n), f32), V((rows, n), f32), V((rows, n), bf16), V((rows, n), bf16),
        pltpu.SemaphoreType.DMA((3, rows // PIECE)), pltpu.SemaphoreType.DMA((3, rows // PIECE)),
        V((2, 2) + q, f32), V(u, bf16),
        V((2, 2, 2, 2) + q, bf16), V((2, 2, 2) + q, bf16), V((2, 2, 2) + q, bf16), V((2, 2) + q, bf16), V((2, 2) + q, bf16),
        V((2, 2) + q, bf16), V((3,) + q, bf16),
        V((2, 2, 2) + o, bf16), V((2, 2) + o, bf16), V((2, 2) + o, bf16), V((2,) + o, bf16), V((2,) + o, bf16),
        V((5, 16, 1024), f32), V((5, 16, 1024), f32),
        pltpu.SemaphoreType.DMA((32,)), pltpu.SemaphoreType.DMA((32,))]
    return pl.pallas_call(
        reduce_kernel,
        out_shape=(S((q[0], 4 * q[1]), f32), S((o[0], 1024), f32), S((u[2], 4 * u[3]), f32), S((16, 1024), f32), S((rows, n), bf16)),
        in_specs=[vm] * 17, out_specs=(vm,) * 5, scratch_shapes=scratch,
        compiler_params=pltpu.CompilerParams(collective_id=cid, has_side_effects=True, vmem_limit_bytes=48 << 20),
        name="reduce_all",
    )(gw_qkv, gw_out, up_sum, part.reshape(2, 2, rows, n), tokens, grad_middle, params, *vectors)


def qk_columns(head):
    return slice(head * HD, head * HD + HD), slice(1024 + head * HD, 1024 + head * HD + HD), slice(2048 + head * HD, 2048 + head * HD + HD)


def head_of(a, b, y, c):
    return a * 8 + b * 4 + y * 2 + c


def start_kernel(q_hbm, u_hbm, o_in, t_in, v_in, wq, wo, up, rows, vec, q_in, u_in, q_src, u_src, send_sem, recv_sem, own_sem):
    a, b, y, c, x = place()
    barrier = pltpu.get_barrier_semaphore()

    def at(pa, pb, py, pc, px):
        return (pa * 8 + pb * 4 + py * 2 + pc, px)

    to_x, to_y, to_a = at(a, b, y, c, 1 - x), at(a, b, 1 - y, c, x), at(1 - a, b, y, c, x)
    ranks = [(lax.rem(b + k // 2, 2), lax.rem(c + k % 2, 2)) for k in range(4)]
    to_rank = [at(a, pb, y, pc, x) for pb, pc in ranks]
    for dev in [to_x, to_y, to_a] + to_rank[1:]:
        pl.semaphore_signal(barrier, inc=1, device_id=dev, device_id_type=MESH)

    loads = [pltpu.make_async_copy(q_hbm, q_in, own_sem.at[5]), pltpu.make_async_copy(u_hbm, u_in, own_sem.at[6])]
    for copy in loads:
        copy.start()
    for copy in loads:
        copy.wait()

    for pb in range(2):
        for pc in range(2):
            for j in range(4):
                q, k, v = qk_columns(head_of(j // 2, pb, j % 2, pc))
                q_src[pb, pc, :, j * 128:j * 128 + 128] = jnp.concatenate([q_in[:, q], q_in[:, k]], 1)
            for j in range(2):
                v0 = qk_columns(head_of(j, pb, 0, pc))[2]
                v1 = qk_columns(head_of(j, pb, 1, pc))[2]
                q_src[pb, pc, :, 512 + j * 128:640 + j * 128] = jnp.concatenate([q_in[:, v0], q_in[:, v1]], 1)
            for j in range(4):
                col = (head_of(j // 2, pb, j % 2, pc)) * 256
                u_src[pb, pc, :, j * 256:j * 256 + 256] = u_in[:, col:col + 256]
    own = [pltpu.make_async_copy(src, dst, own_sem.at[k]) for k, (src, dst) in enumerate((
        (q_src.at[b, c], wq.at[a, b, y, c, x]), (u_src.at[b, c], up.at[0, b, c]), (o_in, wo.at[a, y, x]),
        (t_in, rows.at[0]), (v_in, vec.at[a, b, y, c, x])))]
    for copy in own:
        copy.start()
    pl.semaphore_wait(barrier, 6)

    made = []

    def remote(src, dst, dev):
        k = len(made)
        made.append(pltpu.make_async_remote_copy(
            src_ref=src, dst_ref=dst, send_sem=send_sem.at[k], recv_sem=recv_sem.at[k],
            device_id=dev, device_id_type=MESH))
        return made[-1]

    places = [a, 1 - a]
    halves = [slice(0, 512), slice(512, 1024)]
    lateral = [(to_y, to_x), (to_x, to_y)]

    def same(ref, dev):
        return remote(ref, ref, dev)

    q_rank = [remote(q_src.at[ranks[k][0], ranks[k][1]], wq.at[a, b, y, c, x], to_rank[k]) for k in range(1, 4)]
    u_rank = [remote(u_src.at[ranks[k][0], ranks[k][1]], up.at[0, b, c], to_rank[k]) for k in range(1, 4)]
    v_rank = [remote(v_in, vec.at[a, b, y, c, x], to_rank[k]) for k in range(1, 4)]
    t_core, t_near = remote(t_in, rows.at[1], to_rank[1]), remote(t_in, rows.at[2], to_rank[2])
    t_far = remote(rows.at[2], rows.at[3], to_rank[1])
    u_cube = remote(up.at[0], up.at[1], to_a)
    v_cube = [same(vec.at[a, :, y, :, x], to_a), same(vec.at[:, :, y, :, x], to_y), same(vec.at[:, :, :, :, x], to_x)]
    q_cube = [same(wq.at[a, s, y, :, x], to_a) for s in range(2)]
    o_cube = [remote(o_in.at[:, halves[s]], wo.at[a, y, x, :, halves[s]], to_a) for s in range(2)]
    q_side, o_side = {}, {}
    for i in range(2):
        for s in range(2):
            one, two = lateral[s]
            oy, ox = (1 - y, x) if s == 0 else (y, 1 - x)
            p = places[i]
            mine, theirs = wq.at[p, s, y, :, x], wq.at[p, s, oy, :, ox]
            q_side[s, i] = (same(mine, one), same(mine, two), same(theirs, two))
            mine, theirs = wo.at[p, y, x, :, halves[s]], wo.at[p, oy, ox, :, halves[s]]
            first = o_in.at[:, halves[s]] if i == 0 else mine
            o_side[s, i] = (remote(first, mine, one), remote(first, mine, two), same(theirs, two))

    for k in (2, 1, 0):
        q_rank[k].start()
        v_rank[k].start()
    for s in range(2):
        o_cube[s].start()
        o_side[s, 0][0].start()
        o_side[s, 0][1].start()
    t_near.start()
    t_core.start()
    own[0].wait()
    for copy in q_rank:
        copy.wait_recv()
    for s in range(2):
        q_cube[s].start()
        q_side[s, 0][0].start()
        q_side[s, 0][1].start()
    own[4].wait()
    for copy in v_rank:
        copy.wait_recv()
    v_cube[0].start()
    for k in (2, 1, 0):
        u_rank[k].start()
    for s in range(2):
        o_side[s, 0][0].wait_recv()
        o_side[s, 0][2].start()
    for s in range(2):
        o_cube[s].wait_recv()
        o_side[s, 1][0].start()
        o_side[s, 1][1].start()
    t_near.wait_recv()
    t_far.start()
    for s in range(2):
        q_side[s, 0][0].wait_recv()
        q_side[s, 0][2].start()
    for s in range(2):
        q_cube[s].wait_recv()
        q_side[s, 1][0].start()
        q_side[s, 1][1].start()
    v_cube[0].wait_recv()
    v_cube[1].start()
    own[1].wait()
    for copy in u_rank:
        copy.wait_recv()
    u_cube.start()
    for s in range(2):
        o_side[s, 1][0].wait_recv()
        o_side[s, 1][2].start()
    v_cube[1].wait_recv()
    v_cube[2].start()
    for s in range(2):
        q_side[s, 1][0].wait_recv()
        q_side[s, 1][2].start()
    v_cube[2].wait_recv()
    t_core.wait_recv()
    t_far.wait_recv()
    for i in range(2):
        for s in range(2):
            for k in (1, 2):
                q_side[s, i][k].wait_recv()
                o_side[s, i][k].wait_recv()
    u_cube.wait_recv()
    for k in (2, 3):
        own[k].wait()
    for copy in made:
        copy.wait_send()


def start_gather(w_qkv, w_up, w_out, tokens, vectors, cid):
    bf16 = jnp.bfloat16
    S = lambda *shape: jax.ShapeDtypeStruct(shape, bf16)
    vm, anywhere = pl.BlockSpec(memory_space=pltpu.VMEM), pl.BlockSpec(memory_space=pl.ANY)
    return pl.pallas_call(
        start_kernel,
        out_shape=(S(2, 2, 2, 2, 2, 32, 768), S(2, 2, 2, 32, 1024), S(2, 2, 2, 32, 1024), S(4, 128, 1024),
                   S(2, 2, 2, 2, 2, 16, 128)),
        in_specs=[pl.BlockSpec(memory_space=pltpu.HBM)] * 4 + [vm], out_specs=(anywhere,) * 5,
        scratch_shapes=[
            pltpu.VMEM(w_qkv.shape, bf16), pltpu.VMEM(w_up.shape, bf16),
            pltpu.VMEM((2, 2, 32, 768), bf16), pltpu.VMEM((2, 2, 32, 1024), bf16),
            pltpu.SemaphoreType.DMA((48,)), pltpu.SemaphoreType.DMA((48,)), pltpu.SemaphoreType.DMA((7,))],
        compiler_params=pltpu.CompilerParams(collective_id=cid, has_side_effects=True, vmem_limit_bytes=63 << 20),
        cost_estimate=pl.CostEstimate(flops=0, bytes_accessed=100 << 20, transcendentals=0),
        name="start_gather",
    )(w_qkv, w_up, w_out, tokens, vectors)


PIECE = 32


def rows_kernel(step, gather, count_in, count_out, part, *refs):
    ins, outs = refs[:count_in], refs[count_in:count_in + count_out]
    rest = refs[count_in + count_out:]
    rows = rest[0] if gather else None
    got_far, got_near, sums, got_sums, send_sem, recv_sem = rest[-6:]
    a, b, y, c, x = place()

    def at(pb, pc):
        return (a * 8 + pb * 4 + y * 2 + pc, x)

    to_b, to_core = at(1 - b, c), at(b, 1 - c)
    barrier = pltpu.get_barrier_semaphore()
    for dev in (to_b, to_core):
        pl.semaphore_signal(barrier, inc=1, device_id=dev, device_id_type=MESH)
    pl.semaphore_wait(barrier, 2)
    pieces = part.shape[2] // PIECE

    def span(r):
        return pl.ds(pl.multiple_of(r * PIECE, PIECE), PIECE)

    def remote(kind, r, src, dst, dev):
        return pltpu.make_async_remote_copy(
            src_ref=src, dst_ref=dst, send_sem=send_sem.at[kind, r], recv_sem=recv_sem.at[kind, r],
            device_id=dev, device_id_type=MESH)

    def far(r):
        return remote(0, r, part.at[1, 1, span(r)], got_far.at[span(r)], to_core)

    def near(r):
        return remote(1, r, part.at[0, 1, span(r)], got_near.at[span(r)], to_core)

    def across(r):
        return remote(2, r, sums.at[span(r)], got_sums.at[span(r)], to_b)

    def row_near(r):
        return remote(3, r, rows.at[0, span(r)], rows.at[2, span(r)], to_b)

    def row_core(r):
        return remote(4, r, rows.at[0, span(r)], rows.at[1, span(r)], to_core)

    def row_far(r):
        return remote(5, r, rows.at[2, span(r)], rows.at[3, span(r)], to_core)

    for r in range(pieces):
        far(r).start()
    for r in range(pieces):
        near(r).start()

    def send_across(r, _):
        far(r).wait_recv()
        sums[span(r)] = (part[1, 0, span(r)] + got_far[span(r)]).astype(jnp.bfloat16)
        across(r).start()
        return 0

    lax.fori_loop(0, pieces, send_across, 0)
    for ref in outs:
        if ref.shape[0] == 1:
            ref[...] = jnp.zeros_like(ref)

    def take(r, _):
        near(r).wait_recv()
        across(r).wait_recv()
        total = part[0, 0, span(r)] + got_near[span(r)] + got_sums[span(r)].astype(jnp.float32)
        piece = step(span(r), total, ins, outs)
        if gather:
            rows[0, span(r)] = piece
            row_near(r).start()
            row_core(r).start()
        return 0

    lax.fori_loop(0, pieces, take, 0)

    def relay(r, _):
        row_near(r).wait_recv()
        row_far(r).start()
        return 0

    def finish(r, _):
        if gather:
            row_core(r).wait_recv()
            row_far(r).wait_recv()
            row_near(r).wait_send()
            row_core(r).wait_send()
            row_far(r).wait_send()
        far(r).wait_send()
        near(r).wait_send()
        across(r).wait_send()
        return 0

    if gather:
        lax.fori_loop(0, pieces, relay, 0)
    lax.fori_loop(0, pieces, finish, 0)


def sum_rows(step, part, ins, outs, gather, cid):
    rows, n = part.shape[0] // 4, part.shape[1]
    vm = pl.BlockSpec(memory_space=pltpu.VMEM)
    shapes = tuple(outs) + ((jax.ShapeDtypeStruct((4, rows, n), jnp.bfloat16),) if gather else ())
    V = pltpu.VMEM
    return pl.pallas_call(
        functools.partial(rows_kernel, step, gather, len(ins), len(outs)),
        out_shape=shapes, in_specs=[vm] * (1 + len(ins)), out_specs=(vm,) * len(shapes),
        scratch_shapes=[V((rows, n), jnp.float32), V((rows, n), jnp.float32), V((rows, n), jnp.bfloat16), V((rows, n), jnp.bfloat16),
                        pltpu.SemaphoreType.DMA((6, rows // PIECE)), pltpu.SemaphoreType.DMA((6, rows // PIECE))],
        compiler_params=pltpu.CompilerParams(collective_id=cid, has_side_effects=True, vmem_limit_bytes=32 << 20),
        cost_estimate=pl.CostEstimate(flops=0, bytes_accessed=50 << 20, transcendentals=0),
        name="sum_rows",
    )(part.reshape(2, 2, rows, n), *ins)


def norm_vectors(vectors, k):
    return vectors[4 + k:5 + k], vectors[8 + k:9 + k]


def attended_step(span, total, ins, outs):
    tokens, vectors = ins
    branch = total + vectors[2:3]
    middle = tokens[span].astype(jnp.float32) + norm_rows(branch, *norm_vectors(vectors, 1))
    outs[0][span] = branch
    outs[1][span] = middle
    return norm_rows(middle, *norm_vectors(vectors, 2)).astype(jnp.bfloat16)


def output_step(span, total, ins, outs):
    middle, grad_out, vectors = ins
    normed, pull = jax.vjp(norm_rows, total + vectors[3:4], *norm_vectors(vectors, 3))
    outs[0][span] = (middle[span] + normed).astype(jnp.bfloat16)
    grad_down, grad_gain, grad_shift = pull(grad_out[span])
    grad_down = grad_down.astype(jnp.bfloat16)
    outs[1][...] += grad_gain
    outs[2][...] += grad_shift
    outs[3][...] += jnp.sum(grad_down.astype(jnp.float32), 0, keepdims=True)
    return grad_down


def middle_step(span, total, ins, outs):
    middle, branch, grad_out, vectors = ins
    _, pull = jax.vjp(norm_rows, middle[span], *norm_vectors(vectors, 2))
    part, grad_gain2, grad_shift2 = pull(total)
    grad_middle = grad_out[span] + part
    _, pull = jax.vjp(norm_rows, branch[span], *norm_vectors(vectors, 1))
    grad_branch, grad_gain1, grad_shift1 = pull(grad_middle)
    grad_branch = grad_branch.astype(jnp.bfloat16)
    outs[0][span] = grad_middle
    for ref, value in zip(outs[1:], (grad_gain2, grad_shift2, grad_gain1, grad_shift1,
                                     jnp.sum(grad_branch.astype(jnp.float32), 0, keepdims=True))):
        ref[...] += value
    return grad_branch


def fast_body(tokens, cotangent, lengths, assign, w_qkv, qv_bias, w_out, out_bias, w_up, up_bias, w_down, down_bias,
              norm_gain, norm_shift):
    bf16, f32 = jnp.bfloat16, jnp.float32
    a, b, y, c, x = place()
    spot = jnp.stack([a, y, x]).astype(jnp.int32)
    width = tokens.shape[2]
    place_two = jnp.arange(2, dtype=jnp.int32)
    sequence = jnp.sum(jnp.where(place_two == x, assign.astype(jnp.int32), 0))
    valid = jnp.sum(jnp.where(place_two == sequence, lengths.astype(jnp.int32), 0))

    small, row = jnp.zeros((16, 128), bf16), 0
    for block in (qv_bias, out_bias[None], down_bias[None], norm_gain, norm_shift, up_bias[None]):
        small += jnp.pad(block, ((row, 16 - row - block.shape[0]), (0, 128 - block.shape[1])))
        row += block.shape[0]
    wqkv, wo, up_one, rows, small = start_gather(w_qkv, w_up, w_out, tokens[0], small, 6)
    down_one = after(w_down, wqkv)
    down_one = jnp.stack([down_one, flip_a(down_one)])
    wqkv, wo, rows = wqkv.reshape(width, 768), wo.reshape(256, width), rows.reshape(512, width)

    vectors = small[..., :12, :32].reshape(32, 12, 32).transpose(1, 0, 2).reshape(12, width).astype(f32)
    qv_half = pick(pick(vectors[:2].reshape(2, 2, 2, 2, 2, HD), b, 2), c, 3).reshape(2, 4, HD)
    qk_shift = jnp.concatenate([qv_half[0], jnp.zeros((4, HD), f32)], 1).reshape(512)
    v_shift = qv_half[1].reshape(256)
    up_shift = pick(pick(small[..., 12, :], b, 1), c, 2).reshape(1024).astype(f32)

    first = norm_rows(rows.astype(f32), vectors[4:5], vectors[8:9]).astype(bf16)
    up_two = cube_one(flip_x, up_one)
    projected = (dot_nn(first, wqkv) + jnp.concatenate([qk_shift, v_shift])).astype(bf16)
    packed = exchange(after(projected, up_two, down_one), True, 1).reshape(8, 384, 128)
    down_two = cube_one(flip_y, after(down_one, packed))
    attended = attend(valid[None], packed).reshape(2, 2, 2, 128, 128)
    attended = exchange(after(attended, down_two), False, 2)
    up_far, down_far = flip_y(after(up_two, attended)), flip_x(after(down_two, attended))
    own_spot = lax.axis_index("seq") * 128 + jnp.arange(128, dtype=jnp.int32)
    grad_out = cotangent[0].astype(f32) * (own_spot < valid).astype(f32)[:, None]
    S = jax.ShapeDtypeStruct
    wide, low, line = S((128, width), f32), S((128, width), bf16), S((1, width), f32)
    branch, middle, third = sum_rows(
        attended_step, dot_nn(attended, wo), (tokens[0], vectors),
        (wide, wide), True, 7)
    third = third.reshape(512, width)
    wu = arrange(spot, False, up_two, up_far).reshape(width, 1024)
    active, slope = up_gelu(third, wu, up_shift.reshape(1, 1024))
    wd = arrange(spot, True, down_two, after(down_far, active)).reshape(1024, width)
    output, gain4, shift4, bias_down, down_rows = sum_rows(
        output_step, dot_nn(active, wd), (middle, grad_out, vectors), (low, line, line, line), True, 8)
    down_rows = down_rows.reshape(512, width)
    gw_down = contract_rows(active, down_rows).astype(bf16).reshape(2, 2, 2, 128, width)
    down_term = flip_y(pick(gw_down, 1 - y, 1, True))
    grad_up = (dot_nt(after(down_rows, gw_down), wd) * slope).astype(bf16)
    gw_up = contract_rows(third, grad_up).astype(bf16).reshape(2, 2, 2, 2, 2, 32, 1024)
    up_term = flip_x(pick(gw_up, 1 - x, 4, True))
    grad_middle, gain3, shift3, gain2, shift2, bias_out, branch_rows = sum_rows(
        middle_step, after(dot_nt(grad_up, wu), gw_up),
        (middle, branch, grad_out, vectors), (wide,) + (line,) * 5, True, 9)
    branch_rows = branch_rows.reshape(512, width)
    grad_att = dot_nt(branch_rows, wo).astype(bf16)
    down_sum = add_low(pick(gw_down, y, 1, True), down_term)
    down_term = flip_x(pick(down_sum, 1 - x, 2, True))
    grad_packed = exchange(after(grad_att, down_sum), True, 3).reshape(8, 128, 128)
    up_sum = add_low(pick(gw_up, x, 4, True), after(up_term, grad_packed))
    up_term = flip_y(pick(up_sum, 1 - y, 2, True))
    down_sum = add_low(pick(down_sum, x, 2, True), after(down_term, grad_packed))
    down_term = flip_a(pick(down_sum, 1 - a, 0))
    back = attend_back(valid[None], packed, grad_packed)

    up_sum = add_low(pick(up_sum, y, 2, True), up_term)
    gw_out = contract_rows(attended, branch_rows).astype(bf16).reshape(2, 2, 2, 32, width)
    grad_qkv = exchange(after(back, up_sum, down_term).reshape(2, 2, 2, 384, 128), False, 4)
    up_term = flip_a(pick(after(up_sum, grad_qkv), 1 - a, 0))
    gw_qkv = contract_rows(first, grad_qkv).astype(bf16).reshape(2, 2, 2, 2, 2, 32, 768)
    def sums(block):
        return jnp.sum(block.astype(f32), 0, keepdims=True)

    sums_of = [sums(grad_qkv), sums(grad_up), bias_out, bias_down, gain2, gain3, gain4, shift2, shift3, shift4]
    up_sum = (pick(up_sum, a, 0).astype(f32) + up_term.astype(f32)).astype(bf16).reshape(2, 2, 32, 1024)
    r_qkv, r_out, r_up, vectors, input_grad = reduce_all(
        gw_qkv, gw_out, up_sum, dot_nt(grad_qkv, wqkv), tokens[0], grad_middle, vectors, sums_of, 5)
    r_down = (pick(down_sum, a, 0).astype(f32) + down_term.astype(f32)).reshape(128, width)
    index = lax.axis_index("seq") * 2 + x
    small_up = lax.dynamic_slice(vectors, (12 + index // 8, index % 8 * 128), (1, 128)).reshape(128)
    vectors = lax.dynamic_slice(vectors, (0, index * 32), (12, 32))

    return (
        output[None], input_grad[None], r_qkv, vectors[:2], r_out,
        vectors[2], r_up, small_up, r_down, vectors[3], vectors[4:8], vectors[8:12])


def solution(mesh):
    return jax.shard_map(
        fast_body if is_small(mesh) else body,
        mesh=mesh,
        in_specs=(
            P("dp", "seq", None),
            P("dp", "seq", None),
            P(),
            P(),
            P(("seq", "dp"), None),
            P(None, ("seq", "dp")),
            P(("seq", "dp"), None),
            P(("seq", "dp")),
            P(("seq", "dp"), None),
            P(("seq", "dp")),
            P(("seq", "dp"), None),
            P(("seq", "dp")),
            P(None, ("seq", "dp")),
            P(None, ("seq", "dp")),
        ),
        out_specs=(
            P("dp", "seq", None),
            P("dp", "seq", None),
            P(("seq", "dp"), None),
            P(None, ("seq", "dp")),
            P(("seq", "dp"), None),
            P(("seq", "dp")),
            P(("seq", "dp"), None),
            P(("seq", "dp")),
            P(("seq", "dp"), None),
            P(("seq", "dp")),
            P(None, ("seq", "dp")),
            P(None, ("seq", "dp")),
        ),
        check_vma=False,
    )
```

```python
import functools
import math

import jax
import jax.numpy as jnp
from jax import lax
from jax.experimental import pallas as pl
from jax.experimental.pallas import tpu as pltpu
from jax.sharding import PartitionSpec as P


HD = 64


RELAX_SCALE = 32.0
NORM_EPSILON = 1e-05


def norm_rows(values, gain, shift):
    center = values - jnp.mean(values, -1, keepdims=True)
    spread = jnp.mean(center * center, -1, keepdims=True)
    return center * lax.rsqrt(spread + NORM_EPSILON) * gain + shift


def exact_gelu(values):
    return jax.nn.gelu(values, approximate=False)


def contract_rows(left, right):
    return lax.dot_general(
        left, right, (((0,), (0,)), ((), ())), preferred_element_type=jnp.float32
    )


def contract_cols(left, right):
    return lax.dot_general(
        left, right, (((1,), (1,)), ((), ())), preferred_element_type=jnp.float32
    )


def split_heads(block):
    return block.reshape(block.shape[0], 2, HD)


def pair_scores(query_part, key_part):
    factor = 1.0 / (RELAX_SCALE * math.sqrt(HD))
    return (
        jnp.einsum(
            "qhd,khd->hqk",
            split_heads(query_part),
            split_heads(key_part),
            preferred_element_type=jnp.float32,
        )
        * factor
    )


def kept_probs(scores, allowed, row_max, row_total):
    exp_terms = jnp.exp(jnp.where(allowed, RELAX_SCALE * (scores - row_max), -jnp.inf))
    return exp_terms / row_total


def body(
    tokens,
    cotangent,
    lengths,
    assign,
    w_qkv,
    qv_bias,
    w_out,
    out_bias,
    w_up,
    up_bias,
    w_down,
    down_bias,
    norm_gain,
    norm_shift,
):
    gathered = (
        lax.all_gather(w_qkv, ("seq", "dp"), axis=0, tiled=True),
        lax.all_gather(w_out, ("seq", "dp"), axis=0, tiled=True),
        lax.all_gather(w_up, ("seq", "dp"), axis=0, tiled=True),
        lax.all_gather(w_down, ("seq", "dp"), axis=0, tiled=True),
        lax.all_gather(qv_bias, ("seq", "dp"), axis=1, tiled=True),
        lax.all_gather(out_bias, ("seq", "dp"), axis=0, tiled=True),
        lax.all_gather(up_bias, ("seq", "dp"), axis=0, tiled=True),
        lax.all_gather(down_bias, ("seq", "dp"), axis=0, tiled=True),
        lax.all_gather(norm_gain, ("seq", "dp"), axis=1, tiled=True),
        lax.all_gather(norm_shift, ("seq", "dp"), axis=1, tiled=True),
    )
    qkv_full, out_full, up_full, down_full = (gathered[0], gathered[1], gathered[2], gathered[3])
    qv_shift = gathered[4].astype(jnp.float32)
    out_shift = gathered[5].astype(jnp.float32)
    up_shift = gathered[6].astype(jnp.float32)
    down_shift = gathered[7].astype(jnp.float32)
    gains = gathered[8].astype(jnp.float32)
    shifts = gathered[9].astype(jnp.float32)
    row_count = tokens.shape[1]
    model_width = tokens.shape[2]
    pair_cols = 2 * HD
    pair_count = model_width // pair_cols
    slot_rows = row_count * lax.axis_size("seq")
    factor = 1.0 / (RELAX_SCALE * math.sqrt(HD))
    valid = lengths[assign[lax.axis_index("dp")]]
    own_place = lax.axis_index("seq") * row_count + jnp.arange(row_count, dtype=jnp.int32)
    all_place = jnp.arange(slot_rows, dtype=jnp.int32)
    allowed = (all_place[None, :] <= own_place[:, None]) & (all_place[None, :] < valid)
    pair_ids = jnp.arange(pair_count, dtype=jnp.int32)
    hidden = tokens[0].astype(jnp.float32)
    normed_first, pull_first = jax.vjp(norm_rows, hidden, gains[0], shifts[0])
    normed_low = normed_first.astype(jnp.bfloat16)
    projected = jnp.dot(normed_low, qkv_full, preferred_element_type=jnp.float32)
    queries = (projected[:, :model_width] + qv_shift[0]).astype(jnp.bfloat16)
    key_own = projected[:, model_width : 2 * model_width].astype(jnp.bfloat16)
    value_own = (projected[:, 2 * model_width :] + qv_shift[1]).astype(jnp.bfloat16)
    keys, values = (
        lax.all_gather(key_own, "seq", axis=0, tiled=True),
        lax.all_gather(value_own, "seq", axis=0, tiled=True),
    )

    def columns(block, pair_index):
        return lax.dynamic_slice_in_dim(block, pair_index * pair_cols, pair_cols, 1)

    def merge_pairs(stack):
        return stack.transpose(1, 0, 2).reshape(stack.shape[1], model_width)

    def attend(pair_index):
        scores = pair_scores(columns(queries, pair_index), columns(keys, pair_index))
        row_max = jnp.max(jnp.where(allowed, scores, -jnp.inf), -1, keepdims=True)
        exp_terms = jnp.exp(jnp.where(allowed, RELAX_SCALE * (scores - row_max), -jnp.inf))
        row_total = jnp.sum(exp_terms, -1, keepdims=True)
        probs = (exp_terms / row_total).astype(jnp.bfloat16)
        mixed = jnp.einsum(
            "hqk,khd->qhd",
            probs,
            split_heads(columns(values, pair_index)),
            preferred_element_type=jnp.float32,
        )
        return (mixed.reshape(row_count, pair_cols), row_max[..., 0], row_total[..., 0])

    mixed_pairs, max_pairs, total_pairs = lax.map(attend, pair_ids)
    attended = merge_pairs(mixed_pairs).astype(jnp.bfloat16)
    branch = jnp.dot(attended, out_full, preferred_element_type=jnp.float32) + out_shift
    normed_second, pull_second = jax.vjp(norm_rows, branch, gains[1], shifts[1])
    middle = hidden + normed_second
    normed_third, pull_third = jax.vjp(norm_rows, middle, gains[2], shifts[2])
    third_low = normed_third.astype(jnp.bfloat16)
    up_pre = jnp.dot(third_low, up_full, preferred_element_type=jnp.float32) + up_shift
    activated, pull_gelu = jax.vjp(exact_gelu, up_pre)
    active_low = activated.astype(jnp.bfloat16)
    down_pre = jnp.dot(active_low, down_full, preferred_element_type=jnp.float32) + down_shift
    normed_fourth, pull_fourth = jax.vjp(norm_rows, down_pre, gains[3], shifts[3])
    output = (middle + normed_fourth).astype(jnp.bfloat16)[None]
    again = (
        lax.all_gather(w_qkv, ("seq", "dp"), axis=0, tiled=True),
        lax.all_gather(w_out, ("seq", "dp"), axis=0, tiled=True),
        lax.all_gather(w_up, ("seq", "dp"), axis=0, tiled=True),
        lax.all_gather(w_down, ("seq", "dp"), axis=0, tiled=True),
    )
    qkv_back, out_back, up_back, down_back = (again[0], again[1], again[2], again[3])
    keep_rows = (own_place < valid).astype(jnp.float32)[:, None]
    grad_out = cotangent[0].astype(jnp.float32) * keep_rows
    grad_down, grad_gain_four, grad_shift_four = pull_fourth(grad_out)
    grad_down_low = grad_down.astype(jnp.bfloat16)
    grad_w_down = contract_rows(active_low, grad_down_low)
    grad_b_down = jnp.sum(grad_down_low.astype(jnp.float32), 0)
    (grad_up,) = pull_gelu(contract_cols(grad_down_low, down_back))
    grad_up_low = grad_up.astype(jnp.bfloat16)
    grad_w_up = contract_rows(third_low, grad_up_low)
    grad_b_up = jnp.sum(grad_up_low.astype(jnp.float32), 0)
    grad_middle_part, grad_gain_three, grad_shift_three = pull_third(
        contract_cols(grad_up_low, up_back)
    )
    grad_middle = grad_out + grad_middle_part
    grad_branch, grad_gain_two, grad_shift_two = pull_second(grad_middle)
    grad_branch_low = grad_branch.astype(jnp.bfloat16)
    grad_w_out = contract_rows(attended, grad_branch_low)
    grad_b_out = jnp.sum(grad_branch_low.astype(jnp.float32), 0)
    grad_attended = contract_cols(grad_branch_low, out_back).astype(jnp.bfloat16)

    def query_side(pair_index):
        scores = pair_scores(columns(queries, pair_index), columns(keys, pair_index))
        probs = kept_probs(
            scores, allowed, max_pairs[pair_index][..., None], total_pairs[pair_index][..., None]
        )
        grad_part = columns(grad_attended, pair_index)
        grad_probs = jnp.einsum(
            "qhd,khd->hqk",
            split_heads(grad_part),
            split_heads(columns(values, pair_index)),
            preferred_element_type=jnp.float32,
        )
        delta = jnp.sum(probs * grad_probs, -1, keepdims=True)
        grad_scores = (RELAX_SCALE * probs * (grad_probs - delta)).astype(jnp.bfloat16)
        grad_query = (
            jnp.einsum(
                "hqk,khd->qhd",
                grad_scores,
                split_heads(columns(keys, pair_index)),
                preferred_element_type=jnp.float32,
            )
            * factor
        )
        return (grad_query.reshape(row_count, pair_cols), grad_scores, probs, delta)

    def both_sides(pair_index):
        grad_query, grad_scores, probs, delta = query_side(pair_index)
        grad_part = columns(grad_attended, pair_index)
        grad_key = (
            jnp.einsum(
                "hqk,qhd->khd",
                grad_scores,
                split_heads(columns(queries, pair_index)),
                preferred_element_type=jnp.float32,
            )
            * factor
        )
        grad_value = jnp.einsum(
            "hqk,qhd->khd",
            probs.astype(jnp.bfloat16),
            split_heads(grad_part),
            preferred_element_type=jnp.float32,
        )
        return (
            grad_query,
            grad_key.reshape(slot_rows, pair_cols),
            grad_value.reshape(slot_rows, pair_cols),
        )

    query_pairs, key_terms, value_terms = lax.map(both_sides, pair_ids)
    key_pairs, value_pairs = (
        lax.psum_scatter(
            key_terms.astype(jnp.bfloat16), "seq", scatter_dimension=1, tiled=True
        ).astype(jnp.float32),
        lax.psum_scatter(
            value_terms.astype(jnp.bfloat16), "seq", scatter_dimension=1, tiled=True
        ).astype(jnp.float32),
    )
    grad_q_low = merge_pairs(query_pairs).astype(jnp.bfloat16)
    grad_k_low = merge_pairs(key_pairs).astype(jnp.bfloat16)
    grad_v_low = merge_pairs(value_pairs).astype(jnp.bfloat16)
    grad_projected = jnp.concatenate([grad_q_low, grad_k_low, grad_v_low], 1)
    grad_w_qkv = contract_rows(normed_low, grad_projected)
    grad_qv = jnp.stack(
        [jnp.sum(grad_q_low.astype(jnp.float32), 0), jnp.sum(grad_v_low.astype(jnp.float32), 0)]
    )
    grad_hidden_part, grad_gain_one, grad_shift_one = pull_first(
        contract_cols(grad_projected, qkv_back)
    )
    input_grad = (grad_middle + grad_hidden_part).astype(jnp.bfloat16)[None]
    grad_gains = jnp.stack([grad_gain_one, grad_gain_two, grad_gain_three, grad_gain_four])
    grad_shifts = jnp.stack([grad_shift_one, grad_shift_two, grad_shift_three, grad_shift_four])
    owned = (
        lax.psum_scatter(grad_w_qkv, ("seq", "dp"), scatter_dimension=0, tiled=True),
        lax.psum_scatter(grad_w_out, ("seq", "dp"), scatter_dimension=0, tiled=True),
        lax.psum_scatter(grad_w_up, ("seq", "dp"), scatter_dimension=0, tiled=True),
        lax.psum_scatter(grad_w_down, ("seq", "dp"), scatter_dimension=0, tiled=True),
        lax.psum_scatter(grad_qv, ("seq", "dp"), scatter_dimension=1, tiled=True),
        lax.psum_scatter(grad_b_out, ("seq", "dp"), scatter_dimension=0, tiled=True),
        lax.psum_scatter(grad_b_up, ("seq", "dp"), scatter_dimension=0, tiled=True),
        lax.psum_scatter(grad_b_down, ("seq", "dp"), scatter_dimension=0, tiled=True),
        lax.psum_scatter(grad_gains, ("seq", "dp"), scatter_dimension=1, tiled=True),
        lax.psum_scatter(grad_shifts, ("seq", "dp"), scatter_dimension=1, tiled=True),
    )
    return (
        output,
        input_grad,
        owned[0],
        owned[4],
        owned[1],
        owned[5],
        owned[2],
        owned[6],
        owned[3],
        owned[7],
        owned[8],
        owned[9],
    )


MESH = pl.DeviceIdType.MESH


def is_small(mesh):
    return mesh.shape["seq"] == 16 and mesh.shape["dp"] == 2


def place():
    seq = lax.axis_index("seq")
    return seq // 8, (seq // 4) % 2, (seq // 2) % 2, seq % 2, lax.axis_index("dp")


def exchange_copies(scatter, src, out, send_sem, recv_sem, own_sem):
    a, b, y, c, x = place()

    def peer(k):
        return lax.rem(a + k // 2, 2), lax.rem(y + k % 2, 2)

    def device(k):
        pa, py = peer(k)
        return (pa * 8 + b * 4 + py * 2 + c, x)

    def source(k):
        pa, py = peer(k)
        return src.at[pa * 2 + py] if scatter else src.at[pa, :, py]

    def target(k):
        pa, py = peer(k)
        return out.at[pa, :, py] if scatter else out.at[pa * 2 + py]

    def copy(k, dst):
        return pltpu.make_async_remote_copy(
            src_ref=source(k), dst_ref=target(dst), send_sem=send_sem.at[k], recv_sem=recv_sem.at[k],
            device_id=device(k), device_id_type=MESH)

    def greet():
        barrier = pltpu.get_barrier_semaphore()
        for k in range(1, 4):
            pl.semaphore_signal(barrier, inc=1, device_id=device(k), device_id_type=MESH)

    def run():
        own = pltpu.make_async_copy(source(0), target(0), own_sem)
        own.start()
        pl.semaphore_wait(pltpu.get_barrier_semaphore(), 3)
        for k in (3, 2, 1):
            copy(k, 0).start()
        own.wait()
        for k in (3, 2, 1):
            copy(k, k).wait_recv()
        for k in (3, 2, 1):
            copy(k, 0).wait_send()

    return greet, run


def row_block(i, j):
    _, b, _, c, _ = place()
    return pl.ds(pl.multiple_of(lax.rem(b + i, 2) * 256 + lax.rem(c + j, 2) * 128, 128), 128)


def to_heads_kernel(rows_ref, out, src, *sems):
    greet, run = exchange_copies(True, src, out, *sems)
    greet()
    low = src.shape[2] - 128
    for g in range(4):
        values = slice(low * 2 + g * HD, low * 2 + g * HD + HD)
        for i in range(2):
            if low:
                for j in range(2):
                    src[g, i, j * 128:j * 128 + 128] = rows_ref[row_block(i, j), g * 128:g * 128 + 128]
            src[g, i, low:] = jnp.concatenate([rows_ref[row_block(i, j), values] for j in range(2)], 1)
    run()


def from_heads_kernel(heads_ref, out, got, *sems):
    greet, run = exchange_copies(False, heads_ref, got, *sems)
    greet()
    run()
    low = got.shape[2] - 128
    c = place()[3]
    for i in range(2):
        if low:
            for j in range(2):
                for g in range(4):
                    out[row_block(i, j), g * 128:g * 128 + 128] = got[g, i, j * 128:j * 128 + 128]
        for g in (0, 2):
            left, right = got[g, i, low:], got[g + 1, i, low:]
            cols = slice(low * 2 + g * HD, low * 2 + g * HD + 128)
            for j in range(2):
                lanes = slice(j * HD, j * HD + HD)
                out[row_block(i, j), cols] = jnp.concatenate([left[:, lanes], right[:, lanes]], 1)


def exchange(blocks, scatter, cid):
    vm = pl.BlockSpec(memory_space=pltpu.VMEM)
    rows = blocks.shape[-1] // 2 if scatter else blocks.shape[-2]
    shape, held = (2, 2, 2, rows, 128), (4, 2, rows, 128)
    return pl.pallas_call(
        to_heads_kernel if scatter else from_heads_kernel,
        out_shape=jax.ShapeDtypeStruct(shape if scatter else (512, rows * 2), blocks.dtype),
        in_specs=[vm], out_specs=vm,
        scratch_shapes=[pltpu.VMEM(held, blocks.dtype), pltpu.SemaphoreType.DMA((4,)), pltpu.SemaphoreType.DMA((4,)),
                        pltpu.SemaphoreType.DMA],
        compiler_params=pltpu.CompilerParams(collective_id=cid, has_side_effects=True),
        cost_estimate=pl.CostEstimate(flops=0, bytes_accessed=rows * 100000, transcendentals=0),
        name="to_heads" if scatter else "from_heads",
    )(blocks)


def dot_nt(a, b):
    return lax.dot_general(a, b, (((1,), (1,)), ((), ())), preferred_element_type=jnp.float32)


def dot_nn(a, b):
    return jnp.dot(a, b, preferred_element_type=jnp.float32)


BQ = 256
MASKED = -1e30


def load_heads(valid, packed, q_ref, k_ref):
    rows = q_ref.shape[0]
    qk = packed[:, :256].reshape(rows, 128)
    kq = jnp.concatenate([qk[:, 64:], qk[:, :64]], axis=1)
    lane = lax.broadcasted_iota(jnp.int32, (rows, 128), 1)
    spot = lax.broadcasted_iota(jnp.int32, (rows, 128), 0)
    past = jnp.where(spot < valid, 0.0, MASKED)
    q_ref[...] = jnp.where(lane < 64, qk.astype(jnp.float32), jnp.where(lane == 64, 1.0, 0.0)).astype(jnp.bfloat16)
    k_ref[...] = jnp.where(lane < 64, kq.astype(jnp.float32), jnp.where(lane == 64, past, 0.0)).astype(jnp.bfloat16)


def unpack_rows(halves):
    n = halves.shape[0]
    return jnp.concatenate([halves[:, :, :64], halves[:, :, 64:]], axis=1).reshape(n * 256, 64)


def block_probs(q_ref, k_ref, i):
    n = (i + 1) * BQ
    scores = dot_nt(k_ref[:n], q_ref[i * BQ:n])
    key = lax.broadcasted_iota(jnp.int32, (BQ, BQ), 0)
    query = lax.broadcasted_iota(jnp.int32, (BQ, BQ), 1)
    corner = jnp.where(key <= query, scores[n - BQ:], MASKED)
    scores = jnp.concatenate([scores[:n - BQ], corner], axis=0) if i else corner
    top = jnp.max(scores, axis=0, keepdims=True)
    terms = jnp.exp((scores - top) * 0.125)
    return terms, 1.0 / jnp.sum(terms, axis=0, keepdims=True)


def attend_kernel(valid_ref, packed, out_ref, q_ref, k_ref, vt_ref):
    load_heads(valid_ref[0], packed, q_ref, k_ref)
    unit = jnp.where(
        lax.broadcasted_iota(jnp.int32, (64, 64), 0) == lax.broadcasted_iota(jnp.int32, (64, 64), 1), 1.0, 0.0
    ).astype(jnp.bfloat16)
    vt_ref[...] = dot_nt(unit, unpack_rows(packed[:, 256:])).astype(jnp.bfloat16)
    for i in range(q_ref.shape[0] // BQ):
        n = (i + 1) * BQ
        terms, scale = block_probs(q_ref, k_ref, i)
        probs = (terms * scale).astype(jnp.bfloat16)
        mixed = dot_nn(vt_ref[:, :n], probs).T
        out_ref[i] = jnp.concatenate([mixed[:128], mixed[128:]], axis=1).astype(jnp.bfloat16)


def attend_back_kernel(valid_ref, packed, grad, out_ref, q_ref, k_ref, v_ref, g_ref, kt_ref, dk_ref, dv_ref):
    load_heads(valid_ref[0], packed, q_ref, k_ref)
    v_ref[...] = unpack_rows(packed[:, 256:])
    g_ref[...] = unpack_rows(grad[...])
    unit = jnp.where(
        lax.broadcasted_iota(jnp.int32, (64, 128), 0) == lax.broadcasted_iota(jnp.int32, (64, 128), 1), 1.0, 0.0
    ).astype(jnp.bfloat16)
    kt_ref[...] = dot_nt(unit, k_ref[...]).astype(jnp.bfloat16)
    dk_ref[...] = jnp.zeros_like(dk_ref)
    dv_ref[...] = jnp.zeros_like(dv_ref)
    blocks = q_ref.shape[0] // BQ
    for i in range(blocks):
        n = (i + 1) * BQ
        terms, scale = block_probs(q_ref, k_ref, i)
        probs = terms * scale
        grad_probs = dot_nt(v_ref[:n], g_ref[i * BQ:n])
        delta = jnp.sum(probs * grad_probs, axis=0, keepdims=True)
        grad_scores = (probs * (grad_probs - delta)).astype(jnp.bfloat16)
        grad_query = dot_nn(kt_ref[:, :n], grad_scores).T * 0.125
        out_ref[i, :256, :64] = grad_query.astype(jnp.bfloat16)
        dk_ref[:n] += dot_nn(grad_scores, q_ref[i * BQ:n])
        dv_ref[:n] += dot_nn(probs.astype(jnp.bfloat16), g_ref[i * BQ:n])
    for i in range(blocks):
        rows = slice(i * BQ, (i + 1) * BQ)
        out_ref[i, :256, 64:] = (dk_ref[rows, :64] * 0.125).astype(jnp.bfloat16)
        value = dv_ref[rows].astype(jnp.bfloat16)
        out_ref[i, 256:] = jnp.concatenate([value[:128], value[128:]], axis=1)


def attend(valid, packed):
    rows = packed.shape[0] * 256
    vm = pl.BlockSpec(memory_space=pltpu.VMEM)
    return pl.pallas_call(
        attend_kernel,
        out_shape=jax.ShapeDtypeStruct((packed.shape[0], 128, 128), jnp.bfloat16),
        in_specs=[pl.BlockSpec(memory_space=pltpu.SMEM), vm], out_specs=vm,
        scratch_shapes=[pltpu.VMEM((rows, 128), jnp.bfloat16)] * 2 + [pltpu.VMEM((64, rows), jnp.bfloat16)],
        compiler_params=pltpu.CompilerParams(vmem_limit_bytes=48 << 20),
        name="attend",
    )(valid, packed)


def attend_back(valid, packed, grad):
    rows = packed.shape[0] * 256
    vm = pl.BlockSpec(memory_space=pltpu.VMEM)
    return pl.pallas_call(
        attend_back_kernel,
        out_shape=jax.ShapeDtypeStruct(packed.shape, jnp.bfloat16),
        in_specs=[pl.BlockSpec(memory_space=pltpu.SMEM), vm, vm], out_specs=vm,
        scratch_shapes=[pltpu.VMEM((rows, 128), jnp.bfloat16)] * 2 + [pltpu.VMEM((rows, 64), jnp.bfloat16)] * 2
        + [pltpu.VMEM((64, rows), jnp.bfloat16), pltpu.VMEM((rows, 128), jnp.float32), pltpu.VMEM((rows, 64), jnp.float32)],
        compiler_params=pltpu.CompilerParams(vmem_limit_bytes=48 << 20),
        name="attend_back",
    )(valid, packed, grad)


def flip(bits, block):
    return lax.ppermute(block, "seq", [(s, s ^ bits) for s in range(16)])


flip_a, flip_y = (functools.partial(flip, bits) for bits in (8, 2))


def flip_x(block):
    return lax.ppermute(block, "dp", [(0, 1), (1, 0)])


def after(value, *others):
    return lax.optimization_barrier((value,) + others)[0]


def pick(block, index, axis, keepdims=False):
    return lax.dynamic_index_in_dim(block, index, axis, keepdims=keepdims)


def cube_one(flip_one, block):
    return jnp.concatenate([block, flip_one(block)], 0)


def arrange_kernel(spot_ref, kept, received, out):
    def put(block):
        for step in range(2):
            a = lax.rem(spot_ref[0] + step, 2)
            if len(out.shape) == 7:
                for j in range(2):
                    for k in range(2):
                        out[a, j, 0, k, 0] = block[step, j, k]
            else:
                out[a, 0, 0] = block[step]

    @pl.when(pl.program_id(0) < 2)
    def _():
        put(kept)

    @pl.when(pl.program_id(0) >= 2)
    def _():
        put(received)


def arrange(spot, y_first, kept, received):
    def coords(i, r):
        second, first = i // 2, i % 2
        y, x = (first, second) if y_first else (second, first)
        return lax.rem(r[1] + y, 2), lax.rem(r[2] + x, 2)

    shape = kept.shape

    def spec(block, low):
        rest = (0,) * (block.ndim - 1)
        return pl.BlockSpec((2,) + block.shape[1:], lambda i, r: (jnp.clip(i - low, 0, 1),) + rest)

    if len(shape) == 5:
        def out_place(i, r):
            y, x = coords(i, r)
            return 0, 0, y, 0, x, 0, 0
        out_block, out_shape = (2, 2, 1, 2, 1) + shape[3:], (2,) * 5 + shape[3:]
    else:
        def out_place(i, r):
            return (0,) + coords(i, r) + (0, 0)
        out_block, out_shape = (2, 1, 1) + shape[1:], (2, 2, 2) + shape[1:]
    return pl.pallas_call(
        arrange_kernel,
        out_shape=jax.ShapeDtypeStruct(out_shape, kept.dtype),
        grid_spec=pltpu.PrefetchScalarGridSpec(
            num_scalar_prefetch=1, grid=(4,), in_specs=[spec(kept, 0), spec(received, 2)],
            out_specs=pl.BlockSpec(out_block, out_place)),
        compiler_params=pltpu.CompilerParams(vmem_limit_bytes=32 << 20),
        cost_estimate=pl.CostEstimate(flops=0, bytes_accessed=8 << 20, transcendentals=0),
        name="arrange",
    )(spot, kept, received)


def up_kernel(rows_ref, w_ref, shift_ref, active_ref, slope_ref):
    for r in range(0, rows_ref.shape[0], 128):
        span = slice(r, r + 128)
        t = dot_nn(rows_ref[span], w_ref[...]) + shift_ref[...]
        half = 0.5 + 0.5 * lax.erf(t * math.sqrt(0.5))
        active_ref[span] = (t * half).astype(jnp.bfloat16)
        slope_ref[span] = half + t * jnp.exp(t * t * -0.5) * (1.0 / math.sqrt(2.0 * math.pi))


def up_gelu(rows, w, shift):
    m, k = rows.shape
    n, block = w.shape[1], 256
    return pl.pallas_call(
        up_kernel, grid=(n // block,),
        out_shape=(jax.ShapeDtypeStruct((m, n), jnp.bfloat16), jax.ShapeDtypeStruct((m, n), jnp.float32)),
        in_specs=[pl.BlockSpec((m, k), lambda i: (0, 0)), pl.BlockSpec((k, block), lambda i: (0, i)),
                  pl.BlockSpec((1, block), lambda i: (0, i))],
        out_specs=(pl.BlockSpec((m, block), lambda i: (0, i)),) * 2,
        compiler_params=pltpu.CompilerParams(vmem_limit_bytes=32 << 20),
        cost_estimate=pl.CostEstimate(flops=2 * m * n * k, bytes_accessed=24 << 20, transcendentals=2 * m * n),
        name="up_gelu",
    )(rows, w, shift)


def add_low(mine, other):
    return (mine.astype(jnp.float32) + other.astype(jnp.float32)).astype(jnp.bfloat16)


def fold(terms, flip_one, index, axis):
    return add_low(pick(terms, index, axis, True), flip_one(pick(terms, 1 - index, axis, True)))


def reduce_kernel(q_ref, o_ref, u_ref, part, tokens, grad_middle, vectors, *refs):
    vec_refs, (out_q, ro, out_u, vec, input_grad, got_far, got_near, low_sums, got_sums, row_send, row_recv, rq, gu, r1q, t2q, r2q, t3q, r3q, fq, gq, r1o, t2o, r2o, t3o, r3o,
               run, got, send_sem, recv_sem) = refs[:10], refs[10:]
    a, b, y, c, x = place()
    f32, bf16 = jnp.float32, jnp.bfloat16
    barrier = pltpu.get_barrier_semaphore()

    def at(pa, pb, py, pc, px):
        return (pa * 8 + pb * 4 + py * 2 + pc, px)

    to_x, to_y, to_a = at(a, b, y, c, 1 - x), at(a, b, 1 - y, c, x), at(1 - a, b, y, c, x)
    ranks = [(lax.rem(b + k // 2, 2), lax.rem(c + k % 2, 2)) for k in range(4)]
    to_rank = [at(a, ranks[k][0], y, ranks[k][1], x) for k in range(4)]
    to_b, to_c = to_rank[2], to_rank[1]
    for dev in [to_x, to_y, to_a] + to_rank[1:]:
        pl.semaphore_signal(barrier, inc=1, device_id=dev, device_id_type=MESH)
    for pb in range(2):
        for j in range(4):
            for row, cols in ((0, slice(j * 128, j * 128 + HD)), (1, slice(512 + j * HD, 512 + j * HD + HD))):
                piece = vec_refs[0][:, cols]
                pair = [jnp.where((b == pb) & (c == pc), piece, 0.0) for pc in range(2)]
                h = head_of(j // 2, pb, j % 2, 0) * HD
                run[0, row:row + 1, h:h + 128] = jnp.concatenate(pair, 1)
            for pc in range(2):
                col = head_of(j // 2, pb, j % 2, pc) * 256
                piece = vec_refs[1][:, j * 256:j * 256 + 256]
                run[0, 12 + col // 1024:13 + col // 1024, col % 1024:col % 1024 + 256] = jnp.where(
                    (b == pb) & (c == pc), piece, 0.0)
    for k, row in enumerate((2, 3, 5, 6, 7, 9, 10, 11)):
        run[0, row:row + 1] = vec_refs[2 + k][...]
    for row in (4, 8):
        run[0, row:row + 1] = jnp.zeros((1, 1024), f32)
    pl.semaphore_wait(barrier, 6)

    made = []

    def remote(src, dst, dev):
        k = len(made)
        made.append(pltpu.make_async_remote_copy(
            src_ref=src, dst_ref=dst, send_sem=send_sem.at[k], recv_sem=recv_sem.at[k],
            device_id=dev, device_id_type=MESH))
        return made[-1]

    def low(*values):
        return sum(v.astype(f32) for v in values)

    places = [1 - a, a]
    halves = [slice(0, 512), slice(512, 1024)]
    lateral = [(to_x, to_y), (to_y, to_x)]

    q1, q2, o1, o2 = {}, {}, {}, {}
    for i in range(2):
        for s in range(2):
            p = places[i]
            q1[s, i] = remote(q_ref.at[p, 0, :, :, 1 - x] if s == 0 else q_ref.at[p, 1, 1 - y], r1q.at[s, i], lateral[s][0])
            o1[s, i] = remote(o_ref.at[p, :, 1 - x, :, halves[0]] if s == 0 else o_ref.at[p, 1 - y, :, :, halves[1]],
                              r1o.at[s, i], lateral[s][0])
            q2[s, i] = remote(t2q.at[s, i], r2q.at[s, i], lateral[s][1])
            o2[s, i] = remote(t2o.at[s, i], r2o.at[s, i], lateral[s][1])
    q3 = [remote(t3q.at[s], r3q.at[s], to_a) for s in range(2)]
    o3 = [remote(t3o.at[s], r3o.at[s], to_a) for s in range(2)]
    qr = [remote(fq.at[ranks[k][0], ranks[k][1]], gq.at[k - 1], to_rank[k]) for k in range(1, 4)]
    ur = [remote(u_ref.at[ranks[k][0], ranks[k][1]], gu.at[b, c], to_rank[k]) for k in range(1, 4)]
    vs = [remote(run.at[k], got.at[k], dev) for k, dev in enumerate((to_x, to_y, to_a, to_b, to_c))]

    def next_sum(k):
        vs[k].wait_recv()
        if k < 4:
            run[k + 1] = run[k] + got[k]
            vs[k + 1].start()
        else:
            vec[...] = run[k] + got[k]

    pieces = part.shape[2] // PIECE

    def span(r):
        return pl.ds(pl.multiple_of(r * PIECE, PIECE), PIECE)

    def row_copy(kind, r):
        src, dst, dev = ((part.at[1, 1, span(r)], got_far.at[span(r)], to_c), (part.at[0, 1, span(r)], got_near.at[span(r)], to_c),
                         (low_sums.at[span(r)], got_sums.at[span(r)], to_b))[kind]
        return pltpu.make_async_remote_copy(
            src_ref=src, dst_ref=dst, send_sem=row_send.at[kind, r], recv_sem=row_recv.at[kind, r],
            device_id=dev, device_id_type=MESH)

    def send_across(r, _):
        row_copy(0, r).wait_recv()
        low_sums[span(r)] = (part[1, 0, span(r)] + got_far[span(r)]).astype(bf16)
        row_copy(2, r).start()
        return 0

    def take(r, _):
        row_copy(1, r).wait_recv()
        row_copy(2, r).wait_recv()
        total = part[0, 0, span(r)] + got_near[span(r)] + got_sums[span(r)].astype(f32)
        _, pull = jax.vjp(norm_rows, tokens[span(r)].astype(f32), *norm_vectors(vectors, 0))
        term, grad_gain, grad_shift = pull(total)
        input_grad[span(r)] = (grad_middle[span(r)] + term).astype(bf16)
        run[0, 4:5] += grad_gain
        run[0, 8:9] += grad_shift
        for kind in range(3):
            row_copy(kind, r).wait_send()
        return 0

    for kind in range(2):
        for r in range(pieces):
            row_copy(kind, r).start()
    for s in range(2):
        q1[s, 0].start()
        o1[s, 0].start()
    for k in (3, 2, 1):
        ur[k - 1].start()
    for s in range(2):
        o1[s, 1].start()
    lax.fori_loop(0, pieces, send_across, 0)

    def q_terms(s, i, far):
        p = places[i]
        if s == 0:
            v = 1 - y if far else y
            return q_ref[p, 0, v, :, x], r1q[0, i, v]
        v = 1 - x if far else x
        return q_ref[p, 1, y, :, v], r1q[1, i, :, v]

    def o_terms(s, i, far):
        p = places[i]
        if s == 0:
            v = 1 - y if far else y
            return o_ref[p, v, x, :, halves[0]], r1o[0, i, v]
        v = 1 - x if far else x
        return o_ref[p, y, v, :, halves[1]], r1o[1, i, v]

    for i in range(2):
        for s in range(2):
            q1[s, i].wait_recv()
            t2q[s, i] = low(*q_terms(s, i, True)).astype(bf16)
            q2[s, i].start()
            o1[s, i].wait_recv()
            t2o[s, i] = low(*o_terms(s, i, True)).astype(bf16)
            o2[s, i].start()
        if i == 0:
            for s in range(2):
                q1[s, 1].start()
            lax.fori_loop(0, pieces, take, 0)
            vs[0].start()
            for s in range(2):
                q2[s, 0].wait_recv()
                t3q[s] = low(*q_terms(s, 0, False), r2q[s, 0]).astype(bf16)
                q3[s].start()
                o2[s, 0].wait_recv()
                t3o[s] = low(*o_terms(s, 0, False), r2o[s, 0]).astype(bf16)
                o3[s].start()
    next_sum(0)
    for s in range(2):
        q2[s, 1].wait_recv()
        o2[s, 1].wait_recv()
        q3[s].wait_recv()
        total = low(*q_terms(s, 1, False), r2q[s, 1], r3q[s])
        fq[s] = total.astype(bf16)
        for j in range(2):
            @pl.when((b == s) & (c == j))
            def _():
                rq[s, j] = total[j]
        o3[s].wait_recv()
        ro[:, halves[s]] = low(*o_terms(s, 1, False), r2o[s, 1], r3o[s])
        next_sum(1 + s)
    for k in (3, 2, 1):
        qr[k - 1].start()
    gu[b, c] = u_ref[b, c]
    for k in (1, 2, 3):
        ur[k - 1].wait_recv()
    next_sum(3)
    for k in (1, 2, 3):
        pb, pc = ranks[k]
        qr[k - 1].wait_recv()
        rq[pb, pc] = gq[k - 1].astype(f32)
    for pb in range(2):
        for j in range(4):
            zero, one = rq[pb, 0], rq[pb, 1]
            h = head_of(j // 2, pb, j % 2, 0) * HD
            q, k = slice(j * 128, j * 128 + HD), slice(j * 128 + HD, j * 128 + 128)
            v = slice(512 + j * HD, 512 + j * HD + HD)
            for t, cols in enumerate((q, k, v)):
                out_q[:, t * 1024 + h:t * 1024 + h + 128] = jnp.concatenate([zero[:, cols], one[:, cols]], 1)
            for pc in range(2):
                col = head_of(j // 2, pb, j % 2, pc) * 256
                out_u[:, col:col + 256] = gu[pb, pc, :, j * 256:j * 256 + 256].astype(f32)
    next_sum(4)
    for copy in made:
        copy.wait_send()


def reduce_all(gw_qkv, gw_out, up_sum, part, tokens, grad_middle, params, vectors, cid):
    f32, bf16 = jnp.float32, jnp.bfloat16
    V = pltpu.VMEM
    vm = pl.BlockSpec(memory_space=V)
    S = jax.ShapeDtypeStruct
    q, o, u = gw_qkv.shape[5:], (gw_out.shape[3], 512), up_sum.shape
    rows, n = grad_middle.shape
    scratch = [
        V((rows, n), f32), V((rows, n), f32), V((rows, n), bf16), V((rows, n), bf16),
        pltpu.SemaphoreType.DMA((3, rows // PIECE)), pltpu.SemaphoreType.DMA((3, rows // PIECE)),
        V((2, 2) + q, f32), V(u, bf16),
        V((2, 2, 2, 2) + q, bf16), V((2, 2, 2) + q, bf16), V((2, 2, 2) + q, bf16), V((2, 2) + q, bf16), V((2, 2) + q, bf16),
        V((2, 2) + q, bf16), V((3,) + q, bf16),
        V((2, 2, 2) + o, bf16), V((2, 2) + o, bf16), V((2, 2) + o, bf16), V((2,) + o, bf16), V((2,) + o, bf16),
        V((5, 16, 1024), f32), V((5, 16, 1024), f32),
        pltpu.SemaphoreType.DMA((32,)), pltpu.SemaphoreType.DMA((32,))]
    return pl.pallas_call(
        reduce_kernel,
        out_shape=(S((q[0], 4 * q[1]), f32), S((o[0], 1024), f32), S((u[2], 4 * u[3]), f32), S((16, 1024), f32), S((rows, n), bf16)),
        in_specs=[vm] * 17, out_specs=(vm,) * 5, scratch_shapes=scratch,
        compiler_params=pltpu.CompilerParams(collective_id=cid, has_side_effects=True, vmem_limit_bytes=48 << 20),
        name="reduce_all",
    )(gw_qkv, gw_out, up_sum, part.reshape(2, 2, rows, n), tokens, grad_middle, params, *vectors)


def qk_columns(head):
    return slice(head * HD, head * HD + HD), slice(1024 + head * HD, 1024 + head * HD + HD), slice(2048 + head * HD, 2048 + head * HD + HD)


def head_of(a, b, y, c):
    return a * 8 + b * 4 + y * 2 + c


def start_kernel(q_hbm, u_hbm, o_in, t_in, v_in, wq, wo, up, rows, vec, q_in, u_in, q_src, u_src, send_sem, recv_sem, own_sem):
    a, b, y, c, x = place()
    barrier = pltpu.get_barrier_semaphore()

    def at(pa, pb, py, pc, px):
        return (pa * 8 + pb * 4 + py * 2 + pc, px)

    to_x, to_y, to_a = at(a, b, y, c, 1 - x), at(a, b, 1 - y, c, x), at(1 - a, b, y, c, x)
    ranks = [(lax.rem(b + k // 2, 2), lax.rem(c + k % 2, 2)) for k in range(4)]
    to_rank = [at(a, pb, y, pc, x) for pb, pc in ranks]
    for dev in [to_x, to_y, to_a] + to_rank[1:]:
        pl.semaphore_signal(barrier, inc=1, device_id=dev, device_id_type=MESH)

    loads = [pltpu.make_async_copy(q_hbm, q_in, own_sem.at[5]), pltpu.make_async_copy(u_hbm, u_in, own_sem.at[6])]
    for copy in loads:
        copy.start()
    for copy in loads:
        copy.wait()

    for pb in range(2):
        for pc in range(2):
            for j in range(4):
                q, k, v = qk_columns(head_of(j // 2, pb, j % 2, pc))
                q_src[pb, pc, :, j * 128:j * 128 + 128] = jnp.concatenate([q_in[:, q], q_in[:, k]], 1)
            for j in range(2):
                v0 = qk_columns(head_of(j, pb, 0, pc))[2]
                v1 = qk_columns(head_of(j, pb, 1, pc))[2]
                q_src[pb, pc, :, 512 + j * 128:640 + j * 128] = jnp.concatenate([q_in[:, v0], q_in[:, v1]], 1)
            for j in range(4):
                col = (head_of(j // 2, pb, j % 2, pc)) * 256
                u_src[pb, pc, :, j * 256:j * 256 + 256] = u_in[:, col:col + 256]
    own = [pltpu.make_async_copy(src, dst, own_sem.at[k]) for k, (src, dst) in enumerate((
        (q_src.at[b, c], wq.at[a, b, y, c, x]), (u_src.at[b, c], up.at[0, b, c]), (o_in, wo.at[a, y, x]),
        (t_in, rows.at[0]), (v_in, vec.at[a, b, y, c, x])))]
    for copy in own:
        copy.start()
    pl.semaphore_wait(barrier, 6)

    made = []

    def remote(src, dst, dev):
        k = len(made)
        made.append(pltpu.make_async_remote_copy(
            src_ref=src, dst_ref=dst, send_sem=send_sem.at[k], recv_sem=recv_sem.at[k],
            device_id=dev, device_id_type=MESH))
        return made[-1]

    places = [a, 1 - a]
    halves = [slice(0, 512), slice(512, 1024)]
    lateral = [(to_y, to_x), (to_x, to_y)]

    def same(ref, dev):
        return remote(ref, ref, dev)

    q_rank = [remote(q_src.at[ranks[k][0], ranks[k][1]], wq.at[a, b, y, c, x], to_rank[k]) for k in range(1, 4)]
    u_rank = [remote(u_src.at[ranks[k][0], ranks[k][1]], up.at[0, b, c], to_rank[k]) for k in range(1, 4)]
    v_rank = [remote(v_in, vec.at[a, b, y, c, x], to_rank[k]) for k in range(1, 4)]
    t_core, t_near = remote(t_in, rows.at[1], to_rank[1]), remote(t_in, rows.at[2], to_rank[2])
    t_far = remote(rows.at[2], rows.at[3], to_rank[1])
    u_cube = remote(up.at[0], up.at[1], to_a)
    v_cube = [same(vec.at[a, :, y, :, x], to_a), same(vec.at[:, :, y, :, x], to_y), same(vec.at[:, :, :, :, x], to_x)]
    q_cube = [same(wq.at[a, s, y, :, x], to_a) for s in range(2)]
    o_cube = [remote(o_in.at[:, halves[s]], wo.at[a, y, x, :, halves[s]], to_a) for s in range(2)]
    q_side, o_side = {}, {}
    for i in range(2):
        for s in range(2):
            one, two = lateral[s]
            oy, ox = (1 - y, x) if s == 0 else (y, 1 - x)
            p = places[i]
            mine, theirs = wq.at[p, s, y, :, x], wq.at[p, s, oy, :, ox]
            q_side[s, i] = (same(mine, one), same(mine, two), same(theirs, two))
            mine, theirs = wo.at[p, y, x, :, halves[s]], wo.at[p, oy, ox, :, halves[s]]
            first = o_in.at[:, halves[s]] if i == 0 else mine
            o_side[s, i] = (remote(first, mine, one), remote(first, mine, two), same(theirs, two))

    for k in (2, 1, 0):
        q_rank[k].start()
        v_rank[k].start()
    for s in range(2):
        o_cube[s].start()
        o_side[s, 0][0].start()
        o_side[s, 0][1].start()
    t_near.start()
    t_core.start()
    own[0].wait()
    for copy in q_rank:
        copy.wait_recv()
    for s in range(2):
        q_cube[s].start()
        q_side[s, 0][0].start()
        q_side[s, 0][1].start()
    own[4].wait()
    for copy in v_rank:
        copy.wait_recv()
    v_cube[0].start()
    for k in (2, 1, 0):
        u_rank[k].start()
    for s in range(2):
        o_side[s, 0][0].wait_recv()
        o_side[s, 0][2].start()
    for s in range(2):
        o_cube[s].wait_recv()
        o_side[s, 1][0].start()
        o_side[s, 1][1].start()
    t_near.wait_recv()
    t_far.start()
    for s in range(2):
        q_side[s, 0][0].wait_recv()
        q_side[s, 0][2].start()
    for s in range(2):
        q_cube[s].wait_recv()
        q_side[s, 1][0].start()
        q_side[s, 1][1].start()
    v_cube[0].wait_recv()
    v_cube[1].start()
    own[1].wait()
    for copy in u_rank:
        copy.wait_recv()
    u_cube.start()
    for s in range(2):
        o_side[s, 1][0].wait_recv()
        o_side[s, 1][2].start()
    v_cube[1].wait_recv()
    v_cube[2].start()
    for s in range(2):
        q_side[s, 1][0].wait_recv()
        q_side[s, 1][2].start()
    v_cube[2].wait_recv()
    t_core.wait_recv()
    t_far.wait_recv()
    for i in range(2):
        for s in range(2):
            for k in (1, 2):
                q_side[s, i][k].wait_recv()
                o_side[s, i][k].wait_recv()
    u_cube.wait_recv()
    for k in (2, 3):
        own[k].wait()
    for copy in made:
        copy.wait_send()


def start_gather(w_qkv, w_up, w_out, tokens, vectors, cid):
    bf16 = jnp.bfloat16
    S = lambda *shape: jax.ShapeDtypeStruct(shape, bf16)
    vm, anywhere = pl.BlockSpec(memory_space=pltpu.VMEM), pl.BlockSpec(memory_space=pl.ANY)
    return pl.pallas_call(
        start_kernel,
        out_shape=(S(2, 2, 2, 2, 2, 32, 768), S(2, 2, 2, 32, 1024), S(2, 2, 2, 32, 1024), S(4, 128, 1024),
                   S(2, 2, 2, 2, 2, 16, 128)),
        in_specs=[pl.BlockSpec(memory_space=pltpu.HBM)] * 4 + [vm], out_specs=(anywhere,) * 5,
        scratch_shapes=[
            pltpu.VMEM(w_qkv.shape, bf16), pltpu.VMEM(w_up.shape, bf16),
            pltpu.VMEM((2, 2, 32, 768), bf16), pltpu.VMEM((2, 2, 32, 1024), bf16),
            pltpu.SemaphoreType.DMA((48,)), pltpu.SemaphoreType.DMA((48,)), pltpu.SemaphoreType.DMA((7,))],
        compiler_params=pltpu.CompilerParams(collective_id=cid, has_side_effects=True, vmem_limit_bytes=63 << 20),
        cost_estimate=pl.CostEstimate(flops=0, bytes_accessed=100 << 20, transcendentals=0),
        name="start_gather",
    )(w_qkv, w_up, w_out, tokens, vectors)


PIECE = 32


def rows_kernel(step, gather, count_in, count_out, part, *refs):
    ins, outs = refs[:count_in], refs[count_in:count_in + count_out]
    rest = refs[count_in + count_out:]
    rows = rest[0] if gather else None
    got_far, got_near, sums, got_sums, send_sem, recv_sem = rest[-6:]
    a, b, y, c, x = place()

    def at(pb, pc):
        return (a * 8 + pb * 4 + y * 2 + pc, x)

    to_b, to_core = at(1 - b, c), at(b, 1 - c)
    barrier = pltpu.get_barrier_semaphore()
    for dev in (to_b, to_core):
        pl.semaphore_signal(barrier, inc=1, device_id=dev, device_id_type=MESH)
    pl.semaphore_wait(barrier, 2)
    pieces = part.shape[2] // PIECE

    def span(r):
        return pl.ds(pl.multiple_of(r * PIECE, PIECE), PIECE)

    def remote(kind, r, src, dst, dev):
        return pltpu.make_async_remote_copy(
            src_ref=src, dst_ref=dst, send_sem=send_sem.at[kind, r], recv_sem=recv_sem.at[kind, r],
            device_id=dev, device_id_type=MESH)

    def far(r):
        return remote(0, r, part.at[1, 1, span(r)], got_far.at[span(r)], to_core)

    def near(r):
        return remote(1, r, part.at[0, 1, span(r)], got_near.at[span(r)], to_core)

    def across(r):
        return remote(2, r, sums.at[span(r)], got_sums.at[span(r)], to_b)

    def row_near(r):
        return remote(3, r, rows.at[0, span(r)], rows.at[2, span(r)], to_b)

    def row_core(r):
        return remote(4, r, rows.at[0, span(r)], rows.at[1, span(r)], to_core)

    def row_far(r):
        return remote(5, r, rows.at[2, span(r)], rows.at[3, span(r)], to_core)

    for r in range(pieces):
        far(r).start()
    for r in range(pieces):
        near(r).start()

    def send_across(r, _):
        far(r).wait_recv()
        sums[span(r)] = (part[1, 0, span(r)] + got_far[span(r)]).astype(jnp.bfloat16)
        across(r).start()
        return 0

    lax.fori_loop(0, pieces, send_across, 0)
    for ref in outs:
        if ref.shape[0] == 1:
            ref[...] = jnp.zeros_like(ref)

    def take(r, _):
        near(r).wait_recv()
        across(r).wait_recv()
        total = part[0, 0, span(r)] + got_near[span(r)] + got_sums[span(r)].astype(jnp.float32)
        piece = step(span(r), total, ins, outs)
        if gather:
            rows[0, span(r)] = piece
            row_near(r).start()
            row_core(r).start()
        return 0

    lax.fori_loop(0, pieces, take, 0)

    def relay(r, _):
        row_near(r).wait_recv()
        row_far(r).start()
        return 0

    def finish(r, _):
        if gather:
            row_core(r).wait_recv()
            row_far(r).wait_recv()
            row_near(r).wait_send()
            row_core(r).wait_send()
            row_far(r).wait_send()
        far(r).wait_send()
        near(r).wait_send()
        across(r).wait_send()
        return 0

    if gather:
        lax.fori_loop(0, pieces, relay, 0)
    lax.fori_loop(0, pieces, finish, 0)


def sum_rows(step, part, ins, outs, gather, cid):
    rows, n = part.shape[0] // 4, part.shape[1]
    vm = pl.BlockSpec(memory_space=pltpu.VMEM)
    shapes = tuple(outs) + ((jax.ShapeDtypeStruct((4, rows, n), jnp.bfloat16),) if gather else ())
    V = pltpu.VMEM
    return pl.pallas_call(
        functools.partial(rows_kernel, step, gather, len(ins), len(outs)),
        out_shape=shapes, in_specs=[vm] * (1 + len(ins)), out_specs=(vm,) * len(shapes),
        scratch_shapes=[V((rows, n), jnp.float32), V((rows, n), jnp.float32), V((rows, n), jnp.bfloat16), V((rows, n), jnp.bfloat16),
                        pltpu.SemaphoreType.DMA((6, rows // PIECE)), pltpu.SemaphoreType.DMA((6, rows // PIECE))],
        compiler_params=pltpu.CompilerParams(collective_id=cid, has_side_effects=True, vmem_limit_bytes=32 << 20),
        cost_estimate=pl.CostEstimate(flops=0, bytes_accessed=50 << 20, transcendentals=0),
        name="sum_rows",
    )(part.reshape(2, 2, rows, n), *ins)


def norm_vectors(vectors, k):
    return vectors[4 + k:5 + k], vectors[8 + k:9 + k]


def attended_step(span, total, ins, outs):
    tokens, vectors = ins
    branch = total + vectors[2:3]
    middle = tokens[span].astype(jnp.float32) + norm_rows(branch, *norm_vectors(vectors, 1))
    outs[0][span] = branch
    outs[1][span] = middle
    return norm_rows(middle, *norm_vectors(vectors, 2)).astype(jnp.bfloat16)


def output_step(span, total, ins, outs):
    middle, grad_out, vectors = ins
    normed, pull = jax.vjp(norm_rows, total + vectors[3:4], *norm_vectors(vectors, 3))
    outs[0][span] = (middle[span] + normed).astype(jnp.bfloat16)
    grad_down, grad_gain, grad_shift = pull(grad_out[span])
    grad_down = grad_down.astype(jnp.bfloat16)
    outs[1][...] += grad_gain
    outs[2][...] += grad_shift
    outs[3][...] += jnp.sum(grad_down.astype(jnp.float32), 0, keepdims=True)
    return grad_down


def middle_step(span, total, ins, outs):
    middle, branch, grad_out, vectors = ins
    _, pull = jax.vjp(norm_rows, middle[span], *norm_vectors(vectors, 2))
    part, grad_gain2, grad_shift2 = pull(total)
    grad_middle = grad_out[span] + part
    _, pull = jax.vjp(norm_rows, branch[span], *norm_vectors(vectors, 1))
    grad_branch, grad_gain1, grad_shift1 = pull(grad_middle)
    grad_branch = grad_branch.astype(jnp.bfloat16)
    outs[0][span] = grad_middle
    for ref, value in zip(outs[1:], (grad_gain2, grad_shift2, grad_gain1, grad_shift1,
                                     jnp.sum(grad_branch.astype(jnp.float32), 0, keepdims=True))):
        ref[...] += value
    return grad_branch


def fast_body(tokens, cotangent, lengths, assign, w_qkv, qv_bias, w_out, out_bias, w_up, up_bias, w_down, down_bias,
              norm_gain, norm_shift):
    bf16, f32 = jnp.bfloat16, jnp.float32
    a, b, y, c, x = place()
    spot = jnp.stack([a, y, x]).astype(jnp.int32)
    width = tokens.shape[2]
    place_two = jnp.arange(2, dtype=jnp.int32)
    sequence = jnp.sum(jnp.where(place_two == x, assign.astype(jnp.int32), 0))
    valid = jnp.sum(jnp.where(place_two == sequence, lengths.astype(jnp.int32), 0))

    small, row = jnp.zeros((16, 128), bf16), 0
    for block in (qv_bias, out_bias[None], down_bias[None], norm_gain, norm_shift, up_bias[None]):
        small += jnp.pad(block, ((row, 16 - row - block.shape[0]), (0, 128 - block.shape[1])))
        row += block.shape[0]
    wqkv, wo, up_one, rows, small = start_gather(w_qkv, w_up, w_out, tokens[0], small, 6)
    down_one = after(w_down, wqkv)
    down_one = jnp.stack([down_one, flip_a(down_one)])
    wqkv, wo, rows = wqkv.reshape(width, 768), wo.reshape(256, width), rows.reshape(512, width)

    vectors = small[..., :12, :32].reshape(32, 12, 32).transpose(1, 0, 2).reshape(12, width).astype(f32)
    qv_half = pick(pick(vectors[:2].reshape(2, 2, 2, 2, 2, HD), b, 2), c, 3).reshape(2, 4, HD)
    qk_shift = jnp.concatenate([qv_half[0], jnp.zeros((4, HD), f32)], 1).reshape(512)
    v_shift = qv_half[1].reshape(256)
    up_shift = pick(pick(small[..., 12, :], b, 1), c, 2).reshape(1024).astype(f32)

    first = norm_rows(rows.astype(f32), vectors[4:5], vectors[8:9]).astype(bf16)
    up_two = cube_one(flip_x, up_one)
    projected = (dot_nn(first, wqkv) + jnp.concatenate([qk_shift, v_shift])).astype(bf16)
    packed = exchange(after(projected, up_two, down_one), True, 1).reshape(8, 384, 128)
    down_two = cube_one(flip_y, after(down_one, packed))
    attended = attend(valid[None], packed).reshape(2, 2, 2, 128, 128)
    attended = exchange(after(attended, down_two), False, 2)
    up_far, down_far = flip_y(after(up_two, attended)), flip_x(after(down_two, attended))
    own_spot = lax.axis_index("seq") * 128 + jnp.arange(128, dtype=jnp.int32)
    grad_out = cotangent[0].astype(f32) * (own_spot < valid).astype(f32)[:, None]
    S = jax.ShapeDtypeStruct
    wide, low, line = S((128, width), f32), S((128, width), bf16), S((1, width), f32)
    branch, middle, third = sum_rows(
        attended_step, dot_nn(attended, wo), (tokens[0], vectors),
        (wide, wide), True, 7)
    third = third.reshape(512, width)
    wu = arrange(spot, False, up_two, up_far).reshape(width, 1024)
    active, slope = up_gelu(third, wu, up_shift.reshape(1, 1024))
    wd = arrange(spot, True, down_two, after(down_far, active)).reshape(1024, width)
    output, gain4, shift4, bias_down, down_rows = sum_rows(
        output_step, dot_nn(active, wd), (middle, grad_out, vectors), (low, line, line, line), True, 8)
    down_rows = down_rows.reshape(512, width)
    gw_down = contract_rows(active, down_rows).astype(bf16).reshape(2, 2, 2, 128, width)
    down_term = flip_y(pick(gw_down, 1 - y, 1, True))
    grad_up = (dot_nt(after(down_rows, gw_down), wd) * slope).astype(bf16)
    gw_up = contract_rows(third, grad_up).astype(bf16).reshape(2, 2, 2, 2, 2, 32, 1024)
    up_term = flip_x(pick(gw_up, 1 - x, 4, True))
    grad_middle, gain3, shift3, gain2, shift2, bias_out, branch_rows = sum_rows(
        middle_step, after(dot_nt(grad_up, wu), gw_up),
        (middle, branch, grad_out, vectors), (wide,) + (line,) * 5, True, 9)
    branch_rows = branch_rows.reshape(512, width)
    grad_att = dot_nt(branch_rows, wo).astype(bf16)
    down_sum = add_low(pick(gw_down, y, 1, True), down_term)
    down_term = flip_x(pick(down_sum, 1 - x, 2, True))
    grad_packed = exchange(after(grad_att, down_sum), True, 3).reshape(8, 128, 128)
    up_sum = add_low(pick(gw_up, x, 4, True), after(up_term, grad_packed))
    up_term = flip_y(pick(up_sum, 1 - y, 2, True))
    down_sum = add_low(pick(down_sum, x, 2, True), after(down_term, grad_packed))
    down_term = flip_a(pick(down_sum, 1 - a, 0))
    back = attend_back(valid[None], packed, grad_packed)

    up_sum = add_low(pick(up_sum, y, 2, True), up_term)
    gw_out = contract_rows(attended, branch_rows).astype(bf16).reshape(2, 2, 2, 32, width)
    grad_qkv = exchange(after(back, up_sum, down_term).reshape(2, 2, 2, 384, 128), False, 4)
    up_term = flip_a(pick(after(up_sum, grad_qkv), 1 - a, 0))
    gw_qkv = contract_rows(first, grad_qkv).astype(bf16).reshape(2, 2, 2, 2, 2, 32, 768)
    def sums(block):
        return jnp.sum(block.astype(f32), 0, keepdims=True)

    sums_of = [sums(grad_qkv), sums(grad_up), bias_out, bias_down, gain2, gain3, gain4, shift2, shift3, shift4]
    up_sum = (pick(up_sum, a, 0).astype(f32) + up_term.astype(f32)).astype(bf16).reshape(2, 2, 32, 1024)
    r_qkv, r_out, r_up, vectors, input_grad = reduce_all(
        gw_qkv, gw_out, up_sum, dot_nt(grad_qkv, wqkv), tokens[0], grad_middle, vectors, sums_of, 5)
    r_down = (pick(down_sum, a, 0).astype(f32) + down_term.astype(f32)).reshape(128, width)
    index = lax.axis_index("seq") * 2 + x
    small_up = lax.dynamic_slice(vectors, (12 + index // 8, index % 8 * 128), (1, 128)).reshape(128)
    vectors = lax.dynamic_slice(vectors, (0, index * 32), (12, 32))

    return (
        output[None], input_grad[None], r_qkv, vectors[:2], r_out,
        vectors[2], r_up, small_up, r_down, vectors[3], vectors[4:8], vectors[8:12])


def solution(mesh):
    return jax.shard_map(
        fast_body if is_small(mesh) else body,
        mesh=mesh,
        in_specs=(
            P("dp", "seq", None),
            P("dp", "seq", None),
            P(),
            P(),
            P(("seq", "dp"), None),
            P(None, ("seq", "dp")),
            P(("seq", "dp"), None),
            P(("seq", "dp")),
            P(("seq", "dp"), None),
            P(("seq", "dp")),
            P(("seq", "dp"), None),
            P(("seq", "dp")),
            P(None, ("seq", "dp")),
            P(None, ("seq", "dp")),
        ),
        out_specs=(
            P("dp", "seq", None),
            P("dp", "seq", None),
            P(("seq", "dp"), None),
            P(None, ("seq", "dp")),
            P(("seq", "dp"), None),
            P(("seq", "dp")),
            P(("seq", "dp"), None),
            P(("seq", "dp")),
            P(("seq", "dp"), None),
            P(("seq", "dp")),
            P(None, ("seq", "dp")),
            P(None, ("seq", "dp")),
        ),
        check_vma=False,
    )
```
